32 devices in a mesh: clip: 4 (over x, core), seq: 8 (over z, y).
Axes of the slice: x: 2, y: 2, z: 4, core: 2. Of those that a mesh axis runs over, the one named last changes fastest.
Arguments:
- tokens: bfloat16 [8, 4096, 1024], P('clip', 'seq'), may hold values from -6 to 6
- ctx_count: int32 [8], P('clip'), may hold values from 1 to 15
- noise_level: int32 [8, 16], P('clip'), may hold values from 1 to 999
- mod_weight: bfloat16 [1024, 6144], P(('clip', 'seq')), may hold values from -0.1875 to 0.1875
- mod_bias: bfloat16 [6144], P(('clip', 'seq')), may hold values from -3 to 3
- qkv_weight: bfloat16 [1024, 3072], P(('clip', 'seq')), may hold values from -0.1875 to 0.1875
- qkv_bias: bfloat16 [3072], P(('clip', 'seq')), may hold values from -2 to 2
- out_weight: bfloat16 [1024, 1024], P(('clip', 'seq')), may hold values from -6 to 6
- out_bias: bfloat16 [1024], P(('clip', 'seq')), may hold values from -3 to 3
- up_weight: bfloat16 [1024, 4096], P(('clip', 'seq')), may hold values from -0.1875 to 0.1875
- up_bias: bfloat16 [4096], P(('clip', 'seq')), may hold values from -3 to 3
- down_weight: bfloat16 [4096, 1024], P(('clip', 'seq')), may hold values from -0.09375 to 0.09375
- down_bias: bfloat16 [1024], P(('clip', 'seq')), may hold values from -3 to 3
- cotangent: bfloat16 [8, 4096, 1024], P('clip', 'seq'), may hold values from -6 to 6
Outputs:
- output: bfloat16 [8, 4096, 1024], P('clip', 'seq')
- grad_tokens: float32 [8, 4096, 1024], P('clip', 'seq')
- grad_mod_weight: float32 [1024, 6144], P(('clip', 'seq'))
- grad_mod_bias: float32 [6144], P(('clip', 'seq'))
- grad_qkv_weight: float32 [1024, 3072], P(('clip', 'seq'))
- grad_qkv_bias: float32 [3072], P(('clip', 'seq'))
- grad_out_weight: float32 [1024, 1024], P(('clip', 'seq'))
- grad_out_bias: float32 [1024], P(('clip', 'seq'))
- grad_up_weight: float32 [1024, 4096], P(('clip', 'seq'))
- grad_up_bias: float32 [4096], P(('clip', 'seq'))
- grad_down_weight: float32 [4096, 1024], P(('clip', 'seq'))
- grad_down_bias: float32 [1024], P(('clip', 'seq'))
The draws below stay inside these ranges and needn't reach their ends.
All inputs are finite; a program needn't handle non-finite values.
Results may differ from the reference program's by a relative error of at most 0.014.
The reference program's roundings to bfloat16 on the way count: a program that leaves them out, or rounds other values in their place, can miss the bound.
Values may be sent and summed in bfloat16 or wider, within the bound.
No kernel may reach another device: no remote copies, remote signals or barrier semaphores. Data moves between devices by JAX's collectives and lax.ppermute only.
A program may use at most 320 MiB of HBM per device.

```python
import math
import jax
import jax.numpy as jnp
from jax import lax

D = 1024
HEADS = 16
HEAD_DIM = 64
FF = 4096
FRAMES = 16
PATCHES = 256
LEVELS = 1000
SEQ_LEN = 4096
CLIPS = 8


def with_ends(values, stream_key, least, high):
    extent = values.shape
    spot = [jax.random.randint(jax.random.fold_in(stream_key, axis), (), 0, extent[axis]) for axis in range(len(extent))]
    values = values.at[tuple(spot)].set(least)
    longest = extent.index(max(extent))
    spot[longest] = (spot[longest] + 1) % extent[longest]
    return values.at[tuple(spot)].set(high)


def block_levels(key, dims, cuts, smallest, largest):
    level = 1.0
    for dim, blocks in cuts:
        draws = jax.random.uniform(jax.random.fold_in(jax.random.fold_in(key, 6), dim), (blocks,), jnp.float32, smallest / len(cuts), largest / len(cuts))
        level = level * jnp.repeat(jnp.exp(draws), dims[dim] // blocks).reshape((-1,) + (1,) * (len(dims) - 1 - dim))
    return level


def gaussian(own_key, dims, scale, bound, cuts=(), kind=jnp.bfloat16):
    loudness = block_levels(own_key, dims, cuts, -0.22, 0.18) if cuts else 1.0
    values = jax.random.normal(own_key, dims, jnp.float32) * scale * loudness
    return jnp.minimum(jnp.maximum(values, -bound), bound).astype(kind)


def setup_inputs(seed: int = 0) -> dict:
    key_list = jax.random.split(jax.random.key(seed), 15)
    return {
        "tokens": gaussian(key_list[0], (CLIPS, SEQ_LEN, D), 1.0, 6.0, ((0, 4), (1, 8))),
        "ctx_count": with_ends(jax.random.randint(key_list[1], (CLIPS,), 1, FRAMES), jax.random.fold_in(key_list[1], 1), 1, FRAMES - 1).astype(jnp.int32),
        "noise_level": with_ends(jax.random.randint(key_list[2], (CLIPS, FRAMES), 1, LEVELS), jax.random.fold_in(key_list[2], 1), 1, LEVELS - 1).astype(jnp.int32),
        "mod_weight": gaussian(key_list[3], (D, 6 * D), D ** -0.5, 0.1875, ((0, 32),)),
        "mod_bias": gaussian(key_list[4], (6 * D,), 0.5, 3.0, ((0, 32),)),
        "qkv_weight": gaussian(key_list[5], (D, 3 * D), D ** -0.5, 0.1875, ((0, 32),)),
        "qkv_bias": gaussian(key_list[6], (3 * D,), 0.3, 2.0, ((0, 32),)),
        "out_weight": gaussian(key_list[7], (D, D), (max(D * 2 // SEQ_LEN, 1)) ** -0.5, 6.0, ((0, 32),)),
        "out_bias": gaussian(key_list[8], (D,), 0.5, 3.0, ((0, 32),)),
        "up_weight": gaussian(key_list[9], (D, FF), D ** -0.5, 0.1875, ((0, 32),)),
        "up_bias": gaussian(key_list[10], (FF,), 0.5, 3.0, ((0, 32),)),
        "down_weight": gaussian(key_list[11], (FF, D), FF ** -0.5, 0.09375, ((0, 32),)),
        "down_bias": gaussian(key_list[12], (D,), 0.5, 3.0, ((0, 32),)),
        "cotangent": gaussian(key_list[13], (CLIPS, SEQ_LEN, D), 1.0, 6.0, ((0, 4), (1, 8))),
    }


@jax.custom_vjp
def low(v):
    return lax.optimization_barrier(v.astype(jnp.bfloat16)).astype(jnp.float32)

@jax.custom_vjp
def low_back(v):
    return v

def low_keep(v):
    return (low(v), None)

def low_pass(kept, grad):
    return (grad,)

def back_keep(v):
    return (v, None)

def back_low(kept, grad):
    return (low(grad),)
low.defvjp(low_keep, low_pass)
low_back.defvjp(back_keep, back_low)
highest = lax.Precision.HIGHEST

def layer_norm(values):
    centre = values - lax.optimization_barrier(jnp.mean(values, axis=-1, keepdims=True))
    spread = lax.optimization_barrier(jnp.mean(centre * centre, axis=-1, keepdims=True))
    return centre * lax.rsqrt(spread + 1e-06)

def modulate(values, shifts, scales):
    return layer_norm(values) * (1.0 + scales) + shifts

def level_embed(levels, embed_width):
    half_width = embed_width // 2
    freqs = jnp.exp(-math.log(10000.0) * jnp.arange(half_width, dtype=jnp.float32) / half_width)
    angles = levels.astype(jnp.float32)[..., None] * freqs
    return jnp.concatenate([jnp.sin(angles), jnp.cos(angles)], axis=-1)

def rotary_tables(positions):
    half_dim = HEAD_DIM // 2
    freqs = jnp.exp(-math.log(10000.0) * 2.0 * jnp.arange(half_dim, dtype=jnp.float32) / HEAD_DIM)
    angles = positions.astype(jnp.float32)[:, None] * freqs[None, :]
    return (jnp.cos(angles), jnp.sin(angles))

def rotate(values, cosine, sine):
    heads_view = values.reshape(values.shape[:-1] + (HEADS, HEAD_DIM))
    half_dim = HEAD_DIM // 2
    first_half = heads_view[..., :half_dim]
    second_half = heads_view[..., half_dim:]
    cos_part = cosine[:, None, :]
    sin_part = sine[:, None, :]
    turned = jnp.concatenate([first_half * cos_part - second_half * sin_part, second_half * cos_part + first_half * sin_part], axis=-1)
    return turned.reshape(values.shape)

def attention(queries, keys_in, vals_in):
    seq_total = queries.shape[0]
    block_rows = min(512, seq_total)
    block_count = seq_total // block_rows
    score_scale = 1.0 / math.sqrt(HEAD_DIM)
    frames_all = jnp.arange(seq_total, dtype=jnp.int32) // PATCHES
    key_heads = keys_in.reshape(seq_total, HEADS, HEAD_DIM)
    val_heads = vals_in.reshape(seq_total, HEADS, HEAD_DIM)

    def one_block(pieces):
        query_block, query_frame = pieces
        query_heads = query_block.reshape(block_rows, HEADS, HEAD_DIM)
        scores = jnp.einsum('qhd,khd->hqk', query_heads, key_heads, precision=highest) * score_scale
        scores = low_back(scores)
        allowed = frames_all[None, :] <= query_frame[:, None]
        scores = jnp.where(allowed[None], scores, -1e+30)
        probs = low(jax.nn.softmax(scores, axis=-1))
        mixed = jnp.einsum('hqk,khd->qhd', probs, val_heads, precision=highest)
        return mixed.reshape(block_rows, HEADS * HEAD_DIM)
    outputs = lax.map(jax.checkpoint(one_block), (queries.reshape(block_count, block_rows, -1), frames_all.reshape(block_count, block_rows)))
    return outputs.reshape(seq_total, -1)

def block_forward(tokens_in, params, levels):
    mod_weight, mod_bias, qkv_weight, qkv_bias, out_weight, out_bias, up_weight, up_bias, down_weight, down_bias = params
    cond = low(jax.nn.silu(level_embed(levels, D)))
    modulation = jnp.dot(cond, mod_weight, precision=highest) + mod_bias
    frame_ids = jnp.arange(SEQ_LEN, dtype=jnp.int32) // PATCHES
    per_token = modulation[frame_ids]
    shift_one, scale_one, gate_one, shift_two, scale_two, gate_two = jnp.split(per_token, 6, axis=-1)
    normed = low(modulate(tokens_in, shift_one, scale_one))
    projected = low_back(jnp.dot(normed, qkv_weight, precision=highest) + qkv_bias)
    query_raw, key_raw, value_raw = jnp.split(projected, 3, axis=-1)
    cosine, sine = rotary_tables(jnp.arange(SEQ_LEN, dtype=jnp.int32))
    queries = low(rotate(query_raw, cosine, sine))
    keys_rot = low(rotate(key_raw, cosine, sine))
    values = low(value_raw)
    mixed = low_back(low(attention(queries, keys_rot, values)))
    attn_out = low_back(jnp.dot(mixed, out_weight, precision=highest) + out_bias)
    resid = tokens_in + gate_one * attn_out
    normed_two = low(modulate(resid, shift_two, scale_two))
    hidden = low_back(jnp.dot(normed_two, up_weight, precision=highest) + up_bias)
    active = low(jax.nn.gelu(hidden))
    mlp_out = low_back(jnp.dot(active, down_weight, precision=highest) + down_bias)
    return resid + gate_two * mlp_out

def reference(tokens, ctx_count, noise_level, mod_weight, mod_bias, qkv_weight, qkv_bias, out_weight, out_bias, up_weight, up_bias, down_weight, down_bias, cotangent):
    params = tuple((piece.astype(jnp.float32) for piece in (mod_weight, mod_bias, qkv_weight, qkv_bias, out_weight, out_bias, up_weight, up_bias, down_weight, down_bias)))
    frame_index = jnp.arange(FRAMES, dtype=jnp.int32)

    def per_clip(carry, inputs):
        clip_tokens, clip_ctx, clip_noise, clip_cot = inputs
        levels = jnp.where(frame_index < clip_ctx, 0, clip_noise).astype(jnp.int32)

        def forward(tokens_val, params_val):
            return block_forward(tokens_val, params_val, levels)
        result, pull = jax.vjp(forward, clip_tokens.astype(jnp.float32), params)
        d_tokens, d_params = pull(clip_cot.astype(jnp.float32))
        carry = jax.tree.map(jnp.add, carry, d_params)
        return (carry, (result.astype(jnp.bfloat16), d_tokens))
    zeros = tuple((jnp.zeros_like(piece) for piece in params))
    grads, (outputs, grad_tokens) = lax.scan(per_clip, zeros, (tokens, ctx_count, noise_level, cotangent))
    return (outputs, grad_tokens, grads[0], grads[1], grads[2], grads[3], grads[4], grads[5], grads[6], grads[7], grads[8], grads[9])
```

```python
import functools
import math

import jax
import jax.numpy as jnp
from jax import lax
from jax.experimental import pallas as pl
from jax.experimental.pallas import tpu as pltpu
from jax.sharding import PartitionSpec as P

HEADS = 16
HEAD_DIM = 64
FRAMES = 16
PATCHES = 256
BOTH = ("clip", "seq")
NT = (((1,), (1,)), ((), ()))
NN = (((1,), (0,)), ((), ()))
TN = (((0,), (0,)), ((), ()))
bf16 = jnp.bfloat16
f32 = jnp.float32
highest = lax.Precision.HIGHEST


def dot(left, right, dims=NN):
    return lax.dot_general(left, right, dims, preferred_element_type=f32)


def swap_bit(value, axis, bit):
    count = lax.axis_size(axis)
    return lax.ppermute(value, axis, [(i, i ^ bit) for i in range(count)])


def own_bit(axis, bit):
    return (lax.axis_index(axis) // bit) % 2


def axis_bits(axis):
    bits = []
    bit = 1
    while bit < lax.axis_size(axis):
        bits.append((axis, bit))
        bit *= 2
    return bits[::-1]


def exchange_order(bits):
    return sorted(range(len(bits)), key=lambda place: bits[place])


def mesh_bits():
    return axis_bits("clip") + axis_bits("seq")


def halve_sum(parts, bits, wire=f32):
    parts = parts.reshape((2,) * len(bits) + parts.shape[1:])
    for place in exchange_order(bits):
        axis, bit = bits[place]
        mine = own_bit(axis, bit)
        keep = lax.dynamic_index_in_dim(parts, mine, place)
        send = lax.dynamic_index_in_dim(parts, 1 - mine, place)
        parts = keep + swap_bit(send.astype(wire), axis, bit).astype(f32)
    return parts.reshape(parts.shape[len(bits) :])


def double_rows(row, bits):
    rows = row[None]
    for axis, bit in reversed(bits):
        other = swap_bit(rows, axis, bit)
        low = own_bit(axis, bit) == 0
        rows = jnp.concatenate([jnp.where(low, rows, other), jnp.where(low, other, rows)], axis=0)
    return rows


def weight_grad(left, right):
    tokens, rows = left.shape
    quarter = rows // lax.axis_size("clip")
    mine = lax.axis_index("clip")

    def part(flip):
        piece = lax.dynamic_slice_in_dim(left, (mine ^ flip) * quarter, quarter, 1)
        return dot(piece, right, TN)

    far = swap_bit(part(3).astype(bf16), "clip", 1)
    near = swap_bit(part(1).astype(bf16), "clip", 1)
    across = swap_bit((part(2) + far.astype(f32)).astype(bf16), "clip", 2)
    total = part(0) + near.astype(f32) + across.astype(f32)
    return halve_sum(total.reshape((lax.axis_size("seq"), -1, right.shape[1])), axis_bits("seq"), bf16)


def norm_parts(values):
    centre = values - jnp.mean(values, axis=-1, keepdims=True)
    spread = jnp.mean(centre * centre, axis=-1, keepdims=True)
    inverse = lax.rsqrt(spread + 1e-06)
    return centre * inverse, inverse


def norm_back(unit, inverse, grad, scales):
    scaled = grad * (1.0 + scales)
    mean = jnp.mean(scaled, axis=-1, keepdims=True)
    along = jnp.mean(scaled * unit, axis=-1, keepdims=True)
    return inverse * (scaled - mean - unit * along)


def rotary_lanes(positions, width):
    half = HEAD_DIM // 2
    lane = jnp.arange(width, dtype=jnp.int32) % HEAD_DIM
    freqs = jnp.exp(-math.log(10000.0) * 2.0 * (lane % half).astype(f32) / HEAD_DIM)
    angles = positions.astype(f32)[:, None] * freqs[None, :]
    sign = jnp.where(lane < half, -1.0, 1.0).astype(f32)
    return jnp.cos(angles), jnp.sin(angles) * sign[None, :]


def partner(values):
    width = values.shape[1]
    half = HEAD_DIM // 2
    lane = lax.broadcasted_iota(jnp.int32, (1, width), 1) % HEAD_DIM
    return jnp.where(lane < half, pltpu.roll(values, width - half, 1), pltpu.roll(values, half, 1))


def project_kernel(x_ref, wq_ref, wk_ref, wv_ref, bq_ref, bk_ref, bv_ref, cos_ref, sin_ref, out_ref, *, span):
    x = x_ref[...]
    cosine, sine = cos_ref[...], sin_ref[...]
    groups = wq_ref.shape[1] // span
    for place, (w_ref, b_ref) in enumerate(((wq_ref, bq_ref), (wk_ref, bk_ref), (wv_ref, bv_ref))):
        value = dot(x, w_ref[...]) + b_ref[...]
        if place < 2:
            value = value * cosine + partner(value) * sine
        value = value.astype(bf16)
        for g in range(groups):
            out_ref[g, :, place * span : (place + 1) * span] = value[:, g * span : (g + 1) * span]


def project(x, weight, bias, cosine, sine, groups):
    rows, width = x.shape
    span = width // groups
    block = max(span, 256)
    per_step = block // span
    steps = groups // per_step
    weight_specs = [
        pl.BlockSpec((width, block), functools.partial(lambda p, j: (0, p * steps + j), p)) for p in range(3)
    ]
    bias_specs = [pl.BlockSpec((1, block), functools.partial(lambda p, j: (0, p * steps + j), p)) for p in range(3)]
    whole = pl.BlockSpec((rows, block), lambda j: (0, 0))
    return pl.pallas_call(
        functools.partial(project_kernel, span=span),
        grid=(steps,),
        in_specs=[pl.BlockSpec((rows, width), lambda j: (0, 0))] + weight_specs + bias_specs + [whole, whole],
        out_specs=pl.BlockSpec((per_step, rows, 3 * span), lambda j: (j, 0, 0)),
        out_shape=jax.ShapeDtypeStruct((groups, rows, 3 * span), bf16),
        compiler_params=pltpu.CompilerParams(vmem_limit_bytes=32 << 20),
        cost_estimate=pl.CostEstimate(
            flops=2 * rows * width * 3 * width, bytes_accessed=2 * width * 3 * width + 8 * rows * width, transcendentals=0
        ),
        name="project",
    )(x, weight, weight, weight, bias, bias, bias, cosine, sine)


def attend_kernel(qkv_ref, mix_ref, full_ref, log_ref, vt_ref, *, total, span, block):
    heads = span // HEAD_DIM
    head = lax.broadcasted_iota(jnp.int32, (1, span), 1) // HEAD_DIM
    key_frame = lax.broadcasted_iota(jnp.int32, (block, block), 0) // PATCHES
    query_frame = lax.broadcasted_iota(jnp.int32, (block, block), 1) // PATCHES
    kept = key_frame <= query_frame

    def flip(j, carry):
        rows = pl.ds(pl.multiple_of(j * block, block), block)
        vt_ref[:, rows] = jnp.transpose(qkv_ref[rows, 2 * span : 3 * span])
        return carry

    lax.fori_loop(0, total // block, flip, 0)

    def query_block(i, carry):
        rows = pl.ds(pl.multiple_of(i * block, block), block)
        query = qkv_ref[rows, 0:span] * jnp.asarray(HEAD_DIM**-0.5, bf16)
        queries = [jnp.where(head == h, query, jnp.zeros_like(query)) for h in range(heads)]

        def step(j, state, masked):
            peaks, sums, mixes = state
            columns = pl.ds(pl.multiple_of(j * block, block), block)
            key = qkv_ref[columns, span : 2 * span]
            new = ([], [], [])
            for h in range(heads):
                scores = dot(key, queries[h], NT)
                if masked:
                    scores = jnp.where(kept, scores, -1e30)
                peak = jnp.maximum(peaks[h], jnp.max(scores, axis=0, keepdims=True))
                raised = jnp.exp(scores - peak)
                fade = jnp.exp(peaks[h] - peak)
                new[0].append(peak)
                new[1].append(fade * sums[h] + jnp.sum(raised, axis=0, keepdims=True))
                term = dot(vt_ref[h * HEAD_DIM : (h + 1) * HEAD_DIM, columns], raised.astype(bf16))
                new[2].append(mixes[h] * fade + term)
            return tuple(map(tuple, new))

        state = (
            tuple(jnp.full((1, block), -1e30, f32) for _ in range(heads)),
            tuple(jnp.zeros((1, block), f32) for _ in range(heads)),
            tuple(jnp.zeros((HEAD_DIM, block), f32) for _ in range(heads)),
        )
        state = lax.fori_loop(0, i, lambda j, s: step(j, s, False), state)
        peaks, sums, mixes = step(i, state, True)
        mixed = jnp.transpose(jnp.concatenate([mixes[h] / sums[h] for h in range(heads)], axis=0))
        full_ref[rows, :] = mixed
        mix_ref[rows, :] = mixed.astype(bf16)
        for h in range(heads):
            log_ref[h : h + 1, rows] = peaks[h] + jnp.log(sums[h])
        return carry

    lax.fori_loop(0, total // block, query_block, 0)


def attend(qkv, span):
    total = qkv.shape[0]
    heads = span // HEAD_DIM
    block = min(1024, total)
    return pl.pallas_call(
        functools.partial(attend_kernel, total=total, span=span, block=block),
        out_shape=(
            jax.ShapeDtypeStruct((total, span), bf16),
            jax.ShapeDtypeStruct((total, span), f32),
            jax.ShapeDtypeStruct((heads, total), f32),
        ),
        scratch_shapes=[pltpu.VMEM((span, total), bf16)],
        compiler_params=pltpu.CompilerParams(vmem_limit_bytes=52 << 20),
        cost_estimate=pl.CostEstimate(
            flops=8 * total * total * span, bytes_accessed=12 * total * span, transcendentals=total * total * heads // 2
        ),
        name="attend",
    )(qkv)


def attend_back_kernel(
    qkv_ref, grad_ref, full_ref, log_ref, cos_ref, sin_ref, out_ref, dq_ref, dk_ref, dv_ref, along_ref, *, total, span, block
):
    heads = span // HEAD_DIM
    scale = HEAD_DIM**-0.5
    head = lax.broadcasted_iota(jnp.int32, (1, span), 1) // HEAD_DIM
    key_frame = lax.broadcasted_iota(jnp.int32, (block, block), 0) // PATCHES
    query_frame = lax.broadcasted_iota(jnp.int32, (block, block), 1) // PATCHES
    kept = key_frame <= query_frame
    blocks = total // block
    dq_ref[...] = jnp.zeros_like(dq_ref)

    def only(value, h):
        return jnp.where(head == h, value, jnp.zeros_like(value))

    def lead(i, carry):
        rows = pl.ds(pl.multiple_of(i * block, block), block)
        product = jnp.transpose(grad_ref[rows, :].astype(f32) * full_ref[rows, :])
        for h in range(heads):
            along_ref[h : h + 1, rows] = jnp.sum(product[h * HEAD_DIM : (h + 1) * HEAD_DIM], axis=0, keepdims=True)
        return carry

    lax.fori_loop(0, blocks, lead, 0)

    def key_block(j, carry):
        columns = pl.ds(pl.multiple_of(j * block, block), block)
        key = qkv_ref[columns, span : 2 * span]
        value = qkv_ref[columns, 2 * span : 3 * span]
        key_flat = jnp.transpose(key)
        dk_ref[...] = jnp.zeros_like(dk_ref)
        dv_ref[...] = jnp.zeros_like(dv_ref)

        def step(i, masked):
            rows = pl.ds(pl.multiple_of(i * block, block), block)
            query = qkv_ref[rows, 0:span] * jnp.asarray(scale, bf16)
            grad = grad_ref[rows, :]
            dk = dv = None
            for h in range(heads):
                query_h, grad_h = only(query, h), only(grad, h)
                scores = dot(key, query_h, NT)
                if masked:
                    scores = jnp.where(kept, scores, -1e30)
                probs = jnp.exp(scores - log_ref[h : h + 1, rows])
                d_probs = dot(value, grad_h, NT)
                d_scores = (probs * (d_probs - along_ref[h : h + 1, rows])).astype(bf16)
                dv_term = dot(probs.astype(bf16), grad_h)
                dk_term = dot(d_scores, query_h)
                band = slice(h * HEAD_DIM, (h + 1) * HEAD_DIM)
                dq_ref[band, rows] += dot(key_flat[band], d_scores)
                dv = dv_term if dv is None else dv + dv_term
                dk = dk_term if dk is None else dk + dk_term
            dv_ref[...] += dv
            dk_ref[...] += dk

        step(j, True)

        def later(i, c):
            step(i, False)
            return c

        lax.fori_loop(j + 1, blocks, later, 0)
        dk = dk_ref[...]
        out_ref[columns, span : 2 * span] = (dk * cos_ref[columns, :] - partner(dk) * sin_ref[columns, :]).astype(bf16)
        out_ref[columns, 2 * span : 3 * span] = dv_ref[...].astype(bf16)
        return carry

    lax.fori_loop(0, blocks, key_block, 0)

    def last(i, carry):
        rows = pl.ds(pl.multiple_of(i * block, block), block)
        dq = jnp.transpose(dq_ref[:, rows]) * scale
        out_ref[rows, 0:span] = (dq * cos_ref[rows, :] - partner(dq) * sin_ref[rows, :]).astype(bf16)
        return carry

    lax.fori_loop(0, blocks, last, 0)


def attend_back(qkv, grad, full, logs, cosine, sine, span):
    total = qkv.shape[0]
    heads = span // HEAD_DIM
    block = min(1024, total)
    return pl.pallas_call(
        functools.partial(attend_back_kernel, total=total, span=span, block=block),
        out_shape=jax.ShapeDtypeStruct((total, 3 * span), bf16),
        scratch_shapes=[
            pltpu.VMEM((span, total), f32),
            pltpu.VMEM((block, span), f32),
            pltpu.VMEM((block, span), f32),
            pltpu.VMEM((heads, total), f32),
        ],
        compiler_params=pltpu.CompilerParams(vmem_limit_bytes=56 << 20),
        cost_estimate=pl.CostEstimate(
            flops=20 * total * total * span, bytes_accessed=26 * total * span, transcendentals=total * total * heads // 2
        ),
        name="attend_back",
    )(qkv, grad, full, logs, cosine, sine)


def gathered_forward(queries, keys, values, allowed):
    def one(pieces):
        q, k, v = pieces
        scores = jnp.where(allowed, dot(q, k, NT) * HEAD_DIM**-0.5, -1e30)
        peak = jnp.max(scores, axis=-1, keepdims=True)
        raised = jnp.exp(scores - peak)
        totals = jnp.sum(raised, axis=-1, keepdims=True)
        return dot((raised / totals).astype(bf16), v), peak + jnp.log(totals)

    return lax.map(one, (queries, keys, values))


def gathered_back(queries, keys, values, grads, logs, allowed):
    scale = HEAD_DIM**-0.5

    def one(pieces):
        q, k, v, grad, log = pieces
        scores = jnp.where(allowed, dot(q, k, NT) * scale, -1e30)
        probs = jnp.exp(scores - log)
        d_probs = dot(grad, v, NT)
        centre = jnp.sum(probs * d_probs, axis=-1, keepdims=True)
        d_scores = (probs * (d_probs - centre)).astype(bf16)
        dv = dot(probs.astype(bf16), grad, TN)
        return dot(d_scores, k) * scale, dot(d_scores, q, TN) * scale, dv

    return lax.map(one, (queries, keys, values, grads, logs))


def body(
    tokens,
    ctx_count,
    noise_level,
    mod_weight,
    mod_bias,
    qkv_weight,
    qkv_bias,
    out_weight,
    out_bias,
    up_weight,
    up_bias,
    down_weight,
    down_bias,
    cotangent,
):
    clips, rows, width = tokens.shape
    seq_devices = lax.axis_size("seq")
    devices = lax.axis_size("clip") * seq_devices
    bits = mesh_bits()
    here = lax.axis_index("clip") * seq_devices + lax.axis_index("seq")
    total = rows * seq_devices
    frames = max(1, rows // PATCHES)
    patch_rows = rows // frames
    by_heads = HEADS % seq_devices == 0
    span = width // seq_devices

    full_qkv = lax.all_gather(qkv_weight, BOTH, axis=0, tiled=True)
    full_out = lax.all_gather(out_weight, BOTH, axis=0, tiled=True)
    full_up = lax.all_gather(up_weight, BOTH, axis=0, tiled=True)
    full_down = lax.all_gather(down_weight, BOTH, axis=0, tiled=True)
    biases = (qkv_bias, out_bias, up_bias, down_bias)
    bias_rows = double_rows(jnp.concatenate(biases).astype(f32), bits)
    full_biases = []
    first = 0
    for piece in biases:
        full_biases.append(bias_rows[:, first : first + piece.shape[0]].reshape(1, -1))
        first += piece.shape[0]
    bias_qkv, bias_out, bias_up, bias_down = full_biases

    plan = jnp.concatenate([ctx_count[:, None], noise_level], axis=1)
    plan = double_rows(plan, axis_bits("clip"))
    levels = jnp.where(jnp.arange(FRAMES, dtype=jnp.int32) < plan[..., :1], 0, plan[..., 1:])
    if rows < PATCHES:
        levels = jnp.repeat(levels, PATCHES // rows, axis=-1)
    levels = levels.reshape(-1, clips, seq_devices, frames).transpose(0, 2, 1, 3)
    depth = mod_weight.shape[0]
    half_width = width // 2
    feature = here * depth + jnp.arange(depth, dtype=jnp.int32)
    freqs = jnp.exp(-math.log(10000.0) * (feature % half_width).astype(f32) / half_width)
    angles = levels.reshape(devices * clips * frames, 1).astype(f32) * freqs
    cond = jax.nn.silu(jnp.where(feature < half_width, jnp.sin(angles), jnp.cos(angles))).astype(bf16)
    mod_width = mod_weight.shape[1]
    bias_place = lax.dynamic_update_slice_in_dim(
        jnp.zeros((mod_width,), f32), mod_bias.astype(f32), here * mod_bias.shape[0], 0
    )
    partial = dot(cond, mod_weight) + bias_place
    modulation = halve_sum(partial.reshape(devices, clips * frames, mod_width), bits)
    modulation = modulation.reshape(clips, frames, 1, mod_width)

    positions = lax.axis_index("seq") * rows + jnp.arange(rows, dtype=jnp.int32)
    cos_local, sin_local = rotary_lanes(positions, max(span, 256))
    if by_heads:
        cos_all, sin_all = rotary_lanes(jnp.arange(total, dtype=jnp.int32), span)
    else:
        key_frame = jnp.arange(total, dtype=jnp.int32) // PATCHES
        allowed = key_frame[None, :] <= (positions // PATCHES)[:, None]

    def flat(value):
        return value.reshape(rows, value.shape[-1])

    def split(value):
        return value.reshape(frames, patch_rows, value.shape[-1])

    def to_heads(value):
        return value.reshape(rows, HEADS, HEAD_DIM).transpose(1, 0, 2)

    saved = []
    for c in range(clips):
        mods = jnp.split(modulation[c], 6, axis=-1)
        tokens_now = split(tokens[c].astype(f32))
        unit, inverse = norm_parts(tokens_now)
        normed = flat((unit * (1.0 + mods[1]) + mods[0]).astype(bf16))
        if by_heads:
            sent = project(normed, full_qkv, bias_qkv, cos_local, sin_local, seq_devices)
            qkv = lax.all_to_all(sent, "seq", 0, 0, tiled=True).reshape(total, 3 * span)
            mix, full, logs = attend(qkv, span)
            back = lax.all_to_all(mix.reshape(seq_devices, rows, span), "seq", 0, 0, tiled=True)
            mixed = back.transpose(1, 0, 2).reshape(rows, width)
            kept = (qkv, full, logs)
        else:
            projected = dot(normed, full_qkv) + bias_qkv
            views = []
            for place in range(3):
                view = to_heads(projected[:, place * width : (place + 1) * width])
                if place < 2:
                    cosine, sine = cos_local[:, :HEAD_DIM], sin_local[:, :HEAD_DIM]
                    view = view * cosine + jnp.roll(view, HEAD_DIM // 2, -1) * sine
                views.append(view.astype(bf16))
            queries, keys, values = views
            keys = lax.all_gather(keys, "seq", axis=1, tiled=True)
            values = lax.all_gather(values, "seq", axis=1, tiled=True)
            mix, logs = gathered_forward(queries, keys, values, allowed)
            mixed = mix.transpose(1, 0, 2).reshape(rows, width).astype(bf16)
            kept = (queries, keys, values, logs)
        saved.append((mods, tokens_now, unit, inverse, normed, kept, mixed))

    outputs = []
    middle = []
    for c in range(clips):
        mods, tokens_now, unit, inverse, normed, kept, mixed = saved[c]
        _, _, gate_one, shift_two, scale_two, gate_two = mods
        attn_out = split(dot(mixed, full_out) + bias_out)
        resid = tokens_now + gate_one * attn_out
        unit_two, inverse_two = norm_parts(resid)
        normed_two = flat((unit_two * (1.0 + scale_two) + shift_two).astype(bf16))
        hidden = dot(normed_two, full_up) + bias_up
        active_full, gelu_back = jax.vjp(jax.nn.gelu, hidden)
        active = active_full.astype(bf16)
        mlp_out = split(dot(active, full_down) + bias_down)
        outputs.append(flat((resid + gate_two * mlp_out).astype(bf16)))
        grad_out = split(cotangent[c].astype(f32))
        d_mlp = flat((gate_two * grad_out).astype(bf16))
        d_hidden = gelu_back(dot(d_mlp, full_down, NT))[0].astype(bf16)
        d_normed_two = split(dot(d_hidden, full_up, NT))
        d_resid = grad_out + norm_back(unit_two, inverse_two, d_normed_two, scale_two)
        d_attn = flat((gate_one * d_resid).astype(bf16))
        d_mixed = dot(d_attn, full_out, NT).astype(bf16)
        d_early = jnp.concatenate(
            [
                jnp.sum(d_resid * attn_out, axis=1),
                jnp.sum(d_normed_two, axis=1),
                jnp.sum(d_normed_two * unit_two, axis=1),
                jnp.sum(grad_out * mlp_out, axis=1),
            ],
            axis=-1,
        )
        middle.append((mixed, d_attn, normed_two, d_hidden, active, d_mlp, d_resid, d_mixed, d_early))

    def both(place):
        return jnp.concatenate([m[place] for m in middle], axis=0)

    d_attn_all, d_hidden_all, d_mlp_all = both(1), both(3), both(5)
    grad_down = weight_grad(both(4), d_mlp_all)
    grad_up = weight_grad(both(2), d_hidden_all)
    grad_out_weight = weight_grad(both(0), d_attn_all)
    early_rows = lax.all_gather(both(8), BOTH, axis=0, tiled=True)

    inputs_grad = []
    late = []
    projected_grads = []
    for c in range(clips):
        mods, tokens_now, unit, inverse, normed, kept, mixed = saved[c]
        d_resid, d_mixed = middle[c][6], middle[c][7]
        if by_heads:
            sent = d_mixed.reshape(rows, seq_devices, span).transpose(1, 0, 2)
            grad = lax.all_to_all(sent, "seq", 0, 0, tiled=True).reshape(total, span)
            qkv, full, logs = kept
            d_qkv = attend_back(qkv, grad, full, logs, cos_all, sin_all, span)
            back = lax.all_to_all(d_qkv.reshape(seq_devices, rows, 3 * span), "seq", 0, 0, tiled=True)
            d_projected = back.reshape(seq_devices, rows, 3, span).transpose(1, 2, 0, 3).reshape(rows, 3 * width)
        else:
            queries, keys, values, logs = kept
            dq, dk, dv = gathered_back(queries, keys, values, to_heads(d_mixed), logs, allowed)
            dk = lax.psum_scatter(dk.astype(bf16), "seq", scatter_dimension=1, tiled=True).astype(f32)
            dv = lax.psum_scatter(dv.astype(bf16), "seq", scatter_dimension=1, tiled=True).astype(f32)
            cosine, sine = cos_local[:, :HEAD_DIM], sin_local[:, :HEAD_DIM]
            views = [g * cosine - jnp.roll(g, HEAD_DIM // 2, -1) * sine for g in (dq, dk)] + [dv]
            d_projected = jnp.concatenate([g.transpose(1, 0, 2).reshape(rows, width) for g in views], axis=1).astype(bf16)
        projected_grads.append(d_projected)
        d_normed = split(dot(d_projected, full_qkv, NT))
        inputs_grad.append(flat(d_resid + norm_back(unit, inverse, d_normed, mods[1])))
        late.append(jnp.concatenate([jnp.sum(d_normed, axis=1), jnp.sum(d_normed * unit, axis=1)], axis=-1))

    d_projected_all = jnp.concatenate(projected_grads, axis=0)
    grad_qkv = weight_grad(jnp.concatenate([s[4] for s in saved], axis=0), d_projected_all)
    bias_grads = [
        jnp.sum(g.astype(f32), axis=0).reshape(devices, -1) for g in (d_projected_all, d_attn_all, d_hidden_all, d_mlp_all)
    ]
    bias_sum = halve_sum(jnp.concatenate(bias_grads, axis=1), bits)
    grad_biases = []
    first = 0
    for piece in bias_grads:
        grad_biases.append(bias_sum[first : first + piece.shape[1]])
        first += piece.shape[1]

    late_rows = double_rows(jnp.concatenate(late, axis=0), bits).reshape(-1, 2 * width)
    grad_mod = jnp.concatenate(
        [
            lax.dot_general(cond.astype(f32), r, TN, precision=highest, preferred_element_type=f32)
            for r in (late_rows, early_rows)
        ],
        axis=1,
    )
    mod_sum = jnp.concatenate([jnp.sum(late_rows, axis=0), jnp.sum(early_rows, axis=0)])
    grad_mod_bias = lax.dynamic_slice_in_dim(mod_sum, here * mod_bias.shape[0], mod_bias.shape[0], 0)
    return (
        jnp.stack(outputs),
        jnp.stack(inputs_grad),
        grad_mod,
        grad_mod_bias,
        grad_qkv,
        grad_biases[0],
        grad_out_weight,
        grad_biases[1],
        grad_up,
        grad_biases[2],
        grad_down,
        grad_biases[3],
    )


def solution(mesh):
    token_place = P("clip", "seq", None)
    matrix, vector = P(BOTH, None), P(BOTH)
    weights = (matrix, vector) * 5
    return jax.shard_map(
        body,
        mesh=mesh,
        in_specs=(token_place, P("clip"), P("clip", None)) + weights + (token_place,),
        out_specs=(token_place, token_place) + weights,
        check_vma=False,
    )
```

```python
import functools
import math

import jax
import jax.numpy as jnp
from jax import lax
from jax.experimental import pallas as pl
from jax.experimental.pallas import tpu as pltpu
from jax.sharding import PartitionSpec as P

HEADS = 16
HEAD_DIM = 64
FRAMES = 16
PATCHES = 256
BOTH = ("clip", "seq")
NT = (((1,), (1,)), ((), ()))
NN = (((1,), (0,)), ((), ()))
TN = (((0,), (0,)), ((), ()))
bf16 = jnp.bfloat16
f32 = jnp.float32
highest = lax.Precision.HIGHEST


def dot(left, right, dims=NN):
    return lax.dot_general(left, right, dims, preferred_element_type=f32)


def swap_bit(value, axis, bit):
    count = lax.axis_size(axis)
    return lax.ppermute(value, axis, [(i, i ^ bit) for i in range(count)])


def own_bit(axis, bit):
    return lax.shift_right_logical(lax.axis_index(axis), bit.bit_length() - 1) & 1


def axis_bits(axis):
    bits = []
    bit = 1
    while bit < lax.axis_size(axis):
        bits.append((axis, bit))
        bit *= 2
    return bits[::-1]


def exchange_order(bits):
    return sorted(range(len(bits)), key=lambda place: bits[place])


def mesh_bits():
    return axis_bits("clip") + axis_bits("seq")


def halve_sum(parts, bits, wire=f32):
    parts = parts.reshape((2,) * len(bits) + parts.shape[1:])
    for place in exchange_order(bits):
        axis, bit = bits[place]
        mine = own_bit(axis, bit)
        keep = lax.dynamic_index_in_dim(parts, mine, place)
        send = lax.dynamic_index_in_dim(parts, 1 - mine, place)
        parts = keep + swap_bit(send.astype(wire), axis, bit).astype(f32)
    return parts.reshape(parts.shape[len(bits) :])


def near_order():
    return axis_bits("clip")[::-1] + axis_bits("seq")[::-1]


def halve_rows(parts, bits):
    for axis, bit in bits:
        half = parts.shape[0] // 2
        mine = own_bit(axis, bit)
        keep = lax.dynamic_slice_in_dim(parts, mine * half, half, 0)
        send = lax.dynamic_slice_in_dim(parts, (1 - mine) * half, half, 0)
        parts = keep + swap_bit(send, axis, bit)
    return parts


def spread_rows(rows, bits):
    for axis, bit in reversed(bits):
        other = swap_bit(rows, axis, bit)
        low = own_bit(axis, bit) == 0
        rows = jnp.concatenate([jnp.where(low, rows, other), jnp.where(low, other, rows)], axis=0)
    return rows


def after(value, *others):
    return lax.optimization_barrier((value,) + others)[0]


def double_rows(row, bits):
    rows = row[None]
    for axis, bit in reversed(bits):
        other = swap_bit(rows, axis, bit)
        low = own_bit(axis, bit) == 0
        rows = jnp.concatenate([jnp.where(low, rows, other), jnp.where(low, other, rows)], axis=0)
    return rows


def weight_grad(left, right):
    tokens, rows = left.shape
    quarter = rows // lax.axis_size("clip")
    mine = lax.axis_index("clip")

    def part(flip):
        piece = lax.dynamic_slice_in_dim(left, (mine ^ flip) * quarter, quarter, 1)
        return dot(piece, right, TN)

    far = swap_bit(part(3).astype(bf16), "clip", 1)
    near = swap_bit(part(1).astype(bf16), "clip", 1)
    across = swap_bit((part(2) + far.astype(f32)).astype(bf16), "clip", 2)
    total = part(0) + near.astype(f32) + across.astype(f32)
    return halve_sum(total.reshape((lax.axis_size("seq"), -1, right.shape[1])), axis_bits("seq"), bf16)


def norm_parts(values):
    centre = values - jnp.mean(values, axis=-1, keepdims=True)
    spread = jnp.mean(centre * centre, axis=-1, keepdims=True)
    inverse = lax.rsqrt(spread + 1e-06)
    return centre * inverse, inverse


def norm_back(unit, inverse, grad, scales):
    scaled = grad * (1.0 + scales)
    mean = jnp.mean(scaled, axis=-1, keepdims=True)
    along = jnp.mean(scaled * unit, axis=-1, keepdims=True)
    return inverse * (scaled - mean - unit * along)


def rotary_lanes(positions, width):
    half = HEAD_DIM // 2
    lane = jnp.arange(width, dtype=jnp.int32) % HEAD_DIM
    freqs = jnp.exp(-math.log(10000.0) * 2.0 * (lane % half).astype(f32) / HEAD_DIM)
    angles = positions.astype(f32)[:, None] * freqs[None, :]
    sign = jnp.where(lane < half, -1.0, 1.0).astype(f32)
    return jnp.cos(angles), jnp.sin(angles) * sign[None, :]


def partner(values):
    width = values.shape[1]
    half = HEAD_DIM // 2
    lane = lax.broadcasted_iota(jnp.int32, (1, width), 1) % HEAD_DIM
    return jnp.where(lane < half, pltpu.roll(values, width - half, 1), pltpu.roll(values, half, 1))


def project_kernel(
    token_ref, mod_ref, wq_ref, wk_ref, wv_ref, bq_ref, bk_ref, bv_ref, cos_ref, sin_ref, out_ref, normed_ref, *, span
):
    frames = mod_ref.shape[1]
    patch = token_ref.shape[0] // frames

    @pl.when(pl.program_id(0) == 0)
    def _():
        for f in range(frames):
            rows = slice(f * patch, (f + 1) * patch)
            unit, _ = norm_parts(token_ref[rows, :].astype(f32))
            normed_ref[rows, :] = (unit * (1.0 + mod_ref[1, f : f + 1, :]) + mod_ref[0, f : f + 1, :]).astype(bf16)

    x = normed_ref[...]
    cosine, sine = cos_ref[...], sin_ref[...]
    groups = wq_ref.shape[1] // span
    for place, (w_ref, b_ref) in enumerate(((wq_ref, bq_ref), (wk_ref, bk_ref), (wv_ref, bv_ref))):
        value = dot(x, w_ref[...]) + b_ref[...]
        if place < 2:
            value = value * cosine + partner(value) * sine
        value = value.astype(bf16)
        for g in range(groups):
            out_ref[g, :, place * span : (place + 1) * span] = value[:, g * span : (g + 1) * span]


def whole_block(shape):
    return pl.BlockSpec(shape, lambda j: (0,) * len(shape))


def column_specs(height, block, steps):
    return [pl.BlockSpec((height, block), functools.partial(lambda p, j: (0, p * steps + j), p)) for p in range(3)]


def project(tokens, mods, weight, bias, cosine, sine, groups):
    rows, width = tokens.shape
    span = width // groups
    block = max(span, 256)
    per_step = block // span
    steps = groups // per_step
    return pl.pallas_call(
        functools.partial(project_kernel, span=span),
        grid=(steps,),
        in_specs=[whole_block((rows, width)), whole_block(mods.shape)]
        + column_specs(width, block, steps)
        + column_specs(1, block, steps)
        + [whole_block((rows, block))] * 2,
        out_specs=(pl.BlockSpec((per_step, rows, 3 * span), lambda j: (j, 0, 0)), whole_block((rows, width))),
        out_shape=(
            jax.ShapeDtypeStruct((groups, rows, 3 * span), bf16),
            jax.ShapeDtypeStruct((rows, width), bf16),
        ),
        compiler_params=pltpu.CompilerParams(vmem_limit_bytes=32 << 20),
        cost_estimate=pl.CostEstimate(
            flops=6 * rows * width * width, bytes_accessed=6 * width * width + 10 * rows * width, transcendentals=0
        ),
        name="project",
    )(tokens, mods, weight, weight, weight, bias, bias, bias, cosine, sine)


def project_back_kernel(
    back_ref, wq_ref, wk_ref, wv_ref, token_ref, scale_ref, resid_ref, grad_ref, proj_ref, sums_ref, bias_ref, acc_ref, *, span
):
    frames = scale_ref.shape[0]
    rows_all, width = token_ref.shape
    patch = rows_all // frames
    step = pl.program_id(0)
    block = wq_ref.shape[1]

    @pl.when(step == 0)
    def _():
        acc_ref[...] = jnp.zeros_like(acc_ref)

    for place, w_ref in enumerate((wq_ref, wk_ref, wv_ref)):
        band = slice(place * span, (place + 1) * span)
        piece = jnp.concatenate([back_ref[g, :, band] for g in range(block // span)], axis=1)
        columns = pl.ds(pl.multiple_of(place * width + step * block, block), block)
        proj_ref[:, columns] = piece
        bias_ref[:, columns] = jnp.sum(piece.astype(f32), axis=0, keepdims=True)
        acc_ref[...] += dot(piece, w_ref[...], NT)

    @pl.when(step == pl.num_programs(0) - 1)
    def _():
        for f in range(frames):
            rows = slice(f * patch, (f + 1) * patch)
            unit, inverse = norm_parts(token_ref[rows, :].astype(f32))
            grad = acc_ref[rows, :]
            grad_ref[rows, :] = resid_ref[rows, :] + norm_back(unit, inverse, grad, scale_ref[f : f + 1, :])
            sums_ref[0, f : f + 1, :] = jnp.sum(grad, axis=0, keepdims=True)
            sums_ref[1, f : f + 1, :] = jnp.sum(grad * unit, axis=0, keepdims=True)


def project_back(back, weight, tokens, scales, d_resid):
    groups, rows, _ = back.shape
    width = tokens.shape[1]
    span = width // groups
    block = max(span, 256)
    per_step = block // span
    steps = groups // per_step
    return pl.pallas_call(
        functools.partial(project_back_kernel, span=span),
        grid=(steps,),
        in_specs=[pl.BlockSpec((per_step, rows, 3 * span), lambda j: (j, 0, 0))]
        + column_specs(width, block, steps)
        + [whole_block((rows, width)), whole_block(scales.shape), whole_block((rows, width))],
        out_specs=(
            whole_block((rows, width)),
            whole_block((rows, 3 * width)),
            whole_block((2,) + scales.shape),
            whole_block((1, 3 * width)),
        ),
        out_shape=(
            jax.ShapeDtypeStruct((rows, width), f32),
            jax.ShapeDtypeStruct((rows, 3 * width), bf16),
            jax.ShapeDtypeStruct((2,) + scales.shape, f32),
            jax.ShapeDtypeStruct((1, 3 * width), f32),
        ),
        scratch_shapes=[pltpu.VMEM((rows, width), f32)],
        compiler_params=pltpu.CompilerParams(vmem_limit_bytes=40 << 20),
        cost_estimate=pl.CostEstimate(
            flops=6 * rows * width * width, bytes_accessed=6 * width * width + 22 * rows * width, transcendentals=0
        ),
        name="project_back",
    )(back, weight, weight, weight, tokens, scales, d_resid)


GELU_RATE = math.sqrt(2.0 / math.pi)
GELU_CUBE = 0.044715


def middle_kernel(
    back_ref,
    token_ref,
    cot_ref,
    mod_ref,
    wo_ref,
    bo_ref,
    up_ref,
    bup_ref,
    down_ref,
    bdown_ref,
    out_ref,
    dres_ref,
    mixed_ref,
    normed_ref,
    act_ref,
    dhid_ref,
    dmlp_ref,
    dattn_ref,
    dmix_ref,
    sums_ref,
    bup_sum_ref,
    bsum_ref,
    attn_ref,
    res_ref,
    mlp_ref,
    dn_ref,
):
    groups, rows_all, span = back_ref.shape
    width = token_ref.shape[1]
    frames = mod_ref.shape[1]
    patch = rows_all // frames
    step = pl.program_id(0)

    @pl.when(step == 0)
    def _():
        for g in range(groups):
            mixed_ref[:, g * span : (g + 1) * span] = back_ref[g]
        attn_ref[...] = dot(mixed_ref[...], wo_ref[...].reshape(width, width)) + bo_ref[...]
        for f in range(frames):
            rows = slice(f * patch, (f + 1) * patch)
            resid = token_ref[rows, :].astype(f32) + mod_ref[0, f : f + 1, :] * attn_ref[rows, :]
            res_ref[rows, :] = resid
            unit, _ = norm_parts(resid)
            normed_ref[rows, :] = (unit * (1.0 + mod_ref[2, f : f + 1, :]) + mod_ref[1, f : f + 1, :]).astype(bf16)
            dmlp_ref[rows, :] = (mod_ref[3, f : f + 1, :] * cot_ref[rows, :].astype(f32)).astype(bf16)
        mlp_ref[...] = jnp.zeros_like(mlp_ref)
        dn_ref[...] = jnp.zeros_like(dn_ref)

    up = up_ref[...].reshape(width, -1)
    down = down_ref[...].reshape(-1, width)
    hidden = dot(normed_ref[...], up) + bup_ref[...]
    square = hidden * hidden
    bend = jnp.tanh(GELU_RATE * (hidden + GELU_CUBE * (square * hidden)))
    share = 0.5 * (1.0 + bend)
    active = (hidden * share).astype(bf16)
    act_ref[...] = active
    mlp_ref[...] += dot(active, down)
    slope = share + 0.5 * hidden * (1.0 - bend * bend) * (GELU_RATE + (3.0 * GELU_RATE * GELU_CUBE) * square)
    d_hidden = (dot(dmlp_ref[...], down, NT) * slope).astype(bf16)
    dhid_ref[...] = d_hidden
    bup_sum_ref[...] = jnp.sum(d_hidden.astype(f32), axis=0, keepdims=True)
    dn_ref[...] += dot(d_hidden, up, NT)

    @pl.when(step == pl.num_programs(0) - 1)
    def _():
        bsum = None
        for f in range(frames):
            rows = slice(f * patch, (f + 1) * patch)
            resid = res_ref[rows, :]
            mlp = mlp_ref[rows, :] + bdown_ref[...]
            out_ref[rows, :] = (resid + mod_ref[3, f : f + 1, :] * mlp).astype(bf16)
            cot = cot_ref[rows, :].astype(f32)
            sums_ref[3, f : f + 1, :] = jnp.sum(cot * mlp, axis=0, keepdims=True)
            unit, inverse = norm_parts(resid)
            grad = dn_ref[rows, :]
            sums_ref[1, f : f + 1, :] = jnp.sum(grad, axis=0, keepdims=True)
            sums_ref[2, f : f + 1, :] = jnp.sum(grad * unit, axis=0, keepdims=True)
            d_resid = cot + norm_back(unit, inverse, grad, mod_ref[2, f : f + 1, :])
            dres_ref[rows, :] = d_resid
            sums_ref[0, f : f + 1, :] = jnp.sum(d_resid * attn_ref[rows, :], axis=0, keepdims=True)
            d_attn = (mod_ref[0, f : f + 1, :] * d_resid).astype(bf16)
            dattn_ref[rows, :] = d_attn
            term = jnp.concatenate(
                [
                    jnp.sum(d_attn.astype(f32), axis=0, keepdims=True),
                    jnp.sum(dmlp_ref[rows, :].astype(f32), axis=0, keepdims=True),
                ],
                axis=0,
            )
            bsum = term if bsum is None else bsum + term
        bsum_ref[...] = bsum
        d_mixed = dot(dattn_ref[...], wo_ref[...].reshape(width, width), NT).astype(bf16)
        for g in range(groups):
            dmix_ref[g] = d_mixed[:, g * span : (g + 1) * span]


def middle(back, tokens, cot, mods, packed, biases):
    groups, rows, span = back.shape
    width = tokens.shape[1]
    devices, _, piece, _ = packed.shape
    hidden = 4 * width
    steps = 8
    block = hidden // steps
    halves = width // block
    owners = block // (4 * piece)
    bias_out, bias_up, bias_down = biases
    token_block = whole_block((rows, width))
    hidden_block = pl.BlockSpec((rows, block), lambda j: (0, j))
    return pl.pallas_call(
        middle_kernel,
        grid=(steps,),
        in_specs=[
            whole_block(back.shape),
            token_block,
            token_block,
            whole_block(mods.shape),
            pl.BlockSpec((devices, 1, piece, width), lambda j: (0, 8, 0, 0), pipeline_mode=pl.Buffered(1)),
            whole_block((1, width)),
            pl.BlockSpec((devices, 1, piece, block), lambda j: (0, 4 + j // halves, 0, j % halves)),
            pl.BlockSpec((1, block), lambda j: (0, j)),
            pl.BlockSpec((owners, 4, piece, width), lambda j: (j, 0, 0, 0)),
            whole_block((1, width)),
        ],
        out_specs=(
            token_block,
            token_block,
            token_block,
            token_block,
            hidden_block,
            hidden_block,
            token_block,
            token_block,
            whole_block(back.shape),
            whole_block(mods.shape),
            pl.BlockSpec((1, block), lambda j: (0, j)),
            whole_block((2, width)),
        ),
        out_shape=(
            jax.ShapeDtypeStruct((rows, width), bf16),
            jax.ShapeDtypeStruct((rows, width), f32),
            jax.ShapeDtypeStruct((rows, width), bf16),
            jax.ShapeDtypeStruct((rows, width), bf16),
            jax.ShapeDtypeStruct((rows, hidden), bf16),
            jax.ShapeDtypeStruct((rows, hidden), bf16),
            jax.ShapeDtypeStruct((rows, width), bf16),
            jax.ShapeDtypeStruct((rows, width), bf16),
            jax.ShapeDtypeStruct(back.shape, bf16),
            jax.ShapeDtypeStruct(mods.shape, f32),
            jax.ShapeDtypeStruct((1, hidden), f32),
            jax.ShapeDtypeStruct((2, width), f32),
        ),
        scratch_shapes=[pltpu.VMEM((rows, width), f32)] * 4,
        compiler_params=pltpu.CompilerParams(vmem_limit_bytes=54 << 20),
        cost_estimate=pl.CostEstimate(
            flops=36 * rows * width * width, bytes_accessed=18 * width * width + 50 * rows * width, transcendentals=4 * rows * width
        ),
        name="middle",
    )(back, tokens, cot, mods, packed, bias_out, packed, bias_up, packed, bias_down)


def weight_part_kernel(index_ref, *refs, clips, addends):
    left, right = refs[:clips], refs[clips : 2 * clips]
    extra = refs[2 * clips : 2 * clips + addends]
    out_ref, flat_ref = refs[2 * clips + addends :]
    rows = left[0].shape[0]

    @pl.when(pl.program_id(1) == 0)
    def _():
        for c in range(clips):
            flat_ref[:, c * rows : (c + 1) * rows] = jnp.transpose(left[c][...])

    total = dot(flat_ref[:, 0:rows], right[0][...])
    for c in range(1, clips):
        total += dot(flat_ref[:, c * rows : (c + 1) * rows], right[c][...])
    for ref in extra:
        total += ref[0].astype(f32)
    out_ref[0] = total.astype(out_ref.dtype)


def weight_part(left, right, quarters, addends, kind):
    rows, height = left[0].shape
    columns = right[0].shape[1]
    quarter = height // lax.axis_size("clip")
    block = 512
    count = quarters.shape[0]
    in_specs = [pl.BlockSpec((rows, quarter), lambda i, j, q: (0, q[i]))] * len(left)
    in_specs += [pl.BlockSpec((rows, block), lambda i, j, q: (0, j))] * len(right)
    in_specs += [
        pl.BlockSpec((1, quarter, block), functools.partial(lambda place, i, j, q: (place, 0, j), place)) for _, place in addends
    ]
    return pl.pallas_call(
        functools.partial(weight_part_kernel, clips=len(left), addends=len(addends)),
        grid_spec=pltpu.PrefetchScalarGridSpec(
            num_scalar_prefetch=1,
            grid=(count, columns // block),
            in_specs=in_specs,
            out_specs=pl.BlockSpec((1, quarter, block), lambda i, j, q: (i, 0, j)),
            scratch_shapes=[pltpu.VMEM((quarter, len(left) * rows), bf16)],
        ),
        out_shape=jax.ShapeDtypeStruct((count, quarter, columns), kind),
        compiler_params=pltpu.CompilerParams(vmem_limit_bytes=32 << 20),
        cost_estimate=pl.CostEstimate(
            flops=2 * count * len(left) * rows * quarter * columns,
            bytes_accessed=len(left) * rows * (quarter + columns) * 2 + 4 * count * quarter * columns,
            transcendentals=0,
        ),
        name="weight_part",
    )(quarters, *left, *right, *[array for array, _ in addends])


def weight_grad_kernels(left, right):
    mine = lax.axis_index("clip").astype(jnp.int32)

    def quarters(*flips):
        return jnp.stack([mine ^ flip for flip in flips])

    core = swap_bit(weight_part(left, right, quarters(3, 1), (), bf16), "clip", 1)
    across = swap_bit(weight_part(left, right, quarters(2), ((core, 0),), bf16), "clip", 2)
    total = weight_part(left, right, quarters(0), ((core, 1), (across, 0)), f32)
    return halve_sum(total.reshape((lax.axis_size("seq"), -1, right[0].shape[1])), axis_bits("seq"), bf16)


def attend_kernel(qkv_ref, mix_ref, full_ref, log_ref, vt_ref, *, total, span, block):
    heads = span // HEAD_DIM
    head = lax.broadcasted_iota(jnp.int32, (1, span), 1) // HEAD_DIM
    key_frame = lax.broadcasted_iota(jnp.int32, (block, block), 0) // PATCHES
    query_frame = lax.broadcasted_iota(jnp.int32, (block, block), 1) // PATCHES
    kept = key_frame <= query_frame

    def flip(j, carry):
        rows = pl.ds(pl.multiple_of(j * block, block), block)
        vt_ref[:, rows] = jnp.transpose(qkv_ref[rows, 2 * span : 3 * span])
        return carry

    lax.fori_loop(0, total // block, flip, 0)

    def query_block(i, carry):
        rows = pl.ds(pl.multiple_of(i * block, block), block)
        query = qkv_ref[rows, 0:span] * jnp.asarray(HEAD_DIM**-0.5, bf16)
        queries = [jnp.where(head == h, query, jnp.zeros_like(query)) for h in range(heads)]

        def step(j, state, masked):
            peaks, sums, mixes = state
            columns = pl.ds(pl.multiple_of(j * block, block), block)
            key = qkv_ref[columns, span : 2 * span]
            new = ([], [], [])
            for h in range(heads):
                scores = dot(key, queries[h], NT)
                if masked:
                    scores = jnp.where(kept, scores, -1e30)
                peak = jnp.maximum(peaks[h], jnp.max(scores, axis=0, keepdims=True))
                raised = jnp.exp(scores - peak)
                fade = jnp.exp(peaks[h] - peak)
                new[0].append(peak)
                new[1].append(fade * sums[h] + jnp.sum(raised, axis=0, keepdims=True))
                term = dot(vt_ref[h * HEAD_DIM : (h + 1) * HEAD_DIM, columns], raised.astype(bf16))
                new[2].append(mixes[h] * fade + term)
            return tuple(map(tuple, new))

        state = (
            tuple(jnp.full((1, block), -1e30, f32) for _ in range(heads)),
            tuple(jnp.zeros((1, block), f32) for _ in range(heads)),
            tuple(jnp.zeros((HEAD_DIM, block), f32) for _ in range(heads)),
        )
        state = lax.fori_loop(0, i, lambda j, s: step(j, s, False), state)
        peaks, sums, mixes = step(i, state, True)
        mixed = jnp.transpose(jnp.concatenate([mixes[h] / sums[h] for h in range(heads)], axis=0))
        full_ref[rows, :] = mixed
        mix_ref[rows, :] = mixed.astype(bf16)
        for h in range(heads):
            log_ref[h : h + 1, rows] = peaks[h] + jnp.log(sums[h])
        return carry

    lax.fori_loop(0, total // block, query_block, 0)


def attend(qkv, span):
    total = qkv.shape[0]
    heads = span // HEAD_DIM
    block = min(1024, total)
    return pl.pallas_call(
        functools.partial(attend_kernel, total=total, span=span, block=block),
        out_shape=(
            jax.ShapeDtypeStruct((total, span), bf16),
            jax.ShapeDtypeStruct((total, span), f32),
            jax.ShapeDtypeStruct((heads, total), f32),
        ),
        scratch_shapes=[pltpu.VMEM((span, total), bf16)],
        compiler_params=pltpu.CompilerParams(vmem_limit_bytes=52 << 20),
        cost_estimate=pl.CostEstimate(
            flops=8 * total * total * span, bytes_accessed=12 * total * span, transcendentals=total * total * heads // 2
        ),
        name="attend",
    )(qkv)


def attend_back_kernel(
    qkv_ref, grad_ref, full_ref, log_ref, cos_ref, sin_ref, out_ref, dq_ref, dk_ref, dv_ref, along_ref, *, total, span, block
):
    heads = span // HEAD_DIM
    scale = HEAD_DIM**-0.5
    head = lax.broadcasted_iota(jnp.int32, (1, span), 1) // HEAD_DIM
    key_frame = lax.broadcasted_iota(jnp.int32, (block, block), 0) // PATCHES
    query_frame = lax.broadcasted_iota(jnp.int32, (block, block), 1) // PATCHES
    kept = key_frame <= query_frame
    blocks = total // block
    dq_ref[...] = jnp.zeros_like(dq_ref)

    def only(value, h):
        return jnp.where(head == h, value, jnp.zeros_like(value))

    def lead(i, carry):
        rows = pl.ds(pl.multiple_of(i * block, block), block)
        product = jnp.transpose(grad_ref[rows, :].astype(f32) * full_ref[rows, :])
        for h in range(heads):
            along_ref[h : h + 1, rows] = jnp.sum(product[h * HEAD_DIM : (h + 1) * HEAD_DIM], axis=0, keepdims=True)
        return carry

    lax.fori_loop(0, blocks, lead, 0)

    def key_block(j, carry):
        columns = pl.ds(pl.multiple_of(j * block, block), block)
        key = qkv_ref[columns, span : 2 * span]
        value = qkv_ref[columns, 2 * span : 3 * span]
        key_flat = jnp.transpose(key)
        dk_ref[...] = jnp.zeros_like(dk_ref)
        dv_ref[...] = jnp.zeros_like(dv_ref)

        def step(i, masked):
            rows = pl.ds(pl.multiple_of(i * block, block), block)
            query = qkv_ref[rows, 0:span] * jnp.asarray(scale, bf16)
            grad = grad_ref[rows, :]
            dk = dv = None
            for h in range(heads):
                query_h, grad_h = only(query, h), only(grad, h)
                scores = dot(key, query_h, NT)
                if masked:
                    scores = jnp.where(kept, scores, -1e30)
                probs = jnp.exp(scores - log_ref[h : h + 1, rows])
                d_probs = dot(value, grad_h, NT)
                d_scores = (probs * (d_probs - along_ref[h : h + 1, rows])).astype(bf16)
                dv_term = dot(probs.astype(bf16), grad_h)
                dk_term = dot(d_scores, query_h)
                band = slice(h * HEAD_DIM, (h + 1) * HEAD_DIM)
                dq_ref[band, rows] += dot(key_flat[band], d_scores)
                dv = dv_term if dv is None else dv + dv_term
                dk = dk_term if dk is None else dk + dk_term
            dv_ref[...] += dv
            dk_ref[...] += dk

        step(j, True)

        def later(i, c):
            step(i, False)
            return c

        lax.fori_loop(j + 1, blocks, later, 0)
        dk = dk_ref[...]
        out_ref[columns, span : 2 * span] = (dk * cos_ref[columns, :] - partner(dk) * sin_ref[columns, :]).astype(bf16)
        out_ref[columns, 2 * span : 3 * span] = dv_ref[...].astype(bf16)
        return carry

    lax.fori_loop(0, blocks, key_block, 0)

    def last(i, carry):
        rows = pl.ds(pl.multiple_of(i * block, block), block)
        dq = jnp.transpose(dq_ref[:, rows]) * scale
        out_ref[rows, 0:span] = (dq * cos_ref[rows, :] - partner(dq) * sin_ref[rows, :]).astype(bf16)
        return carry

    lax.fori_loop(0, blocks, last, 0)


def attend_back(qkv, grad, full, logs, cosine, sine, span):
    total = qkv.shape[0]
    heads = span // HEAD_DIM
    block = min(1024, total)
    return pl.pallas_call(
        functools.partial(attend_back_kernel, total=total, span=span, block=block),
        out_shape=jax.ShapeDtypeStruct((total, 3 * span), bf16),
        scratch_shapes=[
            pltpu.VMEM((span, total), f32),
            pltpu.VMEM((block, span), f32),
            pltpu.VMEM((block, span), f32),
            pltpu.VMEM((heads, total), f32),
        ],
        compiler_params=pltpu.CompilerParams(vmem_limit_bytes=56 << 20),
        cost_estimate=pl.CostEstimate(
            flops=20 * total * total * span, bytes_accessed=26 * total * span, transcendentals=total * total * heads // 2
        ),
        name="attend_back",
    )(qkv, grad, full, logs, cosine, sine)


def gathered_forward(queries, keys, values, allowed):
    def one(pieces):
        q, k, v = pieces
        scores = jnp.where(allowed, dot(q, k, NT) * HEAD_DIM**-0.5, -1e30)
        peak = jnp.max(scores, axis=-1, keepdims=True)
        raised = jnp.exp(scores - peak)
        totals = jnp.sum(raised, axis=-1, keepdims=True)
        return dot((raised / totals).astype(bf16), v), peak + jnp.log(totals)

    return lax.map(one, (queries, keys, values))


def gathered_back(queries, keys, values, grads, logs, allowed):
    scale = HEAD_DIM**-0.5

    def one(pieces):
        q, k, v, grad, log = pieces
        scores = jnp.where(allowed, dot(q, k, NT) * scale, -1e30)
        probs = jnp.exp(scores - log)
        d_probs = dot(grad, v, NT)
        centre = jnp.sum(probs * d_probs, axis=-1, keepdims=True)
        d_scores = (probs * (d_probs - centre)).astype(bf16)
        dv = dot(probs.astype(bf16), grad, TN)
        return dot(d_scores, k) * scale, dot(d_scores, q, TN) * scale, dv

    return lax.map(one, (queries, keys, values, grads, logs))


def level_rows(ctx_count, noise_level, rows):
    clips = ctx_count.shape[0]
    seq_devices = lax.axis_size("seq")
    plan = jnp.concatenate([ctx_count[:, None], noise_level], axis=1)
    plan = double_rows(plan, axis_bits("clip"))
    levels = jnp.where(jnp.arange(FRAMES, dtype=jnp.int32) < plan[..., :1], 0, plan[..., 1:])
    if rows < PATCHES:
        levels = jnp.repeat(levels, PATCHES // rows, axis=-1)
    frames = max(1, rows // PATCHES)
    levels = levels.reshape(-1, clips, seq_devices, frames).transpose(0, 2, 1, 3)
    return levels.reshape(-1, seq_devices, clips * frames)


def condition(levels, here, depth, width):
    half_width = width // 2
    feature = here * depth + jnp.arange(depth, dtype=jnp.int32)
    low_half = feature < half_width
    freqs = jnp.exp(-math.log(10000.0) * jnp.where(low_half, feature, feature - half_width).astype(f32) / half_width)
    angles = levels.reshape(-1, 1).astype(f32) * freqs
    return jax.nn.silu(jnp.where(low_half, jnp.sin(angles), jnp.cos(angles))).astype(bf16)


def own_place(shard, here):
    count = lax.axis_size("clip") * lax.axis_size("seq")
    whole = jnp.zeros((count * shard.shape[0],), f32)
    return lax.dynamic_update_slice_in_dim(whole, shard.astype(f32), here * shard.shape[0], 0)


def body_by_heads(
    tokens,
    ctx_count,
    noise_level,
    mod_weight,
    mod_bias,
    qkv_weight,
    qkv_bias,
    out_weight,
    out_bias,
    up_weight,
    up_bias,
    down_weight,
    down_bias,
    cotangent,
):
    clips, rows, width = tokens.shape
    seq_devices = lax.axis_size("seq")
    devices = lax.axis_size("clip") * seq_devices
    order = near_order()
    here = lax.axis_index("clip") * seq_devices + lax.axis_index("seq")
    total = rows * seq_devices
    frames = max(1, rows // PATCHES)
    span = width // seq_devices
    lines = clips * frames
    piece = out_weight.shape[0]

    full_qkv = lax.all_gather(qkv_weight, BOTH, axis=0, tiled=True)
    shards = jnp.concatenate(
        [
            down_weight.reshape(4, piece, width),
            up_weight.reshape(piece, 4, width).transpose(1, 0, 2),
            out_weight[None],
        ],
        axis=0,
    )
    packed = lax.all_gather(shards, BOTH, axis=0)

    levels = level_rows(ctx_count, noise_level, rows)
    flat_bits = (2,) * len(order)
    bits_clip, bits_seq = len(axis_bits("clip")), len(axis_bits("seq"))
    turn = tuple(range(bits_clip))[::-1] + tuple(range(bits_clip, bits_clip + bits_seq))[::-1] + (len(order),)
    near_levels = levels.reshape(flat_bits + (lines,)).transpose(turn)
    cond_near = condition(near_levels, here, mod_weight.shape[0], width)
    cond = condition(levels, here, mod_weight.shape[0], width)
    mod_place = own_place(mod_bias, here)

    def modulate(columns, biases):
        weight = mod_weight[:, columns]
        bias = jnp.concatenate([own_place(b, here) for b in biases]).reshape(lines, -1)
        rest = jnp.concatenate([jnp.broadcast_to(mod_place[columns], (lines, weight.shape[1])), bias], axis=1)
        part = jnp.pad(dot(cond_near, weight), ((0, 0), (0, bias.shape[1])))
        line_rows = halve_rows(part + jnp.tile(rest, (devices, 1)), order)
        return line_rows[:, : weight.shape[1]], line_rows[:, weight.shape[1] :].reshape(1, -1)

    mod_first, bias_qkv = modulate(slice(0, 2 * width), (qkv_bias,))
    mod_rest, bias_rest = modulate(slice(2 * width, 6 * width), (out_bias, up_bias, down_bias))
    bias_out = bias_rest[:, :width]
    bias_up = bias_rest[:, width : 5 * width]
    bias_down = bias_rest[:, 5 * width :]

    def blocks(line_rows):
        return line_rows.reshape(clips, frames, -1, width).transpose(0, 2, 1, 3)

    mods_one, mods_two = blocks(mod_first), blocks(mod_rest)

    positions = lax.axis_index("seq") * rows + jnp.arange(rows, dtype=jnp.int32)
    cos_local, sin_local = rotary_lanes(positions, max(span, 256))
    cos_all, sin_all = rotary_lanes(jnp.arange(total, dtype=jnp.int32), span)

    def exchange(value):
        return lax.all_to_all(value, "seq", 0, 0, tiled=True)

    normed, qkv, mixes, fulls, logs = [], [], [], [], []
    for c in range(clips):
        sent, normed_c = project(tokens[c], mods_one[c], full_qkv, bias_qkv, cos_local, sin_local, seq_devices)
        normed.append(normed_c)
        if qkv:
            sent = after(sent, qkv[-1])
        qkv.append(exchange(sent))
    backs = []
    for c in range(clips):
        mix, full, log = attend(qkv[c].reshape(total, 3 * span), span)
        mixes.append(mix)
        fulls.append(full)
        logs.append(log)
        backs.append(exchange(after(mix.reshape(seq_devices, rows, span), qkv[-1] if c == 0 else backs[-1])))

    results = []
    d_mixed = []
    for c in range(clips):
        back = after(backs[c], mixes[-1])
        results.append(middle(back, tokens[c], cotangent[c], mods_two[c], packed, (bias_out, bias_up, bias_down)))
        d_mixed.append(exchange(after(results[c][8], backs[-1] if c == 0 else d_mixed[-1])))

    d_qkv, exchanged = [], []
    for c in range(clips):
        grad = after(d_mixed[c], results[-1][8] if c == 0 else d_qkv[-1])
        grad = grad.reshape(total, span)
        d_qkv.append(attend_back(qkv[c].reshape(total, 3 * span), grad, fulls[c], logs[c], cos_all, sin_all, span))
        sent = d_qkv[c].reshape(seq_devices, rows, 3 * span)
        exchanged.append(exchange(after(sent, d_mixed[-1] if c == 0 else exchanged[-1])))

    def late(place):
        return list(lax.optimization_barrier(tuple(r[place] for r in results) + (d_qkv[-1],))[:-1])

    mixed_all, normed_two, active, d_hidden, d_mlp, d_attn = [late(place) for place in (2, 3, 4, 5, 6, 7)]
    grad_down = weight_grad_kernels(active, d_mlp)
    grad_up = weight_grad_kernels(normed_two, d_hidden)
    grad_out = weight_grad_kernels(mixed_all, d_attn)

    def line_sums(sums):
        return sums.transpose(1, 0, 2).reshape(frames, -1)

    def with_bias(lines_now, vectors):
        return jnp.concatenate([jnp.concatenate(lines_now, axis=0), jnp.concatenate(vectors).reshape(lines, -1)], axis=1)

    bias_up_sum = sum(r[10][0] for r in results)
    bias_pair = sum(r[11] for r in results)
    early = with_bias([line_sums(r[9]) for r in results], [bias_pair[0], bias_up_sum, bias_pair[1]])
    early_rows = lax.all_gather(early, BOTH, axis=0, tiled=True)

    last = [
        project_back(exchanged[c], full_qkv, tokens[c], mods_one[c][1], results[c][1]) for c in range(clips)
    ]
    grad_qkv = weight_grad_kernels(normed, [r[1] for r in last])
    late_rows = with_bias([line_sums(r[2]) for r in last], [sum(r[3][0] for r in last)])
    late_rows = spread_rows(late_rows, order)

    def own_columns(sums, shard):
        return lax.dynamic_slice_in_dim(sums, here * shard.shape[0], shard.shape[0], 0)

    def spans(all_rows, columns):
        vectors = jnp.sum(all_rows[:, columns:].reshape(devices, -1), axis=0)
        return all_rows[:, :columns], vectors

    late_mod, late_vectors = spans(late_rows, 2 * width)
    early_mod, early_vectors = spans(early_rows, 4 * width)
    grad_mod = jnp.concatenate(
        [
            lax.dot_general(rows_cond.astype(f32), r, TN, precision=highest, preferred_element_type=f32)
            for rows_cond, r in ((cond_near, late_mod), (cond, early_mod))
        ],
        axis=1,
    )
    mod_sum = jnp.concatenate([jnp.sum(late_mod, axis=0), jnp.sum(early_mod, axis=0)])
    return (
        jnp.stack([r[0] for r in results]),
        jnp.stack([r[0] for r in last]),
        grad_mod,
        own_columns(mod_sum, mod_bias),
        grad_qkv,
        own_columns(late_vectors, qkv_bias),
        grad_out,
        own_columns(early_vectors[:width], out_bias),
        grad_up,
        own_columns(early_vectors[width : 5 * width], up_bias),
        grad_down,
        own_columns(early_vectors[5 * width :], down_bias),
    )


def body_gathered(
    tokens,
    ctx_count,
    noise_level,
    mod_weight,
    mod_bias,
    qkv_weight,
    qkv_bias,
    out_weight,
    out_bias,
    up_weight,
    up_bias,
    down_weight,
    down_bias,
    cotangent,
):
    clips, rows, width = tokens.shape
    seq_devices = lax.axis_size("seq")
    devices = lax.axis_size("clip") * seq_devices
    bits = mesh_bits()
    here = lax.axis_index("clip") * seq_devices + lax.axis_index("seq")
    total = rows * seq_devices
    frames = max(1, rows // PATCHES)
    patch_rows = rows // frames

    full_qkv = lax.all_gather(qkv_weight, BOTH, axis=0, tiled=True)
    full_out = lax.all_gather(out_weight, BOTH, axis=0, tiled=True)
    full_up = lax.all_gather(up_weight, BOTH, axis=0, tiled=True)
    full_down = lax.all_gather(down_weight, BOTH, axis=0, tiled=True)
    biases = (qkv_bias, out_bias, up_bias, down_bias)
    bias_rows = double_rows(jnp.concatenate(biases).astype(f32), bits)
    full_biases = []
    first = 0
    for piece in biases:
        full_biases.append(bias_rows[:, first : first + piece.shape[0]].reshape(1, -1))
        first += piece.shape[0]
    bias_qkv, bias_out, bias_up, bias_down = full_biases

    levels = level_rows(ctx_count, noise_level, rows)
    cond = condition(levels, here, mod_weight.shape[0], width)
    mod_width = mod_weight.shape[1]
    partial = dot(cond, mod_weight) + own_place(mod_bias, here)
    modulation = halve_sum(partial.reshape(devices, clips * frames, mod_width), bits)
    modulation = modulation.reshape(clips, frames, 1, mod_width)

    positions = lax.axis_index("seq") * rows + jnp.arange(rows, dtype=jnp.int32)
    cosine, sine = rotary_lanes(positions, HEAD_DIM)
    key_frame = jnp.arange(total, dtype=jnp.int32) // PATCHES
    allowed = key_frame[None, :] <= (positions // PATCHES)[:, None]

    def flat(value):
        return value.reshape(rows, value.shape[-1])

    def split(value):
        return value.reshape(frames, patch_rows, value.shape[-1])

    def to_heads(value):
        return value.reshape(rows, HEADS, HEAD_DIM).transpose(1, 0, 2)

    saved = []
    for c in range(clips):
        mods = jnp.split(modulation[c], 6, axis=-1)
        tokens_now = split(tokens[c].astype(f32))
        unit, inverse = norm_parts(tokens_now)
        normed = flat((unit * (1.0 + mods[1]) + mods[0]).astype(bf16))
        projected = dot(normed, full_qkv) + bias_qkv
        views = []
        for place in range(3):
            view = to_heads(projected[:, place * width : (place + 1) * width])
            if place < 2:
                    view = view * cosine + jnp.roll(view, HEAD_DIM // 2, -1) * sine
            views.append(view.astype(bf16))
        queries, keys, values = views
        keys = lax.all_gather(keys, "seq", axis=1, tiled=True)
        values = lax.all_gather(values, "seq", axis=1, tiled=True)
        mix, logs = gathered_forward(queries, keys, values, allowed)
        mixed = mix.transpose(1, 0, 2).reshape(rows, width).astype(bf16)
        kept = (queries, keys, values, logs)
        saved.append((mods, tokens_now, unit, inverse, normed, kept, mixed))

    outputs = []
    middle = []
    for c in range(clips):
        mods, tokens_now, unit, inverse, normed, kept, mixed = saved[c]
        _, _, gate_one, shift_two, scale_two, gate_two = mods
        attn_out = split(dot(mixed, full_out) + bias_out)
        resid = tokens_now + gate_one * attn_out
        unit_two, inverse_two = norm_parts(resid)
        normed_two = flat((unit_two * (1.0 + scale_two) + shift_two).astype(bf16))
        hidden = dot(normed_two, full_up) + bias_up
        active_full, gelu_back = jax.vjp(jax.nn.gelu, hidden)
        active = active_full.astype(bf16)
        mlp_out = split(dot(active, full_down) + bias_down)
        outputs.append(flat((resid + gate_two * mlp_out).astype(bf16)))
        grad_out = split(cotangent[c].astype(f32))
        d_mlp = flat((gate_two * grad_out).astype(bf16))
        d_hidden = gelu_back(dot(d_mlp, full_down, NT))[0].astype(bf16)
        d_normed_two = split(dot(d_hidden, full_up, NT))
        d_resid = grad_out + norm_back(unit_two, inverse_two, d_normed_two, scale_two)
        d_attn = flat((gate_one * d_resid).astype(bf16))
        d_mixed = dot(d_attn, full_out, NT).astype(bf16)
        d_early = jnp.concatenate(
            [
                jnp.sum(d_resid * attn_out, axis=1),
                jnp.sum(d_normed_two, axis=1),
                jnp.sum(d_normed_two * unit_two, axis=1),
                jnp.sum(grad_out * mlp_out, axis=1),
            ],
            axis=-1,
        )
        middle.append((mixed, d_attn, normed_two, d_hidden, active, d_mlp, d_resid, d_mixed, d_early))

    def both(place):
        return jnp.concatenate([m[place] for m in middle], axis=0)

    d_attn_all, d_hidden_all, d_mlp_all = both(1), both(3), both(5)
    grad_down = weight_grad(both(4), d_mlp_all)
    grad_up = weight_grad(both(2), d_hidden_all)
    grad_out_weight = weight_grad(both(0), d_attn_all)
    early_rows = lax.all_gather(both(8), BOTH, axis=0, tiled=True)

    inputs_grad = []
    late = []
    projected_grads = []
    for c in range(clips):
        mods, tokens_now, unit, inverse, normed, kept, mixed = saved[c]
        d_resid, d_mixed = middle[c][6], middle[c][7]
        queries, keys, values, logs = kept
        dq, dk, dv = gathered_back(queries, keys, values, to_heads(d_mixed), logs, allowed)
        dk = lax.psum_scatter(dk.astype(bf16), "seq", scatter_dimension=1, tiled=True).astype(f32)
        dv = lax.psum_scatter(dv.astype(bf16), "seq", scatter_dimension=1, tiled=True).astype(f32)
        views = [g * cosine - jnp.roll(g, HEAD_DIM // 2, -1) * sine for g in (dq, dk)] + [dv]
        d_projected = jnp.concatenate([g.transpose(1, 0, 2).reshape(rows, width) for g in views], axis=1).astype(bf16)
        projected_grads.append(d_projected)
        d_normed = split(dot(d_projected, full_qkv, NT))
        inputs_grad.append(flat(d_resid + norm_back(unit, inverse, d_normed, mods[1])))
        late.append(jnp.concatenate([jnp.sum(d_normed, axis=1), jnp.sum(d_normed * unit, axis=1)], axis=-1))

    d_projected_all = jnp.concatenate(projected_grads, axis=0)
    grad_qkv = weight_grad(jnp.concatenate([s[4] for s in saved], axis=0), d_projected_all)
    bias_grads = [
        jnp.sum(g.astype(f32), axis=0).reshape(devices, -1) for g in (d_projected_all, d_attn_all, d_hidden_all, d_mlp_all)
    ]
    bias_sum = halve_sum(jnp.concatenate(bias_grads, axis=1), bits)
    grad_biases = []
    first = 0
    for piece in bias_grads:
        grad_biases.append(bias_sum[first : first + piece.shape[1]])
        first += piece.shape[1]

    late_rows = double_rows(jnp.concatenate(late, axis=0), bits).reshape(-1, 2 * width)
    grad_mod = jnp.concatenate(
        [
            lax.dot_general(cond.astype(f32), r, TN, precision=highest, preferred_element_type=f32)
            for r in (late_rows, early_rows)
        ],
        axis=1,
    )
    mod_sum = jnp.concatenate([jnp.sum(late_rows, axis=0), jnp.sum(early_rows, axis=0)])
    grad_mod_bias = lax.dynamic_slice_in_dim(mod_sum, here * mod_bias.shape[0], mod_bias.shape[0], 0)
    return (
        jnp.stack(outputs),
        jnp.stack(inputs_grad),
        grad_mod,
        grad_mod_bias,
        grad_qkv,
        grad_biases[0],
        grad_out_weight,
        grad_biases[1],
        grad_up,
        grad_biases[2],
        grad_down,
        grad_biases[3],
    )


def solution(mesh):
    by_heads = HEADS % mesh.shape["seq"] == 0
    body = body_by_heads if by_heads else body_gathered
    token_place = P("clip", "seq", None)
    matrix, vector = P(BOTH, None), P(BOTH)
    weights = (matrix, vector) * 5
    return jax.shard_map(
        body,
        mesh=mesh,
        in_specs=(token_place, P("clip"), P("clip", None)) + weights + (token_place,),
        out_specs=(token_place, token_place) + weights,
        check_vma=False,
    )
```

```python
import functools
import math

import jax
import jax.numpy as jnp
from jax import lax
from jax.experimental import pallas as pl
from jax.experimental.pallas import tpu as pltpu
from jax.sharding import PartitionSpec as P

HEADS = 16
HEAD_DIM = 64
FRAMES = 16
PATCHES = 256
BOTH = ("clip", "seq")
NT = (((1,), (1,)), ((), ()))
NN = (((1,), (0,)), ((), ()))
TN = (((0,), (0,)), ((), ()))
bf16 = jnp.bfloat16
f32 = jnp.float32
highest = lax.Precision.HIGHEST


def dot(left, right, dims=NN):
    return lax.dot_general(left, right, dims, preferred_element_type=f32)


def swap_bit(value, axis, bit):
    count = lax.axis_size(axis)
    return lax.ppermute(value, axis, [(i, i ^ bit) for i in range(count)])


def own_bit(axis, bit):
    return lax.shift_right_logical(lax.axis_index(axis), bit.bit_length() - 1) & 1


def axis_bits(axis):
    bits = []
    bit = 1
    while bit < lax.axis_size(axis):
        bits.append((axis, bit))
        bit *= 2
    return bits[::-1]


def exchange_order(bits):
    return sorted(range(len(bits)), key=lambda place: bits[place])


def mesh_bits():
    return axis_bits("clip") + axis_bits("seq")


def halve_sum(parts, bits, wire=f32):
    parts = parts.reshape((2,) * len(bits) + parts.shape[1:])
    for place in exchange_order(bits):
        axis, bit = bits[place]
        mine = own_bit(axis, bit)
        keep = lax.dynamic_index_in_dim(parts, mine, place)
        send = lax.dynamic_index_in_dim(parts, 1 - mine, place)
        parts = keep + swap_bit(send.astype(wire), axis, bit).astype(f32)
    return parts.reshape(parts.shape[len(bits) :])


def near_order():
    return axis_bits("clip")[::-1] + axis_bits("seq")[::-1]


def halve_rows(parts, bits, gates=()):
    for place, (axis, bit) in enumerate(bits):
        half = parts.shape[0] // 2
        mine = own_bit(axis, bit)
        keep = lax.dynamic_slice_in_dim(parts, mine * half, half, 0)
        send = lax.dynamic_slice_in_dim(parts, (1 - mine) * half, half, 0)
        other = swap_bit(send, axis, bit)
        if place < len(gates) and gates[place] is not None:
            other = after(other, gates[place])
        parts = keep + other
    return parts


def spread_rows(rows, bits):
    for axis, bit in reversed(bits):
        other = swap_bit(rows, axis, bit)
        low = own_bit(axis, bit) == 0
        rows = jnp.concatenate([jnp.where(low, rows, other), jnp.where(low, other, rows)], axis=0)
    return rows


def after(value, *others):
    return lax.optimization_barrier((value,) + others)[0]


def double_rows(row, bits):
    rows = row[None]
    for axis, bit in reversed(bits):
        other = swap_bit(rows, axis, bit)
        low = own_bit(axis, bit) == 0
        rows = jnp.concatenate([jnp.where(low, rows, other), jnp.where(low, other, rows)], axis=0)
    return rows


def weight_grad(left, right):
    tokens, rows = left.shape
    quarter = rows // lax.axis_size("clip")
    mine = lax.axis_index("clip")

    def part(flip):
        piece = lax.dynamic_slice_in_dim(left, (mine ^ flip) * quarter, quarter, 1)
        return dot(piece, right, TN)

    far = swap_bit(part(3).astype(bf16), "clip", 1)
    near = swap_bit(part(1).astype(bf16), "clip", 1)
    across = swap_bit((part(2) + far.astype(f32)).astype(bf16), "clip", 2)
    total = part(0) + near.astype(f32) + across.astype(f32)
    return halve_sum(total.reshape((lax.axis_size("seq"), -1, right.shape[1])), axis_bits("seq"), bf16)


def norm_parts(values):
    centre = values - jnp.mean(values, axis=-1, keepdims=True)
    spread = jnp.mean(centre * centre, axis=-1, keepdims=True)
    inverse = lax.rsqrt(spread + 1e-06)
    return centre * inverse, inverse


def norm_back(unit, inverse, grad, scales):
    scaled = grad * (1.0 + scales)
    mean = jnp.mean(scaled, axis=-1, keepdims=True)
    along = jnp.mean(scaled * unit, axis=-1, keepdims=True)
    return inverse * (scaled - mean - unit * along)


def rotary_lanes(positions, width):
    half = HEAD_DIM // 2
    lane = jnp.arange(width, dtype=jnp.int32) % HEAD_DIM
    freqs = jnp.exp(-math.log(10000.0) * 2.0 * (lane % half).astype(f32) / HEAD_DIM)
    angles = positions.astype(f32)[:, None] * freqs[None, :]
    sign = jnp.where(lane < half, -1.0, 1.0).astype(f32)
    return jnp.cos(angles), jnp.sin(angles) * sign[None, :]


def partner(values):
    width = values.shape[1]
    half = HEAD_DIM // 2
    lane = lax.broadcasted_iota(jnp.int32, (1, width), 1) % HEAD_DIM
    return jnp.where(lane < half, pltpu.roll(values, width - half, 1), pltpu.roll(values, half, 1))


def project_kernel(
    token_ref, mod_ref, wq_ref, wk_ref, wv_ref, bq_ref, bk_ref, bv_ref, cos_ref, sin_ref, out_ref, normed_ref, *, span
):
    frames = mod_ref.shape[1]
    patch = token_ref.shape[0] // frames

    @pl.when(pl.program_id(0) == 0)
    def _():
        for f in range(frames):
            rows = slice(f * patch, (f + 1) * patch)
            unit, _ = norm_parts(token_ref[rows, :].astype(f32))
            normed_ref[rows, :] = (unit * (1.0 + mod_ref[1, f : f + 1, :]) + mod_ref[0, f : f + 1, :]).astype(bf16)

    x = normed_ref[...]
    cosine, sine = cos_ref[...], sin_ref[...]
    groups = wq_ref.shape[1] // span
    for place, (w_ref, b_ref) in enumerate(((wq_ref, bq_ref), (wk_ref, bk_ref), (wv_ref, bv_ref))):
        value = dot(x, w_ref[...]) + b_ref[...]
        if place < 2:
            value = value * cosine + partner(value) * sine
        value = value.astype(bf16)
        for g in range(groups):
            out_ref[g, :, place * span : (place + 1) * span] = value[:, g * span : (g + 1) * span]


def whole_block(shape):
    return pl.BlockSpec(shape, lambda j: (0,) * len(shape))


def column_specs(height, block, steps):
    return [pl.BlockSpec((height, block), functools.partial(lambda p, j: (0, p * steps + j), p)) for p in range(3)]


def clip_block(shape, c):
    return pl.BlockSpec((None,) + shape[1:], lambda j: (c,) + (0,) * (len(shape) - 1))


def project(tokens, c, mods, weight, bias, cosine, sine, groups):
    _, rows, width = tokens.shape
    span = width // groups
    block = max(span, 256)
    per_step = block // span
    steps = groups // per_step
    return pl.pallas_call(
        functools.partial(project_kernel, span=span),
        grid=(steps,),
        in_specs=[clip_block(tokens.shape, c), whole_block(mods.shape)]
        + column_specs(width, block, steps)
        + column_specs(1, block, steps)
        + [whole_block((rows, block))] * 2,
        out_specs=(pl.BlockSpec((per_step, rows, 3 * span), lambda j: (j, 0, 0)), whole_block((rows, width))),
        out_shape=(
            jax.ShapeDtypeStruct((groups, rows, 3 * span), bf16),
            jax.ShapeDtypeStruct((rows, width), bf16),
        ),
        compiler_params=pltpu.CompilerParams(vmem_limit_bytes=32 << 20),
        cost_estimate=pl.CostEstimate(
            flops=6 * rows * width * width, bytes_accessed=6 * width * width + 10 * rows * width, transcendentals=0
        ),
        name="project",
    )(tokens, mods, weight, weight, weight, bias, bias, bias, cosine, sine)


def project_back_kernel(
    back_ref, wq_ref, wk_ref, wv_ref, token_ref, scale_ref, resid_ref, *rest, span
):
    grad_ref, proj_ref, sums_ref, bias_ref, acc_ref = rest[-5:]
    frames = scale_ref.shape[0]
    rows_all, width = token_ref.shape
    patch = rows_all // frames
    step = pl.program_id(0)
    block = wq_ref.shape[1]

    @pl.when(step == 0)
    def _():
        acc_ref[...] = jnp.zeros_like(acc_ref)

    for place, w_ref in enumerate((wq_ref, wk_ref, wv_ref)):
        band = slice(place * span, (place + 1) * span)
        piece = jnp.concatenate([back_ref[g, :, band] for g in range(block // span)], axis=1)
        columns = pl.ds(pl.multiple_of(place * width + step * block, block), block)
        proj_ref[:, columns] = piece
        bias_ref[:, columns] = jnp.sum(piece.astype(f32), axis=0, keepdims=True)
        acc_ref[...] += dot(piece, w_ref[...], NT)

    @pl.when(step == pl.num_programs(0) - 1)
    def _():
        for f in range(frames):
            rows = slice(f * patch, (f + 1) * patch)
            unit, inverse = norm_parts(token_ref[rows, :].astype(f32))
            grad = acc_ref[rows, :]
            grad_ref[rows, :] = resid_ref[rows, :] + norm_back(unit, inverse, grad, scale_ref[f : f + 1, :])
            sums_ref[0, f : f + 1, :] = jnp.sum(grad, axis=0, keepdims=True)
            sums_ref[1, f : f + 1, :] = jnp.sum(grad * unit, axis=0, keepdims=True)


def project_back(back, weight, tokens, c, scales, d_resid, grads):
    groups, rows, _ = back.shape
    width = tokens.shape[2]
    span = width // groups
    block = max(span, 256)
    per_step = block // span
    steps = groups // per_step
    earlier = [] if grads is None else [grads]
    return pl.pallas_call(
        functools.partial(project_back_kernel, span=span),
        grid=(steps,),
        in_specs=[pl.BlockSpec((per_step, rows, 3 * span), lambda j: (j, 0, 0))]
        + column_specs(width, block, steps)
        + [clip_block(tokens.shape, c), whole_block(scales.shape), whole_block((rows, width))]
        + [pl.BlockSpec(memory_space=pl.ANY)] * len(earlier),
        out_specs=(
            clip_block(tokens.shape, c),
            whole_block((rows, 3 * width)),
            whole_block((2,) + scales.shape),
            whole_block((1, 3 * width)),
        ),
        out_shape=(
            jax.ShapeDtypeStruct(tokens.shape, f32),
            jax.ShapeDtypeStruct((rows, 3 * width), bf16),
            jax.ShapeDtypeStruct((2,) + scales.shape, f32),
            jax.ShapeDtypeStruct((1, 3 * width), f32),
        ),
        input_output_aliases={7: 0} if earlier else {},
        scratch_shapes=[pltpu.VMEM((rows, width), f32)],
        compiler_params=pltpu.CompilerParams(vmem_limit_bytes=40 << 20),
        cost_estimate=pl.CostEstimate(
            flops=6 * rows * width * width, bytes_accessed=6 * width * width + 22 * rows * width, transcendentals=0
        ),
        name="project_back",
    )(back, weight, weight, weight, tokens, scales, d_resid, *earlier)


GELU_RATE = math.sqrt(2.0 / math.pi)
GELU_CUBE = 0.044715


def middle_kernel(clip_ref, back_ref, token_ref, cot_ref, mod_ref, bo_ref, bup_ref, bdown_ref, *refs):
    wo_refs, up_refs, down_refs = refs[0:4], refs[4:8], refs[8:12]
    (
        out_ref,
        dres_ref,
        mixed_ref,
        normed_ref,
        act_ref,
        dhid_ref,
        dmlp_ref,
        dattn_ref,
        dmix_ref,
        sums_ref,
        bup_sum_ref,
        bsum_ref,
        attn_ref,
        res_ref,
        mlp_ref,
        dn_ref,
        wo_ref,
        up_ref,
        down_ref,
    ) = refs[-19:]
    groups, rows_all, span = back_ref.shape
    width = token_ref.shape[1]
    quarter = width // 4
    frames = mod_ref.shape[1]
    patch = rows_all // frames
    step = pl.program_id(0)
    mine = clip_ref[0]

    def owner_rows(place):
        return pl.ds(pl.multiple_of((mine ^ FLIPS[place]) * quarter, quarter), quarter)

    @pl.when(step == 0)
    def _():
        for place in range(4):
            wo_ref[owner_rows(place), :] = wo_refs[place][...].reshape(quarter, width)
        for g in range(groups):
            mixed_ref[:, g * span : (g + 1) * span] = back_ref[g]
        attn_ref[...] = dot(mixed_ref[...], wo_ref[...]) + bo_ref[...]
        for f in range(frames):
            rows = slice(f * patch, (f + 1) * patch)
            resid = token_ref[rows, :].astype(f32) + mod_ref[0, f : f + 1, :] * attn_ref[rows, :]
            res_ref[rows, :] = resid
            unit, _ = norm_parts(resid)
            normed_ref[rows, :] = (unit * (1.0 + mod_ref[2, f : f + 1, :]) + mod_ref[1, f : f + 1, :]).astype(bf16)
            dmlp_ref[rows, :] = (mod_ref[3, f : f + 1, :] * cot_ref[rows, :].astype(f32)).astype(bf16)
        mlp_ref[...] = jnp.zeros_like(mlp_ref)
        dn_ref[...] = jnp.zeros_like(dn_ref)

    for place in range(4):
        up_ref[owner_rows(place), :] = up_refs[place][...].reshape(quarter, -1)

        @pl.when(step // 2 == place)
        def _(place=place):
            down_ref[...] = down_refs[place][...].reshape(-1, width)

    up = up_ref[...]
    down = down_ref[...]
    hidden = dot(normed_ref[...], up) + bup_ref[...]
    square = hidden * hidden
    bend = jnp.tanh(GELU_RATE * (hidden + GELU_CUBE * (square * hidden)))
    share = 0.5 * (1.0 + bend)
    active = (hidden * share).astype(bf16)
    act_ref[...] = active
    mlp_ref[...] += dot(active, down)
    slope = share + 0.5 * hidden * (1.0 - bend * bend) * (GELU_RATE + (3.0 * GELU_RATE * GELU_CUBE) * square)
    d_hidden = (dot(dmlp_ref[...], down, NT) * slope).astype(bf16)
    dhid_ref[...] = d_hidden
    bup_sum_ref[...] = jnp.sum(d_hidden.astype(f32), axis=0, keepdims=True)
    dn_ref[...] += dot(d_hidden, up, NT)

    @pl.when(step == pl.num_programs(0) - 1)
    def _():
        bsum = None
        for f in range(frames):
            rows = slice(f * patch, (f + 1) * patch)
            resid = res_ref[rows, :]
            mlp = mlp_ref[rows, :] + bdown_ref[...]
            out_ref[rows, :] = (resid + mod_ref[3, f : f + 1, :] * mlp).astype(bf16)
            cot = cot_ref[rows, :].astype(f32)
            sums_ref[3, f : f + 1, :] = jnp.sum(cot * mlp, axis=0, keepdims=True)
            unit, inverse = norm_parts(resid)
            grad = dn_ref[rows, :]
            sums_ref[1, f : f + 1, :] = jnp.sum(grad, axis=0, keepdims=True)
            sums_ref[2, f : f + 1, :] = jnp.sum(grad * unit, axis=0, keepdims=True)
            d_resid = cot + norm_back(unit, inverse, grad, mod_ref[2, f : f + 1, :])
            dres_ref[rows, :] = d_resid
            sums_ref[0, f : f + 1, :] = jnp.sum(d_resid * attn_ref[rows, :], axis=0, keepdims=True)
            d_attn = (mod_ref[0, f : f + 1, :] * d_resid).astype(bf16)
            dattn_ref[rows, :] = d_attn
            term = jnp.concatenate(
                [
                    jnp.sum(d_attn.astype(f32), axis=0, keepdims=True),
                    jnp.sum(dmlp_ref[rows, :].astype(f32), axis=0, keepdims=True),
                ],
                axis=0,
            )
            bsum = term if bsum is None else bsum + term
        bsum_ref[...] = bsum
        d_mixed = dot(dattn_ref[...], wo_ref[...], NT).astype(bf16)
        for g in range(groups):
            dmix_ref[g] = d_mixed[:, g * span : (g + 1) * span]


FLIPS = (0, 2, 1, 3)


def middle(back, tokens, cot, c, mods, up_shares, down_shares, biases, outputs):
    groups, rows, span = back.shape
    _, _, width = tokens.shape
    high, low, _, piece, _ = up_shares[0].shape
    hidden = 4 * width
    steps = 8
    block = hidden // steps
    bias_out, bias_up, bias_down = biases
    mine = lax.axis_index("clip").astype(jnp.int32)[None]
    earlier = [] if outputs is None else [outputs]

    def fixed(shape, **options):
        return pl.BlockSpec(shape, lambda j, q: (0,) * len(shape), **options)

    def clip_part(shape):
        return pl.BlockSpec((None,) + shape[1:], lambda j, q: (c,) + (0,) * (len(shape) - 1))

    def unit_block(j, q):
        owner = q[0] ^ jnp.where(j // 2 == 1, 2, jnp.where(j // 2 == 2, 1, j // 2))
        return owner, j % 2

    def up_index(j, q):
        owner, half = unit_block(j, q)
        return (0, 0, owner, 0, half)

    def hidden_index(j, q):
        owner, half = unit_block(j, q)
        return (0, owner * 2 + half)

    def down_index(place, j, q):
        return (0, jnp.clip(j - 2 * place, 0, 1), 0, 0, 0)

    token_block = fixed((rows, width))
    hidden_block = pl.BlockSpec((rows, block), hidden_index)
    out_spec = [
        pl.BlockSpec((high, low, 1, piece, width), lambda j, q: (0, 0, 4, 0, 0), pipeline_mode=pl.Buffered(1)) for _ in range(4)
    ]
    up_spec = [pl.BlockSpec((high, low, 1, piece, block), up_index) for _ in range(4)]
    down_spec = [
        pl.BlockSpec((high, 1, 4, piece, width), functools.partial(down_index, place)) for place in range(4)
    ]
    return pl.pallas_call(
        middle_kernel,
        grid_spec=pltpu.PrefetchScalarGridSpec(
            num_scalar_prefetch=1,
            grid=(steps,),
            in_specs=[
                fixed(back.shape),
                clip_part(tokens.shape),
                clip_part(tokens.shape),
                fixed(mods.shape),
                fixed((1, width)),
                pl.BlockSpec((1, block), hidden_index),
                fixed((1, width)),
            ]
            + out_spec
            + up_spec
            + down_spec
            + [pl.BlockSpec(memory_space=pl.ANY)] * len(earlier),
            out_specs=(
                clip_part(tokens.shape),
                token_block,
                token_block,
                token_block,
                hidden_block,
                hidden_block,
                token_block,
                token_block,
                fixed(back.shape),
                fixed(mods.shape),
                pl.BlockSpec((1, block), hidden_index),
                fixed((2, width)),
            ),
            scratch_shapes=[pltpu.VMEM((rows, width), f32)] * 4
            + [pltpu.VMEM((width, width), bf16), pltpu.VMEM((width, block), bf16), pltpu.VMEM((block, width), bf16)],
        ),
        out_shape=(
            jax.ShapeDtypeStruct(tokens.shape, bf16),
            jax.ShapeDtypeStruct((rows, width), f32),
            jax.ShapeDtypeStruct((rows, width), bf16),
            jax.ShapeDtypeStruct((rows, width), bf16),
            jax.ShapeDtypeStruct((rows, hidden), bf16),
            jax.ShapeDtypeStruct((rows, hidden), bf16),
            jax.ShapeDtypeStruct((rows, width), bf16),
            jax.ShapeDtypeStruct((rows, width), bf16),
            jax.ShapeDtypeStruct(back.shape, bf16),
            jax.ShapeDtypeStruct(mods.shape, f32),
            jax.ShapeDtypeStruct((1, hidden), f32),
            jax.ShapeDtypeStruct((2, width), f32),
        ),
        input_output_aliases={20: 0} if earlier else {},
        compiler_params=pltpu.CompilerParams(vmem_limit_bytes=58 << 20),
        cost_estimate=pl.CostEstimate(
            flops=4 * rows * width * width, bytes_accessed=2 * width * width + 5 * rows * width, transcendentals=rows * width
        ),
        name="middle",
    )(mine, back, tokens, cot, mods, bias_out, bias_up, bias_down, *up_shares, *up_shares, *down_shares, *earlier)


def weight_part_kernel(index_ref, *refs, clips, addends):
    left, right = refs[:clips], refs[clips : 2 * clips]
    extra = refs[2 * clips : 2 * clips + addends]
    out_ref, flat_ref = refs[2 * clips + addends :]
    rows = left[0].shape[0]

    @pl.when(pl.program_id(1) == 0)
    def _():
        for c in range(clips):
            flat_ref[:, c * rows : (c + 1) * rows] = jnp.transpose(left[c][...])

    total = dot(flat_ref[:, 0:rows], right[0][...])
    for c in range(1, clips):
        total += dot(flat_ref[:, c * rows : (c + 1) * rows], right[c][...])
    for ref in extra:
        total += ref[0].astype(f32)
    out_ref[0] = total.astype(out_ref.dtype)


def weight_part(left, right, indices, addends, kind, height):
    rows = left[0].shape[0]
    columns = right[0].shape[1]
    block = 512
    count = indices.shape[0]
    in_specs = [pl.BlockSpec((rows, height), lambda i, j, q: (0, q[i]))] * len(left)
    in_specs += [pl.BlockSpec((rows, block), lambda i, j, q: (0, j))] * len(right)
    in_specs += [
        pl.BlockSpec((1, height, block), functools.partial(lambda first, i, j, q: (first + i, 0, j), first))
        for _, first in addends
    ]
    return pl.pallas_call(
        functools.partial(weight_part_kernel, clips=len(left), addends=len(addends)),
        grid_spec=pltpu.PrefetchScalarGridSpec(
            num_scalar_prefetch=1,
            grid=(count, columns // block),
            in_specs=in_specs,
            out_specs=pl.BlockSpec((1, height, block), lambda i, j, q: (i, 0, j)),
            scratch_shapes=[pltpu.VMEM((height, len(left) * rows), bf16)],
        ),
        out_shape=jax.ShapeDtypeStruct((count, height, columns), kind),
        compiler_params=pltpu.CompilerParams(vmem_limit_bytes=32 << 20),
        cost_estimate=pl.CostEstimate(
            flops=2 * count * len(left) * rows * height * columns,
            bytes_accessed=len(left) * rows * (count * height + columns) * 2 + 4 * count * height * columns,
            transcendentals=0,
        ),
        name="weight_part",
    )(indices, *left, *right, *[array for array, _ in addends])


def mine_on(axis):
    return lax.axis_index(axis).astype(jnp.int32)


def gate(arrays, *others):
    return list(lax.optimization_barrier((tuple(arrays), others))[0])


def across_first(left, right):
    mine = mine_on("clip")
    return weight_part(left, right, jnp.stack([mine ^ 3, mine ^ 1]), (), bf16, left[0].shape[1] // 4)


def across_second(left, right, core):
    return weight_part(left, right, (mine_on("clip") ^ 2)[None], ((core, 0),), bf16, left[0].shape[1] // 4)


def across_total(left, right, core, across):
    height = left[0].shape[1] // 4
    total = weight_part(left, right, mine_on("clip")[None], ((core, 1), (across, 0)), f32, height)
    return halve_sum(total.reshape((lax.axis_size("seq"), -1, right[0].shape[1])), axis_bits("seq"), bf16)


def along_block(clip_flip, low_flip):
    return (mine_on("clip") ^ clip_flip) * 2 + ((mine_on("seq") & 1) ^ low_flip)


def along_first(left, right):
    blocks = jnp.stack([along_block(1, 1), along_block(3, 1), along_block(1, 0), along_block(3, 0)])
    return weight_part(left, right, blocks, (), bf16, left[0].shape[1] // 8)


def along_second(left, right, core):
    blocks = jnp.stack([along_block(0, 1), along_block(2, 1)])
    return weight_part(left, right, blocks, ((core, 0),), bf16, left[0].shape[1] // 8)


def along_total(left, right, core, along):
    height = left[0].shape[1] // 8
    far, near = along_block(2, 0), along_block(0, 0)
    across = weight_part(left, right, far[None], ((core, 3), (along, 1)), bf16, height)
    across = swap_bit(across, "clip", 2)
    total = weight_part(left, right, near[None], ((core, 2), (along, 0), (across, 0)), f32, height)
    bits = axis_bits("seq")[:-1]
    return halve_sum(total.reshape((2 ** len(bits), -1, right[0].shape[1])), bits, bf16)


def attend_kernel(qkv_ref, mix_ref, full_ref, log_ref, vt_ref, *, total, span, block):
    heads = span // HEAD_DIM
    head = lax.broadcasted_iota(jnp.int32, (1, span), 1) // HEAD_DIM
    key_frame = lax.broadcasted_iota(jnp.int32, (block, block), 0) // PATCHES
    query_frame = lax.broadcasted_iota(jnp.int32, (block, block), 1) // PATCHES
    kept = key_frame <= query_frame

    def flip(j, carry):
        rows = pl.ds(pl.multiple_of(j * block, block), block)
        vt_ref[:, rows] = jnp.transpose(qkv_ref[rows, 2 * span : 3 * span])
        return carry

    lax.fori_loop(0, total // block, flip, 0)

    def query_block(i, carry):
        rows = pl.ds(pl.multiple_of(i * block, block), block)
        query = qkv_ref[rows, 0:span] * jnp.asarray(HEAD_DIM**-0.5, bf16)
        queries = [jnp.where(head == h, query, jnp.zeros_like(query)) for h in range(heads)]

        def step(j, state, masked):
            peaks, sums, mixes = state
            columns = pl.ds(pl.multiple_of(j * block, block), block)
            key = qkv_ref[columns, span : 2 * span]
            new = ([], [], [])
            for h in range(heads):
                scores = dot(key, queries[h], NT)
                if masked:
                    scores = jnp.where(kept, scores, -1e30)
                peak = jnp.maximum(peaks[h], jnp.max(scores, axis=0, keepdims=True))
                raised = jnp.exp(scores - peak)
                fade = jnp.exp(peaks[h] - peak)
                new[0].append(peak)
                new[1].append(fade * sums[h] + jnp.sum(raised, axis=0, keepdims=True))
                term = dot(vt_ref[h * HEAD_DIM : (h + 1) * HEAD_DIM, columns], raised.astype(bf16))
                new[2].append(mixes[h] * fade + term)
            return tuple(map(tuple, new))

        state = (
            tuple(jnp.full((1, block), -1e30, f32) for _ in range(heads)),
            tuple(jnp.zeros((1, block), f32) for _ in range(heads)),
            tuple(jnp.zeros((HEAD_DIM, block), f32) for _ in range(heads)),
        )
        state = lax.fori_loop(0, i, lambda j, s: step(j, s, False), state)
        peaks, sums, mixes = step(i, state, True)
        mixed = jnp.transpose(jnp.concatenate([mixes[h] / sums[h] for h in range(heads)], axis=0))
        full_ref[rows, :] = mixed
        mix_ref[rows, :] = mixed.astype(bf16)
        for h in range(heads):
            log_ref[h : h + 1, rows] = peaks[h] + jnp.log(sums[h])
        return carry

    lax.fori_loop(0, total // block, query_block, 0)


def attend(qkv, span):
    total = qkv.shape[0]
    heads = span // HEAD_DIM
    block = min(1024, total)
    return pl.pallas_call(
        functools.partial(attend_kernel, total=total, span=span, block=block),
        out_shape=(
            jax.ShapeDtypeStruct((total, span), bf16),
            jax.ShapeDtypeStruct((total, span), f32),
            jax.ShapeDtypeStruct((heads, total), f32),
        ),
        scratch_shapes=[pltpu.VMEM((span, total), bf16)],
        compiler_params=pltpu.CompilerParams(vmem_limit_bytes=52 << 20),
        cost_estimate=pl.CostEstimate(
            flops=8 * total * total * span, bytes_accessed=12 * total * span, transcendentals=total * total * heads // 2
        ),
        name="attend",
    )(qkv)


def attend_back_kernel(
    qkv_ref, grad_ref, full_ref, log_ref, cos_ref, sin_ref, out_ref, dq_ref, dk_ref, dv_ref, along_ref, *, total, span, block
):
    heads = span // HEAD_DIM
    scale = HEAD_DIM**-0.5
    head = lax.broadcasted_iota(jnp.int32, (1, span), 1) // HEAD_DIM
    key_frame = lax.broadcasted_iota(jnp.int32, (block, block), 0) // PATCHES
    query_frame = lax.broadcasted_iota(jnp.int32, (block, block), 1) // PATCHES
    kept = key_frame <= query_frame
    blocks = total // block
    dq_ref[...] = jnp.zeros_like(dq_ref)

    def only(value, h):
        return jnp.where(head == h, value, jnp.zeros_like(value))

    def lead(i, carry):
        rows = pl.ds(pl.multiple_of(i * block, block), block)
        product = jnp.transpose(grad_ref[rows, :].astype(f32) * full_ref[rows, :])
        for h in range(heads):
            along_ref[h : h + 1, rows] = jnp.sum(product[h * HEAD_DIM : (h + 1) * HEAD_DIM], axis=0, keepdims=True)
        return carry

    lax.fori_loop(0, blocks, lead, 0)

    def key_block(j, carry):
        columns = pl.ds(pl.multiple_of(j * block, block), block)
        key = qkv_ref[columns, span : 2 * span]
        value = qkv_ref[columns, 2 * span : 3 * span]
        key_flat = jnp.transpose(key)
        dk_ref[...] = jnp.zeros_like(dk_ref)
        dv_ref[...] = jnp.zeros_like(dv_ref)

        def step(i, masked):
            rows = pl.ds(pl.multiple_of(i * block, block), block)
            query = qkv_ref[rows, 0:span] * jnp.asarray(scale, bf16)
            grad = grad_ref[rows, :]
            dk = dv = None
            for h in range(heads):
                query_h, grad_h = only(query, h), only(grad, h)
                scores = dot(key, query_h, NT)
                if masked:
                    scores = jnp.where(kept, scores, -1e30)
                probs = jnp.exp(scores - log_ref[h : h + 1, rows])
                d_probs = dot(value, grad_h, NT)
                d_scores = (probs * (d_probs - along_ref[h : h + 1, rows])).astype(bf16)
                dv_term = dot(probs.astype(bf16), grad_h)
                dk_term = dot(d_scores, query_h)
                band = slice(h * HEAD_DIM, (h + 1) * HEAD_DIM)
                dq_ref[band, rows] += dot(key_flat[band], d_scores)
                dv = dv_term if dv is None else dv + dv_term
                dk = dk_term if dk is None else dk + dk_term
            dv_ref[...] += dv
            dk_ref[...] += dk

        step(j, True)

        def later(i, c):
            step(i, False)
            return c

        lax.fori_loop(j + 1, blocks, later, 0)
        dk = dk_ref[...]
        out_ref[columns, span : 2 * span] = (dk * cos_ref[columns, :] - partner(dk) * sin_ref[columns, :]).astype(bf16)
        out_ref[columns, 2 * span : 3 * span] = dv_ref[...].astype(bf16)
        return carry

    lax.fori_loop(0, blocks, key_block, 0)

    def last(i, carry):
        rows = pl.ds(pl.multiple_of(i * block, block), block)
        dq = jnp.transpose(dq_ref[:, rows]) * scale
        out_ref[rows, 0:span] = (dq * cos_ref[rows, :] - partner(dq) * sin_ref[rows, :]).astype(bf16)
        return carry

    lax.fori_loop(0, blocks, last, 0)


def attend_back(qkv, grad, full, logs, cosine, sine, span):
    total = qkv.shape[0]
    heads = span // HEAD_DIM
    block = min(1024, total)
    return pl.pallas_call(
        functools.partial(attend_back_kernel, total=total, span=span, block=block),
        out_shape=jax.ShapeDtypeStruct((total, 3 * span), bf16),
        scratch_shapes=[
            pltpu.VMEM((span, total), f32),
            pltpu.VMEM((block, span), f32),
            pltpu.VMEM((block, span), f32),
            pltpu.VMEM((heads, total), f32),
        ],
        compiler_params=pltpu.CompilerParams(vmem_limit_bytes=56 << 20),
        cost_estimate=pl.CostEstimate(
            flops=20 * total * total * span, bytes_accessed=26 * total * span, transcendentals=total * total * heads // 2
        ),
        name="attend_back",
    )(qkv, grad, full, logs, cosine, sine)


def gathered_forward(queries, keys, values, allowed):
    def one(pieces):
        q, k, v = pieces
        scores = jnp.where(allowed, dot(q, k, NT) * HEAD_DIM**-0.5, -1e30)
        peak = jnp.max(scores, axis=-1, keepdims=True)
        raised = jnp.exp(scores - peak)
        totals = jnp.sum(raised, axis=-1, keepdims=True)
        return dot((raised / totals).astype(bf16), v), peak + jnp.log(totals)

    return lax.map(one, (queries, keys, values))


def gathered_back(queries, keys, values, grads, logs, allowed):
    scale = HEAD_DIM**-0.5

    def one(pieces):
        q, k, v, grad, log = pieces
        scores = jnp.where(allowed, dot(q, k, NT) * scale, -1e30)
        probs = jnp.exp(scores - log)
        d_probs = dot(grad, v, NT)
        centre = jnp.sum(probs * d_probs, axis=-1, keepdims=True)
        d_scores = (probs * (d_probs - centre)).astype(bf16)
        dv = dot(probs.astype(bf16), grad, TN)
        return dot(d_scores, k) * scale, dot(d_scores, q, TN) * scale, dv

    return lax.map(one, (queries, keys, values, grads, logs))


def level_rows(ctx_count, noise_level, rows):
    clips = ctx_count.shape[0]
    seq_devices = lax.axis_size("seq")
    plan = jnp.concatenate([ctx_count[:, None], noise_level], axis=1)
    plan = double_rows(plan, axis_bits("clip"))
    levels = jnp.where(jnp.arange(FRAMES, dtype=jnp.int32) < plan[..., :1], 0, plan[..., 1:])
    if rows < PATCHES:
        levels = jnp.repeat(levels, PATCHES // rows, axis=-1)
    frames = max(1, rows // PATCHES)
    levels = levels.reshape(-1, clips, seq_devices, frames).transpose(0, 2, 1, 3)
    return levels.reshape(-1, seq_devices, clips * frames)


def condition(levels, here, depth, width):
    half_width = width // 2
    feature = here * depth + jnp.arange(depth, dtype=jnp.int32)
    low_half = feature < half_width
    freqs = jnp.exp(-math.log(10000.0) * jnp.where(low_half, feature, feature - half_width).astype(f32) / half_width)
    angles = levels.reshape(-1, 1).astype(f32) * freqs
    return jax.nn.silu(jnp.where(low_half, jnp.sin(angles), jnp.cos(angles))).astype(bf16)


def own_place(shard, here):
    count = lax.axis_size("clip") * lax.axis_size("seq")
    whole = jnp.zeros((count * shard.shape[0],), f32)
    return lax.dynamic_update_slice_in_dim(whole, shard.astype(f32), here * shard.shape[0], 0)


def body_by_heads(
    tokens,
    ctx_count,
    noise_level,
    mod_weight,
    mod_bias,
    qkv_weight,
    qkv_bias,
    out_weight,
    out_bias,
    up_weight,
    up_bias,
    down_weight,
    down_bias,
    cotangent,
):
    clips, rows, width = tokens.shape
    seq_devices = lax.axis_size("seq")
    devices = lax.axis_size("clip") * seq_devices
    order = near_order()
    here = lax.axis_index("clip") * seq_devices + lax.axis_index("seq")
    total = rows * seq_devices
    frames = max(1, rows // PATCHES)
    span = width // seq_devices
    lines = clips * frames
    piece = out_weight.shape[0]

    full_qkv = lax.all_gather(qkv_weight, BOTH, axis=0, tiled=True)
    unit = down_weight.shape[0]
    owners = (4, seq_devices // 2, 2, unit)
    near_owners = (4, 2, seq_devices // 2, unit)
    down_shard = down_weight.reshape(4, piece, width)
    up_shard = up_weight.reshape((piece,) + owners).transpose(1, 0, 3, 2, 4).reshape(4, piece, width)
    up_shard = jnp.concatenate([up_shard, out_weight[None]], axis=0)

    levels = level_rows(ctx_count, noise_level, rows)
    flat_bits = (2,) * len(order)
    bits_clip, bits_seq = len(axis_bits("clip")), len(axis_bits("seq"))
    turn = tuple(range(bits_clip))[::-1] + tuple(range(bits_clip, bits_clip + bits_seq))[::-1] + (len(order),)
    near_levels = levels.reshape(flat_bits + (lines,)).transpose(turn)
    cond_near = condition(near_levels, here, mod_weight.shape[0], width)
    cond = condition(levels, here, mod_weight.shape[0], width)
    mod_place = own_place(mod_bias, here)

    def modulate(columns, biases, gates=()):
        weight = mod_weight[:, columns]
        bias = jnp.concatenate([own_place(b, here) for b in biases]).reshape(lines, -1)
        rest = jnp.concatenate([jnp.broadcast_to(mod_place[columns], (lines, weight.shape[1])), bias], axis=1)
        part = jnp.pad(dot(cond_near, weight), ((0, 0), (0, bias.shape[1])))
        line_rows = halve_rows((part.reshape(devices, lines, -1) + rest).reshape(devices * lines, -1), order, gates)
        return line_rows[:, : weight.shape[1]], line_rows[:, weight.shape[1] :].reshape(1, -1)

    def blocks(line_rows):
        return line_rows.reshape(clips, frames, -1, width).transpose(0, 2, 1, 3)

    mod_first, bias_qkv = modulate(slice(0, 2 * width), (qkv_bias,))
    mods_one = blocks(mod_first)

    positions = lax.axis_index("seq") * rows + jnp.arange(rows, dtype=jnp.int32)
    cos_local, sin_local = rotary_lanes(positions, max(span, 256))
    cos_row, sin_row = rotary_lanes(jnp.arange(rows, dtype=jnp.int32), span)
    cos_far, sin_far = rotary_lanes(jnp.arange(seq_devices, dtype=jnp.int32) * rows, span)
    cos_all = (cos_far[:, None] * cos_row[None] - sin_far[:, None] * sin_row[None]).reshape(total, span)
    sin_all = (sin_far[:, None] * cos_row[None] + cos_far[:, None] * sin_row[None]).reshape(total, span)

    def exchange(value):
        return lax.all_to_all(value, "seq", 0, 0, tiled=True)

    def doubled(share, axis, bit):
        other = swap_bit(share, axis, bit)
        mine = own_bit(axis, bit) == 0
        pair = jnp.stack([jnp.where(mine, share, other), jnp.where(mine, other, share)], axis=1)
        return pair.reshape((-1,) + share.shape[1:])

    high_bits, low_bit = axis_bits("seq")[:-1], axis_bits("seq")[-1]
    down_share, up_share = down_shard[None], up_shard[None]
    for axis, bit in high_bits:
        down_share, up_share = doubled(down_share, axis, bit), doubled(up_share, axis, bit)
    full_qkv = after(full_qkv, down_share, up_share)
    up_pair = (up_share, swap_bit(up_share, "clip", 2))
    down_share = doubled(down_share, *low_bit)

    normed, qkv, mixes, fulls, logs, sents = [], [], [], [], [], []
    for c in range(clips):
        weight = full_qkv if c == 0 else after(full_qkv, down_share, up_pair[1])
        sent, normed_c = project(tokens, c, mods_one[c], weight, bias_qkv, cos_local, sin_local, seq_devices)
        normed.append(normed_c)
        if qkv:
            sent = after(sent, qkv[-1])
        qkv.append(exchange(sent))
    backs = []
    for c in range(clips):
        mix, full, log = attend(qkv[c].reshape(total, 3 * span), span)
        mixes.append(mix)
        fulls.append(full)
        logs.append(log)
        backs.append(exchange(after(mix.reshape(seq_devices, rows, span), qkv[-1] if c == 0 else backs[-1])))

    mod_rest, bias_rest = modulate(
        slice(2 * width, 6 * width), (out_bias, up_bias, down_bias), (None, None, normed[-1], mixes[0], mixes[-1])
    )
    mods_two = blocks(mod_rest)
    bias_out = bias_rest[:, :width]
    bias_up = bias_rest[:, width : 5 * width].reshape(owners).transpose(0, 2, 1, 3).reshape(1, -1)
    bias_down = bias_rest[:, 5 * width :]
    def from_clips(pair):
        near, across = [p.reshape((seq_devices // 2, 2) + p.shape[1:]) for p in pair]
        far = swap_bit(after(across, qkv[-1]), "clip", 1)
        return (near, across, swap_bit(near, "clip", 1), far)

    down_shares = from_clips((down_share, swap_bit(down_share, "clip", 2)))
    up_shares = from_clips([doubled(p, *low_bit) for p in up_pair])

    results = []
    d_mixed = []
    for c in range(clips):
        back = after(backs[c], mixes[-1])
        outputs = results[-1][0] if results else None
        results.append(middle(back, tokens, cotangent, c, mods_two[c], up_shares, down_shares, (bias_out, bias_up, bias_down), outputs))
        d_mixed.append(exchange(after(results[c][8], backs[-1] if c == 0 else d_mixed[-1])))

    d_qkv, exchanged = [], []
    for c in range(clips):
        grad = after(d_mixed[c], results[-1][8] if c == 0 else d_qkv[-1])
        grad = grad.reshape(total, span)
        d_qkv.append(attend_back(qkv[c].reshape(total, 3 * span), grad, fulls[c], logs[c], cos_all, sin_all, span))
        sent = d_qkv[c].reshape(seq_devices, rows, 3 * span)
        exchanged.append(exchange(after(sent, d_mixed[-1]) if c == 0 else sent))

    def late(place):
        return [r[place] for r in results]

    mixed_all, normed_two, active, d_hidden, d_mlp, d_attn = [late(place) for place in (2, 3, 4, 5, 6, 7)]
    active = gate(active, d_qkv[-1])
    down_first = along_first(active, d_mlp)
    normed_two = gate(normed_two, down_first)
    up_first = across_first(normed_two, d_hidden)
    down_core, up_core = swap_bit(down_first, "clip", 1), swap_bit(up_first, "clip", 1)
    d_mlp = gate(d_mlp, up_first)
    down_second = along_second(active, d_mlp, down_core)
    d_hidden = gate(d_hidden, down_second)
    up_second = across_second(normed_two, d_hidden, up_core)
    mixed_all = gate(mixed_all, up_second)
    out_first = across_first(mixed_all, d_attn)
    out_core = swap_bit(out_first, "clip", 1)
    down_along, up_across = swap_bit(down_second, "seq", 1), swap_bit(up_second, "clip", 2)
    exchanged[0] = after(exchanged[0], out_first)
    exchanged[-1] = after(exchanged[-1], down_along)

    def line_sums(sums):
        return sums.transpose(1, 0, 2).reshape(frames, -1)

    def with_bias(lines_now, vectors):
        return jnp.concatenate([jnp.concatenate(lines_now, axis=0), jnp.concatenate(vectors).reshape(lines, -1)], axis=1)

    bias_up_sum = sum(r[10][0] for r in results).reshape(near_owners).transpose(0, 2, 1, 3).reshape(-1)
    bias_pair = sum(r[11] for r in results)
    early = with_bias([line_sums(r[9]) for r in results], [bias_pair[0], bias_up_sum, bias_pair[1]])
    early_rows = lax.all_gather(early, BOTH, axis=0, tiled=True)

    last = []
    for c in range(clips):
        grads = last[-1][0] if last else None
        last.append(project_back(exchanged[c], full_qkv, tokens, c, mods_one[c][1], results[c][1], grads))
    d_projected = [r[1] for r in last]
    d_attn = gate(d_attn, last[0][1])
    out_across = swap_bit(across_second(mixed_all, d_attn, out_core), "clip", 2)
    qkv_first = across_first(normed, d_projected)
    qkv_core = swap_bit(qkv_first, "clip", 1)
    grad_down = along_total(active, gate(d_mlp, qkv_first), down_core, down_along)
    qkv_across = swap_bit(across_second(gate(normed, up_across), d_projected, qkv_core), "clip", 2)
    grad_up = across_total(normed_two, gate(d_hidden, qkv_first), up_core, up_across)
    grad_up = grad_up.reshape((-1,) + near_owners).transpose(0, 1, 3, 2, 4).reshape(-1, 4 * width)
    grad_out = across_total(mixed_all, gate(d_attn, qkv_first), out_core, out_across)
    grad_qkv = across_total(normed, d_projected, qkv_core, qkv_across)
    late_rows = with_bias([line_sums(r[2]) for r in last], [sum(r[3][0] for r in last)])
    late_rows = spread_rows(after(late_rows, qkv_first), order)

    def own_columns(sums, shard):
        return lax.dynamic_slice_in_dim(sums, here * shard.shape[0], shard.shape[0], 0)

    def spans(all_rows, columns):
        vectors = jnp.sum(all_rows[:, columns:].reshape(devices, -1), axis=0)
        return all_rows[:, :columns], vectors

    late_mod, late_vectors = spans(late_rows, 2 * width)
    early_mod, early_vectors = spans(early_rows, 4 * width)
    grad_mod = jnp.concatenate(
        [
            lax.dot_general(rows_cond.astype(f32), r, TN, precision=highest, preferred_element_type=f32)
            for rows_cond, r in ((cond_near, late_mod), (cond, early_mod))
        ],
        axis=1,
    )
    mod_sum = jnp.concatenate([jnp.sum(late_mod, axis=0), jnp.sum(early_mod, axis=0)])
    return (
        results[-1][0],
        last[-1][0],
        grad_mod,
        own_columns(mod_sum, mod_bias),
        grad_qkv,
        own_columns(late_vectors, qkv_bias),
        grad_out,
        own_columns(early_vectors[:width], out_bias),
        grad_up,
        own_columns(early_vectors[width : 5 * width], up_bias),
        grad_down,
        own_columns(early_vectors[5 * width :], down_bias),
    )


def body_gathered(
    tokens,
    ctx_count,
    noise_level,
    mod_weight,
    mod_bias,
    qkv_weight,
    qkv_bias,
    out_weight,
    out_bias,
    up_weight,
    up_bias,
    down_weight,
    down_bias,
    cotangent,
):
    clips, rows, width = tokens.shape
    seq_devices = lax.axis_size("seq")
    devices = lax.axis_size("clip") * seq_devices
    bits = mesh_bits()
    here = lax.axis_index("clip") * seq_devices + lax.axis_index("seq")
    total = rows * seq_devices
    frames = max(1, rows // PATCHES)
    patch_rows = rows // frames

    full_qkv = lax.all_gather(qkv_weight, BOTH, axis=0, tiled=True)
    full_out = lax.all_gather(out_weight, BOTH, axis=0, tiled=True)
    full_up = lax.all_gather(up_weight, BOTH, axis=0, tiled=True)
    full_down = lax.all_gather(down_weight, BOTH, axis=0, tiled=True)
    biases = (qkv_bias, out_bias, up_bias, down_bias)
    bias_rows = double_rows(jnp.concatenate(biases).astype(f32), bits)
    full_biases = []
    first = 0
    for piece in biases:
        full_biases.append(bias_rows[:, first : first + piece.shape[0]].reshape(1, -1))
        first += piece.shape[0]
    bias_qkv, bias_out, bias_up, bias_down = full_biases

    levels = level_rows(ctx_count, noise_level, rows)
    cond = condition(levels, here, mod_weight.shape[0], width)
    mod_width = mod_weight.shape[1]
    partial = dot(cond, mod_weight) + own_place(mod_bias, here)
    modulation = halve_sum(partial.reshape(devices, clips * frames, mod_width), bits)
    modulation = modulation.reshape(clips, frames, 1, mod_width)

    positions = lax.axis_index("seq") * rows + jnp.arange(rows, dtype=jnp.int32)
    cosine, sine = rotary_lanes(positions, HEAD_DIM)
    key_frame = jnp.arange(total, dtype=jnp.int32) // PATCHES
    allowed = key_frame[None, :] <= (positions // PATCHES)[:, None]

    def flat(value):
        return value.reshape(rows, value.shape[-1])

    def split(value):
        return value.reshape(frames, patch_rows, value.shape[-1])

    def to_heads(value):
        return value.reshape(rows, HEADS, HEAD_DIM).transpose(1, 0, 2)

    saved = []
    for c in range(clips):
        mods = jnp.split(modulation[c], 6, axis=-1)
        tokens_now = split(tokens[c].astype(f32))
        unit, inverse = norm_parts(tokens_now)
        normed = flat((unit * (1.0 + mods[1]) + mods[0]).astype(bf16))
        projected = dot(normed, full_qkv) + bias_qkv
        views = []
        for place in range(3):
            view = to_heads(projected[:, place * width : (place + 1) * width])
            if place < 2:
                    view = view * cosine + jnp.roll(view, HEAD_DIM // 2, -1) * sine
            views.append(view.astype(bf16))
        queries, keys, values = views
        keys = lax.all_gather(keys, "seq", axis=1, tiled=True)
        values = lax.all_gather(values, "seq", axis=1, tiled=True)
        mix, logs = gathered_forward(queries, keys, values, allowed)
        mixed = mix.transpose(1, 0, 2).reshape(rows, width).astype(bf16)
        kept = (queries, keys, values, logs)
        saved.append((mods, tokens_now, unit, inverse, normed, kept, mixed))

    outputs = []
    middle = []
    for c in range(clips):
        mods, tokens_now, unit, inverse, normed, kept, mixed = saved[c]
        _, _, gate_one, shift_two, scale_two, gate_two = mods
        attn_out = split(dot(mixed, full_out) + bias_out)
        resid = tokens_now + gate_one * attn_out
        unit_two, inverse_two = norm_parts(resid)
        normed_two = flat((unit_two * (1.0 + scale_two) + shift_two).astype(bf16))
        hidden = dot(normed_two, full_up) + bias_up
        active_full, gelu_back = jax.vjp(jax.nn.gelu, hidden)
        active = active_full.astype(bf16)
        mlp_out = split(dot(active, full_down) + bias_down)
        outputs.append(flat((resid + gate_two * mlp_out).astype(bf16)))
        grad_out = split(cotangent[c].astype(f32))
        d_mlp = flat((gate_two * grad_out).astype(bf16))
        d_hidden = gelu_back(dot(d_mlp, full_down, NT))[0].astype(bf16)
        d_normed_two = split(dot(d_hidden, full_up, NT))
        d_resid = grad_out + norm_back(unit_two, inverse_two, d_normed_two, scale_two)
        d_attn = flat((gate_one * d_resid).astype(bf16))
        d_mixed = dot(d_attn, full_out, NT).astype(bf16)
        d_early = jnp.concatenate(
            [
                jnp.sum(d_resid * attn_out, axis=1),
                jnp.sum(d_normed_two, axis=1),
                jnp.sum(d_normed_two * unit_two, axis=1),
                jnp.sum(grad_out * mlp_out, axis=1),
            ],
            axis=-1,
        )
        middle.append((mixed, d_attn, normed_two, d_hidden, active, d_mlp, d_resid, d_mixed, d_early))

    def both(place):
        return jnp.concatenate([m[place] for m in middle], axis=0)

    d_attn_all, d_hidden_all, d_mlp_all = both(1), both(3), both(5)
    grad_down = weight_grad(both(4), d_mlp_all)
    grad_up = weight_grad(both(2), d_hidden_all)
    grad_out_weight = weight_grad(both(0), d_attn_all)
    early_rows = lax.all_gather(both(8), BOTH, axis=0, tiled=True)

    inputs_grad = []
    late = []
    projected_grads = []
    for c in range(clips):
        mods, tokens_now, unit, inverse, normed, kept, mixed = saved[c]
        d_resid, d_mixed = middle[c][6], middle[c][7]
        queries, keys, values, logs = kept
        dq, dk, dv = gathered_back(queries, keys, values, to_heads(d_mixed), logs, allowed)
        dk = lax.psum_scatter(dk.astype(bf16), "seq", scatter_dimension=1, tiled=True).astype(f32)
        dv = lax.psum_scatter(dv.astype(bf16), "seq", scatter_dimension=1, tiled=True).astype(f32)
        views = [g * cosine - jnp.roll(g, HEAD_DIM // 2, -1) * sine for g in (dq, dk)] + [dv]
        d_projected = jnp.concatenate([g.transpose(1, 0, 2).reshape(rows, width) for g in views], axis=1).astype(bf16)
        projected_grads.append(d_projected)
        d_normed = split(dot(d_projected, full_qkv, NT))
        inputs_grad.append(flat(d_resid + norm_back(unit, inverse, d_normed, mods[1])))
        late.append(jnp.concatenate([jnp.sum(d_normed, axis=1), jnp.sum(d_normed * unit, axis=1)], axis=-1))

    d_projected_all = jnp.concatenate(projected_grads, axis=0)
    grad_qkv = weight_grad(jnp.concatenate([s[4] for s in saved], axis=0), d_projected_all)
    bias_grads = [
        jnp.sum(g.astype(f32), axis=0).reshape(devices, -1) for g in (d_projected_all, d_attn_all, d_hidden_all, d_mlp_all)
    ]
    bias_sum = halve_sum(jnp.concatenate(bias_grads, axis=1), bits)
    grad_biases = []
    first = 0
    for piece in bias_grads:
        grad_biases.append(bias_sum[first : first + piece.shape[1]])
        first += piece.shape[1]

    late_rows = double_rows(jnp.concatenate(late, axis=0), bits).reshape(-1, 2 * width)
    grad_mod = jnp.concatenate(
        [
            lax.dot_general(cond.astype(f32), r, TN, precision=highest, preferred_element_type=f32)
            for r in (late_rows, early_rows)
        ],
        axis=1,
    )
    mod_sum = jnp.concatenate([jnp.sum(late_rows, axis=0), jnp.sum(early_rows, axis=0)])
    grad_mod_bias = lax.dynamic_slice_in_dim(mod_sum, here * mod_bias.shape[0], mod_bias.shape[0], 0)
    return (
        jnp.stack(outputs),
        jnp.stack(inputs_grad),
        grad_mod,
        grad_mod_bias,
        grad_qkv,
        grad_biases[0],
        grad_out_weight,
        grad_biases[1],
        grad_up,
        grad_biases[2],
        grad_down,
        grad_biases[3],
    )


def solution(mesh):
    by_heads = HEADS % mesh.shape["seq"] == 0
    body = body_by_heads if by_heads else body_gathered
    token_place = P("clip", "seq", None)
    matrix, vector = P(BOTH, None), P(BOTH)
    weights = (matrix, vector) * 5
    return jax.shard_map(
        body,
        mesh=mesh,
        in_specs=(token_place, P("clip"), P("clip", None)) + weights + (token_place,),
        out_specs=(token_place, token_place) + weights,
        check_vma=False,
    )
```

```python
import functools
import math

import jax
import jax.numpy as jnp
from jax import lax
from jax.experimental import pallas as pl
from jax.experimental.pallas import tpu as pltpu
from jax.sharding import PartitionSpec as P

HEADS = 16
HEAD_DIM = 64
FRAMES = 16
PATCHES = 256
BOTH = ("clip", "seq")
NT = (((1,), (1,)), ((), ()))
NN = (((1,), (0,)), ((), ()))
TN = (((0,), (0,)), ((), ()))
bf16 = jnp.bfloat16
f32 = jnp.float32
highest = lax.Precision.HIGHEST


def dot(left, right, dims=NN):
    return lax.dot_general(left, right, dims, preferred_element_type=f32)


def swap_bit(value, axis, bit):
    count = lax.axis_size(axis)
    return lax.ppermute(value, axis, [(i, i ^ bit) for i in range(count)])


def own_bit(axis, bit):
    return lax.shift_right_logical(lax.axis_index(axis), bit.bit_length() - 1) & 1


def axis_bits(axis):
    bits = []
    bit = 1
    while bit < lax.axis_size(axis):
        bits.append((axis, bit))
        bit *= 2
    return bits[::-1]


def exchange_order(bits):
    return sorted(range(len(bits)), key=lambda place: bits[place])


def mesh_bits():
    return axis_bits("clip") + axis_bits("seq")


def halve_sum(parts, bits, wire=f32):
    parts = parts.reshape((2,) * len(bits) + parts.shape[1:])
    for place in exchange_order(bits):
        axis, bit = bits[place]
        mine = own_bit(axis, bit)
        keep = lax.dynamic_index_in_dim(parts, mine, place)
        send = lax.dynamic_index_in_dim(parts, 1 - mine, place)
        parts = keep + swap_bit(send.astype(wire), axis, bit).astype(f32)
    return parts.reshape(parts.shape[len(bits) :])


def near_order():
    return axis_bits("clip")[::-1] + axis_bits("seq")[::-1]


def halve_rows(parts, bits, gates=()):
    for place, (axis, bit) in enumerate(bits):
        half = parts.shape[0] // 2
        mine = own_bit(axis, bit)
        keep = lax.dynamic_slice_in_dim(parts, mine * half, half, 0)
        send = lax.dynamic_slice_in_dim(parts, (1 - mine) * half, half, 0)
        other = swap_bit(send, axis, bit)
        if place < len(gates) and gates[place] is not None:
            other = after(other, gates[place])
        parts = keep + other
    return parts


def spread_rows(rows, bits):
    for axis, bit in reversed(bits):
        other = swap_bit(rows, axis, bit)
        low = own_bit(axis, bit) == 0
        rows = jnp.concatenate([jnp.where(low, rows, other), jnp.where(low, other, rows)], axis=0)
    return rows


def after(value, *others):
    return lax.optimization_barrier((value,) + others)[0]


def double_rows(row, bits):
    rows = row[None]
    for axis, bit in reversed(bits):
        other = swap_bit(rows, axis, bit)
        low = own_bit(axis, bit) == 0
        rows = jnp.concatenate([jnp.where(low, rows, other), jnp.where(low, other, rows)], axis=0)
    return rows


def weight_grad(left, right):
    tokens, rows = left.shape
    quarter = rows // lax.axis_size("clip")
    mine = lax.axis_index("clip")

    def part(flip):
        piece = lax.dynamic_slice_in_dim(left, (mine ^ flip) * quarter, quarter, 1)
        return dot(piece, right, TN)

    far = swap_bit(part(3).astype(bf16), "clip", 1)
    near = swap_bit(part(1).astype(bf16), "clip", 1)
    across = swap_bit((part(2) + far.astype(f32)).astype(bf16), "clip", 2)
    total = part(0) + near.astype(f32) + across.astype(f32)
    return halve_sum(total.reshape((lax.axis_size("seq"), -1, right.shape[1])), axis_bits("seq"), bf16)


def norm_parts(values):
    centre = values - jnp.mean(values, axis=-1, keepdims=True)
    spread = jnp.mean(centre * centre, axis=-1, keepdims=True)
    inverse = lax.rsqrt(spread + 1e-06)
    return centre * inverse, inverse


def norm_back(unit, inverse, grad, scales):
    scaled = grad * (1.0 + scales)
    mean = jnp.mean(scaled, axis=-1, keepdims=True)
    along = jnp.mean(scaled * unit, axis=-1, keepdims=True)
    return inverse * (scaled - mean - unit * along)


def rotary_lanes(positions, width):
    half = HEAD_DIM // 2
    lane = jnp.arange(width, dtype=jnp.int32) % HEAD_DIM
    freqs = jnp.exp(-math.log(10000.0) * 2.0 * (lane % half).astype(f32) / HEAD_DIM)
    angles = positions.astype(f32)[:, None] * freqs[None, :]
    sign = jnp.where(lane < half, -1.0, 1.0).astype(f32)
    return jnp.cos(angles), jnp.sin(angles) * sign[None, :]


def partner(values):
    width = values.shape[1]
    half = HEAD_DIM // 2
    lane = lax.broadcasted_iota(jnp.int32, (1, width), 1) % HEAD_DIM
    return jnp.where(lane < half, pltpu.roll(values, width - half, 1), pltpu.roll(values, half, 1))


def project_kernel(
    token_ref, mod_ref, wq_ref, wk_ref, wv_ref, bq_ref, bk_ref, bv_ref, cos_ref, sin_ref, out_ref, normed_ref, *, span
):
    frames = mod_ref.shape[1]
    patch = token_ref.shape[0] // frames

    @pl.when(pl.program_id(0) == 0)
    def _():
        for f in range(frames):
            rows = slice(f * patch, (f + 1) * patch)
            unit, _ = norm_parts(token_ref[rows, :].astype(f32))
            normed_ref[rows, :] = (unit * (1.0 + mod_ref[1, f : f + 1, :]) + mod_ref[0, f : f + 1, :]).astype(bf16)

    x = normed_ref[...]
    cosine, sine = cos_ref[...], sin_ref[...]
    groups = wq_ref.shape[1] // span
    for place, (w_ref, b_ref) in enumerate(((wq_ref, bq_ref), (wk_ref, bk_ref), (wv_ref, bv_ref))):
        value = dot(x, w_ref[...]) + b_ref[...]
        if place < 2:
            value = value * cosine + partner(value) * sine
        value = value.astype(bf16)
        for g in range(groups):
            out_ref[g, :, place * span : (place + 1) * span] = value[:, g * span : (g + 1) * span]


def whole_block(shape):
    return pl.BlockSpec(shape, lambda j: (0,) * len(shape))


def column_specs(height, block, steps):
    return [pl.BlockSpec((height, block), functools.partial(lambda p, j: (0, p * steps + j), p)) for p in range(3)]


def clip_block(shape, c):
    return pl.BlockSpec((None,) + shape[1:], lambda j: (c,) + (0,) * (len(shape) - 1))


def project(tokens, c, mods, weight, bias, cosine, sine, groups):
    _, rows, width = tokens.shape
    span = width // groups
    block = max(span, 256)
    per_step = block // span
    steps = groups // per_step
    return pl.pallas_call(
        functools.partial(project_kernel, span=span),
        grid=(steps,),
        in_specs=[clip_block(tokens.shape, c), whole_block(mods.shape)]
        + column_specs(width, block, steps)
        + column_specs(1, block, steps)
        + [whole_block((rows, block))] * 2,
        out_specs=(pl.BlockSpec((per_step, rows, 3 * span), lambda j: (j, 0, 0)), whole_block((rows, width))),
        out_shape=(
            jax.ShapeDtypeStruct((groups, rows, 3 * span), bf16),
            jax.ShapeDtypeStruct((rows, width), bf16),
        ),
        compiler_params=pltpu.CompilerParams(vmem_limit_bytes=60 << 20),
        cost_estimate=pl.CostEstimate(
            flops=6 * rows * width * width, bytes_accessed=6 * width * width + 10 * rows * width, transcendentals=0
        ),
        name="project",
    )(tokens, mods, weight, weight, weight, bias, bias, bias, cosine, sine)


def project_back_kernel(
    back_ref, wq_ref, wk_ref, wv_ref, token_ref, scale_ref, resid_ref, *rest, span
):
    grad_ref, proj_ref, sums_ref, bias_ref, acc_ref = rest[-5:]
    frames = scale_ref.shape[0]
    rows_all, width = token_ref.shape
    patch = rows_all // frames
    step = pl.program_id(0)
    block = wq_ref.shape[1]

    @pl.when(step == 0)
    def _():
        acc_ref[...] = jnp.zeros_like(acc_ref)

    for place, w_ref in enumerate((wq_ref, wk_ref, wv_ref)):
        band = slice(place * span, (place + 1) * span)
        piece = jnp.concatenate([back_ref[g, :, band] for g in range(block // span)], axis=1)
        columns = pl.ds(pl.multiple_of(place * width + step * block, block), block)
        proj_ref[:, columns] = piece
        bias_ref[:, columns] = jnp.sum(piece.astype(f32), axis=0, keepdims=True)
        acc_ref[...] += dot(piece, w_ref[...], NT)

    @pl.when(step == pl.num_programs(0) - 1)
    def _():
        for f in range(frames):
            rows = slice(f * patch, (f + 1) * patch)
            unit, inverse = norm_parts(token_ref[rows, :].astype(f32))
            grad = acc_ref[rows, :]
            grad_ref[rows, :] = resid_ref[rows, :] + norm_back(unit, inverse, grad, scale_ref[f : f + 1, :])
            sums_ref[0, f : f + 1, :] = jnp.sum(grad, axis=0, keepdims=True)
            sums_ref[1, f : f + 1, :] = jnp.sum(grad * unit, axis=0, keepdims=True)


def project_back(back, weight, tokens, c, scales, d_resid, grads):
    groups, rows, _ = back.shape
    width = tokens.shape[2]
    span = width // groups
    block = max(span, 256)
    per_step = block // span
    steps = groups // per_step
    earlier = [] if grads is None else [grads]
    return pl.pallas_call(
        functools.partial(project_back_kernel, span=span),
        grid=(steps,),
        in_specs=[pl.BlockSpec((per_step, rows, 3 * span), lambda j: (j, 0, 0))]
        + column_specs(width, block, steps)
        + [clip_block(tokens.shape, c), whole_block(scales.shape), whole_block((rows, width))]
        + [pl.BlockSpec(memory_space=pl.ANY)] * len(earlier),
        out_specs=(
            clip_block(tokens.shape, c),
            whole_block((rows, 3 * width)),
            whole_block((2,) + scales.shape),
            whole_block((1, 3 * width)),
        ),
        out_shape=(
            jax.ShapeDtypeStruct(tokens.shape, f32),
            jax.ShapeDtypeStruct((rows, 3 * width), bf16),
            jax.ShapeDtypeStruct((2,) + scales.shape, f32),
            jax.ShapeDtypeStruct((1, 3 * width), f32),
        ),
        input_output_aliases={7: 0} if earlier else {},
        scratch_shapes=[pltpu.VMEM((rows, width), f32)],
        compiler_params=pltpu.CompilerParams(vmem_limit_bytes=60 << 20),
        cost_estimate=pl.CostEstimate(
            flops=6 * rows * width * width, bytes_accessed=6 * width * width + 22 * rows * width, transcendentals=0
        ),
        name="project_back",
    )(back, weight, weight, weight, tokens, scales, d_resid, *earlier)


GELU_RATE = math.sqrt(2.0 / math.pi)
GELU_CUBE = 0.044715


def middle_kernel(clip_ref, back_ref, token_ref, cot_ref, mod_ref, bo_ref, bup_ref, bdown_ref, *refs):
    wo_refs, up_refs, down_refs = refs[0:4], refs[4:8], refs[8:12]
    (
        out_ref,
        dres_ref,
        mixed_ref,
        normed_ref,
        act_ref,
        dhid_ref,
        dmlp_ref,
        dattn_ref,
        dmix_ref,
        sums_ref,
        bup_sum_ref,
        bsum_ref,
        attn_ref,
        res_ref,
        mlp_ref,
        dn_ref,
        wo_ref,
        up_ref,
        down_ref,
    ) = refs[-19:]
    groups, rows_all, span = back_ref.shape
    width = token_ref.shape[1]
    quarter = width // 4
    frames = mod_ref.shape[1]
    patch = rows_all // frames
    step = pl.program_id(0)
    mine = clip_ref[0]

    def owner_rows(place):
        return pl.ds(pl.multiple_of((mine ^ FLIPS[place]) * quarter, quarter), quarter)

    @pl.when(step == 0)
    def _():
        for place in range(4):
            wo_ref[owner_rows(place), :] = wo_refs[place][...].reshape(quarter, width)
        for g in range(groups):
            mixed_ref[:, g * span : (g + 1) * span] = back_ref[g]
        attn_ref[...] = dot(mixed_ref[...], wo_ref[...]) + bo_ref[...]
        for f in range(frames):
            rows = slice(f * patch, (f + 1) * patch)
            resid = token_ref[rows, :].astype(f32) + mod_ref[0, f : f + 1, :] * attn_ref[rows, :]
            res_ref[rows, :] = resid
            unit, _ = norm_parts(resid)
            normed_ref[rows, :] = (unit * (1.0 + mod_ref[2, f : f + 1, :]) + mod_ref[1, f : f + 1, :]).astype(bf16)
            dmlp_ref[rows, :] = (mod_ref[3, f : f + 1, :] * cot_ref[rows, :].astype(f32)).astype(bf16)
        mlp_ref[...] = jnp.zeros_like(mlp_ref)
        dn_ref[...] = jnp.zeros_like(dn_ref)

    for place in range(4):
        up_ref[owner_rows(place), :] = up_refs[place][...].reshape(quarter, -1)

        @pl.when(step // 2 == place)
        def _(place=place):
            down_ref[...] = down_refs[place][...].reshape(-1, width)

    up = up_ref[...]
    down = down_ref[...]
    hidden = dot(normed_ref[...], up) + bup_ref[...]
    square = hidden * hidden
    bend = jnp.tanh(GELU_RATE * (hidden + GELU_CUBE * (square * hidden)))
    share = 0.5 * (1.0 + bend)
    active = (hidden * share).astype(bf16)
    act_ref[...] = active
    mlp_ref[...] += dot(active, down)
    slope = share + 0.5 * hidden * (1.0 - bend * bend) * (GELU_RATE + (3.0 * GELU_RATE * GELU_CUBE) * square)
    d_hidden = (dot(dmlp_ref[...], down, NT) * slope).astype(bf16)
    dhid_ref[...] = d_hidden
    bup_sum_ref[...] = jnp.sum(d_hidden.astype(f32), axis=0, keepdims=True)
    dn_ref[...] += dot(d_hidden, up, NT)

    @pl.when(step == pl.num_programs(0) - 1)
    def _():
        bsum = None
        for f in range(frames):
            rows = slice(f * patch, (f + 1) * patch)
            resid = res_ref[rows, :]
            mlp = mlp_ref[rows, :] + bdown_ref[...]
            out_ref[rows, :] = (resid + mod_ref[3, f : f + 1, :] * mlp).astype(bf16)
            cot = cot_ref[rows, :].astype(f32)
            sums_ref[3, f : f + 1, :] = jnp.sum(cot * mlp, axis=0, keepdims=True)
            unit, inverse = norm_parts(resid)
            grad = dn_ref[rows, :]
            sums_ref[1, f : f + 1, :] = jnp.sum(grad, axis=0, keepdims=True)
            sums_ref[2, f : f + 1, :] = jnp.sum(grad * unit, axis=0, keepdims=True)
            d_resid = cot + norm_back(unit, inverse, grad, mod_ref[2, f : f + 1, :])
            dres_ref[rows, :] = d_resid
            sums_ref[0, f : f + 1, :] = jnp.sum(d_resid * attn_ref[rows, :], axis=0, keepdims=True)
            d_attn = (mod_ref[0, f : f + 1, :] * d_resid).astype(bf16)
            dattn_ref[rows, :] = d_attn
            term = jnp.concatenate(
                [
                    jnp.sum(d_attn.astype(f32), axis=0, keepdims=True),
                    jnp.sum(dmlp_ref[rows, :].astype(f32), axis=0, keepdims=True),
                ],
                axis=0,
            )
            bsum = term if bsum is None else bsum + term
        bsum_ref[...] = bsum
        d_mixed = dot(dattn_ref[...], wo_ref[...], NT).astype(bf16)
        for g in range(groups):
            dmix_ref[g] = d_mixed[:, g * span : (g + 1) * span]


FLIPS = (0, 2, 1, 3)


def middle(back, tokens, cot, c, mods, up_shares, down_shares, biases, outputs):
    groups, rows, span = back.shape
    _, _, width = tokens.shape
    high, low, _, piece, _ = up_shares[0].shape
    hidden = 4 * width
    steps = 8
    block = hidden // steps
    bias_out, bias_up, bias_down = biases
    mine = lax.axis_index("clip").astype(jnp.int32)[None]
    earlier = [] if outputs is None else [outputs]

    def fixed(shape, **options):
        return pl.BlockSpec(shape, lambda j, q: (0,) * len(shape), **options)

    def clip_part(shape):
        return pl.BlockSpec((None,) + shape[1:], lambda j, q: (c,) + (0,) * (len(shape) - 1))

    def unit_block(j, q):
        owner = q[0] ^ jnp.where(j // 2 == 1, 2, jnp.where(j // 2 == 2, 1, j // 2))
        return owner, j % 2

    def up_index(j, q):
        owner, half = unit_block(j, q)
        return (0, 0, owner, 0, half)

    def hidden_index(j, q):
        owner, half = unit_block(j, q)
        return (0, owner * 2 + half)

    def down_index(place, j, q):
        return (0, jnp.clip(j - 2 * place, 0, 1), 0, 0, 0)

    token_block = fixed((rows, width))
    hidden_block = pl.BlockSpec((rows, block), hidden_index)
    out_spec = [
        pl.BlockSpec((high, low, 1, piece, width), lambda j, q: (0, 0, 4, 0, 0), pipeline_mode=pl.Buffered(1)) for _ in range(4)
    ]
    up_spec = [pl.BlockSpec((high, low, 1, piece, block), up_index) for _ in range(4)]
    down_spec = [
        pl.BlockSpec((high, 1, 4, piece, width), functools.partial(down_index, place)) for place in range(4)
    ]
    return pl.pallas_call(
        middle_kernel,
        grid_spec=pltpu.PrefetchScalarGridSpec(
            num_scalar_prefetch=1,
            grid=(steps,),
            in_specs=[
                fixed(back.shape),
                clip_part(tokens.shape),
                clip_part(tokens.shape),
                fixed(mods.shape),
                fixed((1, width)),
                pl.BlockSpec((1, block), hidden_index),
                fixed((1, width)),
            ]
            + out_spec
            + up_spec
            + down_spec
            + [pl.BlockSpec(memory_space=pl.ANY)] * len(earlier),
            out_specs=(
                clip_part(tokens.shape),
                token_block,
                token_block,
                token_block,
                hidden_block,
                hidden_block,
                token_block,
                token_block,
                fixed(back.shape),
                fixed(mods.shape),
                pl.BlockSpec((1, block), hidden_index),
                fixed((2, width)),
            ),
            scratch_shapes=[pltpu.VMEM((rows, width), f32)] * 4
            + [pltpu.VMEM((width, width), bf16), pltpu.VMEM((width, block), bf16), pltpu.VMEM((block, width), bf16)],
        ),
        out_shape=(
            jax.ShapeDtypeStruct(tokens.shape, bf16),
            jax.ShapeDtypeStruct((rows, width), f32),
            jax.ShapeDtypeStruct((rows, width), bf16),
            jax.ShapeDtypeStruct((rows, width), bf16),
            jax.ShapeDtypeStruct((rows, hidden), bf16),
            jax.ShapeDtypeStruct((rows, hidden), bf16),
            jax.ShapeDtypeStruct((rows, width), bf16),
            jax.ShapeDtypeStruct((rows, width), bf16),
            jax.ShapeDtypeStruct(back.shape, bf16),
            jax.ShapeDtypeStruct(mods.shape, f32),
            jax.ShapeDtypeStruct((1, hidden), f32),
            jax.ShapeDtypeStruct((2, width), f32),
        ),
        input_output_aliases={20: 0} if earlier else {},
        compiler_params=pltpu.CompilerParams(vmem_limit_bytes=60 << 20),
        cost_estimate=pl.CostEstimate(
            flops=4 * rows * width * width, bytes_accessed=2 * width * width + 5 * rows * width, transcendentals=rows * width
        ),
        name="middle",
    )(mine, back, tokens, cot, mods, bias_out, bias_up, bias_down, *up_shares, *up_shares, *down_shares, *earlier)


def weight_part_kernel(index_ref, *refs, clips, addends):
    left, right = refs[:clips], refs[clips : 2 * clips]
    extra = refs[2 * clips : 2 * clips + addends]
    out_ref, flat_ref = refs[2 * clips + addends :]
    rows = left[0].shape[0]

    @pl.when(pl.program_id(1) == 0)
    def _():
        for c in range(clips):
            flat_ref[:, c * rows : (c + 1) * rows] = jnp.transpose(left[c][...])

    total = dot(flat_ref[:, 0:rows], right[0][...])
    for c in range(1, clips):
        total += dot(flat_ref[:, c * rows : (c + 1) * rows], right[c][...])
    for ref in extra:
        total += ref[0].astype(f32)
    out_ref[0] = total.astype(out_ref.dtype)


def weight_part(left, right, indices, addends, kind, height, first_column=0, columns=None):
    rows = left[0].shape[0]
    columns = right[0].shape[1] if columns is None else columns
    block = 512
    start = first_column // block
    count = indices.shape[0]
    in_specs = [pl.BlockSpec((rows, height), lambda i, j, q: (0, q[i]))] * len(left)
    in_specs += [pl.BlockSpec((rows, block), lambda i, j, q: (0, start + j))] * len(right)
    for array, first in addends:
        shift = start if array.shape[2] > columns else 0
        where = functools.partial(lambda first, shift, i, j, q: (first + i, 0, shift + j), first, shift)
        in_specs.append(pl.BlockSpec((1, height, block), where))
    return pl.pallas_call(
        functools.partial(weight_part_kernel, clips=len(left), addends=len(addends)),
        grid_spec=pltpu.PrefetchScalarGridSpec(
            num_scalar_prefetch=1,
            grid=(count, columns // block),
            in_specs=in_specs,
            out_specs=pl.BlockSpec((1, height, block), lambda i, j, q: (i, 0, j)),
            scratch_shapes=[pltpu.VMEM((height, len(left) * rows), bf16)],
        ),
        out_shape=jax.ShapeDtypeStruct((count, height, columns), kind),
        compiler_params=pltpu.CompilerParams(vmem_limit_bytes=60 << 20),
        cost_estimate=pl.CostEstimate(
            flops=2 * count * len(left) * rows * height * columns,
            bytes_accessed=len(left) * rows * (count * height + columns) * 2 + 4 * count * height * columns,
            transcendentals=0,
        ),
        name="weight_part",
    )(indices, *left, *right, *[array for array, _ in addends])


def mine_on(axis):
    return lax.axis_index(axis).astype(jnp.int32)


def gate(arrays, *others):
    return list(lax.optimization_barrier((tuple(arrays), others))[0])


def across_first(left, right):
    mine = mine_on("clip")
    return weight_part(left, right, jnp.stack([mine ^ 3, mine ^ 1]), (), bf16, left[0].shape[1] // 4)


def across_second(left, right, core):
    return weight_part(left, right, (mine_on("clip") ^ 2)[None], ((core, 0),), bf16, left[0].shape[1] // 4)


def across_total(left, right, core, across):
    height = left[0].shape[1] // 4
    total = weight_part(left, right, mine_on("clip")[None], ((core, 1), (across, 0)), f32, height)
    return halve_sum(total.reshape((lax.axis_size("seq"), -1, right[0].shape[1])), axis_bits("seq"), bf16)


def along_block(clip_flip, low_flip):
    return (mine_on("clip") ^ clip_flip) * 2 + ((mine_on("seq") & 1) ^ low_flip)


def along_first(left, right):
    blocks = jnp.stack([along_block(1, 1), along_block(3, 1), along_block(1, 0), along_block(3, 0)])
    return weight_part(left, right, blocks, (), bf16, left[0].shape[1] // 8)


def along_second(left, right, core):
    blocks = jnp.stack([along_block(0, 1), along_block(2, 1)])
    return weight_part(left, right, blocks, ((core, 0),), bf16, left[0].shape[1] // 8)


def along_third(left, right, core, along):
    return weight_part(left, right, along_block(2, 0)[None], ((core, 3), (along, 1)), bf16, left[0].shape[1] // 8)


def along_total(left, right, core, along, across):
    addends = ((core, 2), (along, 0), (across, 0))
    total = weight_part(left, right, along_block(0, 0)[None], addends, f32, left[0].shape[1] // 8)
    bits = axis_bits("seq")[:-1]
    return halve_sum(total.reshape((2 ** len(bits), -1, right[0].shape[1])), bits, bf16)


def attend_kernel(qkv_ref, mix_ref, full_ref, log_ref, vt_ref, *, total, span, block):
    heads = span // HEAD_DIM
    head = lax.broadcasted_iota(jnp.int32, (1, span), 1) // HEAD_DIM
    key_frame = lax.broadcasted_iota(jnp.int32, (block, block), 0) // PATCHES
    query_frame = lax.broadcasted_iota(jnp.int32, (block, block), 1) // PATCHES
    kept = key_frame <= query_frame

    def flip(j, carry):
        rows = pl.ds(pl.multiple_of(j * block, block), block)
        vt_ref[:, rows] = jnp.transpose(qkv_ref[rows, 2 * span : 3 * span])
        return carry

    lax.fori_loop(0, total // block, flip, 0)

    def query_block(i, carry):
        rows = pl.ds(pl.multiple_of(i * block, block), block)
        query = qkv_ref[rows, 0:span] * jnp.asarray(HEAD_DIM**-0.5, bf16)
        queries = [jnp.where(head == h, query, jnp.zeros_like(query)) for h in range(heads)]

        def step(j, state, masked):
            peaks, sums, mixes = state
            columns = pl.ds(pl.multiple_of(j * block, block), block)
            key = qkv_ref[columns, span : 2 * span]
            new = ([], [], [])
            for h in range(heads):
                scores = dot(key, queries[h], NT)
                if masked:
                    scores = jnp.where(kept, scores, -1e30)
                peak = jnp.maximum(peaks[h], jnp.max(scores, axis=0, keepdims=True))
                raised = jnp.exp(scores - peak)
                fade = jnp.exp(peaks[h] - peak)
                new[0].append(peak)
                new[1].append(fade * sums[h] + jnp.sum(raised, axis=0, keepdims=True))
                term = dot(vt_ref[h * HEAD_DIM : (h + 1) * HEAD_DIM, columns], raised.astype(bf16))
                new[2].append(mixes[h] * fade + term)
            return tuple(map(tuple, new))

        state = (
            tuple(jnp.full((1, block), -1e30, f32) for _ in range(heads)),
            tuple(jnp.zeros((1, block), f32) for _ in range(heads)),
            tuple(jnp.zeros((HEAD_DIM, block), f32) for _ in range(heads)),
        )
        state = lax.fori_loop(0, i, lambda j, s: step(j, s, False), state)
        peaks, sums, mixes = step(i, state, True)
        mixed = jnp.transpose(jnp.concatenate([mixes[h] / sums[h] for h in range(heads)], axis=0))
        full_ref[rows, :] = mixed
        mix_ref[rows, :] = mixed.astype(bf16)
        for h in range(heads):
            log_ref[h : h + 1, rows] = peaks[h] + jnp.log(sums[h])
        return carry

    lax.fori_loop(0, total // block, query_block, 0)


def attend(qkv, span):
    total = qkv.shape[0]
    heads = span // HEAD_DIM
    block = min(1024, total)
    return pl.pallas_call(
        functools.partial(attend_kernel, total=total, span=span, block=block),
        out_shape=(
            jax.ShapeDtypeStruct((total, span), bf16),
            jax.ShapeDtypeStruct((total, span), f32),
            jax.ShapeDtypeStruct((heads, total), f32),
        ),
        scratch_shapes=[pltpu.VMEM((span, total), bf16)],
        compiler_params=pltpu.CompilerParams(vmem_limit_bytes=60 << 20),
        cost_estimate=pl.CostEstimate(
            flops=8 * total * total * span, bytes_accessed=12 * total * span, transcendentals=total * total * heads // 2
        ),
        name="attend",
    )(qkv)


def attend_back_kernel(
    qkv_ref, grad_ref, full_ref, log_ref, cos_ref, sin_ref, out_ref, dq_ref, dk_ref, dv_ref, along_ref, *, total, span, block
):
    heads = span // HEAD_DIM
    scale = HEAD_DIM**-0.5
    head = lax.broadcasted_iota(jnp.int32, (1, span), 1) // HEAD_DIM
    blocks = total // block
    dq_ref[...] = jnp.zeros_like(dq_ref)

    def only(value, h):
        return jnp.where(head == h, value, jnp.zeros_like(value))

    def lead(i, carry):
        rows = pl.ds(pl.multiple_of(i * block, block), block)
        product = jnp.transpose(grad_ref[rows, :].astype(f32) * full_ref[rows, :])
        for h in range(heads):
            along_ref[h : h + 1, rows] = jnp.sum(product[h * HEAD_DIM : (h + 1) * HEAD_DIM], axis=0, keepdims=True)
        return carry

    lax.fori_loop(0, blocks, lead, 0)

    def key_block(j, carry):
        first = pl.multiple_of(j * block, block)
        columns = pl.ds(first, block)
        key = qkv_ref[columns, span : 2 * span]
        value = qkv_ref[columns, 2 * span : 3 * span]
        key_flat = jnp.transpose(key)
        dk_ref[...] = jnp.zeros_like(dk_ref)
        dv_ref[...] = jnp.zeros_like(dv_ref)

        def tile(rows, keys, h, query_h, grad_h):
            band = slice(h * HEAD_DIM, (h + 1) * HEAD_DIM)
            probs = jnp.exp(dot(key[:keys], query_h, NT) - log_ref[h : h + 1, rows])
            d_probs = dot(value[:keys], grad_h, NT)
            d_scores = (probs * (d_probs - along_ref[h : h + 1, rows])).astype(bf16)
            dq_ref[band, rows] += dot(key_flat[band, :keys], d_scores)
            return dot(probs.astype(bf16), grad_h), dot(d_scores, query_h)

        def heads_of(rows):
            query = qkv_ref[rows, 0:span] * jnp.asarray(scale, bf16)
            grad = grad_ref[rows, :]
            return [(h, only(query, h), only(grad, h)) for h in range(heads)]

        for f in range(block // PATCHES):
            rows = pl.ds(pl.multiple_of(first + f * PATCHES, PATCHES), PATCHES)
            keys = (f + 1) * PATCHES
            for h, query_h, grad_h in heads_of(rows):
                dv, dk = tile(rows, keys, h, query_h, grad_h)
                dv_ref[:keys] += dv
                dk_ref[:keys] += dk

        def later(i, c):
            rows = pl.ds(pl.multiple_of(i * block, block), block)
            terms = [tile(rows, block, h, query_h, grad_h) for h, query_h, grad_h in heads_of(rows)]
            dv_ref[...] += sum(t[0] for t in terms)
            dk_ref[...] += sum(t[1] for t in terms)
            return c

        lax.fori_loop(j + 1, blocks, later, 0)
        dk = dk_ref[...]
        out_ref[columns, span : 2 * span] = (dk * cos_ref[columns, :] - partner(dk) * sin_ref[columns, :]).astype(bf16)
        out_ref[columns, 2 * span : 3 * span] = dv_ref[...].astype(bf16)
        return carry

    lax.fori_loop(0, blocks, key_block, 0)

    def last(i, carry):
        rows = pl.ds(pl.multiple_of(i * block, block), block)
        dq = jnp.transpose(dq_ref[:, rows]) * scale
        out_ref[rows, 0:span] = (dq * cos_ref[rows, :] - partner(dq) * sin_ref[rows, :]).astype(bf16)
        return carry

    lax.fori_loop(0, blocks, last, 0)


def attend_back(qkv, grad, full, logs, cosine, sine, span):
    total = qkv.shape[0]
    heads = span // HEAD_DIM
    block = min(1024, total)
    return pl.pallas_call(
        functools.partial(attend_back_kernel, total=total, span=span, block=block),
        out_shape=jax.ShapeDtypeStruct((total, 3 * span), bf16),
        scratch_shapes=[
            pltpu.VMEM((span, total), f32),
            pltpu.VMEM((block, span), f32),
            pltpu.VMEM((block, span), f32),
            pltpu.VMEM((heads, total), f32),
        ],
        compiler_params=pltpu.CompilerParams(vmem_limit_bytes=60 << 20),
        cost_estimate=pl.CostEstimate(
            flops=20 * total * total * span, bytes_accessed=26 * total * span, transcendentals=total * total * heads // 2
        ),
        name="attend_back",
    )(qkv, grad, full, logs, cosine, sine)


def gathered_forward(queries, keys, values, allowed):
    def one(pieces):
        q, k, v = pieces
        scores = jnp.where(allowed, dot(q, k, NT) * HEAD_DIM**-0.5, -1e30)
        peak = jnp.max(scores, axis=-1, keepdims=True)
        raised = jnp.exp(scores - peak)
        totals = jnp.sum(raised, axis=-1, keepdims=True)
        return dot((raised / totals).astype(bf16), v), peak + jnp.log(totals)

    return lax.map(one, (queries, keys, values))


def gathered_back(queries, keys, values, grads, logs, allowed):
    scale = HEAD_DIM**-0.5

    def one(pieces):
        q, k, v, grad, log = pieces
        scores = jnp.where(allowed, dot(q, k, NT) * scale, -1e30)
        probs = jnp.exp(scores - log)
        d_probs = dot(grad, v, NT)
        centre = jnp.sum(probs * d_probs, axis=-1, keepdims=True)
        d_scores = (probs * (d_probs - centre)).astype(bf16)
        dv = dot(probs.astype(bf16), grad, TN)
        return dot(d_scores, k) * scale, dot(d_scores, q, TN) * scale, dv

    return lax.map(one, (queries, keys, values, grads, logs))


def level_rows(ctx_count, noise_level, rows):
    clips = ctx_count.shape[0]
    seq_devices = lax.axis_size("seq")
    plan = jnp.concatenate([ctx_count[:, None], noise_level], axis=1)
    plan = double_rows(plan, axis_bits("clip"))
    levels = jnp.where(jnp.arange(FRAMES, dtype=jnp.int32) < plan[..., :1], 0, plan[..., 1:])
    if rows < PATCHES:
        levels = jnp.repeat(levels, PATCHES // rows, axis=-1)
    frames = max(1, rows // PATCHES)
    levels = levels.reshape(-1, clips, seq_devices, frames).transpose(0, 2, 1, 3)
    return levels.reshape(-1, seq_devices, clips * frames)


def condition(levels, here, depth, width):
    half_width = width // 2
    feature = here * depth + jnp.arange(depth, dtype=jnp.int32)
    low_half = feature < half_width
    freqs = jnp.exp(-math.log(10000.0) * jnp.where(low_half, feature, feature - half_width).astype(f32) / half_width)
    angles = levels.reshape(-1, 1).astype(f32) * freqs
    return jax.nn.silu(jnp.where(low_half, jnp.sin(angles), jnp.cos(angles))).astype(bf16)


def own_place(shard, here):
    count = lax.axis_size("clip") * lax.axis_size("seq")
    whole = jnp.zeros((count * shard.shape[0],), f32)
    return lax.dynamic_update_slice_in_dim(whole, shard.astype(f32), here * shard.shape[0], 0)


def body_by_heads(
    tokens,
    ctx_count,
    noise_level,
    mod_weight,
    mod_bias,
    qkv_weight,
    qkv_bias,
    out_weight,
    out_bias,
    up_weight,
    up_bias,
    down_weight,
    down_bias,
    cotangent,
):
    clips, rows, width = tokens.shape
    seq_devices = lax.axis_size("seq")
    devices = lax.axis_size("clip") * seq_devices
    order = near_order()
    here = lax.axis_index("clip") * seq_devices + lax.axis_index("seq")
    total = rows * seq_devices
    frames = max(1, rows // PATCHES)
    span = width // seq_devices
    lines = clips * frames
    piece = out_weight.shape[0]

    full_qkv = lax.all_gather(qkv_weight, BOTH, axis=0, tiled=True)
    unit = down_weight.shape[0]
    owners = (4, seq_devices // 2, 2, unit)
    near_owners = (4, 2, seq_devices // 2, unit)
    down_shard = down_weight.reshape(4, piece, width)
    up_shard = up_weight.reshape((piece,) + owners).transpose(1, 0, 3, 2, 4).reshape(4, piece, width)
    up_shard = jnp.concatenate([up_shard, out_weight[None]], axis=0)

    levels = level_rows(ctx_count, noise_level, rows)
    flat_bits = (2,) * len(order)
    bits_clip, bits_seq = len(axis_bits("clip")), len(axis_bits("seq"))
    turn = tuple(range(bits_clip))[::-1] + tuple(range(bits_clip, bits_clip + bits_seq))[::-1] + (len(order),)
    near_levels = levels.reshape(flat_bits + (lines,)).transpose(turn)
    cond_near = condition(near_levels, here, mod_weight.shape[0], width)
    cond = condition(levels, here, mod_weight.shape[0], width)
    mod_place = own_place(mod_bias, here)

    def modulate(columns, biases, gates=()):
        weight = mod_weight[:, columns]
        bias = jnp.concatenate([own_place(b, here) for b in biases]).reshape(lines, -1)
        rest = jnp.concatenate([jnp.broadcast_to(mod_place[columns], (lines, weight.shape[1])), bias], axis=1)
        part = jnp.pad(dot(cond_near, weight), ((0, 0), (0, bias.shape[1])))
        line_rows = halve_rows((part.reshape(devices, lines, -1) + rest).reshape(devices * lines, -1), order, gates)
        return line_rows[:, : weight.shape[1]], line_rows[:, weight.shape[1] :].reshape(1, -1)

    def blocks(line_rows):
        return line_rows.reshape(clips, frames, -1, width).transpose(0, 2, 1, 3)

    mod_first, bias_qkv = modulate(slice(0, 2 * width), (qkv_bias,))
    mods_one = blocks(mod_first)

    positions = lax.axis_index("seq") * rows + jnp.arange(rows, dtype=jnp.int32)
    cos_local, sin_local = rotary_lanes(positions, max(span, 256))
    cos_row, sin_row = rotary_lanes(jnp.arange(rows, dtype=jnp.int32), span)
    cos_far, sin_far = rotary_lanes(jnp.arange(seq_devices, dtype=jnp.int32) * rows, span)
    cos_all = (cos_far[:, None] * cos_row[None] - sin_far[:, None] * sin_row[None]).reshape(total, span)
    sin_all = (sin_far[:, None] * cos_row[None] + cos_far[:, None] * sin_row[None]).reshape(total, span)

    def exchange(value):
        return lax.all_to_all(value, "seq", 0, 0, tiled=True)

    def doubled(share, axis, bit):
        other = swap_bit(share, axis, bit)
        mine = own_bit(axis, bit) == 0
        pair = jnp.stack([jnp.where(mine, share, other), jnp.where(mine, other, share)], axis=1)
        return pair.reshape((-1,) + share.shape[1:])

    high_bits, low_bit = axis_bits("seq")[:-1], axis_bits("seq")[-1]
    down_share, up_share = down_shard[None], up_shard[None]
    for axis, bit in high_bits:
        down_share, up_share = doubled(down_share, axis, bit), doubled(up_share, axis, bit)
    full_qkv = after(full_qkv, down_share, up_share)
    up_pair = (up_share, swap_bit(up_share, "clip", 2))
    down_share = doubled(down_share, *low_bit)

    normed, qkv, mixes, fulls, logs, sents = [], [], [], [], [], []
    for c in range(clips):
        weight = full_qkv if c == 0 else after(full_qkv, down_share, up_pair[1])
        sent, normed_c = project(tokens, c, mods_one[c], weight, bias_qkv, cos_local, sin_local, seq_devices)
        normed.append(normed_c)
        if qkv:
            sent = after(sent, qkv[-1])
        qkv.append(exchange(sent))
    backs = []
    for c in range(clips):
        mix, full, log = attend(qkv[c].reshape(total, 3 * span), span)
        mixes.append(mix)
        fulls.append(full)
        logs.append(log)
        backs.append(exchange(after(mix.reshape(seq_devices, rows, span), qkv[-1] if c == 0 else backs[-1])))

    mod_rest, bias_rest = modulate(
        slice(2 * width, 6 * width), (out_bias, up_bias, down_bias), (None, None, normed[-1], mixes[0], mixes[-1])
    )
    mods_two = blocks(mod_rest)
    bias_out = bias_rest[:, :width]
    bias_up = bias_rest[:, width : 5 * width].reshape(owners).transpose(0, 2, 1, 3).reshape(1, -1)
    bias_down = bias_rest[:, 5 * width :]
    def from_clips(pair):
        near, across = [p.reshape((seq_devices // 2, 2) + p.shape[1:]) for p in pair]
        far = swap_bit(after(across, qkv[-1]), "clip", 1)
        return (near, across, swap_bit(near, "clip", 1), far)

    down_shares = from_clips((down_share, swap_bit(down_share, "clip", 2)))
    up_shares = from_clips([doubled(p, *low_bit) for p in up_pair])

    results = []
    d_mixed = []
    for c in range(clips):
        back = after(backs[c], mixes[-1])
        outputs = results[-1][0] if results else None
        results.append(middle(back, tokens, cotangent, c, mods_two[c], up_shares, down_shares, (bias_out, bias_up, bias_down), outputs))
        d_mixed.append(exchange(after(results[c][8], backs[-1] if c == 0 else d_mixed[-1])))

    d_qkv, exchanged = [], []
    for c in range(clips):
        grad = after(d_mixed[c], results[-1][8] if c == 0 else d_qkv[-1])
        grad = grad.reshape(total, span)
        d_qkv.append(attend_back(qkv[c].reshape(total, 3 * span), grad, fulls[c], logs[c], cos_all, sin_all, span))
        sent = d_qkv[c].reshape(seq_devices, rows, 3 * span)
        exchanged.append(exchange(after(sent, d_mixed[-1]) if c == 0 else sent))

    def late(place):
        return [r[place] for r in results]

    mixed_all, normed_two, active, d_hidden, d_mlp, d_attn = [late(place) for place in (2, 3, 4, 5, 6, 7)]
    active = gate(active, d_qkv[-1], exchanged[0])
    down_first = along_first(active, d_mlp)
    normed_two = gate(normed_two, down_first)
    up_first = across_first(normed_two, d_hidden)
    down_core, up_core = swap_bit(down_first, "clip", 1), swap_bit(up_first, "clip", 1)
    d_mlp = gate(d_mlp, up_first)
    down_second = along_second(active, d_mlp, down_core)
    d_hidden = gate(d_hidden, down_second)
    up_second = across_second(normed_two, d_hidden, up_core)
    mixed_all = gate(mixed_all, up_second)
    out_first = across_first(mixed_all, d_attn)
    out_core = swap_bit(out_first, "clip", 1)
    down_along, up_across = swap_bit(down_second, "seq", 1), swap_bit(up_second, "clip", 2)
    exchanged[0] = after(exchanged[0], out_first)
    exchanged[-1] = after(exchanged[-1], down_along, up_across)

    def line_sums(sums):
        return sums.transpose(1, 0, 2).reshape(frames, -1)

    def with_bias(lines_now, vectors):
        return jnp.concatenate([jnp.concatenate(lines_now, axis=0), jnp.concatenate(vectors).reshape(lines, -1)], axis=1)

    bias_up_sum = sum(r[10][0] for r in results).reshape(near_owners).transpose(0, 2, 1, 3).reshape(-1)
    bias_pair = sum(r[11] for r in results)
    early = with_bias([line_sums(r[9]) for r in results], [bias_pair[0], bias_up_sum, bias_pair[1]])
    early_rows = lax.all_gather(early, BOTH, axis=0, tiled=True)

    last = []
    for c in range(clips):
        grads = last[-1][0] if last else None
        last.append(project_back(exchanged[c], full_qkv, tokens, c, mods_one[c][1], results[c][1], grads))
    d_projected = [r[1] for r in last]
    mine = mine_on("clip")
    height, half = width // 4, 3 * width // 2
    qkv_first = across_first(normed, d_projected)
    qkv_core = swap_bit(qkv_first, "clip", 1)
    down_across = swap_bit(along_third(active, gate(d_mlp, qkv_first), down_core, down_along), "clip", 2)
    qkv_second = weight_part(normed, d_projected, (mine ^ 2)[None], ((qkv_core, 0),), bf16, height, 0, half)
    qkv_across = swap_bit(qkv_second, "clip", 2)
    far_part = weight_part(
        gate(normed, qkv_second), d_projected, (mine ^ 2)[None], ((qkv_core, 0),), f32, height, half, half
    )
    near_part = weight_part(
        gate(normed, qkv_second), d_projected, mine[None], ((qkv_core, 1),), f32, height, half, half
    )
    pair = jnp.stack([near_part[0], far_part[0]]).reshape(2, seq_devices // 2, 2, -1, half)
    low = own_bit("seq", 1)
    along = swap_bit(lax.dynamic_index_in_dim(pair, 1 - low, 2, keepdims=False).astype(bf16), "seq", 1)
    d_attn = gate(d_attn, qkv_second)
    out_across = swap_bit(across_second(mixed_all, d_attn, out_core), "clip", 2)
    pair = lax.dynamic_index_in_dim(pair, low, 2, keepdims=False) + along.astype(f32)
    grad_second = pair[0] + swap_bit(pair[1].astype(bf16), "clip", 2).astype(f32)
    grad_second = halve_sum(grad_second, axis_bits("seq")[:-1], bf16)
    total_first = weight_part(normed, d_projected, mine[None], ((qkv_core, 1), (qkv_across, 0)), f32, height, 0, half)
    grad_first = halve_sum(total_first.reshape(seq_devices, -1, half), axis_bits("seq"), bf16)
    grad_qkv = jnp.concatenate([grad_first, grad_second], axis=1)
    grad_up = across_total(normed_two, gate(d_hidden, qkv_second), up_core, up_across)
    grad_down = along_total(active, gate(d_mlp, qkv_second), down_core, down_along, down_across)
    grad_up = grad_up.reshape((-1,) + near_owners).transpose(0, 1, 3, 2, 4).reshape(-1, 4 * width)
    grad_out = across_total(mixed_all, d_attn, out_core, out_across)
    late_rows = with_bias([line_sums(r[2]) for r in last], [sum(r[3][0] for r in last)])
    late_rows = spread_rows(after(late_rows, qkv_second), order)

    def own_columns(sums, shard):
        return lax.dynamic_slice_in_dim(sums, here * shard.shape[0], shard.shape[0], 0)

    def spans(all_rows, columns):
        vectors = jnp.sum(all_rows[:, columns:].reshape(devices, -1), axis=0)
        return all_rows[:, :columns], vectors

    late_mod, late_vectors = spans(late_rows, 2 * width)
    early_mod, early_vectors = spans(early_rows, 4 * width)
    grad_mod = jnp.concatenate(
        [
            lax.dot_general(rows_cond.astype(f32), r, TN, precision=highest, preferred_element_type=f32)
            for rows_cond, r in ((cond_near, late_mod), (cond, early_mod))
        ],
        axis=1,
    )
    mod_sum = jnp.concatenate([jnp.sum(late_mod, axis=0), jnp.sum(early_mod, axis=0)])
    return (
        results[-1][0],
        last[-1][0],
        grad_mod,
        own_columns(mod_sum, mod_bias),
        grad_qkv,
        own_columns(late_vectors, qkv_bias),
        grad_out,
        own_columns(early_vectors[:width], out_bias),
        grad_up,
        own_columns(early_vectors[width : 5 * width], up_bias),
        grad_down,
        own_columns(early_vectors[5 * width :], down_bias),
    )


def body_gathered(
    tokens,
    ctx_count,
    noise_level,
    mod_weight,
    mod_bias,
    qkv_weight,
    qkv_bias,
    out_weight,
    out_bias,
    up_weight,
    up_bias,
    down_weight,
    down_bias,
    cotangent,
):
    clips, rows, width = tokens.shape
    seq_devices = lax.axis_size("seq")
    devices = lax.axis_size("clip") * seq_devices
    bits = mesh_bits()
    here = lax.axis_index("clip") * seq_devices + lax.axis_index("seq")
    total = rows * seq_devices
    frames = max(1, rows // PATCHES)
    patch_rows = rows // frames

    full_qkv = lax.all_gather(qkv_weight, BOTH, axis=0, tiled=True)
    full_out = lax.all_gather(out_weight, BOTH, axis=0, tiled=True)
    full_up = lax.all_gather(up_weight, BOTH, axis=0, tiled=True)
    full_down = lax.all_gather(down_weight, BOTH, axis=0, tiled=True)
    biases = (qkv_bias, out_bias, up_bias, down_bias)
    bias_rows = double_rows(jnp.concatenate(biases).astype(f32), bits)
    full_biases = []
    first = 0
    for piece in biases:
        full_biases.append(bias_rows[:, first : first + piece.shape[0]].reshape(1, -1))
        first += piece.shape[0]
    bias_qkv, bias_out, bias_up, bias_down = full_biases

    levels = level_rows(ctx_count, noise_level, rows)
    cond = condition(levels, here, mod_weight.shape[0], width)
    mod_width = mod_weight.shape[1]
    partial = dot(cond, mod_weight) + own_place(mod_bias, here)
    modulation = halve_sum(partial.reshape(devices, clips * frames, mod_width), bits)
    modulation = modulation.reshape(clips, frames, 1, mod_width)

    positions = lax.axis_index("seq") * rows + jnp.arange(rows, dtype=jnp.int32)
    cosine, sine = rotary_lanes(positions, HEAD_DIM)
    key_frame = jnp.arange(total, dtype=jnp.int32) // PATCHES
    allowed = key_frame[None, :] <= (positions // PATCHES)[:, None]

    def flat(value):
        return value.reshape(rows, value.shape[-1])

    def split(value):
        return value.reshape(frames, patch_rows, value.shape[-1])

    def to_heads(value):
        return value.reshape(rows, HEADS, HEAD_DIM).transpose(1, 0, 2)

    saved = []
    for c in range(clips):
        mods = jnp.split(modulation[c], 6, axis=-1)
        tokens_now = split(tokens[c].astype(f32))
        unit, inverse = norm_parts(tokens_now)
        normed = flat((unit * (1.0 + mods[1]) + mods[0]).astype(bf16))
        projected = dot(normed, full_qkv) + bias_qkv
        views = []
        for place in range(3):
            view = to_heads(projected[:, place * width : (place + 1) * width])
            if place < 2:
                    view = view * cosine + jnp.roll(view, HEAD_DIM // 2, -1) * sine
            views.append(view.astype(bf16))
        queries, keys, values = views
        keys = lax.all_gather(keys, "seq", axis=1, tiled=True)
        values = lax.all_gather(values, "seq", axis=1, tiled=True)
        mix, logs = gathered_forward(queries, keys, values, allowed)
        mixed = mix.transpose(1, 0, 2).reshape(rows, width).astype(bf16)
        kept = (queries, keys, values, logs)
        saved.append((mods, tokens_now, unit, inverse, normed, kept, mixed))

    outputs = []
    middle = []
    for c in range(clips):
        mods, tokens_now, unit, inverse, normed, kept, mixed = saved[c]
        _, _, gate_one, shift_two, scale_two, gate_two = mods
        attn_out = split(dot(mixed, full_out) + bias_out)
        resid = tokens_now + gate_one * attn_out
        unit_two, inverse_two = norm_parts(resid)
        normed_two = flat((unit_two * (1.0 + scale_two) + shift_two).astype(bf16))
        hidden = dot(normed_two, full_up) + bias_up
        active_full, gelu_back = jax.vjp(jax.nn.gelu, hidden)
        active = active_full.astype(bf16)
        mlp_out = split(dot(active, full_down) + bias_down)
        outputs.append(flat((resid + gate_two * mlp_out).astype(bf16)))
        grad_out = split(cotangent[c].astype(f32))
        d_mlp = flat((gate_two * grad_out).astype(bf16))
        d_hidden = gelu_back(dot(d_mlp, full_down, NT))[0].astype(bf16)
        d_normed_two = split(dot(d_hidden, full_up, NT))
        d_resid = grad_out + norm_back(unit_two, inverse_two, d_normed_two, scale_two)
        d_attn = flat((gate_one * d_resid).astype(bf16))
        d_mixed = dot(d_attn, full_out, NT).astype(bf16)
        d_early = jnp.concatenate(
            [
                jnp.sum(d_resid * attn_out, axis=1),
                jnp.sum(d_normed_two, axis=1),
                jnp.sum(d_normed_two * unit_two, axis=1),
                jnp.sum(grad_out * mlp_out, axis=1),
            ],
            axis=-1,
        )
        middle.append((mixed, d_attn, normed_two, d_hidden, active, d_mlp, d_resid, d_mixed, d_early))

    def both(place):
        return jnp.concatenate([m[place] for m in middle], axis=0)

    d_attn_all, d_hidden_all, d_mlp_all = both(1), both(3), both(5)
    grad_down = weight_grad(both(4), d_mlp_all)
    grad_up = weight_grad(both(2), d_hidden_all)
    grad_out_weight = weight_grad(both(0), d_attn_all)
    early_rows = lax.all_gather(both(8), BOTH, axis=0, tiled=True)

    inputs_grad = []
    late = []
    projected_grads = []
    for c in range(clips):
        mods, tokens_now, unit, inverse, normed, kept, mixed = saved[c]
        d_resid, d_mixed = middle[c][6], middle[c][7]
        queries, keys, values, logs = kept
        dq, dk, dv = gathered_back(queries, keys, values, to_heads(d_mixed), logs, allowed)
        dk = lax.psum_scatter(dk.astype(bf16), "seq", scatter_dimension=1, tiled=True).astype(f32)
        dv = lax.psum_scatter(dv.astype(bf16), "seq", scatter_dimension=1, tiled=True).astype(f32)
        views = [g * cosine - jnp.roll(g, HEAD_DIM // 2, -1) * sine for g in (dq, dk)] + [dv]
        d_projected = jnp.concatenate([g.transpose(1, 0, 2).reshape(rows, width) for g in views], axis=1).astype(bf16)
        projected_grads.append(d_projected)
        d_normed = split(dot(d_projected, full_qkv, NT))
        inputs_grad.append(flat(d_resid + norm_back(unit, inverse, d_normed, mods[1])))
        late.append(jnp.concatenate([jnp.sum(d_normed, axis=1), jnp.sum(d_normed * unit, axis=1)], axis=-1))

    d_projected_all = jnp.concatenate(projected_grads, axis=0)
    grad_qkv = weight_grad(jnp.concatenate([s[4] for s in saved], axis=0), d_projected_all)
    bias_grads = [
        jnp.sum(g.astype(f32), axis=0).reshape(devices, -1) for g in (d_projected_all, d_attn_all, d_hidden_all, d_mlp_all)
    ]
    bias_sum = halve_sum(jnp.concatenate(bias_grads, axis=1), bits)
    grad_biases = []
    first = 0
    for piece in bias_grads:
        grad_biases.append(bias_sum[first : first + piece.shape[1]])
        first += piece.shape[1]

    late_rows = double_rows(jnp.concatenate(late, axis=0), bits).reshape(-1, 2 * width)
    grad_mod = jnp.concatenate(
        [
            lax.dot_general(cond.astype(f32), r, TN, precision=highest, preferred_element_type=f32)
            for r in (late_rows, early_rows)
        ],
        axis=1,
    )
    mod_sum = jnp.concatenate([jnp.sum(late_rows, axis=0), jnp.sum(early_rows, axis=0)])
    grad_mod_bias = lax.dynamic_slice_in_dim(mod_sum, here * mod_bias.shape[0], mod_bias.shape[0], 0)
    return (
        jnp.stack(outputs),
        jnp.stack(inputs_grad),
        grad_mod,
        grad_mod_bias,
        grad_qkv,
        grad_biases[0],
        grad_out_weight,
        grad_biases[1],
        grad_up,
        grad_biases[2],
        grad_down,
        grad_biases[3],
    )


def solution(mesh):
    by_heads = HEADS % mesh.shape["seq"] == 0
    body = body_by_heads if by_heads else body_gathered
    token_place = P("clip", "seq", None)
    matrix, vector = P(BOTH, None), P(BOTH)
    weights = (matrix, vector) * 5
    return jax.shard_map(
        body,
        mesh=mesh,
        in_specs=(token_place, P("clip"), P("clip", None)) + weights + (token_place,),
        out_specs=(token_place, token_place) + weights,
        check_vma=False,
    )
```

```python
import functools
import math

import jax
import jax.numpy as jnp
from jax import lax
from jax.experimental import pallas as pl
from jax.experimental.pallas import tpu as pltpu
from jax.sharding import PartitionSpec as P

HEADS = 16
HEAD_DIM = 64
FRAMES = 16
PATCHES = 256
BOTH = ("clip", "seq")
NT = (((1,), (1,)), ((), ()))
NN = (((1,), (0,)), ((), ()))
TN = (((0,), (0,)), ((), ()))
bf16 = jnp.bfloat16
f32 = jnp.float32
highest = lax.Precision.HIGHEST


def dot(left, right, dims=NN):
    return lax.dot_general(left, right, dims, preferred_element_type=f32)


def swap_bit(value, axis, bit):
    count = lax.axis_size(axis)
    return lax.ppermute(value, axis, [(i, i ^ bit) for i in range(count)])


def own_bit(axis, bit):
    return lax.shift_right_logical(lax.axis_index(axis), bit.bit_length() - 1) & 1


def axis_bits(axis):
    bits = []
    bit = 1
    while bit < lax.axis_size(axis):
        bits.append((axis, bit))
        bit *= 2
    return bits[::-1]


def exchange_order(bits):
    return sorted(range(len(bits)), key=lambda place: bits[place])


def mesh_bits():
    return axis_bits("clip") + axis_bits("seq")


def halve_sum(parts, bits, wire=f32):
    addends = [parts.reshape((2,) * len(bits) + parts.shape[1:])]
    for place in exchange_order(bits):
        axis, bit = bits[place]
        mine = own_bit(axis, bit)
        send = sum(lax.dynamic_index_in_dim(a, 1 - mine, place).astype(f32) for a in addends)
        addends = [lax.dynamic_index_in_dim(a, mine, place) for a in addends]
        addends.append(swap_bit(send.astype(wire), axis, bit))
    total = sum(a.astype(f32) for a in addends)
    return total.reshape(total.shape[len(bits) :])


def near_order():
    return axis_bits("clip")[::-1] + axis_bits("seq")[::-1]


def halve_rows(parts, bits, gates=()):
    for place, (axis, bit) in enumerate(bits):
        half = parts.shape[0] // 2
        mine = own_bit(axis, bit)
        keep = lax.dynamic_slice_in_dim(parts, mine * half, half, 0)
        send = lax.dynamic_slice_in_dim(parts, (1 - mine) * half, half, 0)
        other = swap_bit(send, axis, bit)
        if place < len(gates) and gates[place] is not None:
            other = after(other, gates[place])
        parts = keep + other
    return parts


def collect_rows(rows, bits):
    for axis, bit in reversed(bits):
        rows = jnp.concatenate([rows, swap_bit(rows, axis, bit)], axis=0)
    return rows


def relative_rows(rows, bits):
    shape = rows.shape
    rows = rows.reshape((2,) * len(bits) + (-1,) + shape[1:])
    for place, (axis, bit) in enumerate(bits):
        rows = jnp.where(own_bit(axis, bit) == 0, rows, jnp.flip(rows, place))
    return rows.reshape(shape)


def after(value, *others):
    return lax.optimization_barrier((value,) + others)[0]


def double_rows(row, bits):
    rows = row[None]
    for axis, bit in reversed(bits):
        other = swap_bit(rows, axis, bit)
        low = own_bit(axis, bit) == 0
        rows = jnp.concatenate([jnp.where(low, rows, other), jnp.where(low, other, rows)], axis=0)
    return rows


def weight_grad(left, right):
    tokens, rows = left.shape
    quarter = rows // lax.axis_size("clip")
    mine = lax.axis_index("clip")

    def part(flip):
        piece = lax.dynamic_slice_in_dim(left, (mine ^ flip) * quarter, quarter, 1)
        return dot(piece, right, TN)

    far = swap_bit(part(3).astype(bf16), "clip", 1)
    near = swap_bit(part(1).astype(bf16), "clip", 1)
    across = swap_bit((part(2) + far.astype(f32)).astype(bf16), "clip", 2)
    total = part(0) + near.astype(f32) + across.astype(f32)
    return halve_sum(total.reshape((lax.axis_size("seq"), -1, right.shape[1])), axis_bits("seq"), bf16)


def norm_parts(values):
    centre = values - jnp.mean(values, axis=-1, keepdims=True)
    spread = jnp.mean(centre * centre, axis=-1, keepdims=True)
    inverse = lax.rsqrt(spread + 1e-06)
    return centre * inverse, inverse


def norm_back(unit, inverse, grad, scales):
    scaled = grad * (1.0 + scales)
    mean = jnp.mean(scaled, axis=-1, keepdims=True)
    along = jnp.mean(scaled * unit, axis=-1, keepdims=True)
    return inverse * (scaled - mean - unit * along)


def rotary_lanes(positions, width):
    half = HEAD_DIM // 2
    lane = jnp.arange(width, dtype=jnp.int32) % HEAD_DIM
    freqs = jnp.exp(-math.log(10000.0) * 2.0 * (lane % half).astype(f32) / HEAD_DIM)
    angles = positions.astype(f32)[:, None] * freqs[None, :]
    sign = jnp.where(lane < half, -1.0, 1.0).astype(f32)
    return jnp.cos(angles), jnp.sin(angles) * sign[None, :]


def partner(values):
    width = values.shape[1]
    half = HEAD_DIM // 2
    lane = lax.broadcasted_iota(jnp.int32, (1, width), 1) % HEAD_DIM
    return jnp.where(lane < half, pltpu.roll(values, width - half, 1), pltpu.roll(values, half, 1))


def project_kernel(
    token_ref, mod_ref, wq_ref, wk_ref, wv_ref, bq_ref, bk_ref, bv_ref, cos_ref, sin_ref, out_ref, normed_ref, *, span
):
    frames = mod_ref.shape[1]
    patch = token_ref.shape[0] // frames

    @pl.when(pl.program_id(0) == 0)
    def _():
        for f in range(frames):
            rows = slice(f * patch, (f + 1) * patch)
            unit, _ = norm_parts(token_ref[rows, :].astype(f32))
            normed_ref[rows, :] = (unit * (1.0 + mod_ref[1, f : f + 1, :]) + mod_ref[0, f : f + 1, :]).astype(bf16)

    x = normed_ref[...]
    cosine, sine = cos_ref[...], sin_ref[...]
    groups = wq_ref.shape[1] // span
    for place, (w_ref, b_ref) in enumerate(((wq_ref, bq_ref), (wk_ref, bk_ref), (wv_ref, bv_ref))):
        value = dot(x, w_ref[...]) + b_ref[...]
        if place < 2:
            value = value * cosine + partner(value) * sine
        value = value.astype(bf16)
        for g in range(groups):
            out_ref[g, :, place * span : (place + 1) * span] = value[:, g * span : (g + 1) * span]


def whole_block(shape):
    return pl.BlockSpec(shape, lambda j: (0,) * len(shape))


def column_specs(height, block, steps):
    return [pl.BlockSpec((height, block), functools.partial(lambda p, j: (0, p * steps + j), p)) for p in range(3)]


def clip_block(shape, c):
    return pl.BlockSpec((None,) + shape[1:], lambda j: (c,) + (0,) * (len(shape) - 1))


def project(tokens, c, mods, weight, bias, cosine, sine, groups):
    _, rows, width = tokens.shape
    span = width // groups
    block = max(span, 256)
    per_step = block // span
    steps = groups // per_step
    return pl.pallas_call(
        functools.partial(project_kernel, span=span),
        grid=(steps,),
        in_specs=[clip_block(tokens.shape, c), whole_block(mods.shape)]
        + column_specs(width, block, steps)
        + column_specs(1, block, steps)
        + [whole_block((rows, block))] * 2,
        out_specs=(pl.BlockSpec((per_step, rows, 3 * span), lambda j: (j, 0, 0)), whole_block((rows, width))),
        out_shape=(
            jax.ShapeDtypeStruct((groups, rows, 3 * span), bf16),
            jax.ShapeDtypeStruct((rows, width), bf16),
        ),
        compiler_params=pltpu.CompilerParams(vmem_limit_bytes=32 << 20),
        cost_estimate=pl.CostEstimate(
            flops=6 * rows * width * width, bytes_accessed=6 * width * width + 10 * rows * width, transcendentals=0
        ),
        name="project",
    )(tokens, mods, weight, weight, weight, bias, bias, bias, cosine, sine)


def project_back_kernel(
    back_ref, wq_ref, wk_ref, wv_ref, token_ref, scale_ref, resid_ref, *rest, span
):
    grad_ref, proj_ref, sums_ref, bias_ref, acc_ref = rest[-5:]
    frames = scale_ref.shape[0]
    rows_all, width = token_ref.shape
    patch = rows_all // frames
    step = pl.program_id(0)
    block = wq_ref.shape[1]

    @pl.when(step == 0)
    def _():
        acc_ref[...] = jnp.zeros_like(acc_ref)

    for place, w_ref in enumerate((wq_ref, wk_ref, wv_ref)):
        band = slice(place * span, (place + 1) * span)
        piece = jnp.concatenate([back_ref[g, :, band] for g in range(block // span)], axis=1)
        columns = pl.ds(pl.multiple_of(place * width + step * block, block), block)
        proj_ref[:, columns] = piece
        bias_ref[:, columns] = jnp.sum(piece.astype(f32), axis=0, keepdims=True)
        acc_ref[...] += dot(piece, w_ref[...], NT)

    @pl.when(step == pl.num_programs(0) - 1)
    def _():
        for f in range(frames):
            rows = slice(f * patch, (f + 1) * patch)
            unit, inverse = norm_parts(token_ref[rows, :].astype(f32))
            grad = acc_ref[rows, :]
            grad_ref[rows, :] = resid_ref[rows, :] + norm_back(unit, inverse, grad, scale_ref[f : f + 1, :])
            sums_ref[0, f : f + 1, :] = jnp.sum(grad, axis=0, keepdims=True)
            sums_ref[1, f : f + 1, :] = jnp.sum(grad * unit, axis=0, keepdims=True)


def project_back(back, weight, tokens, c, scales, d_resid, grads):
    groups, rows, _ = back.shape
    width = tokens.shape[2]
    span = width // groups
    block = max(span, 256)
    per_step = block // span
    steps = groups // per_step
    earlier = [] if grads is None else [grads]
    return pl.pallas_call(
        functools.partial(project_back_kernel, span=span),
        grid=(steps,),
        in_specs=[pl.BlockSpec((per_step, rows, 3 * span), lambda j: (j, 0, 0))]
        + column_specs(width, block, steps)
        + [clip_block(tokens.shape, c), whole_block(scales.shape), whole_block((rows, width))]
        + [pl.BlockSpec(memory_space=pl.ANY)] * len(earlier),
        out_specs=(
            clip_block(tokens.shape, c),
            whole_block((rows, 3 * width)),
            whole_block((2,) + scales.shape),
            whole_block((1, 3 * width)),
        ),
        out_shape=(
            jax.ShapeDtypeStruct(tokens.shape, f32),
            jax.ShapeDtypeStruct((rows, 3 * width), bf16),
            jax.ShapeDtypeStruct((2,) + scales.shape, f32),
            jax.ShapeDtypeStruct((1, 3 * width), f32),
        ),
        input_output_aliases={7: 0} if earlier else {},
        scratch_shapes=[pltpu.VMEM((rows, width), f32)],
        compiler_params=pltpu.CompilerParams(vmem_limit_bytes=40 << 20),
        cost_estimate=pl.CostEstimate(
            flops=6 * rows * width * width, bytes_accessed=6 * width * width + 22 * rows * width, transcendentals=0
        ),
        name="project_back",
    )(back, weight, weight, weight, tokens, scales, d_resid, *earlier)


GELU_RATE = math.sqrt(2.0 / math.pi)
GELU_CUBE = 0.044715


def middle_kernel(clip_ref, back_ref, token_ref, cot_ref, mod_ref, bo_ref, bup_ref, bdown_ref, *refs):
    wo_refs, up_refs, down_refs = refs[0:4], refs[4:8], refs[8:12]
    (
        out_ref,
        dres_ref,
        mixed_ref,
        normed_ref,
        act_ref,
        dhid_ref,
        dmlp_ref,
        dattn_ref,
        dmix_ref,
        sums_ref,
        bup_sum_ref,
        bsum_ref,
        attn_ref,
        res_ref,
        mlp_ref,
        dn_ref,
        wo_ref,
        up_ref,
        down_ref,
    ) = refs[-19:]
    groups, rows_all, span = back_ref.shape
    width = token_ref.shape[1]
    quarter = width // 4
    frames = mod_ref.shape[1]
    patch = rows_all // frames
    step = pl.program_id(0)
    mine = clip_ref[0]

    def owner_rows(place):
        return pl.ds(pl.multiple_of((mine ^ FLIPS[place]) * quarter, quarter), quarter)

    @pl.when(step == 0)
    def _():
        for place in range(4):
            wo_ref[owner_rows(place), :] = wo_refs[place][...].reshape(quarter, width)
        for g in range(groups):
            mixed_ref[:, g * span : (g + 1) * span] = back_ref[g]
        attn_ref[...] = dot(mixed_ref[...], wo_ref[...]) + bo_ref[...]
        for f in range(frames):
            rows = slice(f * patch, (f + 1) * patch)
            resid = token_ref[rows, :].astype(f32) + mod_ref[0, f : f + 1, :] * attn_ref[rows, :]
            res_ref[rows, :] = resid
            unit, _ = norm_parts(resid)
            normed_ref[rows, :] = (unit * (1.0 + mod_ref[2, f : f + 1, :]) + mod_ref[1, f : f + 1, :]).astype(bf16)
            dmlp_ref[rows, :] = (mod_ref[3, f : f + 1, :] * cot_ref[rows, :].astype(f32)).astype(bf16)
        mlp_ref[...] = jnp.zeros_like(mlp_ref)
        dn_ref[...] = jnp.zeros_like(dn_ref)

    for place in range(4):
        up_ref[owner_rows(place), :] = up_refs[place][...].reshape(quarter, -1)

        @pl.when(step // 2 == place)
        def _(place=place):
            down_ref[...] = down_refs[place][...].reshape(-1, width)

    up = up_ref[...]
    down = down_ref[...]
    hidden = dot(normed_ref[...], up) + bup_ref[...]
    square = hidden * hidden
    bend = jnp.tanh(GELU_RATE * (hidden + GELU_CUBE * (square * hidden)))
    share = 0.5 * (1.0 + bend)
    active = (hidden * share).astype(bf16)
    act_ref[...] = active
    mlp_ref[...] += dot(active, down)
    slope = share + 0.5 * hidden * (1.0 - bend * bend) * (GELU_RATE + (3.0 * GELU_RATE * GELU_CUBE) * square)
    d_hidden = (dot(dmlp_ref[...], down, NT) * slope).astype(bf16)
    dhid_ref[...] = d_hidden
    bup_sum_ref[...] = jnp.sum(d_hidden.astype(f32), axis=0, keepdims=True)
    dn_ref[...] += dot(d_hidden, up, NT)

    @pl.when(step == pl.num_programs(0) - 1)
    def _():
        bsum = None
        for f in range(frames):
            rows = slice(f * patch, (f + 1) * patch)
            resid = res_ref[rows, :]
            mlp = mlp_ref[rows, :] + bdown_ref[...]
            out_ref[rows, :] = (resid + mod_ref[3, f : f + 1, :] * mlp).astype(bf16)
            cot = cot_ref[rows, :].astype(f32)
            sums_ref[3, f : f + 1, :] = jnp.sum(cot * mlp, axis=0, keepdims=True)
            unit, inverse = norm_parts(resid)
            grad = dn_ref[rows, :]
            sums_ref[1, f : f + 1, :] = jnp.sum(grad, axis=0, keepdims=True)
            sums_ref[2, f : f + 1, :] = jnp.sum(grad * unit, axis=0, keepdims=True)
            d_resid = cot + norm_back(unit, inverse, grad, mod_ref[2, f : f + 1, :])
            dres_ref[rows, :] = d_resid
            sums_ref[0, f : f + 1, :] = jnp.sum(d_resid * attn_ref[rows, :], axis=0, keepdims=True)
            d_attn = (mod_ref[0, f : f + 1, :] * d_resid).astype(bf16)
            dattn_ref[rows, :] = d_attn
            term = jnp.concatenate(
                [
                    jnp.sum(d_attn.astype(f32), axis=0, keepdims=True),
                    jnp.sum(dmlp_ref[rows, :].astype(f32), axis=0, keepdims=True),
                ],
                axis=0,
            )
            bsum = term if bsum is None else bsum + term
        bsum_ref[...] = bsum
        d_mixed = dot(dattn_ref[...], wo_ref[...], NT).astype(bf16)
        for g in range(groups):
            dmix_ref[g] = d_mixed[:, g * span : (g + 1) * span]


FLIPS = (0, 2, 1, 3)


def middle(back, tokens, cot, c, mods, up_shares, down_shares, biases, outputs):
    groups, rows, span = back.shape
    _, _, width = tokens.shape
    high, low, _, piece, _ = up_shares[0].shape
    hidden = 4 * width
    steps = 8
    block = hidden // steps
    bias_out, bias_up, bias_down = biases
    mine = lax.axis_index("clip").astype(jnp.int32)[None]
    earlier = [] if outputs is None else [outputs]

    def fixed(shape, **options):
        return pl.BlockSpec(shape, lambda j, q: (0,) * len(shape), **options)

    def clip_part(shape):
        return pl.BlockSpec((None,) + shape[1:], lambda j, q: (c,) + (0,) * (len(shape) - 1))

    def unit_block(j, q):
        owner = q[0] ^ jnp.where(j // 2 == 1, 2, jnp.where(j // 2 == 2, 1, j // 2))
        return owner, j % 2

    def up_index(j, q):
        owner, half = unit_block(j, q)
        return (0, 0, owner, 0, half)

    def hidden_index(j, q):
        owner, half = unit_block(j, q)
        return (0, owner * 2 + half)

    def down_index(place, j, q):
        return (0, jnp.clip(j - 2 * place, 0, 1), 0, 0, 0)

    token_block = fixed((rows, width))
    hidden_block = pl.BlockSpec((rows, block), hidden_index)
    out_spec = [
        pl.BlockSpec((high, low, 1, piece, width), lambda j, q: (0, 0, 4, 0, 0), pipeline_mode=pl.Buffered(1)) for _ in range(4)
    ]
    up_spec = [pl.BlockSpec((high, low, 1, piece, block), up_index) for _ in range(4)]
    down_spec = [
        pl.BlockSpec((high, 1, 4, piece, width), functools.partial(down_index, place)) for place in range(4)
    ]
    return pl.pallas_call(
        middle_kernel,
        grid_spec=pltpu.PrefetchScalarGridSpec(
            num_scalar_prefetch=1,
            grid=(steps,),
            in_specs=[
                fixed(back.shape),
                clip_part(tokens.shape),
                clip_part(tokens.shape),
                fixed(mods.shape),
                fixed((1, width)),
                pl.BlockSpec((1, block), hidden_index),
                fixed((1, width)),
            ]
            + out_spec
            + up_spec
            + down_spec
            + [pl.BlockSpec(memory_space=pl.ANY)] * len(earlier),
            out_specs=(
                clip_part(tokens.shape),
                token_block,
                token_block,
                token_block,
                hidden_block,
                hidden_block,
                token_block,
                token_block,
                fixed(back.shape),
                fixed(mods.shape),
                pl.BlockSpec((1, block), hidden_index),
                fixed((2, width)),
            ),
            scratch_shapes=[pltpu.VMEM((rows, width), f32)] * 4
            + [pltpu.VMEM((width, width), bf16), pltpu.VMEM((width, block), bf16), pltpu.VMEM((block, width), bf16)],
        ),
        out_shape=(
            jax.ShapeDtypeStruct(tokens.shape, bf16),
            jax.ShapeDtypeStruct((rows, width), f32),
            jax.ShapeDtypeStruct((rows, width), bf16),
            jax.ShapeDtypeStruct((rows, width), bf16),
            jax.ShapeDtypeStruct((rows, hidden), bf16),
            jax.ShapeDtypeStruct((rows, hidden), bf16),
            jax.ShapeDtypeStruct((rows, width), bf16),
            jax.ShapeDtypeStruct((rows, width), bf16),
            jax.ShapeDtypeStruct(back.shape, bf16),
            jax.ShapeDtypeStruct(mods.shape, f32),
            jax.ShapeDtypeStruct((1, hidden), f32),
            jax.ShapeDtypeStruct((2, width), f32),
        ),
        input_output_aliases={20: 0} if earlier else {},
        compiler_params=pltpu.CompilerParams(vmem_limit_bytes=60 << 20),
        cost_estimate=pl.CostEstimate(
            flops=4 * rows * width * width, bytes_accessed=2 * width * width + 5 * rows * width, transcendentals=rows * width
        ),
        name="middle",
    )(mine, back, tokens, cot, mods, bias_out, bias_up, bias_down, *up_shares, *up_shares, *down_shares, *earlier)


def weight_part_kernel(index_ref, *refs, clips, count, widths, addends):
    sets = len(widths)
    per_set = clips * (count + 1)
    extra = refs[sets * per_set : sets * per_set + addends]
    out_ref, flat_ref = refs[sets * per_set + addends :]
    step = pl.program_id(0)
    first = 0
    for place, steps in enumerate(widths):
        given = refs[place * per_set : (place + 1) * per_set]
        left, right = given[: clips * count], given[clips * count :]
        rows = right[0].shape[0]

        @pl.when(step == first)
        def _(left=left, rows=rows):
            for c in range(clips):
                for i in range(count):
                    flat_ref[i, :, c * rows : (c + 1) * rows] = jnp.transpose(left[c * count + i][...])

        @pl.when((step >= first) & (step < first + steps))
        def _(right=right, rows=rows):
            for i in range(count):
                total = dot(flat_ref[i, :, 0:rows], right[0][...])
                for c in range(1, clips):
                    total += dot(flat_ref[i, :, c * rows : (c + 1) * rows], right[c][...])
                for ref in extra:
                    total += ref[i].astype(f32)
                out_ref[i] = total.astype(out_ref.dtype)

        first += steps


def weight_part(pairs, indices, addends, kind, height):
    block = 512
    count = indices.shape[0]
    clips = len(pairs[0][0])
    rows = pairs[0][0][0].shape[0]
    widths = [right[0].shape[1] // block for _, right in pairs]
    columns = sum(widths) * block
    in_specs, operands = [], []
    first = 0
    for (left, right), steps in zip(pairs, widths):
        for array in left:
            for i in range(count):
                in_specs.append(pl.BlockSpec((rows, height), functools.partial(lambda i, j, q: (0, q[i]), i)))
                operands.append(array)
        where = functools.partial(lambda first, steps, j, q: (0, jnp.clip(j - first, 0, steps - 1)), first, steps)
        in_specs += [pl.BlockSpec((rows, block), where)] * clips
        operands += right
        first += steps
    for array, start in addends:
        where = functools.partial(lambda start, j, q: (start, 0, j), start // count)
        in_specs.append(pl.BlockSpec((count, height, block), where))
        operands.append(array)
    return pl.pallas_call(
        functools.partial(weight_part_kernel, clips=clips, count=count, widths=widths, addends=len(addends)),
        grid_spec=pltpu.PrefetchScalarGridSpec(
            num_scalar_prefetch=1,
            grid=(columns // block,),
            in_specs=in_specs,
            out_specs=pl.BlockSpec((count, height, block), lambda j, q: (0, 0, j)),
            scratch_shapes=[pltpu.VMEM((count, height, clips * rows), bf16)],
        ),
        out_shape=jax.ShapeDtypeStruct((count, height, columns), kind),
        compiler_params=pltpu.CompilerParams(vmem_limit_bytes=32 << 20),
        cost_estimate=pl.CostEstimate(
            flops=2 * count * clips * rows * height * columns,
            bytes_accessed=clips * rows * (count * height + columns) * 2 + 4 * count * height * columns,
            transcendentals=0,
        ),
        name="weight_part",
    )(indices, *operands)


def mine_on(axis):
    return lax.axis_index(axis).astype(jnp.int32)


def gate(arrays, *others):
    return list(lax.optimization_barrier((tuple(arrays), others))[0])


def height_of(pairs, parts):
    return pairs[0][0][0].shape[1] // parts


def across_first(pairs):
    mine = mine_on("clip")
    return weight_part(pairs, jnp.stack([mine ^ 3, mine ^ 1]), (), bf16, height_of(pairs, 4))


def across_second(pairs, core):
    return weight_part(pairs, (mine_on("clip") ^ 2)[None], ((core, 0),), bf16, height_of(pairs, 4))


def across_own(pairs, core, across):
    addends = ((core, 1), (across, 0))
    return weight_part(pairs, mine_on("clip")[None], addends, f32, height_of(pairs, 4))


def along_seq(total):
    return halve_sum(total.reshape((lax.axis_size("seq"), -1, total.shape[2])), axis_bits("seq"), bf16)


def along_block(clip_flip, low_flip):
    return (mine_on("clip") ^ clip_flip) * 2 + ((mine_on("seq") & 1) ^ low_flip)


def along_first(pairs):
    blocks = jnp.stack([along_block(1, 1), along_block(3, 1), along_block(1, 0), along_block(3, 0)])
    return weight_part(pairs, blocks, (), bf16, height_of(pairs, 8))


def along_second(pairs, core):
    blocks = jnp.stack([along_block(0, 1), along_block(2, 1)])
    return weight_part(pairs, blocks, ((core, 0),), bf16, height_of(pairs, 8))


def along_third(pairs, core, along):
    return weight_part(pairs, along_block(2, 0)[None], ((core, 3), (along, 1)), bf16, height_of(pairs, 8))


def along_total(pairs, core, along, across):
    addends = ((core, 2), (along, 0), (across, 0))
    total = weight_part(pairs, along_block(0, 0)[None], addends, f32, height_of(pairs, 8))
    bits = axis_bits("seq")[:-1]
    return halve_sum(total.reshape((2 ** len(bits), -1, total.shape[2])), bits, bf16)


def attend_kernel(qkv_ref, mix_ref, full_ref, log_ref, vt_ref, *, total, span, block):
    heads = span // HEAD_DIM
    head = lax.broadcasted_iota(jnp.int32, (1, span), 1) // HEAD_DIM
    key_frame = lax.broadcasted_iota(jnp.int32, (block, block), 0) // PATCHES
    query_frame = lax.broadcasted_iota(jnp.int32, (block, block), 1) // PATCHES
    kept = key_frame <= query_frame

    def flip(j, carry):
        rows = pl.ds(pl.multiple_of(j * block, block), block)
        vt_ref[:, rows] = jnp.transpose(qkv_ref[rows, 2 * span : 3 * span])
        return carry

    lax.fori_loop(0, total // block, flip, 0)

    def query_block(i, carry):
        rows = pl.ds(pl.multiple_of(i * block, block), block)
        query = qkv_ref[rows, 0:span] * jnp.asarray(HEAD_DIM**-0.5, bf16)
        queries = [jnp.where(head == h, query, jnp.zeros_like(query)) for h in range(heads)]

        def step(j, state, masked):
            peaks, sums, mixes = state
            columns = pl.ds(pl.multiple_of(j * block, block), block)
            key = qkv_ref[columns, span : 2 * span]
            new = ([], [], [])
            for h in range(heads):
                scores = dot(key, queries[h], NT)
                if masked:
                    scores = jnp.where(kept, scores, -1e30)
                peak = jnp.maximum(peaks[h], jnp.max(scores, axis=0, keepdims=True))
                raised = jnp.exp(scores - peak)
                fade = jnp.exp(peaks[h] - peak)
                new[0].append(peak)
                new[1].append(fade * sums[h] + jnp.sum(raised, axis=0, keepdims=True))
                term = dot(vt_ref[h * HEAD_DIM : (h + 1) * HEAD_DIM, columns], raised.astype(bf16))
                new[2].append(mixes[h] * fade + term)
            return tuple(map(tuple, new))

        state = (
            tuple(jnp.full((1, block), -1e30, f32) for _ in range(heads)),
            tuple(jnp.zeros((1, block), f32) for _ in range(heads)),
            tuple(jnp.zeros((HEAD_DIM, block), f32) for _ in range(heads)),
        )
        state = lax.fori_loop(0, i, lambda j, s: step(j, s, False), state)
        peaks, sums, mixes = step(i, state, True)
        mixed = jnp.transpose(jnp.concatenate([mixes[h] / sums[h] for h in range(heads)], axis=0))
        full_ref[rows, :] = mixed
        mix_ref[rows, :] = mixed.astype(bf16)
        for h in range(heads):
            log_ref[h : h + 1, rows] = peaks[h] + jnp.log(sums[h])
        return carry

    lax.fori_loop(0, total // block, query_block, 0)


def attend(qkv, span):
    total = qkv.shape[0]
    heads = span // HEAD_DIM
    block = min(1024, total)
    return pl.pallas_call(
        functools.partial(attend_kernel, total=total, span=span, block=block),
        out_shape=(
            jax.ShapeDtypeStruct((total, span), bf16),
            jax.ShapeDtypeStruct((total, span), f32),
            jax.ShapeDtypeStruct((heads, total), f32),
        ),
        scratch_shapes=[pltpu.VMEM((span, total), bf16)],
        compiler_params=pltpu.CompilerParams(vmem_limit_bytes=60 << 20),
        cost_estimate=pl.CostEstimate(
            flops=8 * total * total * span, bytes_accessed=12 * total * span, transcendentals=total * total * heads // 2
        ),
        name="attend",
    )(qkv)


def attend_back_kernel(
    qkv_ref, grad_ref, full_ref, log_ref, cos_ref, sin_ref, out_ref, dq_ref, dk_ref, dv_ref, along_ref, *, total, span, block
):
    heads = span // HEAD_DIM
    scale = HEAD_DIM**-0.5
    head = lax.broadcasted_iota(jnp.int32, (1, span), 1) // HEAD_DIM
    blocks = total // block
    dq_ref[...] = jnp.zeros_like(dq_ref)

    def only(value, h):
        return jnp.where(head == h, value, jnp.zeros_like(value))

    def lead(i, carry):
        rows = pl.ds(pl.multiple_of(i * block, block), block)
        product = jnp.transpose(grad_ref[rows, :].astype(f32) * full_ref[rows, :])
        for h in range(heads):
            along_ref[h : h + 1, rows] = jnp.sum(product[h * HEAD_DIM : (h + 1) * HEAD_DIM], axis=0, keepdims=True)
        return carry

    lax.fori_loop(0, blocks, lead, 0)

    def key_block(j, carry):
        first = pl.multiple_of(j * block, block)
        columns = pl.ds(first, block)
        key = qkv_ref[columns, span : 2 * span]
        value = qkv_ref[columns, 2 * span : 3 * span]
        key_flat = jnp.transpose(key)
        dk_ref[...] = jnp.zeros_like(dk_ref)
        dv_ref[...] = jnp.zeros_like(dv_ref)

        def tile(rows, keys, h, query_h, grad_h):
            band = slice(h * HEAD_DIM, (h + 1) * HEAD_DIM)
            probs = jnp.exp(dot(key[:keys], query_h, NT) - log_ref[h : h + 1, rows])
            d_probs = dot(value[:keys], grad_h, NT)
            d_scores = (probs * (d_probs - along_ref[h : h + 1, rows])).astype(bf16)
            dq_ref[band, rows] += dot(key_flat[band, :keys], d_scores)
            return dot(probs.astype(bf16), grad_h), dot(d_scores, query_h)

        def heads_of(rows):
            query = qkv_ref[rows, 0:span] * jnp.asarray(scale, bf16)
            grad = grad_ref[rows, :]
            return [(h, only(query, h), only(grad, h)) for h in range(heads)]

        for f in range(block // PATCHES):
            rows = pl.ds(pl.multiple_of(first + f * PATCHES, PATCHES), PATCHES)
            keys = (f + 1) * PATCHES
            for h, query_h, grad_h in heads_of(rows):
                dv, dk = tile(rows, keys, h, query_h, grad_h)
                dv_ref[:keys] += dv
                dk_ref[:keys] += dk

        def later(i, c):
            rows = pl.ds(pl.multiple_of(i * block, block), block)
            terms = [tile(rows, block, h, query_h, grad_h) for h, query_h, grad_h in heads_of(rows)]
            dv_ref[...] += sum(t[0] for t in terms)
            dk_ref[...] += sum(t[1] for t in terms)
            return c

        lax.fori_loop(j + 1, blocks, later, 0)
        dk = dk_ref[...]
        out_ref[columns, span : 2 * span] = (dk * cos_ref[columns, :] - partner(dk) * sin_ref[columns, :]).astype(bf16)
        out_ref[columns, 2 * span : 3 * span] = dv_ref[...].astype(bf16)
        return carry

    lax.fori_loop(0, blocks, key_block, 0)

    def last(i, carry):
        rows = pl.ds(pl.multiple_of(i * block, block), block)
        dq = jnp.transpose(dq_ref[:, rows]) * scale
        out_ref[rows, 0:span] = (dq * cos_ref[rows, :] - partner(dq) * sin_ref[rows, :]).astype(bf16)
        return carry

    lax.fori_loop(0, blocks, last, 0)


def attend_back(qkv, grad, full, logs, cosine, sine, span):
    total = qkv.shape[0]
    heads = span // HEAD_DIM
    block = min(1024, total)
    return pl.pallas_call(
        functools.partial(attend_back_kernel, total=total, span=span, block=block),
        out_shape=jax.ShapeDtypeStruct((total, 3 * span), bf16),
        scratch_shapes=[
            pltpu.VMEM((span, total), f32),
            pltpu.VMEM((block, span), f32),
            pltpu.VMEM((block, span), f32),
            pltpu.VMEM((heads, total), f32),
        ],
        compiler_params=pltpu.CompilerParams(vmem_limit_bytes=60 << 20),
        cost_estimate=pl.CostEstimate(
            flops=20 * total * total * span, bytes_accessed=26 * total * span, transcendentals=total * total * heads // 2
        ),
        name="attend_back",
    )(qkv, grad, full, logs, cosine, sine)


def gathered_forward(queries, keys, values, allowed):
    def one(pieces):
        q, k, v = pieces
        scores = jnp.where(allowed, dot(q, k, NT) * HEAD_DIM**-0.5, -1e30)
        peak = jnp.max(scores, axis=-1, keepdims=True)
        raised = jnp.exp(scores - peak)
        totals = jnp.sum(raised, axis=-1, keepdims=True)
        return dot((raised / totals).astype(bf16), v), peak + jnp.log(totals)

    return lax.map(one, (queries, keys, values))


def gathered_back(queries, keys, values, grads, logs, allowed):
    scale = HEAD_DIM**-0.5

    def one(pieces):
        q, k, v, grad, log = pieces
        scores = jnp.where(allowed, dot(q, k, NT) * scale, -1e30)
        probs = jnp.exp(scores - log)
        d_probs = dot(grad, v, NT)
        centre = jnp.sum(probs * d_probs, axis=-1, keepdims=True)
        d_scores = (probs * (d_probs - centre)).astype(bf16)
        dv = dot(probs.astype(bf16), grad, TN)
        return dot(d_scores, k) * scale, dot(d_scores, q, TN) * scale, dv

    return lax.map(one, (queries, keys, values, grads, logs))


def level_rows(ctx_count, noise_level, rows):
    clips = ctx_count.shape[0]
    seq_devices = lax.axis_size("seq")
    plan = jnp.concatenate([ctx_count[:, None], noise_level], axis=1)
    plan = double_rows(plan, axis_bits("clip"))
    levels = jnp.where(jnp.arange(FRAMES, dtype=jnp.int32) < plan[..., :1], 0, plan[..., 1:])
    if rows < PATCHES:
        levels = jnp.repeat(levels, PATCHES // rows, axis=-1)
    frames = max(1, rows // PATCHES)
    levels = levels.reshape(-1, clips, seq_devices, frames).transpose(0, 2, 1, 3)
    return levels.reshape(-1, seq_devices, clips * frames)


def condition(levels, here, depth, width):
    half_width = width // 2
    feature = here * depth + jnp.arange(depth, dtype=jnp.int32)
    low_half = feature < half_width
    freqs = jnp.exp(-math.log(10000.0) * jnp.where(low_half, feature, feature - half_width).astype(f32) / half_width)
    angles = levels.reshape(-1, 1).astype(f32) * freqs
    return jax.nn.silu(jnp.where(low_half, jnp.sin(angles), jnp.cos(angles))).astype(bf16)


def own_place(shard, here):
    count = lax.axis_size("clip") * lax.axis_size("seq")
    whole = jnp.zeros((count * shard.shape[0],), f32)
    return lax.dynamic_update_slice_in_dim(whole, shard.astype(f32), here * shard.shape[0], 0)


def body_by_heads(
    tokens,
    ctx_count,
    noise_level,
    mod_weight,
    mod_bias,
    qkv_weight,
    qkv_bias,
    out_weight,
    out_bias,
    up_weight,
    up_bias,
    down_weight,
    down_bias,
    cotangent,
):
    clips, rows, width = tokens.shape
    seq_devices = lax.axis_size("seq")
    devices = lax.axis_size("clip") * seq_devices
    order = near_order()
    here = lax.axis_index("clip") * seq_devices + lax.axis_index("seq")
    total = rows * seq_devices
    frames = max(1, rows // PATCHES)
    span = width // seq_devices
    lines = clips * frames
    piece = out_weight.shape[0]

    full_qkv = lax.all_gather(qkv_weight, BOTH, axis=0, tiled=True)
    unit = down_weight.shape[0]
    owners = (4, seq_devices // 2, 2, unit)
    near_owners = (4, 2, seq_devices // 2, unit)
    down_shard = down_weight.reshape(4, piece, width)
    up_shard = up_weight.reshape((piece,) + owners).transpose(1, 0, 3, 2, 4).reshape(4, piece, width)
    up_shard = jnp.concatenate([up_shard, out_weight[None]], axis=0)

    levels = level_rows(ctx_count, noise_level, rows)
    flat_bits = (2,) * len(order)
    bits_clip, bits_seq = len(axis_bits("clip")), len(axis_bits("seq"))
    turn = tuple(range(bits_clip))[::-1] + tuple(range(bits_clip, bits_clip + bits_seq))[::-1] + (len(order),)
    near_levels = levels.reshape(flat_bits + (lines,)).transpose(turn)
    cond_near = condition(near_levels, here, mod_weight.shape[0], width)
    cond = condition(levels, here, mod_weight.shape[0], width)
    cond_late = relative_rows(cond_near, order)
    mod_place = own_place(mod_bias, here)

    def modulate(columns, biases, gates=()):
        weight = mod_weight[:, columns]
        bias = jnp.concatenate([own_place(b, here) for b in biases]).reshape(lines, -1)
        rest = jnp.concatenate([jnp.broadcast_to(mod_place[columns], (lines, weight.shape[1])), bias], axis=1)
        part = jnp.pad(dot(cond_near, weight), ((0, 0), (0, bias.shape[1])))
        line_rows = halve_rows((part.reshape(devices, lines, -1) + rest).reshape(devices * lines, -1), order, gates)
        return line_rows[:, : weight.shape[1]], line_rows[:, weight.shape[1] :].reshape(1, -1)

    def blocks(line_rows):
        return line_rows.reshape(clips, frames, -1, width).transpose(0, 2, 1, 3)

    mod_first, bias_qkv = modulate(slice(0, 2 * width), (qkv_bias,))
    mods_one = blocks(mod_first)

    positions = lax.axis_index("seq") * rows + jnp.arange(rows, dtype=jnp.int32)
    cos_local, sin_local = rotary_lanes(positions, max(span, 256))
    cos_row, sin_row = rotary_lanes(jnp.arange(rows, dtype=jnp.int32), span)
    cos_far, sin_far = rotary_lanes(jnp.arange(seq_devices, dtype=jnp.int32) * rows, span)
    cos_all = (cos_far[:, None] * cos_row[None] - sin_far[:, None] * sin_row[None]).reshape(total, span)
    sin_all = (sin_far[:, None] * cos_row[None] + cos_far[:, None] * sin_row[None]).reshape(total, span)

    def exchange(value):
        return lax.all_to_all(value, "seq", 0, 0, tiled=True)

    def doubled(share, axis, bit):
        other = swap_bit(share, axis, bit)
        mine = own_bit(axis, bit) == 0
        pair = jnp.stack([jnp.where(mine, share, other), jnp.where(mine, other, share)], axis=1)
        return pair.reshape((-1,) + share.shape[1:])

    high_bits, low_bit = axis_bits("seq")[:-1], axis_bits("seq")[-1]
    down_share, up_share = down_shard[None], up_shard[None]
    for axis, bit in high_bits:
        down_share, up_share = doubled(down_share, axis, bit), doubled(up_share, axis, bit)
    full_qkv = after(full_qkv, down_share, up_share)
    up_pair = (up_share, swap_bit(up_share, "clip", 2))
    down_share = doubled(down_share, *low_bit)

    normed, qkv, mixes, fulls, logs, sents = [], [], [], [], [], []
    for c in range(clips):
        weight = full_qkv if c == 0 else after(full_qkv, down_share, up_pair[1])
        sent, normed_c = project(tokens, c, mods_one[c], weight, bias_qkv, cos_local, sin_local, seq_devices)
        normed.append(normed_c)
        if qkv:
            sent = after(sent, qkv[-1])
        qkv.append(exchange(sent))
    backs = []
    for c in range(clips):
        mix, full, log = attend(qkv[c].reshape(total, 3 * span), span)
        mixes.append(mix)
        fulls.append(full)
        logs.append(log)
        backs.append(exchange(after(mix.reshape(seq_devices, rows, span), qkv[-1] if c == 0 else backs[-1])))

    mod_rest, bias_rest = modulate(
        slice(2 * width, 6 * width), (out_bias, up_bias, down_bias), (None, None, normed[-1], mixes[0], mixes[-1])
    )
    mods_two = blocks(mod_rest)
    bias_out = bias_rest[:, :width]
    bias_up = bias_rest[:, width : 5 * width].reshape(owners).transpose(0, 2, 1, 3).reshape(1, -1)
    bias_down = bias_rest[:, 5 * width :]
    def from_clips(pair):
        near, across = [p.reshape((seq_devices // 2, 2) + p.shape[1:]) for p in pair]
        far = swap_bit(after(across, qkv[-1]), "clip", 1)
        return (near, across, swap_bit(near, "clip", 1), far)

    down_shares = from_clips((down_share, swap_bit(down_share, "clip", 2)))
    up_shares = from_clips([doubled(p, *low_bit) for p in up_pair])

    results = []
    d_mixed = []
    for c in range(clips):
        back = after(backs[c], mixes[-1])
        outputs = results[-1][0] if results else None
        results.append(middle(back, tokens, cotangent, c, mods_two[c], up_shares, down_shares, (bias_out, bias_up, bias_down), outputs))
        d_mixed.append(exchange(after(results[c][8], backs[-1] if c == 0 else d_mixed[-1])))

    def late(place):
        return [r[place] for r in results]

    mixed_all, normed_two, active, d_hidden, d_mlp, d_attn = [late(place) for place in (2, 3, 4, 5, 6, 7)]
    def line_sums(sums):
        return sums.transpose(1, 0, 2).reshape(frames, -1)

    def with_bias(lines_now, vectors):
        return jnp.concatenate([jnp.concatenate(lines_now, axis=0), jnp.concatenate(vectors).reshape(lines, -1)], axis=1)

    bias_up_sum = sum(r[10][0] for r in results).reshape(near_owners).transpose(0, 2, 1, 3).reshape(-1)
    bias_pair = sum(r[11] for r in results)
    early = with_bias([line_sums(r[9]) for r in results], [bias_pair[0], bias_up_sum, bias_pair[1]])
    early_rows = lax.all_gather(early, BOTH, axis=0, tiled=True)

    d_qkv, exchanged = [], []
    for c in range(clips):
        if c == clips - 1:
            active = gate(active, *d_qkv)
            down_first = along_first([(active, d_mlp)])
            down_core = swap_bit(down_first, "clip", 1)
            normed_two = gate(normed_two, down_first)
            up_first = across_first([(normed_two, d_hidden), (mixed_all, d_attn)])
            up_core = swap_bit(up_first, "clip", 1)
        grad = after(d_mixed[c], results[-1][8] if c == 0 else up_first)
        grad = grad.reshape(total, span)
        d_qkv.append(attend_back(qkv[c].reshape(total, 3 * span), grad, fulls[c], logs[c], cos_all, sin_all, span))
        sent = d_qkv[c].reshape(seq_devices, rows, 3 * span)
        exchanged.append(exchange(after(sent, d_mixed[-1]) if c == 0 else sent))

    d_mlp = gate(d_mlp, exchanged[0])
    down_second = along_second([(active, d_mlp)], down_core)
    d_hidden = gate(d_hidden, down_second)
    up_second = across_second([(normed_two, d_hidden), (mixed_all, d_attn)], up_core)
    down_along, up_across = swap_bit(down_second, "seq", 1), swap_bit(up_second, "clip", 2)
    exchanged[0] = after(exchanged[0], up_second)
    exchanged[-1] = after(exchanged[-1], down_along, up_across)

    last = []
    for c in range(clips):
        grads = last[-1][0] if last else None
        last.append(project_back(exchanged[c], full_qkv, tokens, c, mods_one[c][1], results[c][1], grads))
    d_projected = [r[1] for r in last]
    qkv_pairs = [(normed, d_projected)]
    qkv_core = swap_bit(across_first(qkv_pairs), "clip", 1)
    qkv_second = across_second(qkv_pairs, qkv_core)
    qkv_across = swap_bit(qkv_second, "clip", 2)
    d_hidden = gate(d_hidden, qkv_second)
    up_total = across_own([(normed_two, d_hidden), (mixed_all, d_attn)], up_core, up_across)
    qkv_total = across_own(qkv_pairs, qkv_core, qkv_across)
    d_mlp = gate(d_mlp, qkv_total)
    down_across = swap_bit(along_third([(active, d_mlp)], down_core, down_along), "clip", 2)
    grad_up, grad_qkv = along_seq(up_total), along_seq(qkv_total)
    grad_down = along_total([(active, d_mlp)], down_core, down_along, down_across)
    grad_out = grad_up[:, 4 * width :]
    grad_up = grad_up[:, : 4 * width].reshape((-1,) + near_owners).transpose(0, 1, 3, 2, 4).reshape(-1, 4 * width)
    late_rows = with_bias([line_sums(r[2]) for r in last], [sum(r[3][0] for r in last)])
    late_rows = collect_rows(after(late_rows, qkv_total), order)
    early_rows = after(early_rows, qkv_total)

    def own_columns(sums, shard):
        return lax.dynamic_slice_in_dim(sums, here * shard.shape[0], shard.shape[0], 0)

    def spans(all_rows, columns):
        vectors = jnp.sum(all_rows[:, columns:].reshape(devices, -1), axis=0)
        return all_rows[:, :columns], vectors

    late_mod, late_vectors = spans(late_rows, 2 * width)
    early_mod, early_vectors = spans(early_rows, 4 * width)
    grad_mod = jnp.concatenate(
        [
            lax.dot_general(rows_cond.astype(f32), r, TN, precision=highest, preferred_element_type=f32)
            for rows_cond, r in ((cond_late, late_mod), (cond, early_mod))
        ],
        axis=1,
    )
    mod_sum = jnp.concatenate([jnp.sum(late_mod, axis=0), jnp.sum(early_mod, axis=0)])
    return (
        results[-1][0],
        last[-1][0],
        grad_mod,
        own_columns(mod_sum, mod_bias),
        grad_qkv,
        own_columns(late_vectors, qkv_bias),
        grad_out,
        own_columns(early_vectors[:width], out_bias),
        grad_up,
        own_columns(early_vectors[width : 5 * width], up_bias),
        grad_down,
        own_columns(early_vectors[5 * width :], down_bias),
    )


def body_gathered(
    tokens,
    ctx_count,
    noise_level,
    mod_weight,
    mod_bias,
    qkv_weight,
    qkv_bias,
    out_weight,
    out_bias,
    up_weight,
    up_bias,
    down_weight,
    down_bias,
    cotangent,
):
    clips, rows, width = tokens.shape
    seq_devices = lax.axis_size("seq")
    devices = lax.axis_size("clip") * seq_devices
    bits = mesh_bits()
    here = lax.axis_index("clip") * seq_devices + lax.axis_index("seq")
    total = rows * seq_devices
    frames = max(1, rows // PATCHES)
    patch_rows = rows // frames

    full_qkv = lax.all_gather(qkv_weight, BOTH, axis=0, tiled=True)
    full_out = lax.all_gather(out_weight, BOTH, axis=0, tiled=True)
    full_up = lax.all_gather(up_weight, BOTH, axis=0, tiled=True)
    full_down = lax.all_gather(down_weight, BOTH, axis=0, tiled=True)
    biases = (qkv_bias, out_bias, up_bias, down_bias)
    bias_rows = double_rows(jnp.concatenate(biases).astype(f32), bits)
    full_biases = []
    first = 0
    for piece in biases:
        full_biases.append(bias_rows[:, first : first + piece.shape[0]].reshape(1, -1))
        first += piece.shape[0]
    bias_qkv, bias_out, bias_up, bias_down = full_biases

    levels = level_rows(ctx_count, noise_level, rows)
    cond = condition(levels, here, mod_weight.shape[0], width)
    mod_width = mod_weight.shape[1]
    partial = dot(cond, mod_weight) + own_place(mod_bias, here)
    modulation = halve_sum(partial.reshape(devices, clips * frames, mod_width), bits)
    modulation = modulation.reshape(clips, frames, 1, mod_width)

    positions = lax.axis_index("seq") * rows + jnp.arange(rows, dtype=jnp.int32)
    cosine, sine = rotary_lanes(positions, HEAD_DIM)
    key_frame = jnp.arange(total, dtype=jnp.int32) // PATCHES
    allowed = key_frame[None, :] <= (positions // PATCHES)[:, None]

    def flat(value):
        return value.reshape(rows, value.shape[-1])

    def split(value):
        return value.reshape(frames, patch_rows, value.shape[-1])

    def to_heads(value):
        return value.reshape(rows, HEADS, HEAD_DIM).transpose(1, 0, 2)

    saved = []
    for c in range(clips):
        mods = jnp.split(modulation[c], 6, axis=-1)
        tokens_now = split(tokens[c].astype(f32))
        unit, inverse = norm_parts(tokens_now)
        normed = flat((unit * (1.0 + mods[1]) + mods[0]).astype(bf16))
        projected = dot(normed, full_qkv) + bias_qkv
        views = []
        for place in range(3):
            view = to_heads(projected[:, place * width : (place + 1) * width])
            if place < 2:
                    view = view * cosine + jnp.roll(view, HEAD_DIM // 2, -1) * sine
            views.append(view.astype(bf16))
        queries, keys, values = views
        keys = lax.all_gather(keys, "seq", axis=1, tiled=True)
        values = lax.all_gather(values, "seq", axis=1, tiled=True)
        mix, logs = gathered_forward(queries, keys, values, allowed)
        mixed = mix.transpose(1, 0, 2).reshape(rows, width).astype(bf16)
        kept = (queries, keys, values, logs)
        saved.append((mods, tokens_now, unit, inverse, normed, kept, mixed))

    outputs = []
    middle = []
    for c in range(clips):
        mods, tokens_now, unit, inverse, normed, kept, mixed = saved[c]
        _, _, gate_one, shift_two, scale_two, gate_two = mods
        attn_out = split(dot(mixed, full_out) + bias_out)
        resid = tokens_now + gate_one * attn_out
        unit_two, inverse_two = norm_parts(resid)
        normed_two = flat((unit_two * (1.0 + scale_two) + shift_two).astype(bf16))
        hidden = dot(normed_two, full_up) + bias_up
        active_full, gelu_back = jax.vjp(jax.nn.gelu, hidden)
        active = active_full.astype(bf16)
        mlp_out = split(dot(active, full_down) + bias_down)
        outputs.append(flat((resid + gate_two * mlp_out).astype(bf16)))
        grad_out = split(cotangent[c].astype(f32))
        d_mlp = flat((gate_two * grad_out).astype(bf16))
        d_hidden = gelu_back(dot(d_mlp, full_down, NT))[0].astype(bf16)
        d_normed_two = split(dot(d_hidden, full_up, NT))
        d_resid = grad_out + norm_back(unit_two, inverse_two, d_normed_two, scale_two)
        d_attn = flat((gate_one * d_resid).astype(bf16))
        d_mixed = dot(d_attn, full_out, NT).astype(bf16)
        d_early = jnp.concatenate(
            [
                jnp.sum(d_resid * attn_out, axis=1),
                jnp.sum(d_normed_two, axis=1),
                jnp.sum(d_normed_two * unit_two, axis=1),
                jnp.sum(grad_out * mlp_out, axis=1),
            ],
            axis=-1,
        )
        middle.append((mixed, d_attn, normed_two, d_hidden, active, d_mlp, d_resid, d_mixed, d_early))

    def both(place):
        return jnp.concatenate([m[place] for m in middle], axis=0)

    d_attn_all, d_hidden_all, d_mlp_all = both(1), both(3), both(5)
    grad_down = weight_grad(both(4), d_mlp_all)
    grad_up = weight_grad(both(2), d_hidden_all)
    grad_out_weight = weight_grad(both(0), d_attn_all)
    early_rows = lax.all_gather(both(8), BOTH, axis=0, tiled=True)

    inputs_grad = []
    late = []
    projected_grads = []
    for c in range(clips):
        mods, tokens_now, unit, inverse, normed, kept, mixed = saved[c]
        d_resid, d_mixed = middle[c][6], middle[c][7]
        queries, keys, values, logs = kept
        dq, dk, dv = gathered_back(queries, keys, values, to_heads(d_mixed), logs, allowed)
        dk = lax.psum_scatter(dk.astype(bf16), "seq", scatter_dimension=1, tiled=True).astype(f32)
        dv = lax.psum_scatter(dv.astype(bf16), "seq", scatter_dimension=1, tiled=True).astype(f32)
        views = [g * cosine - jnp.roll(g, HEAD_DIM // 2, -1) * sine for g in (dq, dk)] + [dv]
        d_projected = jnp.concatenate([g.transpose(1, 0, 2).reshape(rows, width) for g in views], axis=1).astype(bf16)
        projected_grads.append(d_projected)
        d_normed = split(dot(d_projected, full_qkv, NT))
        inputs_grad.append(flat(d_resid + norm_back(unit, inverse, d_normed, mods[1])))
        late.append(jnp.concatenate([jnp.sum(d_normed, axis=1), jnp.sum(d_normed * unit, axis=1)], axis=-1))

    d_projected_all = jnp.concatenate(projected_grads, axis=0)
    grad_qkv = weight_grad(jnp.concatenate([s[4] for s in saved], axis=0), d_projected_all)
    bias_grads = [
        jnp.sum(g.astype(f32), axis=0).reshape(devices, -1) for g in (d_projected_all, d_attn_all, d_hidden_all, d_mlp_all)
    ]
    bias_sum = halve_sum(jnp.concatenate(bias_grads, axis=1), bits)
    grad_biases = []
    first = 0
    for piece in bias_grads:
        grad_biases.append(bias_sum[first : first + piece.shape[1]])
        first += piece.shape[1]

    late_rows = double_rows(jnp.concatenate(late, axis=0), bits).reshape(-1, 2 * width)
    grad_mod = jnp.concatenate(
        [
            lax.dot_general(cond.astype(f32), r, TN, precision=highest, preferred_element_type=f32)
            for r in (late_rows, early_rows)
        ],
        axis=1,
    )
    mod_sum = jnp.concatenate([jnp.sum(late_rows, axis=0), jnp.sum(early_rows, axis=0)])
    grad_mod_bias = lax.dynamic_slice_in_dim(mod_sum, here * mod_bias.shape[0], mod_bias.shape[0], 0)
    return (
        jnp.stack(outputs),
        jnp.stack(inputs_grad),
        grad_mod,
        grad_mod_bias,
        grad_qkv,
        grad_biases[0],
        grad_out_weight,
        grad_biases[1],
        grad_up,
        grad_biases[2],
        grad_down,
        grad_biases[3],
    )


def solution(mesh):
    by_heads = HEADS % mesh.shape["seq"] == 0
    body = body_by_heads if by_heads else body_gathered
    token_place = P("clip", "seq", None)
    matrix, vector = P(BOTH, None), P(BOTH)
    weights = (matrix, vector) * 5
    return jax.shard_map(
        body,
        mesh=mesh,
        in_specs=(token_place, P("clip"), P("clip", None)) + weights + (token_place,),
        out_specs=(token_place, token_place) + weights,
        check_vma=False,
    )
```

```python
import functools
import math

import jax
import jax.numpy as jnp
from jax import lax
from jax.experimental import pallas as pl
from jax.experimental.pallas import tpu as pltpu
from jax.sharding import PartitionSpec as P

HEADS = 16
HEAD_DIM = 64
FRAMES = 16
PATCHES = 256
BOTH = ("clip", "seq")
NT = (((1,), (1,)), ((), ()))
NN = (((1,), (0,)), ((), ()))
TN = (((0,), (0,)), ((), ()))
bf16 = jnp.bfloat16
f32 = jnp.float32
highest = lax.Precision.HIGHEST


def dot(left, right, dims=NN):
    return lax.dot_general(left, right, dims, preferred_element_type=f32)


def swap_bit(value, axis, bit):
    count = lax.axis_size(axis)
    return lax.ppermute(value, axis, [(i, i ^ bit) for i in range(count)])


def own_bit(axis, bit):
    return lax.shift_right_logical(lax.axis_index(axis), bit.bit_length() - 1) & 1


def axis_bits(axis):
    bits = []
    bit = 1
    while bit < lax.axis_size(axis):
        bits.append((axis, bit))
        bit *= 2
    return bits[::-1]


def exchange_order(bits):
    return sorted(range(len(bits)), key=lambda place: bits[place])


def mesh_bits():
    return axis_bits("clip") + axis_bits("seq")


def halve_sum(parts, bits, wire=f32, hold=None):
    addends = [parts.reshape((2,) * len(bits) + parts.shape[1:])]
    for place in exchange_order(bits):
        axis, bit = bits[place]
        mine = own_bit(axis, bit)
        send = sum(lax.dynamic_index_in_dim(a, 1 - mine, place).astype(f32) for a in addends)
        addends = [lax.dynamic_index_in_dim(a, mine, place) for a in addends]
        received = swap_bit(send.astype(wire), axis, bit)
        if hold is not None and len(addends) == 1:
            received = after(received, hold)
        addends.append(received)
    total = sum(a.astype(f32) for a in addends)
    return total.reshape(total.shape[len(bits) :])


def near_order():
    return axis_bits("clip")[::-1] + axis_bits("seq")[::-1]


def halve_rows(parts, bits, gates=()):
    for place, (axis, bit) in enumerate(bits):
        half = parts.shape[0] // 2
        mine = own_bit(axis, bit)
        keep = lax.dynamic_slice_in_dim(parts, mine * half, half, 0)
        send = lax.dynamic_slice_in_dim(parts, (1 - mine) * half, half, 0)
        other = swap_bit(send, axis, bit)
        if place < len(gates) and gates[place] is not None:
            other = after(other, gates[place])
        parts = keep + other
    return parts


def collect_rows(rows, bits):
    for axis, bit in reversed(bits):
        rows = jnp.concatenate([rows, swap_bit(rows, axis, bit)], axis=0)
    return rows


def relative_rows(rows, bits):
    shape = rows.shape
    rows = rows.reshape((2,) * len(bits) + (-1,) + shape[1:])
    for place, (axis, bit) in enumerate(bits):
        rows = jnp.where(own_bit(axis, bit) == 0, rows, jnp.flip(rows, place))
    return rows.reshape(shape)


def after(value, *others):
    return lax.optimization_barrier((value,) + others)[0]


def double_rows(row, bits):
    rows = row[None]
    for axis, bit in reversed(bits):
        other = swap_bit(rows, axis, bit)
        low = own_bit(axis, bit) == 0
        rows = jnp.concatenate([jnp.where(low, rows, other), jnp.where(low, other, rows)], axis=0)
    return rows


def weight_grad(left, right):
    tokens, rows = left.shape
    quarter = rows // lax.axis_size("clip")
    mine = lax.axis_index("clip")

    def part(flip):
        piece = lax.dynamic_slice_in_dim(left, (mine ^ flip) * quarter, quarter, 1)
        return dot(piece, right, TN)

    far = swap_bit(part(3).astype(bf16), "clip", 1)
    near = swap_bit(part(1).astype(bf16), "clip", 1)
    across = swap_bit((part(2) + far.astype(f32)).astype(bf16), "clip", 2)
    total = part(0) + near.astype(f32) + across.astype(f32)
    return halve_sum(total.reshape((lax.axis_size("seq"), -1, right.shape[1])), axis_bits("seq"), bf16)


def norm_parts(values):
    centre = values - jnp.mean(values, axis=-1, keepdims=True)
    spread = jnp.mean(centre * centre, axis=-1, keepdims=True)
    inverse = lax.rsqrt(spread + 1e-06)
    return centre * inverse, inverse


def norm_back(unit, inverse, grad, scales):
    scaled = grad * (1.0 + scales)
    mean = jnp.mean(scaled, axis=-1, keepdims=True)
    along = jnp.mean(scaled * unit, axis=-1, keepdims=True)
    return inverse * (scaled - mean - unit * along)


def rotary_lanes(positions, width):
    half = HEAD_DIM // 2
    lane = jnp.arange(width, dtype=jnp.int32) % HEAD_DIM
    freqs = jnp.exp(-math.log(10000.0) * 2.0 * (lane % half).astype(f32) / HEAD_DIM)
    angles = positions.astype(f32)[:, None] * freqs[None, :]
    sign = jnp.where(lane < half, -1.0, 1.0).astype(f32)
    return jnp.cos(angles), jnp.sin(angles) * sign[None, :]


def partner(values):
    width = values.shape[1]
    half = HEAD_DIM // 2
    lane = lax.broadcasted_iota(jnp.int32, (1, width), 1) % HEAD_DIM
    return jnp.where(lane < half, pltpu.roll(values, width - half, 1), pltpu.roll(values, half, 1))


def project_kernel(
    token_ref, mod_ref, wq_ref, wk_ref, wv_ref, bq_ref, bk_ref, bv_ref, cos_ref, sin_ref, out_ref, normed_ref, *, span
):
    frames = mod_ref.shape[1]
    patch = token_ref.shape[0] // frames

    @pl.when(pl.program_id(0) == 0)
    def _():
        for f in range(frames):
            rows = slice(f * patch, (f + 1) * patch)
            unit, _ = norm_parts(token_ref[rows, :].astype(f32))
            normed_ref[rows, :] = (unit * (1.0 + mod_ref[1, f : f + 1, :]) + mod_ref[0, f : f + 1, :]).astype(bf16)

    x = normed_ref[...]
    cosine, sine = cos_ref[...], sin_ref[...]
    groups = wq_ref.shape[1] // span
    for place, (w_ref, b_ref) in enumerate(((wq_ref, bq_ref), (wk_ref, bk_ref), (wv_ref, bv_ref))):
        value = dot(x, w_ref[...]) + b_ref[...]
        if place < 2:
            value = value * cosine + partner(value) * sine
        value = value.astype(bf16)
        for g in range(groups):
            out_ref[g, :, place * span : (place + 1) * span] = value[:, g * span : (g + 1) * span]


def whole_block(shape):
    return pl.BlockSpec(shape, lambda j: (0,) * len(shape))


def column_specs(height, block, steps):
    return [pl.BlockSpec((height, block), functools.partial(lambda p, j: (0, p * steps + j), p)) for p in range(3)]


def clip_block(shape, c):
    return pl.BlockSpec((None,) + shape[1:], lambda j: (c,) + (0,) * (len(shape) - 1))


def project(tokens, c, mods, weight, bias, cosine, sine, groups):
    _, rows, width = tokens.shape
    span = width // groups
    block = max(span, 256)
    per_step = block // span
    steps = groups // per_step
    return pl.pallas_call(
        functools.partial(project_kernel, span=span),
        grid=(steps,),
        in_specs=[clip_block(tokens.shape, c), whole_block(mods.shape)]
        + column_specs(width, block, steps)
        + column_specs(1, block, steps)
        + [whole_block((rows, block))] * 2,
        out_specs=(pl.BlockSpec((per_step, rows, 3 * span), lambda j: (j, 0, 0)), whole_block((rows, width))),
        out_shape=(
            jax.ShapeDtypeStruct((groups, rows, 3 * span), bf16),
            jax.ShapeDtypeStruct((rows, width), bf16),
        ),
        compiler_params=pltpu.CompilerParams(vmem_limit_bytes=32 << 20),
        cost_estimate=pl.CostEstimate(
            flops=6 * rows * width * width, bytes_accessed=6 * width * width + 10 * rows * width, transcendentals=0
        ),
        name="project",
    )(tokens, mods, weight, weight, weight, bias, bias, bias, cosine, sine)


def project_back_kernel(
    back_ref, wq_ref, wk_ref, wv_ref, token_ref, scale_ref, resid_ref, *rest, span
):
    grad_ref, proj_ref, sums_ref, bias_ref, acc_ref = rest[-5:]
    frames = scale_ref.shape[0]
    rows_all, width = token_ref.shape
    patch = rows_all // frames
    step = pl.program_id(0)
    block = wq_ref.shape[1]

    @pl.when(step == 0)
    def _():
        acc_ref[...] = jnp.zeros_like(acc_ref)

    for place, w_ref in enumerate((wq_ref, wk_ref, wv_ref)):
        band = slice(place * span, (place + 1) * span)
        piece = jnp.concatenate([back_ref[g, :, band] for g in range(block // span)], axis=1)
        columns = pl.ds(pl.multiple_of(place * width + step * block, block), block)
        proj_ref[:, columns] = piece
        bias_ref[:, columns] = jnp.sum(piece.astype(f32), axis=0, keepdims=True)
        acc_ref[...] += dot(piece, w_ref[...], NT)

    @pl.when(step == pl.num_programs(0) - 1)
    def _():
        for f in range(frames):
            rows = slice(f * patch, (f + 1) * patch)
            unit, inverse = norm_parts(token_ref[rows, :].astype(f32))
            grad = acc_ref[rows, :]
            grad_ref[rows, :] = resid_ref[rows, :] + norm_back(unit, inverse, grad, scale_ref[f : f + 1, :])
            sums_ref[0, f : f + 1, :] = jnp.sum(grad, axis=0, keepdims=True)
            sums_ref[1, f : f + 1, :] = jnp.sum(grad * unit, axis=0, keepdims=True)


def project_back(back, weight, tokens, c, scales, d_resid, grads):
    groups, rows, _ = back.shape
    width = tokens.shape[2]
    span = width // groups
    block = max(span, 256)
    per_step = block // span
    steps = groups // per_step
    earlier = [] if grads is None else [grads]
    return pl.pallas_call(
        functools.partial(project_back_kernel, span=span),
        grid=(steps,),
        in_specs=[pl.BlockSpec((per_step, rows, 3 * span), lambda j: (j, 0, 0))]
        + column_specs(width, block, steps)
        + [clip_block(tokens.shape, c), whole_block(scales.shape), whole_block((rows, width))]
        + [pl.BlockSpec(memory_space=pl.ANY)] * len(earlier),
        out_specs=(
            clip_block(tokens.shape, c),
            whole_block((rows, 3 * width)),
            whole_block((2,) + scales.shape),
            whole_block((1, 3 * width)),
        ),
        out_shape=(
            jax.ShapeDtypeStruct(tokens.shape, f32),
            jax.ShapeDtypeStruct((rows, 3 * width), bf16),
            jax.ShapeDtypeStruct((2,) + scales.shape, f32),
            jax.ShapeDtypeStruct((1, 3 * width), f32),
        ),
        input_output_aliases={7: 0} if earlier else {},
        scratch_shapes=[pltpu.VMEM((rows, width), f32)],
        compiler_params=pltpu.CompilerParams(vmem_limit_bytes=40 << 20),
        cost_estimate=pl.CostEstimate(
            flops=6 * rows * width * width, bytes_accessed=6 * width * width + 22 * rows * width, transcendentals=0
        ),
        name="project_back",
    )(back, weight, weight, weight, tokens, scales, d_resid, *earlier)


GELU_RATE = math.sqrt(2.0 / math.pi)
GELU_CUBE = 0.044715


def middle_kernel(clip_ref, back_ref, token_ref, cot_ref, mod_ref, bo_ref, bup_ref, bdown_ref, *refs):
    wo_refs, up_refs, down_refs = refs[0:4], refs[4:8], refs[8:12]
    (
        out_ref,
        dres_ref,
        mixed_ref,
        normed_ref,
        act_ref,
        dhid_ref,
        dmlp_ref,
        dattn_ref,
        dmix_ref,
        sums_ref,
        bup_sum_ref,
        bsum_ref,
        attn_ref,
        res_ref,
        mlp_ref,
        dn_ref,
        wo_ref,
        up_ref,
        down_ref,
    ) = refs[-19:]
    groups, rows_all, span = back_ref.shape
    width = token_ref.shape[1]
    quarter = width // 4
    frames = mod_ref.shape[1]
    patch = rows_all // frames
    step = pl.program_id(0)
    mine = clip_ref[0]

    def owner_rows(place):
        return pl.ds(pl.multiple_of((mine ^ FLIPS[place]) * quarter, quarter), quarter)

    @pl.when(step == 0)
    def _():
        for place in range(4):
            wo_ref[owner_rows(place), :] = wo_refs[place][...].reshape(quarter, width)
        for g in range(groups):
            mixed_ref[:, g * span : (g + 1) * span] = back_ref[g]
        attn_ref[...] = dot(mixed_ref[...], wo_ref[...]) + bo_ref[...]
        for f in range(frames):
            rows = slice(f * patch, (f + 1) * patch)
            resid = token_ref[rows, :].astype(f32) + mod_ref[0, f : f + 1, :] * attn_ref[rows, :]
            res_ref[rows, :] = resid
            unit, _ = norm_parts(resid)
            normed_ref[rows, :] = (unit * (1.0 + mod_ref[2, f : f + 1, :]) + mod_ref[1, f : f + 1, :]).astype(bf16)
            dmlp_ref[rows, :] = (mod_ref[3, f : f + 1, :] * cot_ref[rows, :].astype(f32)).astype(bf16)
        mlp_ref[...] = jnp.zeros_like(mlp_ref)
        dn_ref[...] = jnp.zeros_like(dn_ref)

    for place in range(4):
        up_ref[owner_rows(place), :] = up_refs[place][...].reshape(quarter, -1)

        @pl.when(step // 2 == place)
        def _(place=place):
            down_ref[...] = down_refs[place][...].reshape(-1, width)

    up = up_ref[...]
    down = down_ref[...]
    hidden = dot(normed_ref[...], up) + bup_ref[...]
    square = hidden * hidden
    bend = jnp.tanh(GELU_RATE * (hidden + GELU_CUBE * (square * hidden)))
    share = 0.5 * (1.0 + bend)
    active = (hidden * share).astype(bf16)
    act_ref[...] = active
    mlp_ref[...] += dot(active, down)
    slope = share + 0.5 * hidden * (1.0 - bend * bend) * (GELU_RATE + (3.0 * GELU_RATE * GELU_CUBE) * square)
    d_hidden = (dot(dmlp_ref[...], down, NT) * slope).astype(bf16)
    dhid_ref[...] = d_hidden
    bup_sum_ref[...] = jnp.sum(d_hidden.astype(f32), axis=0, keepdims=True)
    dn_ref[...] += dot(d_hidden, up, NT)

    @pl.when(step == pl.num_programs(0) - 1)
    def _():
        bsum = None
        for f in range(frames):
            rows = slice(f * patch, (f + 1) * patch)
            resid = res_ref[rows, :]
            mlp = mlp_ref[rows, :] + bdown_ref[...]
            out_ref[rows, :] = (resid + mod_ref[3, f : f + 1, :] * mlp).astype(bf16)
            cot = cot_ref[rows, :].astype(f32)
            sums_ref[3, f : f + 1, :] = jnp.sum(cot * mlp, axis=0, keepdims=True)
            unit, inverse = norm_parts(resid)
            grad = dn_ref[rows, :]
            sums_ref[1, f : f + 1, :] = jnp.sum(grad, axis=0, keepdims=True)
            sums_ref[2, f : f + 1, :] = jnp.sum(grad * unit, axis=0, keepdims=True)
            d_resid = cot + norm_back(unit, inverse, grad, mod_ref[2, f : f + 1, :])
            dres_ref[rows, :] = d_resid
            sums_ref[0, f : f + 1, :] = jnp.sum(d_resid * attn_ref[rows, :], axis=0, keepdims=True)
            d_attn = (mod_ref[0, f : f + 1, :] * d_resid).astype(bf16)
            dattn_ref[rows, :] = d_attn
            term = jnp.concatenate(
                [
                    jnp.sum(d_attn.astype(f32), axis=0, keepdims=True),
                    jnp.sum(dmlp_ref[rows, :].astype(f32), axis=0, keepdims=True),
                ],
                axis=0,
            )
            bsum = term if bsum is None else bsum + term
        bsum_ref[...] = bsum
        d_mixed = dot(dattn_ref[...], wo_ref[...], NT).astype(bf16)
        for g in range(groups):
            dmix_ref[g] = d_mixed[:, g * span : (g + 1) * span]


FLIPS = (0, 2, 1, 3)


def middle(back, tokens, cot, c, mods, up_shares, down_shares, biases, outputs):
    groups, rows, span = back.shape
    _, _, width = tokens.shape
    high, low, _, piece, _ = up_shares[0].shape
    hidden = 4 * width
    steps = 8
    block = hidden // steps
    bias_out, bias_up, bias_down = biases
    mine = lax.axis_index("clip").astype(jnp.int32)[None]
    earlier = [] if outputs is None else [outputs]

    def fixed(shape, **options):
        return pl.BlockSpec(shape, lambda j, q: (0,) * len(shape), **options)

    def clip_part(shape):
        return pl.BlockSpec((None,) + shape[1:], lambda j, q: (c,) + (0,) * (len(shape) - 1))

    def unit_block(j, q):
        owner = q[0] ^ jnp.where(j // 2 == 1, 2, jnp.where(j // 2 == 2, 1, j // 2))
        return owner, j % 2

    def up_index(j, q):
        owner, half = unit_block(j, q)
        return (0, 0, owner, 0, half)

    def hidden_index(j, q):
        owner, half = unit_block(j, q)
        return (0, owner * 2 + half)

    def down_index(place, j, q):
        return (0, jnp.clip(j - 2 * place, 0, 1), 0, 0, 0)

    token_block = fixed((rows, width))
    hidden_block = pl.BlockSpec((rows, block), hidden_index)
    out_spec = [
        pl.BlockSpec((high, low, 1, piece, width), lambda j, q: (0, 0, 4, 0, 0), pipeline_mode=pl.Buffered(1)) for _ in range(4)
    ]
    up_spec = [pl.BlockSpec((high, low, 1, piece, block), up_index) for _ in range(4)]
    down_spec = [
        pl.BlockSpec((high, 1, 4, piece, width), functools.partial(down_index, place)) for place in range(4)
    ]
    return pl.pallas_call(
        middle_kernel,
        grid_spec=pltpu.PrefetchScalarGridSpec(
            num_scalar_prefetch=1,
            grid=(steps,),
            in_specs=[
                fixed(back.shape),
                clip_part(tokens.shape),
                clip_part(tokens.shape),
                fixed(mods.shape),
                fixed((1, width)),
                pl.BlockSpec((1, block), hidden_index),
                fixed((1, width)),
            ]
            + out_spec
            + up_spec
            + down_spec
            + [pl.BlockSpec(memory_space=pl.ANY)] * len(earlier),
            out_specs=(
                clip_part(tokens.shape),
                token_block,
                token_block,
                token_block,
                hidden_block,
                hidden_block,
                token_block,
                token_block,
                fixed(back.shape),
                fixed(mods.shape),
                pl.BlockSpec((1, block), hidden_index),
                fixed((2, width)),
            ),
            scratch_shapes=[pltpu.VMEM((rows, width), f32)] * 4
            + [pltpu.VMEM((width, width), bf16), pltpu.VMEM((width, block), bf16), pltpu.VMEM((block, width), bf16)],
        ),
        out_shape=(
            jax.ShapeDtypeStruct(tokens.shape, bf16),
            jax.ShapeDtypeStruct((rows, width), f32),
            jax.ShapeDtypeStruct((rows, width), bf16),
            jax.ShapeDtypeStruct((rows, width), bf16),
            jax.ShapeDtypeStruct((rows, hidden), bf16),
            jax.ShapeDtypeStruct((rows, hidden), bf16),
            jax.ShapeDtypeStruct((rows, width), bf16),
            jax.ShapeDtypeStruct((rows, width), bf16),
            jax.ShapeDtypeStruct(back.shape, bf16),
            jax.ShapeDtypeStruct(mods.shape, f32),
            jax.ShapeDtypeStruct((1, hidden), f32),
            jax.ShapeDtypeStruct((2, width), f32),
        ),
        input_output_aliases={20: 0} if earlier else {},
        compiler_params=pltpu.CompilerParams(vmem_limit_bytes=60 << 20),
        cost_estimate=pl.CostEstimate(
            flops=4 * rows * width * width, bytes_accessed=2 * width * width + 5 * rows * width, transcendentals=rows * width
        ),
        name="middle",
    )(mine, back, tokens, cot, mods, bias_out, bias_up, bias_down, *up_shares, *up_shares, *down_shares, *earlier)


def weight_part_kernel(index_ref, *refs, clips, count, widths, addends):
    sets = len(widths)
    per_set = clips * (count + 1)
    extra = refs[sets * per_set : sets * per_set + addends]
    out_ref, flat_ref = refs[sets * per_set + addends :]
    step = pl.program_id(0)
    first = 0
    for place, steps in enumerate(widths):
        given = refs[place * per_set : (place + 1) * per_set]
        left, right = given[: clips * count], given[clips * count :]
        rows = right[0].shape[0]

        @pl.when(step == first)
        def _(left=left, rows=rows):
            for c in range(clips):
                for i in range(count):
                    flat_ref[i, :, c * rows : (c + 1) * rows] = jnp.transpose(left[c * count + i][...])

        @pl.when((step >= first) & (step < first + steps))
        def _(right=right, rows=rows):
            for i in range(count):
                total = dot(flat_ref[i, :, 0:rows], right[0][...])
                for c in range(1, clips):
                    total += dot(flat_ref[i, :, c * rows : (c + 1) * rows], right[c][...])
                for ref in extra:
                    total += ref[i].astype(f32)
                out_ref[i] = total.astype(out_ref.dtype)

        first += steps


def weight_part(pairs, indices, addends, kind, height):
    block = 512
    count = indices.shape[0]
    clips = len(pairs[0][0])
    rows = pairs[0][0][0].shape[0]
    widths = [right[0].shape[1] // block for _, right in pairs]
    columns = sum(widths) * block
    in_specs, operands = [], []
    first = 0
    for (left, right), steps in zip(pairs, widths):
        for array in left:
            for i in range(count):
                in_specs.append(pl.BlockSpec((rows, height), functools.partial(lambda i, j, q: (0, q[i]), i)))
                operands.append(array)
        where = functools.partial(lambda first, steps, j, q: (0, jnp.clip(j - first, 0, steps - 1)), first, steps)
        in_specs += [pl.BlockSpec((rows, block), where)] * clips
        operands += right
        first += steps
    for array, start in addends:
        where = functools.partial(lambda start, j, q: (start, 0, j), start // count)
        in_specs.append(pl.BlockSpec((count, height, block), where))
        operands.append(array)
    return pl.pallas_call(
        functools.partial(weight_part_kernel, clips=clips, count=count, widths=widths, addends=len(addends)),
        grid_spec=pltpu.PrefetchScalarGridSpec(
            num_scalar_prefetch=1,
            grid=(columns // block,),
            in_specs=in_specs,
            out_specs=pl.BlockSpec((count, height, block), lambda j, q: (0, 0, j)),
            scratch_shapes=[pltpu.VMEM((count, height, clips * rows), bf16)],
        ),
        out_shape=jax.ShapeDtypeStruct((count, height, columns), kind),
        compiler_params=pltpu.CompilerParams(vmem_limit_bytes=60 << 20),
        cost_estimate=pl.CostEstimate(
            flops=2 * count * clips * rows * height * columns,
            bytes_accessed=clips * rows * (count * height + columns) * 2 + 4 * count * height * columns,
            transcendentals=0,
        ),
        name="weight_part",
    )(indices, *operands)


def mine_on(axis):
    return lax.axis_index(axis).astype(jnp.int32)


def gate(arrays, *others):
    return list(lax.optimization_barrier((tuple(arrays), others))[0])


def height_of(pairs, parts):
    return pairs[0][0][0].shape[1] // parts


def across_first(pairs):
    mine = mine_on("clip")
    return weight_part(pairs, jnp.stack([mine ^ 3, mine ^ 1]), (), bf16, height_of(pairs, 4))


def across_second(pairs, core):
    return weight_part(pairs, (mine_on("clip") ^ 2)[None], ((core, 0),), bf16, height_of(pairs, 4))


def across_own(pairs, core, across):
    addends = ((core, 1), (across, 0))
    return weight_part(pairs, mine_on("clip")[None], addends, f32, height_of(pairs, 4))


def along_seq(total, hold=None):
    return halve_sum(total.reshape((lax.axis_size("seq"), -1, total.shape[2])), axis_bits("seq"), bf16, hold)


def along_block(clip_flip, low_flip):
    return (mine_on("clip") ^ clip_flip) * 2 + ((mine_on("seq") & 1) ^ low_flip)


def along_first(pairs):
    blocks = jnp.stack([along_block(1, 1), along_block(3, 1), along_block(1, 0), along_block(3, 0)])
    return weight_part(pairs, blocks, (), bf16, height_of(pairs, 8))


def along_second(pairs, core):
    blocks = jnp.stack([along_block(0, 1), along_block(2, 1)])
    return weight_part(pairs, blocks, ((core, 0),), bf16, height_of(pairs, 8))


def along_third(pairs, core, along):
    return weight_part(pairs, along_block(2, 0)[None], ((core, 3), (along, 1)), bf16, height_of(pairs, 8))


def along_own(pairs, core, along, across):
    addends = ((core, 2), (along, 0), (across, 0))
    return weight_part(pairs, along_block(0, 0)[None], addends, f32, height_of(pairs, 8))


def along_high(total, hold=None):
    bits = axis_bits("seq")[:-1]
    return halve_sum(total.reshape((2 ** len(bits), -1, total.shape[2])), bits, bf16, hold)


def attend_kernel(qkv_ref, mix_ref, full_ref, log_ref, vt_ref, *, total, span, block):
    heads = span // HEAD_DIM
    head = lax.broadcasted_iota(jnp.int32, (1, span), 1) // HEAD_DIM
    key_frame = lax.broadcasted_iota(jnp.int32, (block, block), 0) // PATCHES
    query_frame = lax.broadcasted_iota(jnp.int32, (block, block), 1) // PATCHES
    kept = key_frame <= query_frame

    def flip(j, carry):
        rows = pl.ds(pl.multiple_of(j * block, block), block)
        vt_ref[:, rows] = jnp.transpose(qkv_ref[rows, 2 * span : 3 * span])
        return carry

    lax.fori_loop(0, total // block, flip, 0)

    def query_block(i, carry):
        rows = pl.ds(pl.multiple_of(i * block, block), block)
        query = qkv_ref[rows, 0:span] * jnp.asarray(HEAD_DIM**-0.5, bf16)
        queries = [jnp.where(head == h, query, jnp.zeros_like(query)) for h in range(heads)]

        def step(j, state, masked):
            peaks, sums, mixes = state
            columns = pl.ds(pl.multiple_of(j * block, block), block)
            key = qkv_ref[columns, span : 2 * span]
            new = ([], [], [])
            for h in range(heads):
                scores = dot(key, queries[h], NT)
                if masked:
                    scores = jnp.where(kept, scores, -1e30)
                peak = jnp.maximum(peaks[h], jnp.max(scores, axis=0, keepdims=True))
                raised = jnp.exp(scores - peak)
                fade = jnp.exp(peaks[h] - peak)
                new[0].append(peak)
                new[1].append(fade * sums[h] + jnp.sum(raised, axis=0, keepdims=True))
                term = dot(vt_ref[h * HEAD_DIM : (h + 1) * HEAD_DIM, columns], raised.astype(bf16))
                new[2].append(mixes[h] * fade + term)
            return tuple(map(tuple, new))

        state = (
            tuple(jnp.full((1, block), -1e30, f32) for _ in range(heads)),
            tuple(jnp.zeros((1, block), f32) for _ in range(heads)),
            tuple(jnp.zeros((HEAD_DIM, block), f32) for _ in range(heads)),
        )
        state = lax.fori_loop(0, i, lambda j, s: step(j, s, False), state)
        peaks, sums, mixes = step(i, state, True)
        mixed = jnp.transpose(jnp.concatenate([mixes[h] / sums[h] for h in range(heads)], axis=0))
        full_ref[rows, :] = mixed
        mix_ref[rows, :] = mixed.astype(bf16)
        for h in range(heads):
            log_ref[h : h + 1, rows] = peaks[h] + jnp.log(sums[h])
        return carry

    lax.fori_loop(0, total // block, query_block, 0)


def attend(qkv, span):
    total = qkv.shape[0]
    heads = span // HEAD_DIM
    block = min(1024, total)
    return pl.pallas_call(
        functools.partial(attend_kernel, total=total, span=span, block=block),
        out_shape=(
            jax.ShapeDtypeStruct((total, span), bf16),
            jax.ShapeDtypeStruct((total, span), f32),
            jax.ShapeDtypeStruct((heads, total), f32),
        ),
        scratch_shapes=[pltpu.VMEM((span, total), bf16)],
        compiler_params=pltpu.CompilerParams(vmem_limit_bytes=60 << 20),
        cost_estimate=pl.CostEstimate(
            flops=8 * total * total * span, bytes_accessed=12 * total * span, transcendentals=total * total * heads // 2
        ),
        name="attend",
    )(qkv)


def attend_back_kernel(
    qkv_ref, grad_ref, full_ref, log_ref, cos_ref, sin_ref, out_ref, dq_ref, dk_ref, dv_ref, along_ref, *, total, span, block
):
    heads = span // HEAD_DIM
    scale = HEAD_DIM**-0.5
    head = lax.broadcasted_iota(jnp.int32, (1, span), 1) // HEAD_DIM
    blocks = total // block
    dq_ref[...] = jnp.zeros_like(dq_ref)

    def only(value, h):
        return jnp.where(head == h, value, jnp.zeros_like(value))

    def lead(i, carry):
        rows = pl.ds(pl.multiple_of(i * block, block), block)
        product = jnp.transpose(grad_ref[rows, :].astype(f32) * full_ref[rows, :])
        for h in range(heads):
            along_ref[h : h + 1, rows] = jnp.sum(product[h * HEAD_DIM : (h + 1) * HEAD_DIM], axis=0, keepdims=True)
        return carry

    lax.fori_loop(0, blocks, lead, 0)

    def key_block(j, carry):
        first = pl.multiple_of(j * block, block)
        columns = pl.ds(first, block)
        key = qkv_ref[columns, span : 2 * span]
        value = qkv_ref[columns, 2 * span : 3 * span]
        key_flat = jnp.transpose(key)
        dk_ref[...] = jnp.zeros_like(dk_ref)
        dv_ref[...] = jnp.zeros_like(dv_ref)

        def tile(rows, keys, h, query_h, grad_h):
            band = slice(h * HEAD_DIM, (h + 1) * HEAD_DIM)
            probs = jnp.exp(dot(key[:keys], query_h, NT) - log_ref[h : h + 1, rows])
            d_probs = dot(value[:keys], grad_h, NT)
            d_scores = (probs * (d_probs - along_ref[h : h + 1, rows])).astype(bf16)
            dq_ref[band, rows] += dot(key_flat[band, :keys], d_scores)
            return dot(probs.astype(bf16), grad_h), dot(d_scores, query_h)

        def heads_of(rows):
            query = qkv_ref[rows, 0:span] * jnp.asarray(scale, bf16)
            grad = grad_ref[rows, :]
            return [(h, only(query, h), only(grad, h)) for h in range(heads)]

        for f in range(block // PATCHES):
            rows = pl.ds(pl.multiple_of(first + f * PATCHES, PATCHES), PATCHES)
            keys = (f + 1) * PATCHES
            for h, query_h, grad_h in heads_of(rows):
                dv, dk = tile(rows, keys, h, query_h, grad_h)
                dv_ref[:keys] += dv
                dk_ref[:keys] += dk

        def later(i, c):
            rows = pl.ds(pl.multiple_of(i * block, block), block)
            terms = [tile(rows, block, h, query_h, grad_h) for h, query_h, grad_h in heads_of(rows)]
            dv_ref[...] += sum(t[0] for t in terms)
            dk_ref[...] += sum(t[1] for t in terms)
            return c

        lax.fori_loop(j + 1, blocks, later, 0)
        dk = dk_ref[...]
        out_ref[columns, span : 2 * span] = (dk * cos_ref[columns, :] - partner(dk) * sin_ref[columns, :]).astype(bf16)
        out_ref[columns, 2 * span : 3 * span] = dv_ref[...].astype(bf16)
        return carry

    lax.fori_loop(0, blocks, key_block, 0)

    def last(i, carry):
        rows = pl.ds(pl.multiple_of(i * block, block), block)
        dq = jnp.transpose(dq_ref[:, rows]) * scale
        out_ref[rows, 0:span] = (dq * cos_ref[rows, :] - partner(dq) * sin_ref[rows, :]).astype(bf16)
        return carry

    lax.fori_loop(0, blocks, last, 0)


def attend_back(qkv, grad, full, logs, cosine, sine, span):
    total = qkv.shape[0]
    heads = span // HEAD_DIM
    block = min(1024, total)
    return pl.pallas_call(
        functools.partial(attend_back_kernel, total=total, span=span, block=block),
        out_shape=jax.ShapeDtypeStruct((total, 3 * span), bf16),
        scratch_shapes=[
            pltpu.VMEM((span, total), f32),
            pltpu.VMEM((block, span), f32),
            pltpu.VMEM((block, span), f32),
            pltpu.VMEM((heads, total), f32),
        ],
        compiler_params=pltpu.CompilerParams(vmem_limit_bytes=60 << 20),
        cost_estimate=pl.CostEstimate(
            flops=20 * total * total * span, bytes_accessed=26 * total * span, transcendentals=total * total * heads // 2
        ),
        name="attend_back",
    )(qkv, grad, full, logs, cosine, sine)


def gathered_forward(queries, keys, values, allowed):
    def one(pieces):
        q, k, v = pieces
        scores = jnp.where(allowed, dot(q, k, NT) * HEAD_DIM**-0.5, -1e30)
        peak = jnp.max(scores, axis=-1, keepdims=True)
        raised = jnp.exp(scores - peak)
        totals = jnp.sum(raised, axis=-1, keepdims=True)
        return dot((raised / totals).astype(bf16), v), peak + jnp.log(totals)

    return lax.map(one, (queries, keys, values))


def gathered_back(queries, keys, values, grads, logs, allowed):
    scale = HEAD_DIM**-0.5

    def one(pieces):
        q, k, v, grad, log = pieces
        scores = jnp.where(allowed, dot(q, k, NT) * scale, -1e30)
        probs = jnp.exp(scores - log)
        d_probs = dot(grad, v, NT)
        centre = jnp.sum(probs * d_probs, axis=-1, keepdims=True)
        d_scores = (probs * (d_probs - centre)).astype(bf16)
        dv = dot(probs.astype(bf16), grad, TN)
        return dot(d_scores, k) * scale, dot(d_scores, q, TN) * scale, dv

    return lax.map(one, (queries, keys, values, grads, logs))


def level_rows(ctx_count, noise_level, rows):
    clips = ctx_count.shape[0]
    seq_devices = lax.axis_size("seq")
    plan = jnp.concatenate([ctx_count[:, None], noise_level], axis=1)
    plan = double_rows(plan, axis_bits("clip"))
    levels = jnp.where(jnp.arange(FRAMES, dtype=jnp.int32) < plan[..., :1], 0, plan[..., 1:])
    if rows < PATCHES:
        levels = jnp.repeat(levels, PATCHES // rows, axis=-1)
    frames = max(1, rows // PATCHES)
    levels = levels.reshape(-1, clips, seq_devices, frames).transpose(0, 2, 1, 3)
    return levels.reshape(-1, seq_devices, clips * frames)


def condition(levels, here, depth, width):
    half_width = width // 2
    feature = here * depth + jnp.arange(depth, dtype=jnp.int32)
    low_half = feature < half_width
    freqs = jnp.exp(-math.log(10000.0) * jnp.where(low_half, feature, feature - half_width).astype(f32) / half_width)
    angles = levels.reshape(-1, 1).astype(f32) * freqs
    return jax.nn.silu(jnp.where(low_half, jnp.sin(angles), jnp.cos(angles))).astype(bf16)


def own_place(shard, here):
    count = lax.axis_size("clip") * lax.axis_size("seq")
    whole = jnp.zeros((count * shard.shape[0],), f32)
    return lax.dynamic_update_slice_in_dim(whole, shard.astype(f32), here * shard.shape[0], 0)


def body_by_heads(
    tokens,
    ctx_count,
    noise_level,
    mod_weight,
    mod_bias,
    qkv_weight,
    qkv_bias,
    out_weight,
    out_bias,
    up_weight,
    up_bias,
    down_weight,
    down_bias,
    cotangent,
):
    clips, rows, width = tokens.shape
    seq_devices = lax.axis_size("seq")
    devices = lax.axis_size("clip") * seq_devices
    order = near_order()
    here = lax.axis_index("clip") * seq_devices + lax.axis_index("seq")
    total = rows * seq_devices
    frames = max(1, rows // PATCHES)
    span = width // seq_devices
    lines = clips * frames
    piece = out_weight.shape[0]

    full_qkv = lax.all_gather(qkv_weight, BOTH, axis=0, tiled=True)
    unit = down_weight.shape[0]
    owners = (4, seq_devices // 2, 2, unit)
    near_owners = (4, 2, seq_devices // 2, unit)
    down_shard = down_weight.reshape(4, piece, width)
    up_shard = up_weight.reshape((piece,) + owners).transpose(1, 0, 3, 2, 4).reshape(4, piece, width)
    up_shard = jnp.concatenate([up_shard, out_weight[None]], axis=0)

    levels = level_rows(ctx_count, noise_level, rows)
    flat_bits = (2,) * len(order)
    bits_clip, bits_seq = len(axis_bits("clip")), len(axis_bits("seq"))
    turn = tuple(range(bits_clip))[::-1] + tuple(range(bits_clip, bits_clip + bits_seq))[::-1] + (len(order),)
    near_levels = levels.reshape(flat_bits + (lines,)).transpose(turn)
    cond_near = condition(near_levels, here, mod_weight.shape[0], width)
    cond = condition(levels, here, mod_weight.shape[0], width)
    cond_late = relative_rows(cond_near, order)
    mod_place = own_place(mod_bias, here)

    def modulate(columns, biases, gates=()):
        weight = mod_weight[:, columns]
        bias = jnp.concatenate([own_place(b, here) for b in biases]).reshape(lines, -1)
        rest = jnp.concatenate([jnp.broadcast_to(mod_place[columns], (lines, weight.shape[1])), bias], axis=1)
        part = jnp.pad(dot(cond_near, weight), ((0, 0), (0, bias.shape[1])))
        line_rows = halve_rows((part.reshape(devices, lines, -1) + rest).reshape(devices * lines, -1), order, gates)
        return line_rows[:, : weight.shape[1]], line_rows[:, weight.shape[1] :].reshape(1, -1)

    def blocks(line_rows):
        return line_rows.reshape(clips, frames, -1, width).transpose(0, 2, 1, 3)

    mod_first, bias_qkv = modulate(slice(0, 2 * width), (qkv_bias,))
    mods_one = blocks(mod_first)

    positions = lax.axis_index("seq") * rows + jnp.arange(rows, dtype=jnp.int32)
    cos_local, sin_local = rotary_lanes(positions, max(span, 256))
    cos_row, sin_row = rotary_lanes(jnp.arange(rows, dtype=jnp.int32), span)
    cos_far, sin_far = rotary_lanes(jnp.arange(seq_devices, dtype=jnp.int32) * rows, span)
    cos_all = (cos_far[:, None] * cos_row[None] - sin_far[:, None] * sin_row[None]).reshape(total, span)
    sin_all = (sin_far[:, None] * cos_row[None] + cos_far[:, None] * sin_row[None]).reshape(total, span)

    def exchange(value):
        return lax.all_to_all(value, "seq", 0, 0, tiled=True)

    def doubled(share, axis, bit):
        other = swap_bit(share, axis, bit)
        mine = own_bit(axis, bit) == 0
        pair = jnp.stack([jnp.where(mine, share, other), jnp.where(mine, other, share)], axis=1)
        return pair.reshape((-1,) + share.shape[1:])

    high_bits, low_bit = axis_bits("seq")[:-1], axis_bits("seq")[-1]
    down_share, up_share = down_shard[None], up_shard[None]
    for axis, bit in high_bits:
        down_share, up_share = doubled(down_share, axis, bit), doubled(up_share, axis, bit)
    full_qkv = after(full_qkv, down_share, up_share)
    up_pair = (up_share, swap_bit(up_share, "clip", 2))
    down_share = doubled(down_share, *low_bit)

    normed, qkv, mixes, fulls, logs, sents = [], [], [], [], [], []
    for c in range(clips):
        weight = full_qkv if c == 0 else after(full_qkv, down_share, up_pair[1])
        sent, normed_c = project(tokens, c, mods_one[c], weight, bias_qkv, cos_local, sin_local, seq_devices)
        normed.append(normed_c)
        if qkv:
            sent = after(sent, qkv[-1])
        qkv.append(exchange(sent))
    backs = []
    for c in range(clips):
        mix, full, log = attend(qkv[c].reshape(total, 3 * span), span)
        mixes.append(mix)
        fulls.append(full)
        logs.append(log)
        backs.append(exchange(after(mix.reshape(seq_devices, rows, span), qkv[-1] if c == 0 else backs[-1])))

    mod_rest, bias_rest = modulate(
        slice(2 * width, 6 * width), (out_bias, up_bias, down_bias), (None, None, normed[-1], mixes[0], mixes[-1])
    )
    mods_two = blocks(mod_rest)
    bias_out = bias_rest[:, :width]
    bias_up = bias_rest[:, width : 5 * width].reshape(owners).transpose(0, 2, 1, 3).reshape(1, -1)
    bias_down = bias_rest[:, 5 * width :]
    def from_clips(pair):
        near, across = [p.reshape((seq_devices // 2, 2) + p.shape[1:]) for p in pair]
        far = swap_bit(after(across, qkv[-1]), "clip", 1)
        return (near, across, swap_bit(near, "clip", 1), far)

    down_shares = from_clips((down_share, swap_bit(down_share, "clip", 2)))
    up_shares = from_clips([doubled(p, *low_bit) for p in up_pair])

    results = []
    d_mixed = []
    for c in range(clips):
        back = after(backs[c], mixes[-1])
        outputs = results[-1][0] if results else None
        results.append(middle(back, tokens, cotangent, c, mods_two[c], up_shares, down_shares, (bias_out, bias_up, bias_down), outputs))
        d_mixed.append(exchange(after(results[c][8], backs[-1] if c == 0 else d_mixed[-1])))

    def late(place):
        return [r[place] for r in results]

    mixed_all, normed_two, active, d_hidden, d_mlp, d_attn = [late(place) for place in (2, 3, 4, 5, 6, 7)]
    def line_sums(sums):
        return sums.transpose(1, 0, 2).reshape(frames, -1)

    def with_bias(lines_now, vectors):
        return jnp.concatenate([jnp.concatenate(lines_now, axis=0), jnp.concatenate(vectors).reshape(lines, -1)], axis=1)

    bias_up_sum = sum(r[10][0] for r in results).reshape(near_owners).transpose(0, 2, 1, 3).reshape(-1)
    bias_pair = sum(r[11] for r in results)
    early = with_bias([line_sums(r[9]) for r in results], [bias_pair[0], bias_up_sum, bias_pair[1]])
    early_rows = lax.all_gather(early, BOTH, axis=0, tiled=True)

    d_qkv, exchanged = [], []
    for c in range(clips):
        if c == clips - 1:
            active = gate(active, *d_qkv, d_mixed[-1])
            down_pairs, up_pairs = [(active, d_mlp)], [(normed_two, d_hidden), (mixed_all, d_attn)]
            down_first = along_first(down_pairs)
            down_core = swap_bit(down_first, "clip", 1)
            up_pairs[0] = (gate(normed_two, down_first), d_hidden)
            up_first = across_first(up_pairs)
            up_core = swap_bit(up_first, "clip", 1)
            down_pairs = [(active, gate(d_mlp, up_first))]
            down_second = along_second(down_pairs, down_core)
            down_along = swap_bit(down_second, "seq", 1)
            up_pairs[0] = (normed_two, gate(d_hidden, down_second))
            up_second = across_second(up_pairs, up_core)
            up_across = swap_bit(up_second, "clip", 2)
        grad = after(d_mixed[c], results[-1][8] if c == 0 else up_second)
        grad = grad.reshape(total, span)
        d_qkv.append(attend_back(qkv[c].reshape(total, 3 * span), grad, fulls[c], logs[c], cos_all, sin_all, span))
        sent = d_qkv[c].reshape(seq_devices, rows, 3 * span)
        exchanged.append(exchange(after(sent, d_mixed[-1]) if c == 0 else after(sent, down_along, up_across)))

    down_pairs = [(active, gate(d_mlp, exchanged[0]))]
    down_third = along_third(down_pairs, down_core, down_along)
    down_across = swap_bit(down_third, "clip", 2)
    exchanged[0] = after(exchanged[0], down_third)

    last = []
    for c in range(clips):
        grads = last[-1][0] if last else None
        if c == clips - 1:
            up_pairs[0] = (normed_two, gate(d_hidden, last[0][1]))
            up_total = across_own(up_pairs, up_core, up_across)
            down_pairs = [(active, gate(d_mlp, up_total))]
            down_total = along_own(down_pairs, down_core, down_along, down_across)
            exchanged[-1] = after(exchanged[-1], down_total)
        last.append(project_back(exchanged[c], full_qkv, tokens, c, mods_one[c][1], results[c][1], grads))
    d_projected = [r[1] for r in last]
    qkv_pairs = [(normed, d_projected)]
    qkv_core = swap_bit(across_first(qkv_pairs), "clip", 1)
    qkv_second = across_second(qkv_pairs, qkv_core)
    qkv_across = swap_bit(qkv_second, "clip", 2)
    qkv_total = across_own(qkv_pairs, qkv_core, qkv_across)
    grad_up, grad_down = along_seq(up_total, qkv_second), along_high(down_total, qkv_second)
    grad_qkv = along_seq(qkv_total)
    grad_out = grad_up[:, 4 * width :]
    grad_up = grad_up[:, : 4 * width].reshape((-1,) + near_owners).transpose(0, 1, 3, 2, 4).reshape(-1, 4 * width)
    late_rows = with_bias([line_sums(r[2]) for r in last], [sum(r[3][0] for r in last)])
    late_rows = collect_rows(after(late_rows, qkv_total), order)
    early_rows = after(early_rows, qkv_total)

    def own_columns(sums, shard):
        return lax.dynamic_slice_in_dim(sums, here * shard.shape[0], shard.shape[0], 0)

    def spans(all_rows, columns):
        vectors = jnp.sum(all_rows[:, columns:].reshape(devices, -1), axis=0)
        return all_rows[:, :columns], vectors

    late_mod, late_vectors = spans(late_rows, 2 * width)
    early_mod, early_vectors = spans(early_rows, 4 * width)
    grad_mod = jnp.concatenate(
        [
            lax.dot_general(rows_cond.astype(f32), r, TN, precision=highest, preferred_element_type=f32)
            for rows_cond, r in ((cond_late, late_mod), (cond, early_mod))
        ],
        axis=1,
    )
    mod_sum = jnp.concatenate([jnp.sum(late_mod, axis=0), jnp.sum(early_mod, axis=0)])
    return (
        results[-1][0],
        last[-1][0],
        grad_mod,
        own_columns(mod_sum, mod_bias),
        grad_qkv,
        own_columns(late_vectors, qkv_bias),
        grad_out,
        own_columns(early_vectors[:width], out_bias),
        grad_up,
        own_columns(early_vectors[width : 5 * width], up_bias),
        grad_down,
        own_columns(early_vectors[5 * width :], down_bias),
    )


def body_gathered(
    tokens,
    ctx_count,
    noise_level,
    mod_weight,
    mod_bias,
    qkv_weight,
    qkv_bias,
    out_weight,
    out_bias,
    up_weight,
    up_bias,
    down_weight,
    down_bias,
    cotangent,
):
    clips, rows, width = tokens.shape
    seq_devices = lax.axis_size("seq")
    devices = lax.axis_size("clip") * seq_devices
    bits = mesh_bits()
    here = lax.axis_index("clip") * seq_devices + lax.axis_index("seq")
    total = rows * seq_devices
    frames = max(1, rows // PATCHES)
    patch_rows = rows // frames

    full_qkv = lax.all_gather(qkv_weight, BOTH, axis=0, tiled=True)
    full_out = lax.all_gather(out_weight, BOTH, axis=0, tiled=True)
    full_up = lax.all_gather(up_weight, BOTH, axis=0, tiled=True)
    full_down = lax.all_gather(down_weight, BOTH, axis=0, tiled=True)
    biases = (qkv_bias, out_bias, up_bias, down_bias)
    bias_rows = double_rows(jnp.concatenate(biases).astype(f32), bits)
    full_biases = []
    first = 0
    for piece in biases:
        full_biases.append(bias_rows[:, first : first + piece.shape[0]].reshape(1, -1))
        first += piece.shape[0]
    bias_qkv, bias_out, bias_up, bias_down = full_biases

    levels = level_rows(ctx_count, noise_level, rows)
    cond = condition(levels, here, mod_weight.shape[0], width)
    mod_width = mod_weight.shape[1]
    partial = dot(cond, mod_weight) + own_place(mod_bias, here)
    modulation = halve_sum(partial.reshape(devices, clips * frames, mod_width), bits)
    modulation = modulation.reshape(clips, frames, 1, mod_width)

    positions = lax.axis_index("seq") * rows + jnp.arange(rows, dtype=jnp.int32)
    cosine, sine = rotary_lanes(positions, HEAD_DIM)
    key_frame = jnp.arange(total, dtype=jnp.int32) // PATCHES
    allowed = key_frame[None, :] <= (positions // PATCHES)[:, None]

    def flat(value):
        return value.reshape(rows, value.shape[-1])

    def split(value):
        return value.reshape(frames, patch_rows, value.shape[-1])

    def to_heads(value):
        return value.reshape(rows, HEADS, HEAD_DIM).transpose(1, 0, 2)

    saved = []
    for c in range(clips):
        mods = jnp.split(modulation[c], 6, axis=-1)
        tokens_now = split(tokens[c].astype(f32))
        unit, inverse = norm_parts(tokens_now)
        normed = flat((unit * (1.0 + mods[1]) + mods[0]).astype(bf16))
        projected = dot(normed, full_qkv) + bias_qkv
        views = []
        for place in range(3):
            view = to_heads(projected[:, place * width : (place + 1) * width])
            if place < 2:
                    view = view * cosine + jnp.roll(view, HEAD_DIM // 2, -1) * sine
            views.append(view.astype(bf16))
        queries, keys, values = views
        keys = lax.all_gather(keys, "seq", axis=1, tiled=True)
        values = lax.all_gather(values, "seq", axis=1, tiled=True)
        mix, logs = gathered_forward(queries, keys, values, allowed)
        mixed = mix.transpose(1, 0, 2).reshape(rows, width).astype(bf16)
        kept = (queries, keys, values, logs)
        saved.append((mods, tokens_now, unit, inverse, normed, kept, mixed))

    outputs = []
    middle = []
    for c in range(clips):
        mods, tokens_now, unit, inverse, normed, kept, mixed = saved[c]
        _, _, gate_one, shift_two, scale_two, gate_two = mods
        attn_out = split(dot(mixed, full_out) + bias_out)
        resid = tokens_now + gate_one * attn_out
        unit_two, inverse_two = norm_parts(resid)
        normed_two = flat((unit_two * (1.0 + scale_two) + shift_two).astype(bf16))
        hidden = dot(normed_two, full_up) + bias_up
        active_full, gelu_back = jax.vjp(jax.nn.gelu, hidden)
        active = active_full.astype(bf16)
        mlp_out = split(dot(active, full_down) + bias_down)
        outputs.append(flat((resid + gate_two * mlp_out).astype(bf16)))
        grad_out = split(cotangent[c].astype(f32))
        d_mlp = flat((gate_two * grad_out).astype(bf16))
        d_hidden = gelu_back(dot(d_mlp, full_down, NT))[0].astype(bf16)
        d_normed_two = split(dot(d_hidden, full_up, NT))
        d_resid = grad_out + norm_back(unit_two, inverse_two, d_normed_two, scale_two)
        d_attn = flat((gate_one * d_resid).astype(bf16))
        d_mixed = dot(d_attn, full_out, NT).astype(bf16)
        d_early = jnp.concatenate(
            [
                jnp.sum(d_resid * attn_out, axis=1),
                jnp.sum(d_normed_two, axis=1),
                jnp.sum(d_normed_two * unit_two, axis=1),
                jnp.sum(grad_out * mlp_out, axis=1),
            ],
            axis=-1,
        )
        middle.append((mixed, d_attn, normed_two, d_hidden, active, d_mlp, d_resid, d_mixed, d_early))

    def both(place):
        return jnp.concatenate([m[place] for m in middle], axis=0)

    d_attn_all, d_hidden_all, d_mlp_all = both(1), both(3), both(5)
    grad_down = weight_grad(both(4), d_mlp_all)
    grad_up = weight_grad(both(2), d_hidden_all)
    grad_out_weight = weight_grad(both(0), d_attn_all)
    early_rows = lax.all_gather(both(8), BOTH, axis=0, tiled=True)

    inputs_grad = []
    late = []
    projected_grads = []
    for c in range(clips):
        mods, tokens_now, unit, inverse, normed, kept, mixed = saved[c]
        d_resid, d_mixed = middle[c][6], middle[c][7]
        queries, keys, values, logs = kept
        dq, dk, dv = gathered_back(queries, keys, values, to_heads(d_mixed), logs, allowed)
        dk = lax.psum_scatter(dk.astype(bf16), "seq", scatter_dimension=1, tiled=True).astype(f32)
        dv = lax.psum_scatter(dv.astype(bf16), "seq", scatter_dimension=1, tiled=True).astype(f32)
        views = [g * cosine - jnp.roll(g, HEAD_DIM // 2, -1) * sine for g in (dq, dk)] + [dv]
        d_projected = jnp.concatenate([g.transpose(1, 0, 2).reshape(rows, width) for g in views], axis=1).astype(bf16)
        projected_grads.append(d_projected)
        d_normed = split(dot(d_projected, full_qkv, NT))
        inputs_grad.append(flat(d_resid + norm_back(unit, inverse, d_normed, mods[1])))
        late.append(jnp.concatenate([jnp.sum(d_normed, axis=1), jnp.sum(d_normed * unit, axis=1)], axis=-1))

    d_projected_all = jnp.concatenate(projected_grads, axis=0)
    grad_qkv = weight_grad(jnp.concatenate([s[4] for s in saved], axis=0), d_projected_all)
    bias_grads = [
        jnp.sum(g.astype(f32), axis=0).reshape(devices, -1) for g in (d_projected_all, d_attn_all, d_hidden_all, d_mlp_all)
    ]
    bias_sum = halve_sum(jnp.concatenate(bias_grads, axis=1), bits)
    grad_biases = []
    first = 0
    for piece in bias_grads:
        grad_biases.append(bias_sum[first : first + piece.shape[1]])
        first += piece.shape[1]

    late_rows = double_rows(jnp.concatenate(late, axis=0), bits).reshape(-1, 2 * width)
    grad_mod = jnp.concatenate(
        [
            lax.dot_general(cond.astype(f32), r, TN, precision=highest, preferred_element_type=f32)
            for r in (late_rows, early_rows)
        ],
        axis=1,
    )
    mod_sum = jnp.concatenate([jnp.sum(late_rows, axis=0), jnp.sum(early_rows, axis=0)])
    grad_mod_bias = lax.dynamic_slice_in_dim(mod_sum, here * mod_bias.shape[0], mod_bias.shape[0], 0)
    return (
        jnp.stack(outputs),
        jnp.stack(inputs_grad),
        grad_mod,
        grad_mod_bias,
        grad_qkv,
        grad_biases[0],
        grad_out_weight,
        grad_biases[1],
        grad_up,
        grad_biases[2],
        grad_down,
        grad_biases[3],
    )


def solution(mesh):
    by_heads = HEADS % mesh.shape["seq"] == 0
    body = body_by_heads if by_heads else body_gathered
    token_place = P("clip", "seq", None)
    matrix, vector = P(BOTH, None), P(BOTH)
    weights = (matrix, vector) * 5
    return jax.shard_map(
        body,
        mesh=mesh,
        in_specs=(token_place, P("clip"), P("clip", None)) + weights + (token_place,),
        out_specs=(token_place, token_place) + weights,
        check_vma=False,
    )
```

```python
import functools
import math

import jax
import jax.numpy as jnp
from jax import lax
from jax.experimental import pallas as pl
from jax.experimental.pallas import tpu as pltpu
from jax.sharding import PartitionSpec as P

HEADS = 16
HEAD_DIM = 64
FRAMES = 16
PATCHES = 256
BOTH = ("clip", "seq")
NT = (((1,), (1,)), ((), ()))
NN = (((1,), (0,)), ((), ()))
TN = (((0,), (0,)), ((), ()))
bf16 = jnp.bfloat16
f32 = jnp.float32
highest = lax.Precision.HIGHEST


def dot(left, right, dims=NN):
    return lax.dot_general(left, right, dims, preferred_element_type=f32)


def swap_bit(value, axis, bit):
    count = lax.axis_size(axis)
    return lax.ppermute(value, axis, [(i, i ^ bit) for i in range(count)])


def own_bit(axis, bit):
    return lax.shift_right_logical(lax.axis_index(axis), bit.bit_length() - 1) & 1


def axis_bits(axis):
    bits = []
    bit = 1
    while bit < lax.axis_size(axis):
        bits.append((axis, bit))
        bit *= 2
    return bits[::-1]


def exchange_order(bits):
    return sorted(range(len(bits)), key=lambda place: bits[place])


def mesh_bits():
    return axis_bits("clip") + axis_bits("seq")


def halve_sum(parts, bits, wire=f32, hold=None):
    addends = [parts.reshape((2,) * len(bits) + parts.shape[1:])]
    for place in exchange_order(bits):
        axis, bit = bits[place]
        mine = own_bit(axis, bit)
        send = sum(lax.dynamic_index_in_dim(a, 1 - mine, place).astype(f32) for a in addends)
        addends = [lax.dynamic_index_in_dim(a, mine, place) for a in addends]
        received = swap_bit(send.astype(wire), axis, bit)
        if hold is not None and len(addends) == 1:
            received = after(received, hold)
        addends.append(received)
    total = sum(a.astype(f32) for a in addends)
    return total.reshape(total.shape[len(bits) :])


def near_order():
    return axis_bits("clip")[::-1] + axis_bits("seq")[::-1]


def halve_rows(parts, bits, gates=()):
    for place, (axis, bit) in enumerate(bits):
        half = parts.shape[0] // 2
        mine = own_bit(axis, bit)
        keep = lax.dynamic_slice_in_dim(parts, mine * half, half, 0)
        send = lax.dynamic_slice_in_dim(parts, (1 - mine) * half, half, 0)
        other = swap_bit(send, axis, bit)
        if place < len(gates) and gates[place] is not None:
            other = after(other, gates[place])
        parts = keep + other
    return parts


def collect_rows(rows, bits):
    for axis, bit in reversed(bits):
        rows = jnp.concatenate([rows, swap_bit(rows, axis, bit)], axis=0)
    return rows


def relative_rows(rows, bits):
    shape = rows.shape
    rows = rows.reshape((2,) * len(bits) + (-1,) + shape[1:])
    for place, (axis, bit) in enumerate(bits):
        rows = jnp.where(own_bit(axis, bit) == 0, rows, jnp.flip(rows, place))
    return rows.reshape(shape)


def after(value, *others):
    return lax.optimization_barrier((value,) + others)[0]


def double_rows(row, bits):
    rows = row[None]
    for axis, bit in reversed(bits):
        other = swap_bit(rows, axis, bit)
        low = own_bit(axis, bit) == 0
        rows = jnp.concatenate([jnp.where(low, rows, other), jnp.where(low, other, rows)], axis=0)
    return rows


def weight_grad(left, right):
    tokens, rows = left.shape
    quarter = rows // lax.axis_size("clip")
    mine = lax.axis_index("clip")

    def part(flip):
        piece = lax.dynamic_slice_in_dim(left, (mine ^ flip) * quarter, quarter, 1)
        return dot(piece, right, TN)

    far = swap_bit(part(3).astype(bf16), "clip", 1)
    near = swap_bit(part(1).astype(bf16), "clip", 1)
    across = swap_bit((part(2) + far.astype(f32)).astype(bf16), "clip", 2)
    total = part(0) + near.astype(f32) + across.astype(f32)
    return halve_sum(total.reshape((lax.axis_size("seq"), -1, right.shape[1])), axis_bits("seq"), bf16)


def norm_parts(values):
    centre = values - jnp.mean(values, axis=-1, keepdims=True)
    spread = jnp.mean(centre * centre, axis=-1, keepdims=True)
    inverse = lax.rsqrt(spread + 1e-06)
    return centre * inverse, inverse


def norm_back(unit, inverse, grad, scales):
    scaled = grad * (1.0 + scales)
    mean = jnp.mean(scaled, axis=-1, keepdims=True)
    along = jnp.mean(scaled * unit, axis=-1, keepdims=True)
    return inverse * (scaled - mean - unit * along)


def rotary_lanes(positions, width):
    half = HEAD_DIM // 2
    lane = jnp.arange(width, dtype=jnp.int32) % HEAD_DIM
    freqs = jnp.exp(-math.log(10000.0) * 2.0 * (lane % half).astype(f32) / HEAD_DIM)
    angles = positions.astype(f32)[:, None] * freqs[None, :]
    sign = jnp.where(lane < half, -1.0, 1.0).astype(f32)
    return jnp.cos(angles), jnp.sin(angles) * sign[None, :]


def partner(values):
    width = values.shape[1]
    half = HEAD_DIM // 2
    lane = lax.broadcasted_iota(jnp.int32, (1, width), 1) % HEAD_DIM
    return jnp.where(lane < half, pltpu.roll(values, width - half, 1), pltpu.roll(values, half, 1))


def project_kernel(
    token_ref, mod_ref, wq_ref, wk_ref, wv_ref, bq_ref, bk_ref, bv_ref, cos_ref, sin_ref, out_ref, normed_ref, *, span
):
    frames = mod_ref.shape[1]
    patch = token_ref.shape[0] // frames

    @pl.when(pl.program_id(0) == 0)
    def _():
        for f in range(frames):
            rows = slice(f * patch, (f + 1) * patch)
            unit, _ = norm_parts(token_ref[rows, :].astype(f32))
            normed_ref[rows, :] = (unit * (1.0 + mod_ref[1, f : f + 1, :]) + mod_ref[0, f : f + 1, :]).astype(bf16)

    x = normed_ref[...]
    cosine, sine = cos_ref[...], sin_ref[...]
    groups = wq_ref.shape[1] // span
    for place, (w_ref, b_ref) in enumerate(((wq_ref, bq_ref), (wk_ref, bk_ref), (wv_ref, bv_ref))):
        value = dot(x, w_ref[...]) + b_ref[...]
        if place < 2:
            value = value * cosine + partner(value) * sine
        value = value.astype(bf16)
        for g in range(groups):
            out_ref[g, :, place * span : (place + 1) * span] = value[:, g * span : (g + 1) * span]


def whole_block(shape):
    return pl.BlockSpec(shape, lambda j: (0,) * len(shape))


def column_specs(height, block, steps):
    return [pl.BlockSpec((height, block), functools.partial(lambda p, j: (0, p * steps + j), p)) for p in range(3)]


def clip_block(shape, c):
    return pl.BlockSpec((None,) + shape[1:], lambda j: (c,) + (0,) * (len(shape) - 1))


def project(tokens, c, mods, weight, bias, cosine, sine, groups):
    _, rows, width = tokens.shape
    span = width // groups
    block = max(span, 256)
    per_step = block // span
    steps = groups // per_step
    return pl.pallas_call(
        functools.partial(project_kernel, span=span),
        grid=(steps,),
        in_specs=[clip_block(tokens.shape, c), whole_block(mods.shape)]
        + column_specs(width, block, steps)
        + column_specs(1, block, steps)
        + [whole_block((rows, block))] * 2,
        out_specs=(pl.BlockSpec((per_step, rows, 3 * span), lambda j: (j, 0, 0)), whole_block((rows, width))),
        out_shape=(
            jax.ShapeDtypeStruct((groups, rows, 3 * span), bf16),
            jax.ShapeDtypeStruct((rows, width), bf16),
        ),
        compiler_params=pltpu.CompilerParams(vmem_limit_bytes=32 << 20),
        cost_estimate=pl.CostEstimate(
            flops=6 * rows * width * width, bytes_accessed=6 * width * width + 10 * rows * width, transcendentals=0
        ),
        name="project",
    )(tokens, mods, weight, weight, weight, bias, bias, bias, cosine, sine)


def project_back_kernel(
    back_ref, wq_ref, wk_ref, wv_ref, token_ref, scale_ref, resid_ref, *rest, span
):
    grad_ref, proj_ref, sums_ref, bias_ref, acc_ref = rest[-5:]
    frames = scale_ref.shape[0]
    rows_all, width = token_ref.shape
    patch = rows_all // frames
    step = pl.program_id(0)
    block = wq_ref.shape[1]

    @pl.when(step == 0)
    def _():
        acc_ref[...] = jnp.zeros_like(acc_ref)

    for place, w_ref in enumerate((wq_ref, wk_ref, wv_ref)):
        band = slice(place * span, (place + 1) * span)
        piece = jnp.concatenate([back_ref[g, :, band] for g in range(block // span)], axis=1)
        columns = pl.ds(pl.multiple_of(place * width + step * block, block), block)
        proj_ref[:, columns] = piece
        bias_ref[:, columns] = jnp.sum(piece.astype(f32), axis=0, keepdims=True)
        acc_ref[...] += dot(piece, w_ref[...], NT)

    @pl.when(step == pl.num_programs(0) - 1)
    def _():
        for f in range(frames):
            rows = slice(f * patch, (f + 1) * patch)
            unit, inverse = norm_parts(token_ref[rows, :].astype(f32))
            grad = acc_ref[rows, :]
            grad_ref[rows, :] = resid_ref[rows, :] + norm_back(unit, inverse, grad, scale_ref[f : f + 1, :])
            sums_ref[0, f : f + 1, :] = jnp.sum(grad, axis=0, keepdims=True)
            sums_ref[1, f : f + 1, :] = jnp.sum(grad * unit, axis=0, keepdims=True)


def project_back(back, weight, tokens, c, scales, d_resid, grads):
    groups, rows, _ = back.shape
    width = tokens.shape[2]
    span = width // groups
    block = max(span, 256)
    per_step = block // span
    steps = groups // per_step
    earlier = [] if grads is None else [grads]
    return pl.pallas_call(
        functools.partial(project_back_kernel, span=span),
        grid=(steps,),
        in_specs=[pl.BlockSpec((per_step, rows, 3 * span), lambda j: (j, 0, 0))]
        + column_specs(width, block, steps)
        + [clip_block(tokens.shape, c), whole_block(scales.shape), whole_block((rows, width))]
        + [pl.BlockSpec(memory_space=pl.ANY)] * len(earlier),
        out_specs=(
            clip_block(tokens.shape, c),
            whole_block((rows, 3 * width)),
            whole_block((2,) + scales.shape),
            whole_block((1, 3 * width)),
        ),
        out_shape=(
            jax.ShapeDtypeStruct(tokens.shape, f32),
            jax.ShapeDtypeStruct((rows, 3 * width), bf16),
            jax.ShapeDtypeStruct((2,) + scales.shape, f32),
            jax.ShapeDtypeStruct((1, 3 * width), f32),
        ),
        input_output_aliases={7: 0} if earlier else {},
        scratch_shapes=[pltpu.VMEM((rows, width), f32)],
        compiler_params=pltpu.CompilerParams(vmem_limit_bytes=40 << 20),
        cost_estimate=pl.CostEstimate(
            flops=6 * rows * width * width, bytes_accessed=6 * width * width + 22 * rows * width, transcendentals=0
        ),
        name="project_back",
    )(back, weight, weight, weight, tokens, scales, d_resid, *earlier)


GELU_RATE = math.sqrt(2.0 / math.pi)
GELU_CUBE = 0.044715


def middle_kernel(clip_ref, back_ref, token_ref, cot_ref, mod_ref, bo_ref, bup_ref, bdown_ref, *refs):
    wo_refs, up_refs, down_refs = refs[0:4], refs[4:8], refs[8:12]
    (
        out_ref,
        dres_ref,
        mixed_ref,
        normed_ref,
        act_ref,
        dhid_ref,
        dmlp_ref,
        dattn_ref,
        dmix_ref,
        sums_ref,
        bup_sum_ref,
        bsum_ref,
        attn_ref,
        res_ref,
        mlp_ref,
        dn_ref,
        wo_ref,
        up_ref,
        down_ref,
    ) = refs[-19:]
    groups, rows_all, span = back_ref.shape
    width = token_ref.shape[1]
    quarter = width // 4
    frames = mod_ref.shape[1]
    patch = rows_all // frames
    step = pl.program_id(0)
    mine = clip_ref[0]

    def owner_rows(place):
        return pl.ds(pl.multiple_of((mine ^ FLIPS[place]) * quarter, quarter), quarter)

    @pl.when(step == 0)
    def _():
        for place in range(4):
            wo_ref[owner_rows(place), :] = wo_refs[place][...].reshape(quarter, width)
        for g in range(groups):
            mixed_ref[:, g * span : (g + 1) * span] = back_ref[g]
        attn_ref[...] = dot(mixed_ref[...], wo_ref[...]) + bo_ref[...]
        for f in range(frames):
            rows = slice(f * patch, (f + 1) * patch)
            resid = token_ref[rows, :].astype(f32) + mod_ref[0, f : f + 1, :] * attn_ref[rows, :]
            res_ref[rows, :] = resid
            unit, _ = norm_parts(resid)
            normed_ref[rows, :] = (unit * (1.0 + mod_ref[2, f : f + 1, :]) + mod_ref[1, f : f + 1, :]).astype(bf16)
            dmlp_ref[rows, :] = (mod_ref[3, f : f + 1, :] * cot_ref[rows, :].astype(f32)).astype(bf16)
        mlp_ref[...] = jnp.zeros_like(mlp_ref)
        dn_ref[...] = jnp.zeros_like(dn_ref)

    for place in range(4):
        up_ref[owner_rows(place), :] = up_refs[place][...].reshape(quarter, -1)

        @pl.when(step // 2 == place)
        def _(place=place):
            down_ref[...] = down_refs[place][...].reshape(-1, width)

    up = up_ref[...]
    down = down_ref[...]
    hidden = dot(normed_ref[...], up) + bup_ref[...]
    square = hidden * hidden
    bend = jnp.tanh(GELU_RATE * (hidden + GELU_CUBE * (square * hidden)))
    share = 0.5 * (1.0 + bend)
    active = (hidden * share).astype(bf16)
    act_ref[...] = active
    mlp_ref[...] += dot(active, down)
    slope = share + 0.5 * hidden * (1.0 - bend * bend) * (GELU_RATE + (3.0 * GELU_RATE * GELU_CUBE) * square)
    d_hidden = (dot(dmlp_ref[...], down, NT) * slope).astype(bf16)
    dhid_ref[...] = d_hidden
    bup_sum_ref[...] = jnp.sum(d_hidden.astype(f32), axis=0, keepdims=True)
    dn_ref[...] += dot(d_hidden, up, NT)

    @pl.when(step == pl.num_programs(0) - 1)
    def _():
        bsum = None
        for f in range(frames):
            rows = slice(f * patch, (f + 1) * patch)
            resid = res_ref[rows, :]
            mlp = mlp_ref[rows, :] + bdown_ref[...]
            out_ref[rows, :] = (resid + mod_ref[3, f : f + 1, :] * mlp).astype(bf16)
            cot = cot_ref[rows, :].astype(f32)
            sums_ref[3, f : f + 1, :] = jnp.sum(cot * mlp, axis=0, keepdims=True)
            unit, inverse = norm_parts(resid)
            grad = dn_ref[rows, :]
            sums_ref[1, f : f + 1, :] = jnp.sum(grad, axis=0, keepdims=True)
            sums_ref[2, f : f + 1, :] = jnp.sum(grad * unit, axis=0, keepdims=True)
            d_resid = cot + norm_back(unit, inverse, grad, mod_ref[2, f : f + 1, :])
            dres_ref[rows, :] = d_resid
            sums_ref[0, f : f + 1, :] = jnp.sum(d_resid * attn_ref[rows, :], axis=0, keepdims=True)
            d_attn = (mod_ref[0, f : f + 1, :] * d_resid).astype(bf16)
            dattn_ref[rows, :] = d_attn
            term = jnp.concatenate(
                [
                    jnp.sum(d_attn.astype(f32), axis=0, keepdims=True),
                    jnp.sum(dmlp_ref[rows, :].astype(f32), axis=0, keepdims=True),
                ],
                axis=0,
            )
            bsum = term if bsum is None else bsum + term
        bsum_ref[...] = bsum
        d_mixed = dot(dattn_ref[...], wo_ref[...], NT).astype(bf16)
        for g in range(groups):
            dmix_ref[g] = d_mixed[:, g * span : (g + 1) * span]


FLIPS = (0, 2, 1, 3)


def middle(back, tokens, cot, c, mods, up_shares, down_shares, biases, outputs):
    groups, rows, span = back.shape
    _, _, width = tokens.shape
    high, low, _, piece, _ = up_shares[0].shape
    hidden = 4 * width
    steps = 8
    block = hidden // steps
    bias_out, bias_up, bias_down = biases
    mine = lax.axis_index("clip").astype(jnp.int32)[None]
    earlier = [] if outputs is None else [outputs]

    def fixed(shape, **options):
        return pl.BlockSpec(shape, lambda j, q: (0,) * len(shape), **options)

    def clip_part(shape):
        return pl.BlockSpec((None,) + shape[1:], lambda j, q: (c,) + (0,) * (len(shape) - 1))

    def unit_block(j, q):
        owner = q[0] ^ jnp.where(j // 2 == 1, 2, jnp.where(j // 2 == 2, 1, j // 2))
        return owner, j % 2

    def up_index(j, q):
        owner, half = unit_block(j, q)
        return (0, 0, owner, 0, half)

    def hidden_index(j, q):
        owner, half = unit_block(j, q)
        return (0, owner * 2 + half)

    def down_index(place, j, q):
        return (0, jnp.clip(j - 2 * place, 0, 1), 0, 0, 0)

    token_block = fixed((rows, width))
    hidden_block = pl.BlockSpec((rows, block), hidden_index)
    out_spec = [
        pl.BlockSpec((high, low, 1, piece, width), lambda j, q: (0, 0, 4, 0, 0), pipeline_mode=pl.Buffered(1)) for _ in range(4)
    ]
    up_spec = [pl.BlockSpec((high, low, 1, piece, block), up_index) for _ in range(4)]
    down_spec = [
        pl.BlockSpec((high, 1, 4, piece, width), functools.partial(down_index, place)) for place in range(4)
    ]
    return pl.pallas_call(
        middle_kernel,
        grid_spec=pltpu.PrefetchScalarGridSpec(
            num_scalar_prefetch=1,
            grid=(steps,),
            in_specs=[
                fixed(back.shape),
                clip_part(tokens.shape),
                clip_part(tokens.shape),
                fixed(mods.shape),
                fixed((1, width)),
                pl.BlockSpec((1, block), hidden_index),
                fixed((1, width)),
            ]
            + out_spec
            + up_spec
            + down_spec
            + [pl.BlockSpec(memory_space=pl.ANY)] * len(earlier),
            out_specs=(
                clip_part(tokens.shape),
                token_block,
                token_block,
                token_block,
                hidden_block,
                hidden_block,
                token_block,
                token_block,
                fixed(back.shape),
                fixed(mods.shape),
                pl.BlockSpec((1, block), hidden_index),
                fixed((2, width)),
            ),
            scratch_shapes=[pltpu.VMEM((rows, width), f32)] * 4
            + [pltpu.VMEM((width, width), bf16), pltpu.VMEM((width, block), bf16), pltpu.VMEM((block, width), bf16)],
        ),
        out_shape=(
            jax.ShapeDtypeStruct(tokens.shape, bf16),
            jax.ShapeDtypeStruct((rows, width), f32),
            jax.ShapeDtypeStruct((rows, width), bf16),
            jax.ShapeDtypeStruct((rows, width), bf16),
            jax.ShapeDtypeStruct((rows, hidden), bf16),
            jax.ShapeDtypeStruct((rows, hidden), bf16),
            jax.ShapeDtypeStruct((rows, width), bf16),
            jax.ShapeDtypeStruct((rows, width), bf16),
            jax.ShapeDtypeStruct(back.shape, bf16),
            jax.ShapeDtypeStruct(mods.shape, f32),
            jax.ShapeDtypeStruct((1, hidden), f32),
            jax.ShapeDtypeStruct((2, width), f32),
        ),
        input_output_aliases={20: 0} if earlier else {},
        compiler_params=pltpu.CompilerParams(vmem_limit_bytes=60 << 20),
        cost_estimate=pl.CostEstimate(
            flops=4 * rows * width * width, bytes_accessed=2 * width * width + 5 * rows * width, transcendentals=rows * width
        ),
        name="middle",
    )(mine, back, tokens, cot, mods, bias_out, bias_up, bias_down, *up_shares, *up_shares, *down_shares, *earlier)


def near_place(place, count):
    bits = count.bit_length() - 1
    return sum(((place >> b) & 1) << (bits - 1 - b) for b in range(bits))


def weight_grad_kernel(index_ref, *refs, clips, counts, widths, owners, swapped):
    send_ref, keep_ref, flat_ref = refs[-3:]
    step = pl.program_id(0)
    first, taken = 0, 0
    for count, steps in zip(counts, widths):
        left, right = refs[taken : taken + clips * count], refs[taken + clips * count : taken + clips * (count + 1)]
        taken += clips * (count + 1)
        rows, height = left[0].shape
        piece = height // owners

        @pl.when(step == first)
        def _(left=left, count=count, rows=rows, height=height, piece=piece):
            for c in range(clips):
                for i in range(count):
                    flat = jnp.transpose(left[c * count + i][...])
                    for owner in range(owners):
                        place = i * height + near_place(owner, owners) * piece
                        flat_ref[place : place + piece, c * rows : (c + 1) * rows] = flat[owner * piece : (owner + 1) * piece]

        @pl.when((step >= first) & (step < first + steps))
        def _(right=right, rows=rows):
            total = dot(flat_ref[:, 0:rows], right[0][...])
            for c in range(1, clips):
                total += dot(flat_ref[:, c * rows : (c + 1) * rows], right[c][...])
            total = total.astype(bf16)
            if swapped:

                @pl.when(step < pl.num_programs(0) // 2)
                def _():
                    send_ref[0] = total

                @pl.when(step >= pl.num_programs(0) // 2)
                def _():
                    keep_ref[0] = total

            else:
                half = total.shape[0] // 2
                for ref, part in ((send_ref, total[:half]), (keep_ref, total[half:])):
                    for i in range(ref.shape[0]):
                        ref[i] = part[i * ref.shape[1] : (i + 1) * ref.shape[1]]

        first += steps


def weight_grad_call(in_specs, operands, indices, steps, shapes, specs, width, depth, **options):
    return pl.pallas_call(
        functools.partial(weight_grad_kernel, **options),
        grid_spec=pltpu.PrefetchScalarGridSpec(
            num_scalar_prefetch=1,
            grid=(steps,),
            in_specs=in_specs,
            out_specs=specs,
            scratch_shapes=[pltpu.VMEM((width, depth), bf16)],
        ),
        out_shape=tuple(jax.ShapeDtypeStruct(shape, bf16) for shape in shapes),
        compiler_params=pltpu.CompilerParams(vmem_limit_bytes=60 << 20),
        cost_estimate=pl.CostEstimate(
            flops=1024 * steps * width * depth, bytes_accessed=steps * 1024 * (width + depth) + 4 * width * depth, transcendentals=0
        ),
        name="weight_grad",
    )(indices, *operands)


BLOCK = 512


def rows_grad(pairs):
    clips = len(pairs[0][0])
    rows, width = pairs[0][0][0].shape
    height = width // 4
    mine = mine_on("clip")
    widths = [right[0].shape[1] // BLOCK for _, right in pairs]
    in_specs, operands = [], []
    first = 0
    for (left, right), steps in zip(pairs, widths):
        for array in left:
            for i in range(4):
                in_specs.append(pl.BlockSpec((rows, height), functools.partial(lambda i, j, q: (0, q[i]), i)))
                operands.append(array)
        where = functools.partial(lambda first, steps, j, q: (0, jnp.clip(j - first, 0, steps - 1)), first, steps)
        in_specs += [pl.BlockSpec((rows, BLOCK), where)] * clips
        operands += right
        first += steps
    shape = (2, height, first * BLOCK)
    spec = pl.BlockSpec((2, height, BLOCK), lambda j, q: (0, 0, j))
    return weight_grad_call(
        in_specs,
        operands,
        jnp.stack([mine ^ 3, mine ^ 1, mine ^ 2, mine]),
        first,
        (shape, shape),
        (spec, spec),
        width,
        clips * rows,
        clips=clips,
        counts=[4] * len(pairs),
        widths=widths,
        owners=lax.axis_size("seq"),
        swapped=False,
    )


def columns_grad(left, right):
    clips = len(left)
    rows, width = right[0].shape
    mine, low = mine_on("clip"), mine_on("seq") & 1

    def block(clip_flip, low_flip):
        return (mine ^ clip_flip) * 2 + (low ^ low_flip)

    flips = ((0, 1), (2, 1), (0, 0), (2, 0))
    indices = jnp.stack([block(c ^ 1, s) for c, s in flips] + [block(c, s) for c, s in flips])
    in_specs = [pl.BlockSpec((rows, width), lambda j, q: (0, 0))] * clips
    in_specs += [pl.BlockSpec((rows, BLOCK), lambda j, q: (0, q[j]))] * clips
    shape = (4, width, BLOCK)
    return weight_grad_call(
        in_specs,
        right + left,
        indices,
        8,
        (shape, shape),
        (
            pl.BlockSpec((1, width, BLOCK), lambda j, q: (jnp.minimum(j, 3), 0, 0)),
            pl.BlockSpec((1, width, BLOCK), lambda j, q: (jnp.maximum(j - 4, 0), 0, 0)),
        ),
        width,
        clips * rows,
        clips=clips,
        counts=[1],
        widths=[8],
        owners=1,
        swapped=True,
    )


def mine_on(axis):
    return lax.axis_index(axis).astype(jnp.int32)


def rounded_sum(addends):
    return sum(a.astype(f32) for a in addends).astype(bf16)


def halve(addends, bits, dim, hold=None):
    for place, (axis, bit) in enumerate(bits):
        half = addends[0].shape[dim] // 2
        mine = own_bit(axis, bit)
        send = rounded_sum([lax.dynamic_slice_in_dim(a, (1 - mine) * half, half, dim) for a in addends])
        addends = [lax.dynamic_slice_in_dim(a, mine * half, half, dim) for a in addends]
        received = swap_bit(send, axis, bit)
        if hold is not None and place == 0:
            received = after(received, hold)
        addends.append(received)
    return sum(a.astype(f32) for a in addends)


def gate(arrays, *others):
    return list(lax.optimization_barrier((tuple(arrays), others))[0])


def height_of(pairs, parts):
    return pairs[0][0][0].shape[1] // parts


def attend_kernel(qkv_ref, mix_ref, full_ref, log_ref, vt_ref, *, total, span, block):
    heads = span // HEAD_DIM
    head = lax.broadcasted_iota(jnp.int32, (1, span), 1) // HEAD_DIM
    key_frame = lax.broadcasted_iota(jnp.int32, (block, block), 0) // PATCHES
    query_frame = lax.broadcasted_iota(jnp.int32, (block, block), 1) // PATCHES
    kept = key_frame <= query_frame

    def flip(j, carry):
        rows = pl.ds(pl.multiple_of(j * block, block), block)
        vt_ref[:, rows] = jnp.transpose(qkv_ref[rows, 2 * span : 3 * span])
        return carry

    lax.fori_loop(0, total // block, flip, 0)

    def query_block(i, carry):
        rows = pl.ds(pl.multiple_of(i * block, block), block)
        query = qkv_ref[rows, 0:span] * jnp.asarray(HEAD_DIM**-0.5, bf16)
        queries = [jnp.where(head == h, query, jnp.zeros_like(query)) for h in range(heads)]

        def step(j, state, masked):
            peaks, sums, mixes = state
            columns = pl.ds(pl.multiple_of(j * block, block), block)
            key = qkv_ref[columns, span : 2 * span]
            new = ([], [], [])
            for h in range(heads):
                scores = dot(key, queries[h], NT)
                if masked:
                    scores = jnp.where(kept, scores, -1e30)
                peak = jnp.maximum(peaks[h], jnp.max(scores, axis=0, keepdims=True))
                raised = jnp.exp(scores - peak)
                fade = jnp.exp(peaks[h] - peak)
                new[0].append(peak)
                new[1].append(fade * sums[h] + jnp.sum(raised, axis=0, keepdims=True))
                term = dot(vt_ref[h * HEAD_DIM : (h + 1) * HEAD_DIM, columns], raised.astype(bf16))
                new[2].append(mixes[h] * fade + term)
            return tuple(map(tuple, new))

        state = (
            tuple(jnp.full((1, block), -1e30, f32) for _ in range(heads)),
            tuple(jnp.zeros((1, block), f32) for _ in range(heads)),
            tuple(jnp.zeros((HEAD_DIM, block), f32) for _ in range(heads)),
        )
        state = lax.fori_loop(0, i, lambda j, s: step(j, s, False), state)
        peaks, sums, mixes = step(i, state, True)
        mixed = jnp.transpose(jnp.concatenate([mixes[h] / sums[h] for h in range(heads)], axis=0))
        full_ref[rows, :] = mixed
        mix_ref[rows, :] = mixed.astype(bf16)
        for h in range(heads):
            log_ref[h : h + 1, rows] = peaks[h] + jnp.log(sums[h])
        return carry

    lax.fori_loop(0, total // block, query_block, 0)


def attend(qkv, span):
    total = qkv.shape[0]
    heads = span // HEAD_DIM
    block = min(1024, total)
    return pl.pallas_call(
        functools.partial(attend_kernel, total=total, span=span, block=block),
        out_shape=(
            jax.ShapeDtypeStruct((total, span), bf16),
            jax.ShapeDtypeStruct((total, span), f32),
            jax.ShapeDtypeStruct((heads, total), f32),
        ),
        scratch_shapes=[pltpu.VMEM((span, total), bf16)],
        compiler_params=pltpu.CompilerParams(vmem_limit_bytes=60 << 20),
        cost_estimate=pl.CostEstimate(
            flops=8 * total * total * span, bytes_accessed=12 * total * span, transcendentals=total * total * heads // 2
        ),
        name="attend",
    )(qkv)


def attend_back_kernel(
    qkv_ref, grad_ref, full_ref, log_ref, cos_ref, sin_ref, out_ref, dq_ref, dk_ref, dv_ref, along_ref, *, total, span, block
):
    heads = span // HEAD_DIM
    scale = HEAD_DIM**-0.5
    head = lax.broadcasted_iota(jnp.int32, (1, span), 1) // HEAD_DIM
    blocks = total // block
    dq_ref[...] = jnp.zeros_like(dq_ref)

    def only(value, h):
        return jnp.where(head == h, value, jnp.zeros_like(value))

    def lead(i, carry):
        rows = pl.ds(pl.multiple_of(i * block, block), block)
        product = jnp.transpose(grad_ref[rows, :].astype(f32) * full_ref[rows, :])
        for h in range(heads):
            along_ref[h : h + 1, rows] = jnp.sum(product[h * HEAD_DIM : (h + 1) * HEAD_DIM], axis=0, keepdims=True)
        return carry

    lax.fori_loop(0, blocks, lead, 0)

    def key_block(j, carry):
        first = pl.multiple_of(j * block, block)
        columns = pl.ds(first, block)
        key = qkv_ref[columns, span : 2 * span]
        value = qkv_ref[columns, 2 * span : 3 * span]
        key_flat = jnp.transpose(key)
        dk_ref[...] = jnp.zeros_like(dk_ref)
        dv_ref[...] = jnp.zeros_like(dv_ref)

        def tile(rows, keys, h, query_h, grad_h):
            band = slice(h * HEAD_DIM, (h + 1) * HEAD_DIM)
            probs = jnp.exp(dot(key[:keys], query_h, NT) - log_ref[h : h + 1, rows])
            d_probs = dot(value[:keys], grad_h, NT)
            d_scores = (probs * (d_probs - along_ref[h : h + 1, rows])).astype(bf16)
            dq_ref[band, rows] += dot(key_flat[band, :keys], d_scores)
            return dot(probs.astype(bf16), grad_h), dot(d_scores, query_h)

        def heads_of(rows):
            query = qkv_ref[rows, 0:span] * jnp.asarray(scale, bf16)
            grad = grad_ref[rows, :]
            return [(h, only(query, h), only(grad, h)) for h in range(heads)]

        for f in range(block // PATCHES):
            rows = pl.ds(pl.multiple_of(first + f * PATCHES, PATCHES), PATCHES)
            keys = (f + 1) * PATCHES
            for h, query_h, grad_h in heads_of(rows):
                dv, dk = tile(rows, keys, h, query_h, grad_h)
                dv_ref[:keys] += dv
                dk_ref[:keys] += dk

        def later(i, c):
            rows = pl.ds(pl.multiple_of(i * block, block), block)
            terms = [tile(rows, block, h, query_h, grad_h) for h, query_h, grad_h in heads_of(rows)]
            dv_ref[...] += sum(t[0] for t in terms)
            dk_ref[...] += sum(t[1] for t in terms)
            return c

        lax.fori_loop(j + 1, blocks, later, 0)
        dk = dk_ref[...]
        out_ref[columns, span : 2 * span] = (dk * cos_ref[columns, :] - partner(dk) * sin_ref[columns, :]).astype(bf16)
        out_ref[columns, 2 * span : 3 * span] = dv_ref[...].astype(bf16)
        return carry

    lax.fori_loop(0, blocks, key_block, 0)

    def last(i, carry):
        rows = pl.ds(pl.multiple_of(i * block, block), block)
        dq = jnp.transpose(dq_ref[:, rows]) * scale
        out_ref[rows, 0:span] = (dq * cos_ref[rows, :] - partner(dq) * sin_ref[rows, :]).astype(bf16)
        return carry

    lax.fori_loop(0, blocks, last, 0)


def attend_back(qkv, grad, full, logs, cosine, sine, span):
    total = qkv.shape[0]
    heads = span // HEAD_DIM
    block = min(1024, total)
    return pl.pallas_call(
        functools.partial(attend_back_kernel, total=total, span=span, block=block),
        out_shape=jax.ShapeDtypeStruct((total, 3 * span), bf16),
        scratch_shapes=[
            pltpu.VMEM((span, total), f32),
            pltpu.VMEM((block, span), f32),
            pltpu.VMEM((block, span), f32),
            pltpu.VMEM((heads, total), f32),
        ],
        compiler_params=pltpu.CompilerParams(vmem_limit_bytes=60 << 20),
        cost_estimate=pl.CostEstimate(
            flops=20 * total * total * span, bytes_accessed=26 * total * span, transcendentals=total * total * heads // 2
        ),
        name="attend_back",
    )(qkv, grad, full, logs, cosine, sine)


def gathered_forward(queries, keys, values, allowed):
    def one(pieces):
        q, k, v = pieces
        scores = jnp.where(allowed, dot(q, k, NT) * HEAD_DIM**-0.5, -1e30)
        peak = jnp.max(scores, axis=-1, keepdims=True)
        raised = jnp.exp(scores - peak)
        totals = jnp.sum(raised, axis=-1, keepdims=True)
        return dot((raised / totals).astype(bf16), v), peak + jnp.log(totals)

    return lax.map(one, (queries, keys, values))


def gathered_back(queries, keys, values, grads, logs, allowed):
    scale = HEAD_DIM**-0.5

    def one(pieces):
        q, k, v, grad, log = pieces
        scores = jnp.where(allowed, dot(q, k, NT) * scale, -1e30)
        probs = jnp.exp(scores - log)
        d_probs = dot(grad, v, NT)
        centre = jnp.sum(probs * d_probs, axis=-1, keepdims=True)
        d_scores = (probs * (d_probs - centre)).astype(bf16)
        dv = dot(probs.astype(bf16), grad, TN)
        return dot(d_scores, k) * scale, dot(d_scores, q, TN) * scale, dv

    return lax.map(one, (queries, keys, values, grads, logs))


def level_rows(ctx_count, noise_level, rows):
    clips = ctx_count.shape[0]
    seq_devices = lax.axis_size("seq")
    plan = jnp.concatenate([ctx_count[:, None], noise_level], axis=1)
    plan = double_rows(plan, axis_bits("clip"))
    levels = jnp.where(jnp.arange(FRAMES, dtype=jnp.int32) < plan[..., :1], 0, plan[..., 1:])
    if rows < PATCHES:
        levels = jnp.repeat(levels, PATCHES // rows, axis=-1)
    frames = max(1, rows // PATCHES)
    levels = levels.reshape(-1, clips, seq_devices, frames).transpose(0, 2, 1, 3)
    return levels.reshape(-1, seq_devices, clips * frames)


def condition(levels, here, depth, width):
    half_width = width // 2
    feature = here * depth + jnp.arange(depth, dtype=jnp.int32)
    low_half = feature < half_width
    freqs = jnp.exp(-math.log(10000.0) * jnp.where(low_half, feature, feature - half_width).astype(f32) / half_width)
    angles = levels.reshape(-1, 1).astype(f32) * freqs
    return jax.nn.silu(jnp.where(low_half, jnp.sin(angles), jnp.cos(angles))).astype(bf16)


def own_place(shard, here):
    count = lax.axis_size("clip") * lax.axis_size("seq")
    whole = jnp.zeros((count * shard.shape[0],), f32)
    return lax.dynamic_update_slice_in_dim(whole, shard.astype(f32), here * shard.shape[0], 0)


def body_by_heads(
    tokens,
    ctx_count,
    noise_level,
    mod_weight,
    mod_bias,
    qkv_weight,
    qkv_bias,
    out_weight,
    out_bias,
    up_weight,
    up_bias,
    down_weight,
    down_bias,
    cotangent,
):
    clips, rows, width = tokens.shape
    seq_devices = lax.axis_size("seq")
    devices = lax.axis_size("clip") * seq_devices
    order = near_order()
    here = lax.axis_index("clip") * seq_devices + lax.axis_index("seq")
    total = rows * seq_devices
    frames = max(1, rows // PATCHES)
    span = width // seq_devices
    lines = clips * frames
    piece = out_weight.shape[0]

    full_qkv = lax.all_gather(qkv_weight, BOTH, axis=0, tiled=True)
    unit = down_weight.shape[0]
    seq_bits = len(axis_bits("seq"))
    owners = (4,) + (2,) * seq_bits + (unit,)
    by_nearness = (0,) + tuple(range(1, seq_bits + 1))[::-1] + (seq_bits + 1,)

    def reorder(vectors):
        lead = vectors.shape[:-1]
        turn = tuple(range(len(lead))) + tuple(len(lead) + d for d in by_nearness)
        return vectors.reshape(lead + owners).transpose(turn).reshape(vectors.shape)

    down_shard = down_weight.reshape(4, piece, width)
    up_shard = reorder(up_weight).reshape(piece, 4, width).transpose(1, 0, 2)
    up_shard = jnp.concatenate([up_shard, out_weight[None]], axis=0)

    levels = level_rows(ctx_count, noise_level, rows)
    flat_bits = (2,) * len(order)
    bits_clip, bits_seq = len(axis_bits("clip")), len(axis_bits("seq"))
    turn = tuple(range(bits_clip))[::-1] + tuple(range(bits_clip, bits_clip + bits_seq))[::-1] + (len(order),)
    near_levels = levels.reshape(flat_bits + (lines,)).transpose(turn)
    cond_near = condition(near_levels, here, mod_weight.shape[0], width)
    cond = condition(levels, here, mod_weight.shape[0], width)
    cond_late = relative_rows(cond_near, order)
    mod_place = own_place(mod_bias, here)

    def modulate(columns, biases, gates=()):
        weight = mod_weight[:, columns]
        bias = jnp.concatenate([own_place(b, here) for b in biases]).reshape(lines, -1)
        rest = jnp.concatenate([jnp.broadcast_to(mod_place[columns], (lines, weight.shape[1])), bias], axis=1)
        part = jnp.pad(dot(cond_near, weight), ((0, 0), (0, bias.shape[1])))
        line_rows = halve_rows((part.reshape(devices, lines, -1) + rest).reshape(devices * lines, -1), order, gates)
        return line_rows[:, : weight.shape[1]], line_rows[:, weight.shape[1] :].reshape(1, -1)

    def blocks(line_rows):
        return line_rows.reshape(clips, frames, -1, width).transpose(0, 2, 1, 3)

    mod_first, bias_qkv = modulate(slice(0, 2 * width), (qkv_bias,))
    mods_one = blocks(mod_first)

    positions = lax.axis_index("seq") * rows + jnp.arange(rows, dtype=jnp.int32)
    cos_local, sin_local = rotary_lanes(positions, max(span, 256))
    cos_row, sin_row = rotary_lanes(jnp.arange(rows, dtype=jnp.int32), span)
    cos_far, sin_far = rotary_lanes(jnp.arange(seq_devices, dtype=jnp.int32) * rows, span)
    cos_all = (cos_far[:, None] * cos_row[None] - sin_far[:, None] * sin_row[None]).reshape(total, span)
    sin_all = (sin_far[:, None] * cos_row[None] + cos_far[:, None] * sin_row[None]).reshape(total, span)

    def exchange(value):
        return lax.all_to_all(value, "seq", 0, 0, tiled=True)

    def doubled(share, axis, bit, dim=1):
        other = swap_bit(share, axis, bit)
        mine = own_bit(axis, bit) == 0
        pair = jnp.stack([jnp.where(mine, share, other), jnp.where(mine, other, share)], axis=dim)
        return pair.reshape((-1,) + share.shape[1:])

    high_bits, low_bit = axis_bits("seq")[:-1], axis_bits("seq")[-1]
    down_share, up_share = down_shard[None], up_shard[None]
    for axis, bit in high_bits:
        down_share, up_share = doubled(down_share, axis, bit, 0), doubled(up_share, axis, bit)
    full_qkv = after(full_qkv, down_share, up_share)
    up_pair = (up_share, swap_bit(up_share, "clip", 2))
    down_share = doubled(down_share, *low_bit)

    normed, qkv, mixes, fulls, logs, sents = [], [], [], [], [], []
    for c in range(clips):
        weight = full_qkv if c == 0 else after(full_qkv, down_share, up_pair[1])
        sent, normed_c = project(tokens, c, mods_one[c], weight, bias_qkv, cos_local, sin_local, seq_devices)
        normed.append(normed_c)
        if qkv:
            sent = after(sent, qkv[-1])
        qkv.append(exchange(sent))
    backs = []
    for c in range(clips):
        mix, full, log = attend(qkv[c].reshape(total, 3 * span), span)
        mixes.append(mix)
        fulls.append(full)
        logs.append(log)
        backs.append(exchange(after(mix.reshape(seq_devices, rows, span), qkv[-1] if c == 0 else backs[-1])))

    mod_rest, bias_rest = modulate(
        slice(2 * width, 6 * width), (out_bias, up_bias, down_bias), (None, None, normed[-1], mixes[0], mixes[-1])
    )
    mods_two = blocks(mod_rest)
    bias_out = bias_rest[:, :width]
    bias_up = reorder(bias_rest[:, width : 5 * width])
    bias_down = bias_rest[:, 5 * width :]
    def from_clips(pair):
        near, across = [p.reshape((seq_devices // 2, 2) + p.shape[1:]) for p in pair]
        far = swap_bit(after(across, qkv[-1]), "clip", 1)
        return (near, across, swap_bit(near, "clip", 1), far)

    down_shares = from_clips((down_share, swap_bit(down_share, "clip", 2)))
    up_shares = from_clips([doubled(p, *low_bit) for p in up_pair])

    results = []
    d_mixed = []
    for c in range(clips):
        back = after(backs[c], mixes[-1])
        outputs = results[-1][0] if results else None
        results.append(middle(back, tokens, cotangent, c, mods_two[c], up_shares, down_shares, (bias_out, bias_up, bias_down), outputs))
        d_mixed.append(exchange(after(results[c][8], backs[-1] if c == 0 else d_mixed[-1])))

    def late(place):
        return [r[place] for r in results]

    mixed_all, normed_two, active, d_hidden, d_mlp, d_attn = [late(place) for place in (2, 3, 4, 5, 6, 7)]
    def line_sums(sums):
        return sums.transpose(1, 0, 2).reshape(frames, -1)

    def with_bias(lines_now, vectors):
        return jnp.concatenate([jnp.concatenate(lines_now, axis=0), jnp.concatenate(vectors).reshape(lines, -1)], axis=1)

    bias_up_sum = reorder(sum(r[10][0] for r in results))
    bias_pair = sum(r[11] for r in results)
    early = with_bias([line_sums(r[9]) for r in results], [bias_pair[0], bias_up_sum, bias_pair[1]])
    early_rows = lax.all_gather(early, BOTH, axis=0, tiled=True)

    d_qkv, exchanged = [], []
    for c in range(clips):
        if c == clips - 1:
            active = gate(active, *d_qkv, d_mixed[-1])
            down_send, down_keep = columns_grad(active, d_mlp)
            down_core = swap_bit(down_send, "clip", 1)
            normed_two = gate(normed_two, down_send)
            up_send, up_keep = rows_grad([(normed_two, d_hidden), (mixed_all, d_attn)])
            up_core = swap_bit(up_send, "clip", 1)
        grad = after(d_mixed[c], results[-1][8] if c == 0 else up_send)
        grad = grad.reshape(total, span)
        d_qkv.append(attend_back(qkv[c].reshape(total, 3 * span), grad, fulls[c], logs[c], cos_all, sin_all, span))
        sent = d_qkv[c].reshape(seq_devices, rows, 3 * span)
        exchanged.append(exchange(after(sent, d_mixed[-1]) if c == 0 else sent))

    down_core, up_core = gate((down_core, up_core), exchanged[0])
    down_sent = rounded_sum([down_keep[:2], down_core[:2]])
    down_along = swap_bit(down_sent, "seq", 1)
    up_sent = rounded_sum([up_keep[0], up_core[0]])
    up_across = swap_bit(up_sent, "clip", 2)
    exchanged[0] = after(exchanged[0], down_sent, up_sent)
    exchanged[-1] = after(exchanged[-1], down_along, up_across)

    last = []
    for c in range(clips):
        grads = last[-1][0] if last else None
        last.append(project_back(exchanged[c], full_qkv, tokens, c, mods_one[c][1], results[c][1], grads))
    d_projected = [r[1] for r in last]
    qkv_send, qkv_keep = rows_grad([(normed, d_projected)])
    qkv_core = swap_bit(qkv_send, "clip", 1)
    qkv_sent = rounded_sum([qkv_keep[0], qkv_core[0]])
    qkv_across = swap_bit(qkv_sent, "clip", 2)
    down_far = rounded_sum([down_keep[3], down_core[3], after(down_along[1], qkv_send)])
    down_across = swap_bit(down_far, "clip", 2)
    near_seq = axis_bits("seq")[::-1]
    grad_up = halve([up_keep[1], up_core[1], up_across], near_seq, 0, qkv_sent)
    down_addends = [down_keep[2], down_core[2], down_along[0], after(down_across, qkv_sent)]
    grad_down = jnp.transpose(halve(down_addends, near_seq[1:], 1))
    qkv_last = after(qkv_across, up_across)
    grad_qkv = halve([qkv_keep[1], qkv_core[1], qkv_last], near_seq, 0)
    grad_out = grad_up[:, 4 * width :]
    grad_up = reorder(grad_up[:, : 4 * width])
    late_rows = with_bias([line_sums(r[2]) for r in last], [sum(r[3][0] for r in last)])
    late_rows = collect_rows(after(late_rows, qkv_sent), order)
    early_rows = after(early_rows, qkv_sent)

    def own_columns(sums, shard):
        return lax.dynamic_slice_in_dim(sums, here * shard.shape[0], shard.shape[0], 0)

    def spans(all_rows, columns):
        vectors = jnp.sum(all_rows[:, columns:].reshape(devices, -1), axis=0)
        return all_rows[:, :columns], vectors

    late_mod, late_vectors = spans(late_rows, 2 * width)
    early_mod, early_vectors = spans(early_rows, 4 * width)
    grad_mod = jnp.concatenate(
        [
            lax.dot_general(rows_cond.astype(f32), r, TN, precision=highest, preferred_element_type=f32)
            for rows_cond, r in ((cond_late, late_mod), (cond, early_mod))
        ],
        axis=1,
    )
    mod_sum = jnp.concatenate([jnp.sum(late_mod, axis=0), jnp.sum(early_mod, axis=0)])
    return (
        results[-1][0],
        last[-1][0],
        grad_mod,
        own_columns(mod_sum, mod_bias),
        grad_qkv,
        own_columns(late_vectors, qkv_bias),
        grad_out,
        own_columns(early_vectors[:width], out_bias),
        grad_up,
        own_columns(early_vectors[width : 5 * width], up_bias),
        grad_down,
        own_columns(early_vectors[5 * width :], down_bias),
    )


def body_gathered(
    tokens,
    ctx_count,
    noise_level,
    mod_weight,
    mod_bias,
    qkv_weight,
    qkv_bias,
    out_weight,
    out_bias,
    up_weight,
    up_bias,
    down_weight,
    down_bias,
    cotangent,
):
    clips, rows, width = tokens.shape
    seq_devices = lax.axis_size("seq")
    devices = lax.axis_size("clip") * seq_devices
    bits = mesh_bits()
    here = lax.axis_index("clip") * seq_devices + lax.axis_index("seq")
    total = rows * seq_devices
    frames = max(1, rows // PATCHES)
    patch_rows = rows // frames

    full_qkv = lax.all_gather(qkv_weight, BOTH, axis=0, tiled=True)
    full_out = lax.all_gather(out_weight, BOTH, axis=0, tiled=True)
    full_up = lax.all_gather(up_weight, BOTH, axis=0, tiled=True)
    full_down = lax.all_gather(down_weight, BOTH, axis=0, tiled=True)
    biases = (qkv_bias, out_bias, up_bias, down_bias)
    bias_rows = double_rows(jnp.concatenate(biases).astype(f32), bits)
    full_biases = []
    first = 0
    for piece in biases:
        full_biases.append(bias_rows[:, first : first + piece.shape[0]].reshape(1, -1))
        first += piece.shape[0]
    bias_qkv, bias_out, bias_up, bias_down = full_biases

    levels = level_rows(ctx_count, noise_level, rows)
    cond = condition(levels, here, mod_weight.shape[0], width)
    mod_width = mod_weight.shape[1]
    partial = dot(cond, mod_weight) + own_place(mod_bias, here)
    modulation = halve_sum(partial.reshape(devices, clips * frames, mod_width), bits)
    modulation = modulation.reshape(clips, frames, 1, mod_width)

    positions = lax.axis_index("seq") * rows + jnp.arange(rows, dtype=jnp.int32)
    cosine, sine = rotary_lanes(positions, HEAD_DIM)
    key_frame = jnp.arange(total, dtype=jnp.int32) // PATCHES
    allowed = key_frame[None, :] <= (positions // PATCHES)[:, None]

    def flat(value):
        return value.reshape(rows, value.shape[-1])

    def split(value):
        return value.reshape(frames, patch_rows, value.shape[-1])

    def to_heads(value):
        return value.reshape(rows, HEADS, HEAD_DIM).transpose(1, 0, 2)

    saved = []
    for c in range(clips):
        mods = jnp.split(modulation[c], 6, axis=-1)
        tokens_now = split(tokens[c].astype(f32))
        unit, inverse = norm_parts(tokens_now)
        normed = flat((unit * (1.0 + mods[1]) + mods[0]).astype(bf16))
        projected = dot(normed, full_qkv) + bias_qkv
        views = []
        for place in range(3):
            view = to_heads(projected[:, place * width : (place + 1) * width])
            if place < 2:
                    view = view * cosine + jnp.roll(view, HEAD_DIM // 2, -1) * sine
            views.append(view.astype(bf16))
        queries, keys, values = views
        keys = lax.all_gather(keys, "seq", axis=1, tiled=True)
        values = lax.all_gather(values, "seq", axis=1, tiled=True)
        mix, logs = gathered_forward(queries, keys, values, allowed)
        mixed = mix.transpose(1, 0, 2).reshape(rows, width).astype(bf16)
        kept = (queries, keys, values, logs)
        saved.append((mods, tokens_now, unit, inverse, normed, kept, mixed))

    outputs = []
    middle = []
    for c in range(clips):
        mods, tokens_now, unit, inverse, normed, kept, mixed = saved[c]
        _, _, gate_one, shift_two, scale_two, gate_two = mods
        attn_out = split(dot(mixed, full_out) + bias_out)
        resid = tokens_now + gate_one * attn_out
        unit_two, inverse_two = norm_parts(resid)
        normed_two = flat((unit_two * (1.0 + scale_two) + shift_two).astype(bf16))
        hidden = dot(normed_two, full_up) + bias_up
        active_full, gelu_back = jax.vjp(jax.nn.gelu, hidden)
        active = active_full.astype(bf16)
        mlp_out = split(dot(active, full_down) + bias_down)
        outputs.append(flat((resid + gate_two * mlp_out).astype(bf16)))
        grad_out = split(cotangent[c].astype(f32))
        d_mlp = flat((gate_two * grad_out).astype(bf16))
        d_hidden = gelu_back(dot(d_mlp, full_down, NT))[0].astype(bf16)
        d_normed_two = split(dot(d_hidden, full_up, NT))
        d_resid = grad_out + norm_back(unit_two, inverse_two, d_normed_two, scale_two)
        d_attn = flat((gate_one * d_resid).astype(bf16))
        d_mixed = dot(d_attn, full_out, NT).astype(bf16)
        d_early = jnp.concatenate(
            [
                jnp.sum(d_resid * attn_out, axis=1),
                jnp.sum(d_normed_two, axis=1),
                jnp.sum(d_normed_two * unit_two, axis=1),
                jnp.sum(grad_out * mlp_out, axis=1),
            ],
            axis=-1,
        )
        middle.append((mixed, d_attn, normed_two, d_hidden, active, d_mlp, d_resid, d_mixed, d_early))

    def both(place):
        return jnp.concatenate([m[place] for m in middle], axis=0)

    d_attn_all, d_hidden_all, d_mlp_all = both(1), both(3), both(5)
    grad_down = weight_grad(both(4), d_mlp_all)
    grad_up = weight_grad(both(2), d_hidden_all)
    grad_out_weight = weight_grad(both(0), d_attn_all)
    early_rows = lax.all_gather(both(8), BOTH, axis=0, tiled=True)

    inputs_grad = []
    late = []
    projected_grads = []
    for c in range(clips):
        mods, tokens_now, unit, inverse, normed, kept, mixed = saved[c]
        d_resid, d_mixed = middle[c][6], middle[c][7]
        queries, keys, values, logs = kept
        dq, dk, dv = gathered_back(queries, keys, values, to_heads(d_mixed), logs, allowed)
        dk = lax.psum_scatter(dk.astype(bf16), "seq", scatter_dimension=1, tiled=True).astype(f32)
        dv = lax.psum_scatter(dv.astype(bf16), "seq", scatter_dimension=1, tiled=True).astype(f32)
        views = [g * cosine - jnp.roll(g, HEAD_DIM // 2, -1) * sine for g in (dq, dk)] + [dv]
        d_projected = jnp.concatenate([g.transpose(1, 0, 2).reshape(rows, width) for g in views], axis=1).astype(bf16)
        projected_grads.append(d_projected)
        d_normed = split(dot(d_projected, full_qkv, NT))
        inputs_grad.append(flat(d_resid + norm_back(unit, inverse, d_normed, mods[1])))
        late.append(jnp.concatenate([jnp.sum(d_normed, axis=1), jnp.sum(d_normed * unit, axis=1)], axis=-1))

    d_projected_all = jnp.concatenate(projected_grads, axis=0)
    grad_qkv = weight_grad(jnp.concatenate([s[4] for s in saved], axis=0), d_projected_all)
    bias_grads = [
        jnp.sum(g.astype(f32), axis=0).reshape(devices, -1) for g in (d_projected_all, d_attn_all, d_hidden_all, d_mlp_all)
    ]
    bias_sum = halve_sum(jnp.concatenate(bias_grads, axis=1), bits)
    grad_biases = []
    first = 0
    for piece in bias_grads:
        grad_biases.append(bias_sum[first : first + piece.shape[1]])
        first += piece.shape[1]

    late_rows = double_rows(jnp.concatenate(late, axis=0), bits).reshape(-1, 2 * width)
    grad_mod = jnp.concatenate(
        [
            lax.dot_general(cond.astype(f32), r, TN, precision=highest, preferred_element_type=f32)
            for r in (late_rows, early_rows)
        ],
        axis=1,
    )
    mod_sum = jnp.concatenate([jnp.sum(late_rows, axis=0), jnp.sum(early_rows, axis=0)])
    grad_mod_bias = lax.dynamic_slice_in_dim(mod_sum, here * mod_bias.shape[0], mod_bias.shape[0], 0)
    return (
        jnp.stack(outputs),
        jnp.stack(inputs_grad),
        grad_mod,
        grad_mod_bias,
        grad_qkv,
        grad_biases[0],
        grad_out_weight,
        grad_biases[1],
        grad_up,
        grad_biases[2],
        grad_down,
        grad_biases[3],
    )


def solution(mesh):
    by_heads = HEADS % mesh.shape["seq"] == 0
    body = body_by_heads if by_heads else body_gathered
    token_place = P("clip", "seq", None)
    matrix, vector = P(BOTH, None), P(BOTH)
    weights = (matrix, vector) * 5
    return jax.shard_map(
        body,
        mesh=mesh,
        in_specs=(token_place, P("clip"), P("clip", None)) + weights + (token_place,),
        out_specs=(token_place, token_place) + weights,
        check_vma=False,
    )
```

```python
import functools
import math

import jax
import jax.numpy as jnp
from jax import lax
from jax.experimental import pallas as pl
from jax.experimental.pallas import tpu as pltpu
from jax.sharding import PartitionSpec as P

HEADS = 16
HEAD_DIM = 64
FRAMES = 16
PATCHES = 256
BOTH = ("clip", "seq")
NT = (((1,), (1,)), ((), ()))
NN = (((1,), (0,)), ((), ()))
TN = (((0,), (0,)), ((), ()))
bf16 = jnp.bfloat16
f32 = jnp.float32
highest = lax.Precision.HIGHEST


def dot(left, right, dims=NN):
    return lax.dot_general(left, right, dims, preferred_element_type=f32)


def swap_bit(value, axis, bit):
    count = lax.axis_size(axis)
    return lax.ppermute(value, axis, [(i, i ^ bit) for i in range(count)])


def own_bit(axis, bit):
    return lax.shift_right_logical(lax.axis_index(axis), bit.bit_length() - 1) & 1


def axis_bits(axis):
    bits = []
    bit = 1
    while bit < lax.axis_size(axis):
        bits.append((axis, bit))
        bit *= 2
    return bits[::-1]


def exchange_order(bits):
    return sorted(range(len(bits)), key=lambda place: bits[place])


def mesh_bits():
    return axis_bits("clip") + axis_bits("seq")


def halve_sum(parts, bits, wire=f32, hold=None):
    addends = [parts.reshape((2,) * len(bits) + parts.shape[1:])]
    for place in exchange_order(bits):
        axis, bit = bits[place]
        mine = own_bit(axis, bit)
        send = sum(lax.dynamic_index_in_dim(a, 1 - mine, place).astype(f32) for a in addends)
        addends = [lax.dynamic_index_in_dim(a, mine, place) for a in addends]
        received = swap_bit(send.astype(wire), axis, bit)
        if hold is not None and len(addends) == 1:
            received = after(received, hold)
        addends.append(received)
    total = sum(a.astype(f32) for a in addends)
    return total.reshape(total.shape[len(bits) :])


def near_order():
    return axis_bits("clip")[::-1] + axis_bits("seq")[::-1]


def halve_rows(parts, bits, gates=()):
    for place, (axis, bit) in enumerate(bits):
        half = parts.shape[0] // 2
        mine = own_bit(axis, bit)
        keep = lax.dynamic_slice_in_dim(parts, mine * half, half, 0)
        send = lax.dynamic_slice_in_dim(parts, (1 - mine) * half, half, 0)
        other = swap_bit(send, axis, bit)
        if place < len(gates) and gates[place] is not None:
            other = after(other, gates[place])
        parts = keep + other
    return parts


def collect_rows(rows, bits):
    for axis, bit in reversed(bits):
        rows = jnp.concatenate([rows, swap_bit(rows, axis, bit)], axis=0)
    return rows


def relative_rows(rows, bits):
    shape = rows.shape
    rows = rows.reshape((2,) * len(bits) + (-1,) + shape[1:])
    for place, (axis, bit) in enumerate(bits):
        rows = jnp.where(own_bit(axis, bit) == 0, rows, jnp.flip(rows, place))
    return rows.reshape(shape)


def after(value, *others):
    return lax.optimization_barrier((value,) + others)[0]


def double_rows(row, bits):
    rows = row[None]
    for axis, bit in reversed(bits):
        other = swap_bit(rows, axis, bit)
        low = own_bit(axis, bit) == 0
        rows = jnp.concatenate([jnp.where(low, rows, other), jnp.where(low, other, rows)], axis=0)
    return rows


def weight_grad(left, right):
    tokens, rows = left.shape
    quarter = rows // lax.axis_size("clip")
    mine = lax.axis_index("clip")

    def part(flip):
        piece = lax.dynamic_slice_in_dim(left, (mine ^ flip) * quarter, quarter, 1)
        return dot(piece, right, TN)

    far = swap_bit(part(3).astype(bf16), "clip", 1)
    near = swap_bit(part(1).astype(bf16), "clip", 1)
    across = swap_bit((part(2) + far.astype(f32)).astype(bf16), "clip", 2)
    total = part(0) + near.astype(f32) + across.astype(f32)
    return halve_sum(total.reshape((lax.axis_size("seq"), -1, right.shape[1])), axis_bits("seq"), bf16)


def norm_parts(values):
    centre = values - jnp.mean(values, axis=-1, keepdims=True)
    spread = jnp.mean(centre * centre, axis=-1, keepdims=True)
    inverse = lax.rsqrt(spread + 1e-06)
    return centre * inverse, inverse


def norm_back(unit, inverse, grad, scales):
    scaled = grad * (1.0 + scales)
    mean = jnp.mean(scaled, axis=-1, keepdims=True)
    along = jnp.mean(scaled * unit, axis=-1, keepdims=True)
    return inverse * (scaled - mean - unit * along)


def rotary_lanes(positions, width):
    half = HEAD_DIM // 2
    lane = jnp.arange(width, dtype=jnp.int32) % HEAD_DIM
    freqs = jnp.exp(-math.log(10000.0) * 2.0 * (lane % half).astype(f32) / HEAD_DIM)
    angles = positions.astype(f32)[:, None] * freqs[None, :]
    sign = jnp.where(lane < half, -1.0, 1.0).astype(f32)
    return jnp.cos(angles), jnp.sin(angles) * sign[None, :]


def partner(values):
    width = values.shape[1]
    half = HEAD_DIM // 2
    lane = lax.broadcasted_iota(jnp.int32, (1, width), 1) % HEAD_DIM
    return jnp.where(lane < half, pltpu.roll(values, width - half, 1), pltpu.roll(values, half, 1))


def project_kernel(
    token_ref, mod_ref, wq_ref, wk_ref, wv_ref, bq_ref, bk_ref, bv_ref, cos_ref, sin_ref, out_ref, normed_ref, *, span
):
    frames = mod_ref.shape[1]
    patch = token_ref.shape[0] // frames

    @pl.when(pl.program_id(0) == 0)
    def _():
        for f in range(frames):
            rows = slice(f * patch, (f + 1) * patch)
            unit, _ = norm_parts(token_ref[rows, :].astype(f32))
            normed_ref[rows, :] = (unit * (1.0 + mod_ref[1, f : f + 1, :]) + mod_ref[0, f : f + 1, :]).astype(bf16)

    x = normed_ref[...]
    cosine, sine = cos_ref[...], sin_ref[...]
    groups = wq_ref.shape[1] // span
    for place, (w_ref, b_ref) in enumerate(((wq_ref, bq_ref), (wk_ref, bk_ref), (wv_ref, bv_ref))):
        value = dot(x, w_ref[...]) + b_ref[...]
        if place < 2:
            value = value * cosine + partner(value) * sine
        value = value.astype(bf16)
        for g in range(groups):
            out_ref[g, :, place * span : (place + 1) * span] = value[:, g * span : (g + 1) * span]


def whole_block(shape):
    return pl.BlockSpec(shape, lambda j: (0,) * len(shape))


def column_specs(height, block, steps):
    return [pl.BlockSpec((height, block), functools.partial(lambda p, j: (0, p * steps + j), p)) for p in range(3)]


def clip_block(shape, c):
    return pl.BlockSpec((None,) + shape[1:], lambda j: (c,) + (0,) * (len(shape) - 1))


def project(tokens, c, mods, weight, bias, cosine, sine, groups):
    _, rows, width = tokens.shape
    span = width // groups
    block = max(span, 256)
    per_step = block // span
    steps = groups // per_step
    return pl.pallas_call(
        functools.partial(project_kernel, span=span),
        grid=(steps,),
        in_specs=[clip_block(tokens.shape, c), whole_block(mods.shape)]
        + column_specs(width, block, steps)
        + column_specs(1, block, steps)
        + [whole_block((rows, block))] * 2,
        out_specs=(pl.BlockSpec((per_step, rows, 3 * span), lambda j: (j, 0, 0)), whole_block((rows, width))),
        out_shape=(
            jax.ShapeDtypeStruct((groups, rows, 3 * span), bf16),
            jax.ShapeDtypeStruct((rows, width), bf16),
        ),
        compiler_params=pltpu.CompilerParams(vmem_limit_bytes=32 << 20),
        cost_estimate=pl.CostEstimate(
            flops=6 * rows * width * width, bytes_accessed=6 * width * width + 10 * rows * width, transcendentals=0
        ),
        name="project",
    )(tokens, mods, weight, weight, weight, bias, bias, bias, cosine, sine)


def project_back_kernel(
    back_ref, wq_ref, wk_ref, wv_ref, token_ref, scale_ref, resid_ref, *rest, span
):
    grad_ref, proj_ref, sums_ref, bias_ref, acc_ref = rest[-5:]
    frames = scale_ref.shape[0]
    rows_all, width = token_ref.shape
    patch = rows_all // frames
    step = pl.program_id(0)
    block = wq_ref.shape[1]

    @pl.when(step == 0)
    def _():
        acc_ref[...] = jnp.zeros_like(acc_ref)

    for place, w_ref in enumerate((wq_ref, wk_ref, wv_ref)):
        band = slice(place * span, (place + 1) * span)
        piece = jnp.concatenate([back_ref[g, :, band] for g in range(block // span)], axis=1)
        columns = pl.ds(pl.multiple_of(place * width + step * block, block), block)
        proj_ref[:, columns] = piece
        bias_ref[:, columns] = jnp.sum(piece.astype(f32), axis=0, keepdims=True)
        acc_ref[...] += dot(piece, w_ref[...], NT)

    @pl.when(step == pl.num_programs(0) - 1)
    def _():
        for f in range(frames):
            rows = slice(f * patch, (f + 1) * patch)
            unit, inverse = norm_parts(token_ref[rows, :].astype(f32))
            grad = acc_ref[rows, :]
            grad_ref[rows, :] = resid_ref[rows, :] + norm_back(unit, inverse, grad, scale_ref[f : f + 1, :])
            sums_ref[0, f : f + 1, :] = jnp.sum(grad, axis=0, keepdims=True)
            sums_ref[1, f : f + 1, :] = jnp.sum(grad * unit, axis=0, keepdims=True)


def project_back(back, weight, tokens, c, scales, d_resid, grads):
    groups, rows, _ = back.shape
    width = tokens.shape[2]
    span = width // groups
    block = max(span, 256)
    per_step = block // span
    steps = groups // per_step
    earlier = [] if grads is None else [grads]
    return pl.pallas_call(
        functools.partial(project_back_kernel, span=span),
        grid=(steps,),
        in_specs=[pl.BlockSpec((per_step, rows, 3 * span), lambda j: (j, 0, 0))]
        + column_specs(width, block, steps)
        + [clip_block(tokens.shape, c), whole_block(scales.shape), whole_block((rows, width))]
        + [pl.BlockSpec(memory_space=pl.ANY)] * len(earlier),
        out_specs=(
            clip_block(tokens.shape, c),
            whole_block((rows, 3 * width)),
            whole_block((2,) + scales.shape),
            whole_block((1, 3 * width)),
        ),
        out_shape=(
            jax.ShapeDtypeStruct(tokens.shape, f32),
            jax.ShapeDtypeStruct((rows, 3 * width), bf16),
            jax.ShapeDtypeStruct((2,) + scales.shape, f32),
            jax.ShapeDtypeStruct((1, 3 * width), f32),
        ),
        input_output_aliases={7: 0} if earlier else {},
        scratch_shapes=[pltpu.VMEM((rows, width), f32)],
        compiler_params=pltpu.CompilerParams(vmem_limit_bytes=40 << 20),
        cost_estimate=pl.CostEstimate(
            flops=6 * rows * width * width, bytes_accessed=6 * width * width + 22 * rows * width, transcendentals=0
        ),
        name="project_back",
    )(back, weight, weight, weight, tokens, scales, d_resid, *earlier)


GELU_RATE = math.sqrt(2.0 / math.pi)
GELU_CUBE = 0.044715


def middle_kernel(clip_ref, back_ref, token_ref, cot_ref, mod_ref, bo_ref, bup_ref, bdown_ref, *refs):
    wo_refs, up_refs, down_refs = refs[0:4], refs[4:8], refs[8:12]
    (
        out_ref,
        dres_ref,
        mixed_ref,
        normed_ref,
        act_ref,
        dhid_ref,
        dmlp_ref,
        dattn_ref,
        dmix_ref,
        sums_ref,
        bup_sum_ref,
        bsum_ref,
        attn_ref,
        res_ref,
        mlp_ref,
        dn_ref,
        wo_ref,
        up_ref,
        down_ref,
    ) = refs[-19:]
    groups, rows_all, span = back_ref.shape
    width = token_ref.shape[1]
    quarter = width // 4
    frames = mod_ref.shape[1]
    patch = rows_all // frames
    step = pl.program_id(0)
    mine = clip_ref[0]

    def owner_rows(place):
        return pl.ds(pl.multiple_of((mine ^ FLIPS[place]) * quarter, quarter), quarter)

    @pl.when(step == 0)
    def _():
        for place in range(4):
            wo_ref[owner_rows(place), :] = wo_refs[place][...].reshape(quarter, width)
        for g in range(groups):
            mixed_ref[:, g * span : (g + 1) * span] = back_ref[g]
        attn_ref[...] = dot(mixed_ref[...], wo_ref[...]) + bo_ref[...]
        for f in range(frames):
            rows = slice(f * patch, (f + 1) * patch)
            resid = token_ref[rows, :].astype(f32) + mod_ref[0, f : f + 1, :] * attn_ref[rows, :]
            res_ref[rows, :] = resid
            unit, _ = norm_parts(resid)
            normed_ref[rows, :] = (unit * (1.0 + mod_ref[2, f : f + 1, :]) + mod_ref[1, f : f + 1, :]).astype(bf16)
            dmlp_ref[rows, :] = (mod_ref[3, f : f + 1, :] * cot_ref[rows, :].astype(f32)).astype(bf16)
        mlp_ref[...] = jnp.zeros_like(mlp_ref)
        dn_ref[...] = jnp.zeros_like(dn_ref)

    for place in range(4):
        up_ref[owner_rows(place), :] = up_refs[place][...].reshape(quarter, -1)

        @pl.when(step // 2 == place)
        def _(place=place):
            down_ref[...] = down_refs[place][...].reshape(-1, width)

    up = up_ref[...]
    down = down_ref[...]
    hidden = dot(normed_ref[...], up) + bup_ref[...]
    square = hidden * hidden
    bend = jnp.tanh(GELU_RATE * (hidden + GELU_CUBE * (square * hidden)))
    share = 0.5 * (1.0 + bend)
    active = (hidden * share).astype(bf16)
    act_ref[...] = active
    mlp_ref[...] += dot(active, down)
    slope = share + 0.5 * hidden * (1.0 - bend * bend) * (GELU_RATE + (3.0 * GELU_RATE * GELU_CUBE) * square)
    d_hidden = (dot(dmlp_ref[...], down, NT) * slope).astype(bf16)
    dhid_ref[...] = d_hidden
    bup_sum_ref[...] = jnp.sum(d_hidden.astype(f32), axis=0, keepdims=True)
    dn_ref[...] += dot(d_hidden, up, NT)

    @pl.when(step == pl.num_programs(0) - 1)
    def _():
        bsum = None
        for f in range(frames):
            rows = slice(f * patch, (f + 1) * patch)
            resid = res_ref[rows, :]
            mlp = mlp_ref[rows, :] + bdown_ref[...]
            out_ref[rows, :] = (resid + mod_ref[3, f : f + 1, :] * mlp).astype(bf16)
            cot = cot_ref[rows, :].astype(f32)
            sums_ref[3, f : f + 1, :] = jnp.sum(cot * mlp, axis=0, keepdims=True)
            unit, inverse = norm_parts(resid)
            grad = dn_ref[rows, :]
            sums_ref[1, f : f + 1, :] = jnp.sum(grad, axis=0, keepdims=True)
            sums_ref[2, f : f + 1, :] = jnp.sum(grad * unit, axis=0, keepdims=True)
            d_resid = cot + norm_back(unit, inverse, grad, mod_ref[2, f : f + 1, :])
            dres_ref[rows, :] = d_resid
            sums_ref[0, f : f + 1, :] = jnp.sum(d_resid * attn_ref[rows, :], axis=0, keepdims=True)
            d_attn = (mod_ref[0, f : f + 1, :] * d_resid).astype(bf16)
            dattn_ref[rows, :] = d_attn
            term = jnp.concatenate(
                [
                    jnp.sum(d_attn.astype(f32), axis=0, keepdims=True),
                    jnp.sum(dmlp_ref[rows, :].astype(f32), axis=0, keepdims=True),
                ],
                axis=0,
            )
            bsum = term if bsum is None else bsum + term
        bsum_ref[...] = bsum
        d_mixed = dot(dattn_ref[...], wo_ref[...], NT).astype(bf16)
        for g in range(groups):
            dmix_ref[g] = d_mixed[:, g * span : (g + 1) * span]


FLIPS = (0, 2, 1, 3)


def middle(back, tokens, cot, c, mods, up_shares, down_shares, biases, outputs):
    groups, rows, span = back.shape
    _, _, width = tokens.shape
    high, low, _, piece, _ = up_shares[0].shape
    hidden = 4 * width
    steps = 8
    block = hidden // steps
    bias_out, bias_up, bias_down = biases
    mine = lax.axis_index("clip").astype(jnp.int32)[None]
    earlier = [] if outputs is None else [outputs]

    def fixed(shape, **options):
        return pl.BlockSpec(shape, lambda j, q: (0,) * len(shape), **options)

    def clip_part(shape):
        return pl.BlockSpec((None,) + shape[1:], lambda j, q: (c,) + (0,) * (len(shape) - 1))

    def unit_block(j, q):
        owner = q[0] ^ jnp.where(j // 2 == 1, 2, jnp.where(j // 2 == 2, 1, j // 2))
        return owner, j % 2

    def up_index(j, q):
        owner, half = unit_block(j, q)
        return (0, 0, owner, 0, half)

    def hidden_index(j, q):
        owner, half = unit_block(j, q)
        return (0, owner * 2 + half)

    def down_index(place, j, q):
        return (0, jnp.clip(j - 2 * place, 0, 1), 0, 0, 0)

    token_block = fixed((rows, width))
    hidden_block = pl.BlockSpec((rows, block), hidden_index)
    out_spec = [
        pl.BlockSpec((high, low, 1, piece, width), lambda j, q: (0, 0, 4, 0, 0), pipeline_mode=pl.Buffered(1)) for _ in range(4)
    ]
    up_spec = [pl.BlockSpec((high, low, 1, piece, block), up_index) for _ in range(4)]
    down_spec = [
        pl.BlockSpec((high, 1, 4, piece, width), functools.partial(down_index, place)) for place in range(4)
    ]
    return pl.pallas_call(
        middle_kernel,
        grid_spec=pltpu.PrefetchScalarGridSpec(
            num_scalar_prefetch=1,
            grid=(steps,),
            in_specs=[
                fixed(back.shape),
                clip_part(tokens.shape),
                clip_part(tokens.shape),
                fixed(mods.shape),
                fixed((1, width)),
                pl.BlockSpec((1, block), hidden_index),
                fixed((1, width)),
            ]
            + out_spec
            + up_spec
            + down_spec
            + [pl.BlockSpec(memory_space=pl.ANY)] * len(earlier),
            out_specs=(
                clip_part(tokens.shape),
                token_block,
                token_block,
                token_block,
                hidden_block,
                hidden_block,
                token_block,
                token_block,
                fixed(back.shape),
                fixed(mods.shape),
                pl.BlockSpec((1, block), hidden_index),
                fixed((2, width)),
            ),
            scratch_shapes=[pltpu.VMEM((rows, width), f32)] * 4
            + [pltpu.VMEM((width, width), bf16), pltpu.VMEM((width, block), bf16), pltpu.VMEM((block, width), bf16)],
        ),
        out_shape=(
            jax.ShapeDtypeStruct(tokens.shape, bf16),
            jax.ShapeDtypeStruct((rows, width), f32),
            jax.ShapeDtypeStruct((rows, width), bf16),
            jax.ShapeDtypeStruct((rows, width), bf16),
            jax.ShapeDtypeStruct((rows, hidden), bf16),
            jax.ShapeDtypeStruct((rows, hidden), bf16),
            jax.ShapeDtypeStruct((rows, width), bf16),
            jax.ShapeDtypeStruct((rows, width), bf16),
            jax.ShapeDtypeStruct(back.shape, bf16),
            jax.ShapeDtypeStruct(mods.shape, f32),
            jax.ShapeDtypeStruct((1, hidden), f32),
            jax.ShapeDtypeStruct((2, width), f32),
        ),
        input_output_aliases={20: 0} if earlier else {},
        compiler_params=pltpu.CompilerParams(vmem_limit_bytes=60 << 20),
        cost_estimate=pl.CostEstimate(
            flops=4 * rows * width * width, bytes_accessed=2 * width * width + 5 * rows * width, transcendentals=rows * width
        ),
        name="middle",
    )(mine, back, tokens, cot, mods, bias_out, bias_up, bias_down, *up_shares, *up_shares, *down_shares, *earlier)


def near_place(place, count):
    bits = count.bit_length() - 1
    return sum(((place >> b) & 1) << (bits - 1 - b) for b in range(bits))


def weight_grad_kernel(index_ref, *refs, clips, counts, widths, owners, swapped):
    outs = refs[-1 - len(COLUMN_PLACES if swapped else ROW_FLIPS) : -1]
    flat_ref = refs[-1]
    step = pl.program_id(0)
    first, taken = 0, 0
    for count, steps in zip(counts, widths):
        left, right = refs[taken : taken + clips * count], refs[taken + clips * count : taken + clips * (count + 1)]
        taken += clips * (count + 1)
        rows, height = left[0].shape
        piece = height // owners

        @pl.when(step == first)
        def _(left=left, count=count, rows=rows, height=height, piece=piece):
            for c in range(clips):
                for i in range(count):
                    flat = jnp.transpose(left[c * count + i][...])
                    for owner in range(owners):
                        place = i * height + near_place(owner, owners) * piece
                        flat_ref[place : place + piece, c * rows : (c + 1) * rows] = flat[owner * piece : (owner + 1) * piece]

        @pl.when((step >= first) & (step < first + steps))
        def _(right=right, rows=rows):
            total = dot(flat_ref[:, 0:rows], right[0][...])
            for c in range(1, clips):
                total += dot(flat_ref[:, c * rows : (c + 1) * rows], right[c][...])
            total = total.astype(bf16)
            if swapped:
                for ref, (start, blocks) in zip(outs, COLUMN_PLACES):

                    @pl.when((step >= start) & (step < start + blocks))
                    def _(ref=ref):
                        ref[0] = total

            else:
                height = total.shape[0] // len(outs)
                for place, ref in enumerate(outs):
                    ref[...] = total[place * height : (place + 1) * height]

        first += steps


def weight_grad_call(in_specs, operands, indices, steps, shapes, specs, width, depth, **options):
    return pl.pallas_call(
        functools.partial(weight_grad_kernel, **options),
        grid_spec=pltpu.PrefetchScalarGridSpec(
            num_scalar_prefetch=1,
            grid=(steps,),
            in_specs=in_specs,
            out_specs=specs,
            scratch_shapes=[pltpu.VMEM((width, depth), bf16)],
        ),
        out_shape=tuple(jax.ShapeDtypeStruct(shape, bf16) for shape in shapes),
        compiler_params=pltpu.CompilerParams(vmem_limit_bytes=60 << 20),
        cost_estimate=pl.CostEstimate(
            flops=1024 * steps * width * depth, bytes_accessed=steps * 1024 * (width + depth) + 4 * width * depth, transcendentals=0
        ),
        name="weight_grad",
    )(indices, *operands)


BLOCK = 512
ROW_FLIPS = (3, 1, 2, 0)
COLUMN_PLACES = ((0, 2), (2, 1), (3, 1), (4, 2), (6, 1), (7, 1))


def rows_grad(pairs):
    clips = len(pairs[0][0])
    rows, width = pairs[0][0][0].shape
    height = width // 4
    mine = mine_on("clip")
    widths = [right[0].shape[1] // BLOCK for _, right in pairs]
    in_specs, operands = [], []
    first = 0
    for (left, right), steps in zip(pairs, widths):
        for array in left:
            for i in range(4):
                in_specs.append(pl.BlockSpec((rows, height), functools.partial(lambda i, j, q: (0, q[i]), i)))
                operands.append(array)
        where = functools.partial(lambda first, steps, j, q: (0, jnp.clip(j - first, 0, steps - 1)), first, steps)
        in_specs += [pl.BlockSpec((rows, BLOCK), where)] * clips
        operands += right
        first += steps
    shape = (height, first * BLOCK)
    spec = pl.BlockSpec((height, BLOCK), lambda j, q: (0, j))
    return weight_grad_call(
        in_specs,
        operands,
        jnp.stack([mine ^ flip for flip in ROW_FLIPS]),
        first,
        [shape] * 4,
        [spec] * 4,
        width,
        clips * rows,
        clips=clips,
        counts=[4] * len(pairs),
        widths=widths,
        owners=lax.axis_size("seq"),
        swapped=False,
    )


def columns_grad(left, right):
    clips = len(left)
    rows, width = right[0].shape
    mine, low = mine_on("clip"), mine_on("seq") & 1

    def block(clip_flip, low_flip):
        return (mine ^ clip_flip) * 2 + (low ^ low_flip)

    flips = ((0, 1), (2, 1), (0, 0), (2, 0))
    indices = jnp.stack([block(c ^ 1, s) for c, s in flips] + [block(c, s) for c, s in flips])
    in_specs = [pl.BlockSpec((rows, width), lambda j, q: (0, 0))] * clips
    in_specs += [pl.BlockSpec((rows, BLOCK), lambda j, q: (0, q[j]))] * clips
    def place_index(start, blocks, j, q):
        return (jnp.clip(j - start, 0, blocks - 1), 0, 0)

    return weight_grad_call(
        in_specs,
        right + left,
        indices,
        8,
        [(blocks, width, BLOCK) for _, blocks in COLUMN_PLACES],
        [pl.BlockSpec((1, width, BLOCK), functools.partial(place_index, *place)) for place in COLUMN_PLACES],
        width,
        clips * rows,
        clips=clips,
        counts=[1],
        widths=[8],
        owners=1,
        swapped=True,
    )


def mine_on(axis):
    return lax.axis_index(axis).astype(jnp.int32)


def rounded_sum(addends):
    return sum(a.astype(f32) for a in addends).astype(bf16)


def halve(addends, bits, dim, hold=None):
    for place, (axis, bit) in enumerate(bits):
        half = addends[0].shape[dim] // 2
        mine = own_bit(axis, bit)
        send = rounded_sum([lax.dynamic_slice_in_dim(a, (1 - mine) * half, half, dim) for a in addends])
        addends = [lax.dynamic_slice_in_dim(a, mine * half, half, dim) for a in addends]
        received = swap_bit(send, axis, bit)
        if hold is not None and place == 0:
            received = after(received, hold)
        addends.append(received)
    return sum(a.astype(f32) for a in addends)


def gate(arrays, *others):
    return list(lax.optimization_barrier((tuple(arrays), others))[0])


def height_of(pairs, parts):
    return pairs[0][0][0].shape[1] // parts


def attend_kernel(qkv_ref, mix_ref, full_ref, log_ref, vt_ref, *, total, span, block):
    heads = span // HEAD_DIM
    head = lax.broadcasted_iota(jnp.int32, (1, span), 1) // HEAD_DIM
    key_frame = lax.broadcasted_iota(jnp.int32, (block, block), 0) // PATCHES
    query_frame = lax.broadcasted_iota(jnp.int32, (block, block), 1) // PATCHES
    kept = key_frame <= query_frame

    def flip(j, carry):
        rows = pl.ds(pl.multiple_of(j * block, block), block)
        vt_ref[:, rows] = jnp.transpose(qkv_ref[rows, 2 * span : 3 * span])
        return carry

    lax.fori_loop(0, total // block, flip, 0)

    def query_block(i, carry):
        rows = pl.ds(pl.multiple_of(i * block, block), block)
        query = qkv_ref[rows, 0:span] * jnp.asarray(HEAD_DIM**-0.5, bf16)
        queries = [jnp.where(head == h, query, jnp.zeros_like(query)) for h in range(heads)]

        def step(j, state, masked):
            peaks, sums, mixes = state
            columns = pl.ds(pl.multiple_of(j * block, block), block)
            key = qkv_ref[columns, span : 2 * span]
            new = ([], [], [])
            for h in range(heads):
                scores = dot(key, queries[h], NT)
                if masked:
                    scores = jnp.where(kept, scores, -1e30)
                peak = jnp.maximum(peaks[h], jnp.max(scores, axis=0, keepdims=True))
                raised = jnp.exp(scores - peak)
                fade = jnp.exp(peaks[h] - peak)
                new[0].append(peak)
                new[1].append(fade * sums[h] + jnp.sum(raised, axis=0, keepdims=True))
                term = dot(vt_ref[h * HEAD_DIM : (h + 1) * HEAD_DIM, columns], raised.astype(bf16))
                new[2].append(mixes[h] * fade + term)
            return tuple(map(tuple, new))

        state = (
            tuple(jnp.full((1, block), -1e30, f32) for _ in range(heads)),
            tuple(jnp.zeros((1, block), f32) for _ in range(heads)),
            tuple(jnp.zeros((HEAD_DIM, block), f32) for _ in range(heads)),
        )
        state = lax.fori_loop(0, i, lambda j, s: step(j, s, False), state)
        peaks, sums, mixes = step(i, state, True)
        mixed = jnp.transpose(jnp.concatenate([mixes[h] / sums[h] for h in range(heads)], axis=0))
        full_ref[rows, :] = mixed
        mix_ref[rows, :] = mixed.astype(bf16)
        for h in range(heads):
            log_ref[h : h + 1, rows] = peaks[h] + jnp.log(sums[h])
        return carry

    lax.fori_loop(0, total // block, query_block, 0)


def attend(qkv, span):
    total = qkv.shape[0]
    heads = span // HEAD_DIM
    block = min(1024, total)
    return pl.pallas_call(
        functools.partial(attend_kernel, total=total, span=span, block=block),
        out_shape=(
            jax.ShapeDtypeStruct((total, span), bf16),
            jax.ShapeDtypeStruct((total, span), f32),
            jax.ShapeDtypeStruct((heads, total), f32),
        ),
        scratch_shapes=[pltpu.VMEM((span, total), bf16)],
        compiler_params=pltpu.CompilerParams(vmem_limit_bytes=60 << 20),
        cost_estimate=pl.CostEstimate(
            flops=8 * total * total * span, bytes_accessed=12 * total * span, transcendentals=total * total * heads // 2
        ),
        name="attend",
    )(qkv)


def attend_back_kernel(
    qkv_ref, grad_ref, full_ref, log_ref, cos_ref, sin_ref, out_ref, dq_ref, dk_ref, dv_ref, along_ref, *, total, span, block
):
    heads = span // HEAD_DIM
    scale = HEAD_DIM**-0.5
    head = lax.broadcasted_iota(jnp.int32, (1, span), 1) // HEAD_DIM
    blocks = total // block
    dq_ref[...] = jnp.zeros_like(dq_ref)

    def only(value, h):
        return jnp.where(head == h, value, jnp.zeros_like(value))

    def lead(i, carry):
        rows = pl.ds(pl.multiple_of(i * block, block), block)
        product = jnp.transpose(grad_ref[rows, :].astype(f32) * full_ref[rows, :])
        for h in range(heads):
            along_ref[h : h + 1, rows] = jnp.sum(product[h * HEAD_DIM : (h + 1) * HEAD_DIM], axis=0, keepdims=True)
        return carry

    lax.fori_loop(0, blocks, lead, 0)

    def key_block(j, carry):
        first = pl.multiple_of(j * block, block)
        columns = pl.ds(first, block)
        key = qkv_ref[columns, span : 2 * span]
        value = qkv_ref[columns, 2 * span : 3 * span]
        key_flat = jnp.transpose(key)
        dk_ref[...] = jnp.zeros_like(dk_ref)
        dv_ref[...] = jnp.zeros_like(dv_ref)

        def tile(rows, keys, h, query_h, grad_h):
            band = slice(h * HEAD_DIM, (h + 1) * HEAD_DIM)
            probs = jnp.exp(dot(key[:keys], query_h, NT) - log_ref[h : h + 1, rows])
            d_probs = dot(value[:keys], grad_h, NT)
            d_scores = (probs * (d_probs - along_ref[h : h + 1, rows])).astype(bf16)
            dq_ref[band, rows] += dot(key_flat[band, :keys], d_scores)
            return dot(probs.astype(bf16), grad_h), dot(d_scores, query_h)

        def heads_of(rows):
            query = qkv_ref[rows, 0:span] * jnp.asarray(scale, bf16)
            grad = grad_ref[rows, :]
            return [(h, only(query, h), only(grad, h)) for h in range(heads)]

        for f in range(block // PATCHES):
            rows = pl.ds(pl.multiple_of(first + f * PATCHES, PATCHES), PATCHES)
            keys = (f + 1) * PATCHES
            for h, query_h, grad_h in heads_of(rows):
                dv, dk = tile(rows, keys, h, query_h, grad_h)
                dv_ref[:keys] += dv
                dk_ref[:keys] += dk

        def later(i, c):
            rows = pl.ds(pl.multiple_of(i * block, block), block)
            terms = [tile(rows, block, h, query_h, grad_h) for h, query_h, grad_h in heads_of(rows)]
            dv_ref[...] += sum(t[0] for t in terms)
            dk_ref[...] += sum(t[1] for t in terms)
            return c

        lax.fori_loop(j + 1, blocks, later, 0)
        dk = dk_ref[...]
        out_ref[columns, span : 2 * span] = (dk * cos_ref[columns, :] - partner(dk) * sin_ref[columns, :]).astype(bf16)
        out_ref[columns, 2 * span : 3 * span] = dv_ref[...].astype(bf16)
        return carry

    lax.fori_loop(0, blocks, key_block, 0)

    def last(i, carry):
        rows = pl.ds(pl.multiple_of(i * block, block), block)
        dq = jnp.transpose(dq_ref[:, rows]) * scale
        out_ref[rows, 0:span] = (dq * cos_ref[rows, :] - partner(dq) * sin_ref[rows, :]).astype(bf16)
        return carry

    lax.fori_loop(0, blocks, last, 0)


def attend_back(qkv, grad, full, logs, cosine, sine, span):
    total = qkv.shape[0]
    heads = span // HEAD_DIM
    block = min(1024, total)
    return pl.pallas_call(
        functools.partial(attend_back_kernel, total=total, span=span, block=block),
        out_shape=jax.ShapeDtypeStruct((total, 3 * span), bf16),
        scratch_shapes=[
            pltpu.VMEM((span, total), f32),
            pltpu.VMEM((block, span), f32),
            pltpu.VMEM((block, span), f32),
            pltpu.VMEM((heads, total), f32),
        ],
        compiler_params=pltpu.CompilerParams(vmem_limit_bytes=60 << 20),
        cost_estimate=pl.CostEstimate(
            flops=20 * total * total * span, bytes_accessed=26 * total * span, transcendentals=total * total * heads // 2
        ),
        name="attend_back",
    )(qkv, grad, full, logs, cosine, sine)


def gathered_forward(queries, keys, values, allowed):
    def one(pieces):
        q, k, v = pieces
        scores = jnp.where(allowed, dot(q, k, NT) * HEAD_DIM**-0.5, -1e30)
        peak = jnp.max(scores, axis=-1, keepdims=True)
        raised = jnp.exp(scores - peak)
        totals = jnp.sum(raised, axis=-1, keepdims=True)
        return dot((raised / totals).astype(bf16), v), peak + jnp.log(totals)

    return lax.map(one, (queries, keys, values))


def gathered_back(queries, keys, values, grads, logs, allowed):
    scale = HEAD_DIM**-0.5

    def one(pieces):
        q, k, v, grad, log = pieces
        scores = jnp.where(allowed, dot(q, k, NT) * scale, -1e30)
        probs = jnp.exp(scores - log)
        d_probs = dot(grad, v, NT)
        centre = jnp.sum(probs * d_probs, axis=-1, keepdims=True)
        d_scores = (probs * (d_probs - centre)).astype(bf16)
        dv = dot(probs.astype(bf16), grad, TN)
        return dot(d_scores, k) * scale, dot(d_scores, q, TN) * scale, dv

    return lax.map(one, (queries, keys, values, grads, logs))


def level_rows(ctx_count, noise_level, rows):
    clips = ctx_count.shape[0]
    seq_devices = lax.axis_size("seq")
    plan = jnp.concatenate([ctx_count[:, None], noise_level], axis=1)
    plan = double_rows(plan, axis_bits("clip"))
    levels = jnp.where(jnp.arange(FRAMES, dtype=jnp.int32) < plan[..., :1], 0, plan[..., 1:])
    if rows < PATCHES:
        levels = jnp.repeat(levels, PATCHES // rows, axis=-1)
    frames = max(1, rows // PATCHES)
    levels = levels.reshape(-1, clips, seq_devices, frames).transpose(0, 2, 1, 3)
    return levels.reshape(-1, seq_devices, clips * frames)


def condition(levels, here, depth, width):
    half_width = width // 2
    feature = here * depth + jnp.arange(depth, dtype=jnp.int32)
    low_half = feature < half_width
    freqs = jnp.exp(-math.log(10000.0) * jnp.where(low_half, feature, feature - half_width).astype(f32) / half_width)
    angles = levels.reshape(-1, 1).astype(f32) * freqs
    return jax.nn.silu(jnp.where(low_half, jnp.sin(angles), jnp.cos(angles))).astype(bf16)


def own_place(shard, here):
    count = lax.axis_size("clip") * lax.axis_size("seq")
    whole = jnp.zeros((count * shard.shape[0],), f32)
    return lax.dynamic_update_slice_in_dim(whole, shard.astype(f32), here * shard.shape[0], 0)


def body_by_heads(
    tokens,
    ctx_count,
    noise_level,
    mod_weight,
    mod_bias,
    qkv_weight,
    qkv_bias,
    out_weight,
    out_bias,
    up_weight,
    up_bias,
    down_weight,
    down_bias,
    cotangent,
):
    clips, rows, width = tokens.shape
    seq_devices = lax.axis_size("seq")
    devices = lax.axis_size("clip") * seq_devices
    order = near_order()
    here = lax.axis_index("clip") * seq_devices + lax.axis_index("seq")
    total = rows * seq_devices
    frames = max(1, rows // PATCHES)
    span = width // seq_devices
    lines = clips * frames
    piece = out_weight.shape[0]

    full_qkv = lax.all_gather(qkv_weight, BOTH, axis=0, tiled=True)
    unit = down_weight.shape[0]
    seq_bits = len(axis_bits("seq"))
    owners = (4,) + (2,) * seq_bits + (unit,)
    by_nearness = (0,) + tuple(range(1, seq_bits + 1))[::-1] + (seq_bits + 1,)

    def reorder(vectors):
        lead = vectors.shape[:-1]
        turn = tuple(range(len(lead))) + tuple(len(lead) + d for d in by_nearness)
        return vectors.reshape(lead + owners).transpose(turn).reshape(vectors.shape)

    down_shard = down_weight.reshape(4, piece, width)
    up_shard = reorder(up_weight).reshape(piece, 4, width).transpose(1, 0, 2)
    up_shard = jnp.concatenate([up_shard, out_weight[None]], axis=0)

    levels = level_rows(ctx_count, noise_level, rows)
    flat_bits = (2,) * len(order)
    bits_clip, bits_seq = len(axis_bits("clip")), len(axis_bits("seq"))
    turn = tuple(range(bits_clip))[::-1] + tuple(range(bits_clip, bits_clip + bits_seq))[::-1] + (len(order),)
    near_levels = levels.reshape(flat_bits + (lines,)).transpose(turn)
    cond_near = condition(near_levels, here, mod_weight.shape[0], width)
    cond = condition(levels, here, mod_weight.shape[0], width)
    cond_late = relative_rows(cond_near, order)
    mod_place = own_place(mod_bias, here)

    def modulate(columns, biases, gates=()):
        weight = mod_weight[:, columns]
        bias = jnp.concatenate([own_place(b, here) for b in biases]).reshape(lines, -1)
        rest = jnp.concatenate([jnp.broadcast_to(mod_place[columns], (lines, weight.shape[1])), bias], axis=1)
        part = jnp.pad(dot(cond_near, weight), ((0, 0), (0, bias.shape[1])))
        line_rows = halve_rows((part.reshape(devices, lines, -1) + rest).reshape(devices * lines, -1), order, gates)
        return line_rows[:, : weight.shape[1]], line_rows[:, weight.shape[1] :].reshape(1, -1)

    def blocks(line_rows):
        return line_rows.reshape(clips, frames, -1, width).transpose(0, 2, 1, 3)

    mod_first, bias_qkv = modulate(slice(0, 2 * width), (qkv_bias,))
    mods_one = blocks(mod_first)

    positions = lax.axis_index("seq") * rows + jnp.arange(rows, dtype=jnp.int32)
    cos_local, sin_local = rotary_lanes(positions, max(span, 256))
    cos_row, sin_row = rotary_lanes(jnp.arange(rows, dtype=jnp.int32), span)
    cos_far, sin_far = rotary_lanes(jnp.arange(seq_devices, dtype=jnp.int32) * rows, span)
    cos_all = (cos_far[:, None] * cos_row[None] - sin_far[:, None] * sin_row[None]).reshape(total, span)
    sin_all = (sin_far[:, None] * cos_row[None] + cos_far[:, None] * sin_row[None]).reshape(total, span)

    def exchange(value):
        return lax.all_to_all(value, "seq", 0, 0, tiled=True)

    def doubled(share, axis, bit, dim=1):
        other = swap_bit(share, axis, bit)
        mine = own_bit(axis, bit) == 0
        pair = jnp.stack([jnp.where(mine, share, other), jnp.where(mine, other, share)], axis=dim)
        return pair.reshape((-1,) + share.shape[1:])

    high_bits, low_bit = axis_bits("seq")[:-1], axis_bits("seq")[-1]
    down_share, up_share = down_shard[None], up_shard[None]
    for axis, bit in high_bits:
        down_share, up_share = doubled(down_share, axis, bit, 0), doubled(up_share, axis, bit)
    full_qkv = after(full_qkv, down_share, up_share)
    up_pair = (up_share, swap_bit(up_share, "clip", 2))
    down_share = doubled(down_share, *low_bit)

    normed, qkv, mixes, fulls, logs, sents = [], [], [], [], [], []
    for c in range(clips):
        weight = full_qkv if c == 0 else after(full_qkv, down_share, up_pair[1])
        sent, normed_c = project(tokens, c, mods_one[c], weight, bias_qkv, cos_local, sin_local, seq_devices)
        normed.append(normed_c)
        if qkv:
            sent = after(sent, qkv[-1])
        qkv.append(exchange(sent))
    backs = []
    for c in range(clips):
        mix, full, log = attend(qkv[c].reshape(total, 3 * span), span)
        mixes.append(mix)
        fulls.append(full)
        logs.append(log)
        backs.append(exchange(after(mix.reshape(seq_devices, rows, span), qkv[-1] if c == 0 else backs[-1])))

    mod_rest, bias_rest = modulate(
        slice(2 * width, 6 * width), (out_bias, up_bias, down_bias), (None, None, normed[-1], mixes[0], mixes[-1])
    )
    mods_two = blocks(mod_rest)
    bias_out = bias_rest[:, :width]
    bias_up = reorder(bias_rest[:, width : 5 * width])
    bias_down = bias_rest[:, 5 * width :]
    def from_clips(pair):
        near, across = [p.reshape((seq_devices // 2, 2) + p.shape[1:]) for p in pair]
        far = swap_bit(after(across, qkv[-1]), "clip", 1)
        return (near, across, swap_bit(near, "clip", 1), far)

    down_shares = from_clips((down_share, swap_bit(down_share, "clip", 2)))
    up_shares = from_clips([doubled(p, *low_bit) for p in up_pair])

    results = []
    d_mixed = []
    for c in range(clips):
        back = after(backs[c], mixes[-1])
        outputs = results[-1][0] if results else None
        results.append(middle(back, tokens, cotangent, c, mods_two[c], up_shares, down_shares, (bias_out, bias_up, bias_down), outputs))
        d_mixed.append(exchange(after(results[c][8], backs[-1] if c == 0 else d_mixed[-1])))

    def late(place):
        return [r[place] for r in results]

    mixed_all, normed_two, active, d_hidden, d_mlp, d_attn = [late(place) for place in (2, 3, 4, 5, 6, 7)]
    def line_sums(sums):
        return sums.transpose(1, 0, 2).reshape(frames, -1)

    def with_bias(lines_now, vectors):
        return jnp.concatenate([jnp.concatenate(lines_now, axis=0), jnp.concatenate(vectors).reshape(lines, -1)], axis=1)

    bias_up_sum = reorder(sum(r[10][0] for r in results))
    bias_pair = sum(r[11] for r in results)
    early = with_bias([line_sums(r[9]) for r in results], [bias_pair[0], bias_up_sum, bias_pair[1]])
    early_rows = lax.all_gather(early, BOTH, axis=0, tiled=True)

    d_qkv, exchanged = [], []
    for c in range(clips):
        if c == clips - 1:
            active = gate(active, *d_qkv, d_mixed[-1])
            down_parts = columns_grad(active, d_mlp)
            down_core = [swap_bit(p, "clip", 1) for p in down_parts[:3]]
            normed_two = gate(normed_two, down_parts[0])
            up_parts = rows_grad([(normed_two, d_hidden), (mixed_all, d_attn)])
            up_core = [swap_bit(p, "clip", 1) for p in up_parts[:2]]
        grad = after(d_mixed[c], results[-1][8] if c == 0 else up_parts[0])
        grad = grad.reshape(total, span)
        d_qkv.append(attend_back(qkv[c].reshape(total, 3 * span), grad, fulls[c], logs[c], cos_all, sin_all, span))
        sent = d_qkv[c].reshape(seq_devices, rows, 3 * span)
        exchanged.append(exchange(after(sent, d_mixed[-1]) if c == 0 else sent))

    down_core = gate(down_core, exchanged[0])
    down_sent = rounded_sum([down_parts[3], down_core[0]])
    down_along = swap_bit(down_sent, "seq", 1)
    up_sent = rounded_sum([up_parts[2], after(up_core[0], exchanged[0])])
    up_across = swap_bit(up_sent, "clip", 2)
    exchanged[0] = after(exchanged[0], down_sent, up_sent)
    exchanged[-1] = after(exchanged[-1], down_along, up_across)

    last = []
    for c in range(clips):
        grads = last[-1][0] if last else None
        last.append(project_back(exchanged[c], full_qkv, tokens, c, mods_one[c][1], results[c][1], grads))
    d_projected = [r[1] for r in last]
    qkv_parts = rows_grad([(normed, d_projected)])
    qkv_core = [swap_bit(p, "clip", 1) for p in qkv_parts[:2]]
    qkv_sent = rounded_sum([qkv_parts[2], qkv_core[0]])
    qkv_across = swap_bit(qkv_sent, "clip", 2)
    near_seq = axis_bits("seq")[::-1]
    down_along, up_across = after(down_along, qkv_sent), after(up_across, qkv_sent)
    down_across = swap_bit(rounded_sum([down_parts[5][0], down_core[2][0], down_along[1]]), "clip", 2)
    grad_up = halve([up_parts[3], up_core[1], up_across], near_seq, 0)
    down_own = sum(a.astype(f32) for a in (down_parts[4][0], down_core[1][0], down_along[0]))
    grad_down = jnp.transpose(halve([down_own, down_across], near_seq[1:], 1))
    grad_qkv = halve([qkv_parts[3], qkv_core[1], qkv_across], near_seq, 0)
    grad_out = grad_up[:, 4 * width :]
    grad_up = reorder(grad_up[:, : 4 * width])
    late_rows = with_bias([line_sums(r[2]) for r in last], [sum(r[3][0] for r in last)])
    late_rows = collect_rows(after(late_rows, qkv_sent), order)
    early_rows = after(early_rows, qkv_sent)

    def own_columns(sums, shard):
        return lax.dynamic_slice_in_dim(sums, here * shard.shape[0], shard.shape[0], 0)

    def spans(all_rows, columns):
        vectors = jnp.sum(all_rows[:, columns:].reshape(devices, -1), axis=0)
        return all_rows[:, :columns], vectors

    late_mod, late_vectors = spans(late_rows, 2 * width)
    early_mod, early_vectors = spans(early_rows, 4 * width)
    grad_mod = jnp.concatenate(
        [
            lax.dot_general(rows_cond.astype(f32), r, TN, precision=highest, preferred_element_type=f32)
            for rows_cond, r in ((cond_late, late_mod), (cond, early_mod))
        ],
        axis=1,
    )
    mod_sum = jnp.concatenate([jnp.sum(late_mod, axis=0), jnp.sum(early_mod, axis=0)])
    return (
        results[-1][0],
        last[-1][0],
        grad_mod,
        own_columns(mod_sum, mod_bias),
        grad_qkv,
        own_columns(late_vectors, qkv_bias),
        grad_out,
        own_columns(early_vectors[:width], out_bias),
        grad_up,
        own_columns(early_vectors[width : 5 * width], up_bias),
        grad_down,
        own_columns(early_vectors[5 * width :], down_bias),
    )


def body_gathered(
    tokens,
    ctx_count,
    noise_level,
    mod_weight,
    mod_bias,
    qkv_weight,
    qkv_bias,
    out_weight,
    out_bias,
    up_weight,
    up_bias,
    down_weight,
    down_bias,
    cotangent,
):
    clips, rows, width = tokens.shape
    seq_devices = lax.axis_size("seq")
    devices = lax.axis_size("clip") * seq_devices
    bits = mesh_bits()
    here = lax.axis_index("clip") * seq_devices + lax.axis_index("seq")
    total = rows * seq_devices
    frames = max(1, rows // PATCHES)
    patch_rows = rows // frames

    full_qkv = lax.all_gather(qkv_weight, BOTH, axis=0, tiled=True)
    full_out = lax.all_gather(out_weight, BOTH, axis=0, tiled=True)
    full_up = lax.all_gather(up_weight, BOTH, axis=0, tiled=True)
    full_down = lax.all_gather(down_weight, BOTH, axis=0, tiled=True)
    biases = (qkv_bias, out_bias, up_bias, down_bias)
    bias_rows = double_rows(jnp.concatenate(biases).astype(f32), bits)
    full_biases = []
    first = 0
    for piece in biases:
        full_biases.append(bias_rows[:, first : first + piece.shape[0]].reshape(1, -1))
        first += piece.shape[0]
    bias_qkv, bias_out, bias_up, bias_down = full_biases

    levels = level_rows(ctx_count, noise_level, rows)
    cond = condition(levels, here, mod_weight.shape[0], width)
    mod_width = mod_weight.shape[1]
    partial = dot(cond, mod_weight) + own_place(mod_bias, here)
    modulation = halve_sum(partial.reshape(devices, clips * frames, mod_width), bits)
    modulation = modulation.reshape(clips, frames, 1, mod_width)

    positions = lax.axis_index("seq") * rows + jnp.arange(rows, dtype=jnp.int32)
    cosine, sine = rotary_lanes(positions, HEAD_DIM)
    key_frame = jnp.arange(total, dtype=jnp.int32) // PATCHES
    allowed = key_frame[None, :] <= (positions // PATCHES)[:, None]

    def flat(value):
        return value.reshape(rows, value.shape[-1])

    def split(value):
        return value.reshape(frames, patch_rows, value.shape[-1])

    def to_heads(value):
        return value.reshape(rows, HEADS, HEAD_DIM).transpose(1, 0, 2)

    saved = []
    for c in range(clips):
        mods = jnp.split(modulation[c], 6, axis=-1)
        tokens_now = split(tokens[c].astype(f32))
        unit, inverse = norm_parts(tokens_now)
        normed = flat((unit * (1.0 + mods[1]) + mods[0]).astype(bf16))
        projected = dot(normed, full_qkv) + bias_qkv
        views = []
        for place in range(3):
            view = to_heads(projected[:, place * width : (place + 1) * width])
            if place < 2:
                    view = view * cosine + jnp.roll(view, HEAD_DIM // 2, -1) * sine
            views.append(view.astype(bf16))
        queries, keys, values = views
        keys = lax.all_gather(keys, "seq", axis=1, tiled=True)
        values = lax.all_gather(values, "seq", axis=1, tiled=True)
        mix, logs = gathered_forward(queries, keys, values, allowed)
        mixed = mix.transpose(1, 0, 2).reshape(rows, width).astype(bf16)
        kept = (queries, keys, values, logs)
        saved.append((mods, tokens_now, unit, inverse, normed, kept, mixed))

    outputs = []
    middle = []
    for c in range(clips):
        mods, tokens_now, unit, inverse, normed, kept, mixed = saved[c]
        _, _, gate_one, shift_two, scale_two, gate_two = mods
        attn_out = split(dot(mixed, full_out) + bias_out)
        resid = tokens_now + gate_one * attn_out
        unit_two, inverse_two = norm_parts(resid)
        normed_two = flat((unit_two * (1.0 + scale_two) + shift_two).astype(bf16))
        hidden = dot(normed_two, full_up) + bias_up
        active_full, gelu_back = jax.vjp(jax.nn.gelu, hidden)
        active = active_full.astype(bf16)
        mlp_out = split(dot(active, full_down) + bias_down)
        outputs.append(flat((resid + gate_two * mlp_out).astype(bf16)))
        grad_out = split(cotangent[c].astype(f32))
        d_mlp = flat((gate_two * grad_out).astype(bf16))
        d_hidden = gelu_back(dot(d_mlp, full_down, NT))[0].astype(bf16)
        d_normed_two = split(dot(d_hidden, full_up, NT))
        d_resid = grad_out + norm_back(unit_two, inverse_two, d_normed_two, scale_two)
        d_attn = flat((gate_one * d_resid).astype(bf16))
        d_mixed = dot(d_attn, full_out, NT).astype(bf16)
        d_early = jnp.concatenate(
            [
                jnp.sum(d_resid * attn_out, axis=1),
                jnp.sum(d_normed_two, axis=1),
                jnp.sum(d_normed_two * unit_two, axis=1),
                jnp.sum(grad_out * mlp_out, axis=1),
            ],
            axis=-1,
        )
        middle.append((mixed, d_attn, normed_two, d_hidden, active, d_mlp, d_resid, d_mixed, d_early))

    def both(place):
        return jnp.concatenate([m[place] for m in middle], axis=0)

    d_attn_all, d_hidden_all, d_mlp_all = both(1), both(3), both(5)
    grad_down = weight_grad(both(4), d_mlp_all)
    grad_up = weight_grad(both(2), d_hidden_all)
    grad_out_weight = weight_grad(both(0), d_attn_all)
    early_rows = lax.all_gather(both(8), BOTH, axis=0, tiled=True)

    inputs_grad = []
    late = []
    projected_grads = []
    for c in range(clips):
        mods, tokens_now, unit, inverse, normed, kept, mixed = saved[c]
        d_resid, d_mixed = middle[c][6], middle[c][7]
        queries, keys, values, logs = kept
        dq, dk, dv = gathered_back(queries, keys, values, to_heads(d_mixed), logs, allowed)
        dk = lax.psum_scatter(dk.astype(bf16), "seq", scatter_dimension=1, tiled=True).astype(f32)
        dv = lax.psum_scatter(dv.astype(bf16), "seq", scatter_dimension=1, tiled=True).astype(f32)
        views = [g * cosine - jnp.roll(g, HEAD_DIM // 2, -1) * sine for g in (dq, dk)] + [dv]
        d_projected = jnp.concatenate([g.transpose(1, 0, 2).reshape(rows, width) for g in views], axis=1).astype(bf16)
        projected_grads.append(d_projected)
        d_normed = split(dot(d_projected, full_qkv, NT))
        inputs_grad.append(flat(d_resid + norm_back(unit, inverse, d_normed, mods[1])))
        late.append(jnp.concatenate([jnp.sum(d_normed, axis=1), jnp.sum(d_normed * unit, axis=1)], axis=-1))

    d_projected_all = jnp.concatenate(projected_grads, axis=0)
    grad_qkv = weight_grad(jnp.concatenate([s[4] for s in saved], axis=0), d_projected_all)
    bias_grads = [
        jnp.sum(g.astype(f32), axis=0).reshape(devices, -1) for g in (d_projected_all, d_attn_all, d_hidden_all, d_mlp_all)
    ]
    bias_sum = halve_sum(jnp.concatenate(bias_grads, axis=1), bits)
    grad_biases = []
    first = 0
    for piece in bias_grads:
        grad_biases.append(bias_sum[first : first + piece.shape[1]])
        first += piece.shape[1]

    late_rows = double_rows(jnp.concatenate(late, axis=0), bits).reshape(-1, 2 * width)
    grad_mod = jnp.concatenate(
        [
            lax.dot_general(cond.astype(f32), r, TN, precision=highest, preferred_element_type=f32)
            for r in (late_rows, early_rows)
        ],
        axis=1,
    )
    mod_sum = jnp.concatenate([jnp.sum(late_rows, axis=0), jnp.sum(early_rows, axis=0)])
    grad_mod_bias = lax.dynamic_slice_in_dim(mod_sum, here * mod_bias.shape[0], mod_bias.shape[0], 0)
    return (
        jnp.stack(outputs),
        jnp.stack(inputs_grad),
        grad_mod,
        grad_mod_bias,
        grad_qkv,
        grad_biases[0],
        grad_out_weight,
        grad_biases[1],
        grad_up,
        grad_biases[2],
        grad_down,
        grad_biases[3],
    )


def solution(mesh):
    by_heads = HEADS % mesh.shape["seq"] == 0
    body = body_by_heads if by_heads else body_gathered
    token_place = P("clip", "seq", None)
    matrix, vector = P(BOTH, None), P(BOTH)
    weights = (matrix, vector) * 5
    return jax.shard_map(
        body,
        mesh=mesh,
        in_specs=(token_place, P("clip"), P("clip", None)) + weights + (token_place,),
        out_specs=(token_place, token_place) + weights,
        check_vma=False,
    )
```

```python
import functools
import math

import jax
import jax.numpy as jnp
from jax import lax
from jax.experimental import pallas as pl
from jax.experimental.pallas import tpu as pltpu
from jax.sharding import PartitionSpec as P

HEADS = 16
HEAD_DIM = 64
FRAMES = 16
PATCHES = 256
BOTH = ("clip", "seq")
NT = (((1,), (1,)), ((), ()))
NN = (((1,), (0,)), ((), ()))
TN = (((0,), (0,)), ((), ()))
bf16 = jnp.bfloat16
f32 = jnp.float32
highest = lax.Precision.HIGHEST


def dot(left, right, dims=NN):
    return lax.dot_general(left, right, dims, preferred_element_type=f32)


def swap_bit(value, axis, bit):
    count = lax.axis_size(axis)
    return lax.ppermute(value, axis, [(i, i ^ bit) for i in range(count)])


def own_bit(axis, bit):
    return lax.shift_right_logical(lax.axis_index(axis), bit.bit_length() - 1) & 1


def axis_bits(axis):
    bits = []
    bit = 1
    while bit < lax.axis_size(axis):
        bits.append((axis, bit))
        bit *= 2
    return bits[::-1]


def exchange_order(bits):
    return sorted(range(len(bits)), key=lambda place: bits[place])


def mesh_bits():
    return axis_bits("clip") + axis_bits("seq")


def halve_sum(parts, bits, wire=f32, hold=None):
    addends = [parts.reshape((2,) * len(bits) + parts.shape[1:])]
    for place in exchange_order(bits):
        axis, bit = bits[place]
        mine = own_bit(axis, bit)
        send = sum(lax.dynamic_index_in_dim(a, 1 - mine, place).astype(f32) for a in addends)
        addends = [lax.dynamic_index_in_dim(a, mine, place) for a in addends]
        received = swap_bit(send.astype(wire), axis, bit)
        if hold is not None and len(addends) == 1:
            received = after(received, hold)
        addends.append(received)
    total = sum(a.astype(f32) for a in addends)
    return total.reshape(total.shape[len(bits) :])


def near_order():
    return axis_bits("clip")[::-1] + axis_bits("seq")[::-1]


def halve_rows(parts, bits, gates=()):
    for place, (axis, bit) in enumerate(bits):
        half = parts.shape[0] // 2
        mine = own_bit(axis, bit)
        keep = lax.dynamic_slice_in_dim(parts, mine * half, half, 0)
        send = lax.dynamic_slice_in_dim(parts, (1 - mine) * half, half, 0)
        other = swap_bit(send, axis, bit)
        if place < len(gates) and gates[place] is not None:
            other = after(other, gates[place])
        parts = keep + other
    return parts


def collect_rows(rows, bits):
    for axis, bit in reversed(bits):
        rows = jnp.concatenate([rows, swap_bit(rows, axis, bit)], axis=0)
    return rows


def relative_rows(rows, bits):
    shape = rows.shape
    rows = rows.reshape((2,) * len(bits) + (-1,) + shape[1:])
    for place, (axis, bit) in enumerate(bits):
        rows = jnp.where(own_bit(axis, bit) == 0, rows, jnp.flip(rows, place))
    return rows.reshape(shape)


def after(value, *others):
    return lax.optimization_barrier((value,) + others)[0]


def double_rows(row, bits):
    rows = row[None]
    for axis, bit in reversed(bits):
        other = swap_bit(rows, axis, bit)
        low = own_bit(axis, bit) == 0
        rows = jnp.concatenate([jnp.where(low, rows, other), jnp.where(low, other, rows)], axis=0)
    return rows


def weight_grad(left, right):
    tokens, rows = left.shape
    quarter = rows // lax.axis_size("clip")
    mine = lax.axis_index("clip")

    def part(flip):
        piece = lax.dynamic_slice_in_dim(left, (mine ^ flip) * quarter, quarter, 1)
        return dot(piece, right, TN)

    far = swap_bit(part(3).astype(bf16), "clip", 1)
    near = swap_bit(part(1).astype(bf16), "clip", 1)
    across = swap_bit((part(2) + far.astype(f32)).astype(bf16), "clip", 2)
    total = part(0) + near.astype(f32) + across.astype(f32)
    return halve_sum(total.reshape((lax.axis_size("seq"), -1, right.shape[1])), axis_bits("seq"), bf16)


def norm_parts(values):
    centre = values - jnp.mean(values, axis=-1, keepdims=True)
    spread = jnp.mean(centre * centre, axis=-1, keepdims=True)
    inverse = lax.rsqrt(spread + 1e-06)
    return centre * inverse, inverse


def norm_back(unit, inverse, grad, scales):
    scaled = grad * (1.0 + scales)
    mean = jnp.mean(scaled, axis=-1, keepdims=True)
    along = jnp.mean(scaled * unit, axis=-1, keepdims=True)
    return inverse * (scaled - mean - unit * along)


def rotary_lanes(positions, width):
    half = HEAD_DIM // 2
    lane = jnp.arange(width, dtype=jnp.int32) % HEAD_DIM
    freqs = jnp.exp(-math.log(10000.0) * 2.0 * (lane % half).astype(f32) / HEAD_DIM)
    angles = positions.astype(f32)[:, None] * freqs[None, :]
    sign = jnp.where(lane < half, -1.0, 1.0).astype(f32)
    return jnp.cos(angles), jnp.sin(angles) * sign[None, :]


def partner(values):
    width = values.shape[1]
    half = HEAD_DIM // 2
    lane = lax.broadcasted_iota(jnp.int32, (1, width), 1) % HEAD_DIM
    return jnp.where(lane < half, pltpu.roll(values, width - half, 1), pltpu.roll(values, half, 1))


def project_kernel(
    token_ref, mod_ref, wq_ref, wk_ref, wv_ref, bq_ref, bk_ref, bv_ref, cos_ref, sin_ref, out_ref, normed_ref, *, span
):
    frames = mod_ref.shape[1]
    patch = token_ref.shape[0] // frames

    @pl.when(pl.program_id(0) == 0)
    def _():
        for f in range(frames):
            rows = slice(f * patch, (f + 1) * patch)
            unit, _ = norm_parts(token_ref[rows, :].astype(f32))
            normed_ref[rows, :] = (unit * (1.0 + mod_ref[1, f : f + 1, :]) + mod_ref[0, f : f + 1, :]).astype(bf16)

    x = normed_ref[...]
    cosine, sine = cos_ref[...], sin_ref[...]
    groups = wq_ref.shape[1] // span
    for place, (w_ref, b_ref) in enumerate(((wq_ref, bq_ref), (wk_ref, bk_ref), (wv_ref, bv_ref))):
        value = dot(x, w_ref[...]) + b_ref[...]
        if place < 2:
            value = value * cosine + partner(value) * sine
        value = value.astype(bf16)
        for g in range(groups):
            out_ref[g, :, place * span : (place + 1) * span] = value[:, g * span : (g + 1) * span]


def whole_block(shape):
    return pl.BlockSpec(shape, lambda j: (0,) * len(shape))


def column_specs(height, block, steps):
    return [pl.BlockSpec((height, block), functools.partial(lambda p, j: (0, p * steps + j), p)) for p in range(3)]


def clip_block(shape, c):
    return pl.BlockSpec((None,) + shape[1:], lambda j: (c,) + (0,) * (len(shape) - 1))


def project(tokens, c, mods, weight, bias, cosine, sine, groups):
    _, rows, width = tokens.shape
    span = width // groups
    block = max(span, 256)
    per_step = block // span
    steps = groups // per_step
    return pl.pallas_call(
        functools.partial(project_kernel, span=span),
        grid=(steps,),
        in_specs=[clip_block(tokens.shape, c), whole_block(mods.shape)]
        + column_specs(width, block, steps)
        + column_specs(1, block, steps)
        + [whole_block((rows, block))] * 2,
        out_specs=(pl.BlockSpec((per_step, rows, 3 * span), lambda j: (j, 0, 0)), whole_block((rows, width))),
        out_shape=(
            jax.ShapeDtypeStruct((groups, rows, 3 * span), bf16),
            jax.ShapeDtypeStruct((rows, width), bf16),
        ),
        compiler_params=pltpu.CompilerParams(vmem_limit_bytes=32 << 20),
        cost_estimate=pl.CostEstimate(
            flops=6 * rows * width * width, bytes_accessed=6 * width * width + 10 * rows * width, transcendentals=0
        ),
        name="project",
    )(tokens, mods, weight, weight, weight, bias, bias, bias, cosine, sine)


def project_back_kernel(
    back_ref, wq_ref, wk_ref, wv_ref, token_ref, scale_ref, resid_ref, *rest, span
):
    grad_ref, proj_ref, sums_ref, bias_ref, acc_ref = rest[-5:]
    frames = scale_ref.shape[0]
    rows_all, width = token_ref.shape
    patch = rows_all // frames
    step = pl.program_id(0)
    block = wq_ref.shape[1]

    @pl.when(step == 0)
    def _():
        acc_ref[...] = jnp.zeros_like(acc_ref)

    for place, w_ref in enumerate((wq_ref, wk_ref, wv_ref)):
        band = slice(place * span, (place + 1) * span)
        piece = jnp.concatenate([back_ref[g, :, band] for g in range(block // span)], axis=1)
        columns = pl.ds(pl.multiple_of(place * width + step * block, block), block)
        proj_ref[:, columns] = piece
        bias_ref[:, columns] = jnp.sum(piece.astype(f32), axis=0, keepdims=True)
        acc_ref[...] += dot(piece, w_ref[...], NT)

    @pl.when(step == pl.num_programs(0) - 1)
    def _():
        for f in range(frames):
            rows = slice(f * patch, (f + 1) * patch)
            unit, inverse = norm_parts(token_ref[rows, :].astype(f32))
            grad = acc_ref[rows, :]
            grad_ref[rows, :] = resid_ref[rows, :] + norm_back(unit, inverse, grad, scale_ref[f : f + 1, :])
            sums_ref[0, f : f + 1, :] = jnp.sum(grad, axis=0, keepdims=True)
            sums_ref[1, f : f + 1, :] = jnp.sum(grad * unit, axis=0, keepdims=True)


def project_back(back, weight, tokens, c, scales, d_resid, grads):
    groups, rows, _ = back.shape
    width = tokens.shape[2]
    span = width // groups
    block = max(span, 256)
    per_step = block // span
    steps = groups // per_step
    earlier = [] if grads is None else [grads]
    return pl.pallas_call(
        functools.partial(project_back_kernel, span=span),
        grid=(steps,),
        in_specs=[pl.BlockSpec((per_step, rows, 3 * span), lambda j: (j, 0, 0))]
        + column_specs(width, block, steps)
        + [clip_block(tokens.shape, c), whole_block(scales.shape), whole_block((rows, width))]
        + [pl.BlockSpec(memory_space=pl.ANY)] * len(earlier),
        out_specs=(
            clip_block(tokens.shape, c),
            whole_block((rows, 3 * width)),
            whole_block((2,) + scales.shape),
            whole_block((1, 3 * width)),
        ),
        out_shape=(
            jax.ShapeDtypeStruct(tokens.shape, f32),
            jax.ShapeDtypeStruct((rows, 3 * width), bf16),
            jax.ShapeDtypeStruct((2,) + scales.shape, f32),
            jax.ShapeDtypeStruct((1, 3 * width), f32),
        ),
        input_output_aliases={7: 0} if earlier else {},
        scratch_shapes=[pltpu.VMEM((rows, width), f32)],
        compiler_params=pltpu.CompilerParams(vmem_limit_bytes=40 << 20),
        cost_estimate=pl.CostEstimate(
            flops=6 * rows * width * width, bytes_accessed=6 * width * width + 22 * rows * width, transcendentals=0
        ),
        name="project_back",
    )(back, weight, weight, weight, tokens, scales, d_resid, *earlier)


GELU_RATE = math.sqrt(2.0 / math.pi)
GELU_CUBE = 0.044715


def middle_kernel(clip_ref, back_ref, token_ref, cot_ref, mod_ref, bo_ref, bup_ref, bdown_ref, *refs):
    wo_refs, up_refs, down_refs = refs[0:4], refs[4:8], refs[8:12]
    (
        out_ref,
        dres_ref,
        mixed_ref,
        normed_ref,
        act_ref,
        dhid_ref,
        dmlp_ref,
        dattn_ref,
        dmix_ref,
        sums_ref,
        bup_sum_ref,
        bsum_ref,
        attn_ref,
        res_ref,
        mlp_ref,
        dn_ref,
        wo_ref,
        up_ref,
        down_ref,
    ) = refs[-19:]
    groups, rows_all, span = back_ref.shape
    width = token_ref.shape[1]
    quarter = width // 4
    frames = mod_ref.shape[1]
    patch = rows_all // frames
    step = pl.program_id(0)
    mine = clip_ref[0]

    def owner_rows(place):
        return pl.ds(pl.multiple_of((mine ^ FLIPS[place]) * quarter, quarter), quarter)

    @pl.when(step == 0)
    def _():
        for place in range(4):
            wo_ref[owner_rows(place), :] = wo_refs[place][...].reshape(quarter, width)
        for g in range(groups):
            mixed_ref[:, g * span : (g + 1) * span] = back_ref[g]
        attn_ref[...] = dot(mixed_ref[...], wo_ref[...]) + bo_ref[...]
        for f in range(frames):
            rows = slice(f * patch, (f + 1) * patch)
            resid = token_ref[rows, :].astype(f32) + mod_ref[0, f : f + 1, :] * attn_ref[rows, :]
            res_ref[rows, :] = resid
            unit, _ = norm_parts(resid)
            normed_ref[rows, :] = (unit * (1.0 + mod_ref[2, f : f + 1, :]) + mod_ref[1, f : f + 1, :]).astype(bf16)
            dmlp_ref[rows, :] = (mod_ref[3, f : f + 1, :] * cot_ref[rows, :].astype(f32)).astype(bf16)
        mlp_ref[...] = jnp.zeros_like(mlp_ref)
        dn_ref[...] = jnp.zeros_like(dn_ref)

    for place in range(4):
        up_ref[owner_rows(place), :] = up_refs[place][...].reshape(quarter, -1)

        @pl.when(step // 2 == place)
        def _(place=place):
            down_ref[...] = down_refs[place][...].reshape(-1, width)

    up = up_ref[...]
    down = down_ref[...]
    hidden = dot(normed_ref[...], up) + bup_ref[...]
    square = hidden * hidden
    bend = jnp.tanh(GELU_RATE * (hidden + GELU_CUBE * (square * hidden)))
    share = 0.5 * (1.0 + bend)
    active = (hidden * share).astype(bf16)
    act_ref[...] = active
    mlp_ref[...] += dot(active, down)
    slope = share + 0.5 * hidden * (1.0 - bend * bend) * (GELU_RATE + (3.0 * GELU_RATE * GELU_CUBE) * square)
    d_hidden = (dot(dmlp_ref[...], down, NT) * slope).astype(bf16)
    dhid_ref[...] = d_hidden
    bup_sum_ref[...] = jnp.sum(d_hidden.astype(f32), axis=0, keepdims=True)
    dn_ref[...] += dot(d_hidden, up, NT)

    @pl.when(step == pl.num_programs(0) - 1)
    def _():
        bsum = None
        for f in range(frames):
            rows = slice(f * patch, (f + 1) * patch)
            resid = res_ref[rows, :]
            mlp = mlp_ref[rows, :] + bdown_ref[...]
            out_ref[rows, :] = (resid + mod_ref[3, f : f + 1, :] * mlp).astype(bf16)
            cot = cot_ref[rows, :].astype(f32)
            sums_ref[3, f : f + 1, :] = jnp.sum(cot * mlp, axis=0, keepdims=True)
            unit, inverse = norm_parts(resid)
            grad = dn_ref[rows, :]
            sums_ref[1, f : f + 1, :] = jnp.sum(grad, axis=0, keepdims=True)
            sums_ref[2, f : f + 1, :] = jnp.sum(grad * unit, axis=0, keepdims=True)
            d_resid = cot + norm_back(unit, inverse, grad, mod_ref[2, f : f + 1, :])
            dres_ref[rows, :] = d_resid
            sums_ref[0, f : f + 1, :] = jnp.sum(d_resid * attn_ref[rows, :], axis=0, keepdims=True)
            d_attn = (mod_ref[0, f : f + 1, :] * d_resid).astype(bf16)
            dattn_ref[rows, :] = d_attn
            term = jnp.concatenate(
                [
                    jnp.sum(d_attn.astype(f32), axis=0, keepdims=True),
                    jnp.sum(dmlp_ref[rows, :].astype(f32), axis=0, keepdims=True),
                ],
                axis=0,
            )
            bsum = term if bsum is None else bsum + term
        bsum_ref[...] = bsum
        d_mixed = dot(dattn_ref[...], wo_ref[...], NT).astype(bf16)
        for g in range(groups):
            dmix_ref[g] = d_mixed[:, g * span : (g + 1) * span]


FLIPS = (0, 2, 1, 3)


def middle(back, tokens, cot, c, mods, up_shares, down_shares, biases, outputs):
    groups, rows, span = back.shape
    _, _, width = tokens.shape
    high, low, _, piece, _ = up_shares[0].shape
    hidden = 4 * width
    steps = 8
    block = hidden // steps
    bias_out, bias_up, bias_down = biases
    mine = lax.axis_index("clip").astype(jnp.int32)[None]
    earlier = [] if outputs is None else [outputs]

    def fixed(shape, **options):
        return pl.BlockSpec(shape, lambda j, q: (0,) * len(shape), **options)

    def clip_part(shape):
        return pl.BlockSpec((None,) + shape[1:], lambda j, q: (c,) + (0,) * (len(shape) - 1))

    def unit_block(j, q):
        owner = q[0] ^ jnp.where(j // 2 == 1, 2, jnp.where(j // 2 == 2, 1, j // 2))
        return owner, j % 2

    def up_index(j, q):
        owner, half = unit_block(j, q)
        return (0, 0, owner, 0, half)

    def hidden_index(j, q):
        owner, half = unit_block(j, q)
        return (0, owner * 2 + half)

    def down_index(place, j, q):
        return (0, jnp.clip(j - 2 * place, 0, 1), 0, 0, 0)

    token_block = fixed((rows, width))
    hidden_block = pl.BlockSpec((rows, block), hidden_index)
    out_spec = [
        pl.BlockSpec((high, low, 1, piece, width), lambda j, q: (0, 0, 4, 0, 0), pipeline_mode=pl.Buffered(1)) for _ in range(4)
    ]
    up_spec = [pl.BlockSpec((high, low, 1, piece, block), up_index) for _ in range(4)]
    down_spec = [
        pl.BlockSpec((high, 1, 4, piece, width), functools.partial(down_index, place)) for place in range(4)
    ]
    return pl.pallas_call(
        middle_kernel,
        grid_spec=pltpu.PrefetchScalarGridSpec(
            num_scalar_prefetch=1,
            grid=(steps,),
            in_specs=[
                fixed(back.shape),
                clip_part(tokens.shape),
                clip_part(tokens.shape),
                fixed(mods.shape),
                fixed((1, width)),
                pl.BlockSpec((1, block), hidden_index),
                fixed((1, width)),
            ]
            + out_spec
            + up_spec
            + down_spec
            + [pl.BlockSpec(memory_space=pl.ANY)] * len(earlier),
            out_specs=(
                clip_part(tokens.shape),
                token_block,
                token_block,
                token_block,
                hidden_block,
                hidden_block,
                token_block,
                token_block,
                fixed(back.shape),
                fixed(mods.shape),
                pl.BlockSpec((1, block), hidden_index),
                fixed((2, width)),
            ),
            scratch_shapes=[pltpu.VMEM((rows, width), f32)] * 4
            + [pltpu.VMEM((width, width), bf16), pltpu.VMEM((width, block), bf16), pltpu.VMEM((block, width), bf16)],
        ),
        out_shape=(
            jax.ShapeDtypeStruct(tokens.shape, bf16),
            jax.ShapeDtypeStruct((rows, width), f32),
            jax.ShapeDtypeStruct((rows, width), bf16),
            jax.ShapeDtypeStruct((rows, width), bf16),
            jax.ShapeDtypeStruct((rows, hidden), bf16),
            jax.ShapeDtypeStruct((rows, hidden), bf16),
            jax.ShapeDtypeStruct((rows, width), bf16),
            jax.ShapeDtypeStruct((rows, width), bf16),
            jax.ShapeDtypeStruct(back.shape, bf16),
            jax.ShapeDtypeStruct(mods.shape, f32),
            jax.ShapeDtypeStruct((1, hidden), f32),
            jax.ShapeDtypeStruct((2, width), f32),
        ),
        input_output_aliases={20: 0} if earlier else {},
        compiler_params=pltpu.CompilerParams(vmem_limit_bytes=60 << 20),
        cost_estimate=pl.CostEstimate(
            flops=4 * rows * width * width, bytes_accessed=2 * width * width + 5 * rows * width, transcendentals=rows * width
        ),
        name="middle",
    )(mine, back, tokens, cot, mods, bias_out, bias_up, bias_down, *up_shares, *up_shares, *down_shares, *earlier)


def near_place(place, count):
    bits = count.bit_length() - 1
    return sum(((place >> b) & 1) << (bits - 1 - b) for b in range(bits))


def weight_grad_kernel(index_ref, *refs, clips, counts, widths, owners, swapped):
    outs = refs[-1 - len(COLUMN_PLACES if swapped else ROW_FLIPS) : -1]
    flat_ref = refs[-1]
    step = pl.program_id(0)
    first, taken = 0, 0
    for count, steps in zip(counts, widths):
        left, right = refs[taken : taken + clips * count], refs[taken + clips * count : taken + clips * (count + 1)]
        taken += clips * (count + 1)
        rows, height = left[0].shape
        piece = height // owners

        @pl.when(step == first)
        def _(left=left, count=count, rows=rows, height=height, piece=piece):
            for c in range(clips):
                for i in range(count):
                    flat = jnp.transpose(left[c * count + i][...])
                    for owner in range(owners):
                        place = i * height + near_place(owner, owners) * piece
                        flat_ref[place : place + piece, c * rows : (c + 1) * rows] = flat[owner * piece : (owner + 1) * piece]

        @pl.when((step >= first) & (step < first + steps))
        def _(right=right, rows=rows):
            total = dot(flat_ref[:, 0:rows], right[0][...])
            for c in range(1, clips):
                total += dot(flat_ref[:, c * rows : (c + 1) * rows], right[c][...])
            total = total.astype(bf16)
            if swapped:
                for ref, (start, blocks) in zip(outs, COLUMN_PLACES):

                    @pl.when((step >= start) & (step < start + blocks))
                    def _(ref=ref):
                        ref[0] = total

            else:
                height = total.shape[0] // len(outs)
                for place, ref in enumerate(outs):
                    ref[...] = total[place * height : (place + 1) * height]

        first += steps


def weight_grad_call(in_specs, operands, indices, steps, shapes, specs, width, depth, **options):
    return pl.pallas_call(
        functools.partial(weight_grad_kernel, **options),
        grid_spec=pltpu.PrefetchScalarGridSpec(
            num_scalar_prefetch=1,
            grid=(steps,),
            in_specs=in_specs,
            out_specs=specs,
            scratch_shapes=[pltpu.VMEM((width, depth), bf16)],
        ),
        out_shape=tuple(jax.ShapeDtypeStruct(shape, bf16) for shape in shapes),
        compiler_params=pltpu.CompilerParams(vmem_limit_bytes=60 << 20),
        cost_estimate=pl.CostEstimate(
            flops=1024 * steps * width * depth, bytes_accessed=steps * 1024 * (width + depth) + 4 * width * depth, transcendentals=0
        ),
        name="weight_grad",
    )(indices, *operands)


BLOCK = 512
ROW_FLIPS = (3, 1, 2, 0)
COLUMN_PLACES = ((0, 2), (2, 1), (3, 1), (4, 2), (6, 1), (7, 1))


def rows_grad(pairs):
    clips = len(pairs[0][0])
    rows, width = pairs[0][0][0].shape
    height = width // 4
    mine = mine_on("clip")
    widths = [right[0].shape[1] // BLOCK for _, right in pairs]
    in_specs, operands = [], []
    first = 0
    for (left, right), steps in zip(pairs, widths):
        for array in left:
            for i in range(4):
                in_specs.append(pl.BlockSpec((rows, height), functools.partial(lambda i, j, q: (0, q[i]), i)))
                operands.append(array)
        where = functools.partial(lambda first, steps, j, q: (0, jnp.clip(j - first, 0, steps - 1)), first, steps)
        in_specs += [pl.BlockSpec((rows, BLOCK), where)] * clips
        operands += right
        first += steps
    shape = (height, first * BLOCK)
    spec = pl.BlockSpec((height, BLOCK), lambda j, q: (0, j))
    return weight_grad_call(
        in_specs,
        operands,
        jnp.stack([mine ^ flip for flip in ROW_FLIPS]),
        first,
        [shape] * 4,
        [spec] * 4,
        width,
        clips * rows,
        clips=clips,
        counts=[4] * len(pairs),
        widths=widths,
        owners=lax.axis_size("seq"),
        swapped=False,
    )


def columns_grad(left, right):
    clips = len(left)
    rows, width = right[0].shape
    mine, low = mine_on("clip"), mine_on("seq") & 1

    def block(clip_flip, low_flip):
        return (mine ^ clip_flip) * 2 + (low ^ low_flip)

    flips = ((0, 1), (2, 1), (0, 0), (2, 0))
    indices = jnp.stack([block(c ^ 1, s) for c, s in flips] + [block(c, s) for c, s in flips])
    in_specs = [pl.BlockSpec((rows, width), lambda j, q: (0, 0))] * clips
    in_specs += [pl.BlockSpec((rows, BLOCK), lambda j, q: (0, q[j]))] * clips
    def place_index(start, blocks, j, q):
        return (jnp.clip(j - start, 0, blocks - 1), 0, 0)

    return weight_grad_call(
        in_specs,
        right + left,
        indices,
        8,
        [(blocks, width, BLOCK) for _, blocks in COLUMN_PLACES],
        [pl.BlockSpec((1, width, BLOCK), functools.partial(place_index, *place)) for place in COLUMN_PLACES],
        width,
        clips * rows,
        clips=clips,
        counts=[1],
        widths=[8],
        owners=1,
        swapped=True,
    )


def mine_on(axis):
    return lax.axis_index(axis).astype(jnp.int32)


def rounded_sum(addends):
    return sum(a.astype(f32) for a in addends).astype(bf16)


def halve(addends, bits, dim, trace=None):
    for axis, bit in bits:
        half = addends[0].shape[dim] // 2
        mine = own_bit(axis, bit)
        send = rounded_sum([lax.dynamic_slice_in_dim(a, (1 - mine) * half, half, dim) for a in addends])
        addends = [lax.dynamic_slice_in_dim(a, mine * half, half, dim) for a in addends]
        received = swap_bit(send, axis, bit)
        if trace is not None:
            trace.append((send, received))
        addends.append(received)
    return sum(a.astype(f32) for a in addends)


def gate(arrays, *others):
    return list(lax.optimization_barrier((tuple(arrays), others))[0])


def height_of(pairs, parts):
    return pairs[0][0][0].shape[1] // parts


def attend_kernel(qkv_ref, mix_ref, full_ref, log_ref, vt_ref, *, total, span, block):
    heads = span // HEAD_DIM
    head = lax.broadcasted_iota(jnp.int32, (1, span), 1) // HEAD_DIM
    key_frame = lax.broadcasted_iota(jnp.int32, (block, block), 0) // PATCHES
    query_frame = lax.broadcasted_iota(jnp.int32, (block, block), 1) // PATCHES
    kept = key_frame <= query_frame

    def flip(j, carry):
        rows = pl.ds(pl.multiple_of(j * block, block), block)
        vt_ref[:, rows] = jnp.transpose(qkv_ref[rows, 2 * span : 3 * span])
        return carry

    lax.fori_loop(0, total // block, flip, 0)

    def query_block(i, carry):
        rows = pl.ds(pl.multiple_of(i * block, block), block)
        query = qkv_ref[rows, 0:span] * jnp.asarray(HEAD_DIM**-0.5, bf16)
        queries = [jnp.where(head == h, query, jnp.zeros_like(query)) for h in range(heads)]

        def step(j, state, masked):
            peaks, sums, mixes = state
            columns = pl.ds(pl.multiple_of(j * block, block), block)
            key = qkv_ref[columns, span : 2 * span]
            new = ([], [], [])
            for h in range(heads):
                scores = dot(key, queries[h], NT)
                if masked:
                    scores = jnp.where(kept, scores, -1e30)
                peak = jnp.maximum(peaks[h], jnp.max(scores, axis=0, keepdims=True))
                raised = jnp.exp(scores - peak)
                fade = jnp.exp(peaks[h] - peak)
                new[0].append(peak)
                new[1].append(fade * sums[h] + jnp.sum(raised, axis=0, keepdims=True))
                term = dot(vt_ref[h * HEAD_DIM : (h + 1) * HEAD_DIM, columns], raised.astype(bf16))
                new[2].append(mixes[h] * fade + term)
            return tuple(map(tuple, new))

        state = (
            tuple(jnp.full((1, block), -1e30, f32) for _ in range(heads)),
            tuple(jnp.zeros((1, block), f32) for _ in range(heads)),
            tuple(jnp.zeros((HEAD_DIM, block), f32) for _ in range(heads)),
        )
        state = lax.fori_loop(0, i, lambda j, s: step(j, s, False), state)
        peaks, sums, mixes = step(i, state, True)
        mixed = jnp.transpose(jnp.concatenate([mixes[h] / sums[h] for h in range(heads)], axis=0))
        full_ref[rows, :] = mixed
        mix_ref[rows, :] = mixed.astype(bf16)
        for h in range(heads):
            log_ref[h : h + 1, rows] = peaks[h] + jnp.log(sums[h])
        return carry

    lax.fori_loop(0, total // block, query_block, 0)


def attend(qkv, span):
    total = qkv.shape[0]
    heads = span // HEAD_DIM
    block = min(1024, total)
    return pl.pallas_call(
        functools.partial(attend_kernel, total=total, span=span, block=block),
        out_shape=(
            jax.ShapeDtypeStruct((total, span), bf16),
            jax.ShapeDtypeStruct((total, span), f32),
            jax.ShapeDtypeStruct((heads, total), f32),
        ),
        scratch_shapes=[pltpu.VMEM((span, total), bf16)],
        compiler_params=pltpu.CompilerParams(vmem_limit_bytes=60 << 20),
        cost_estimate=pl.CostEstimate(
            flops=8 * total * total * span, bytes_accessed=12 * total * span, transcendentals=total * total * heads // 2
        ),
        name="attend",
    )(qkv)


def attend_back_kernel(
    qkv_ref, grad_ref, full_ref, log_ref, cos_ref, sin_ref, out_ref, dq_ref, dk_ref, dv_ref, along_ref, *, total, span, block
):
    heads = span // HEAD_DIM
    scale = HEAD_DIM**-0.5
    head = lax.broadcasted_iota(jnp.int32, (1, span), 1) // HEAD_DIM
    blocks = total // block
    dq_ref[...] = jnp.zeros_like(dq_ref)

    def only(value, h):
        return jnp.where(head == h, value, jnp.zeros_like(value))

    def lead(i, carry):
        rows = pl.ds(pl.multiple_of(i * block, block), block)
        product = jnp.transpose(grad_ref[rows, :].astype(f32) * full_ref[rows, :])
        for h in range(heads):
            along_ref[h : h + 1, rows] = jnp.sum(product[h * HEAD_DIM : (h + 1) * HEAD_DIM], axis=0, keepdims=True)
        return carry

    lax.fori_loop(0, blocks, lead, 0)

    def key_block(j, carry):
        first = pl.multiple_of(j * block, block)
        columns = pl.ds(first, block)
        key = qkv_ref[columns, span : 2 * span]
        value = qkv_ref[columns, 2 * span : 3 * span]
        key_flat = jnp.transpose(key)
        dk_ref[...] = jnp.zeros_like(dk_ref)
        dv_ref[...] = jnp.zeros_like(dv_ref)

        def tile(rows, keys, h, query_h, grad_h):
            band = slice(h * HEAD_DIM, (h + 1) * HEAD_DIM)
            probs = jnp.exp(dot(key[:keys], query_h, NT) - log_ref[h : h + 1, rows])
            d_probs = dot(value[:keys], grad_h, NT)
            d_scores = (probs * (d_probs - along_ref[h : h + 1, rows])).astype(bf16)
            dq_ref[band, rows] += dot(key_flat[band, :keys], d_scores)
            return dot(probs.astype(bf16), grad_h), dot(d_scores, query_h)

        def heads_of(rows):
            query = qkv_ref[rows, 0:span] * jnp.asarray(scale, bf16)
            grad = grad_ref[rows, :]
            return [(h, only(query, h), only(grad, h)) for h in range(heads)]

        for f in range(block // PATCHES):
            rows = pl.ds(pl.multiple_of(first + f * PATCHES, PATCHES), PATCHES)
            keys = (f + 1) * PATCHES
            for h, query_h, grad_h in heads_of(rows):
                dv, dk = tile(rows, keys, h, query_h, grad_h)
                dv_ref[:keys] += dv
                dk_ref[:keys] += dk

        def later(i, c):
            rows = pl.ds(pl.multiple_of(i * block, block), block)
            terms = [tile(rows, block, h, query_h, grad_h) for h, query_h, grad_h in heads_of(rows)]
            dv_ref[...] += sum(t[0] for t in terms)
            dk_ref[...] += sum(t[1] for t in terms)
            return c

        lax.fori_loop(j + 1, blocks, later, 0)
        dk = dk_ref[...]
        out_ref[columns, span : 2 * span] = (dk * cos_ref[columns, :] - partner(dk) * sin_ref[columns, :]).astype(bf16)
        out_ref[columns, 2 * span : 3 * span] = dv_ref[...].astype(bf16)
        return carry

    lax.fori_loop(0, blocks, key_block, 0)

    def last(i, carry):
        rows = pl.ds(pl.multiple_of(i * block, block), block)
        dq = jnp.transpose(dq_ref[:, rows]) * scale
        out_ref[rows, 0:span] = (dq * cos_ref[rows, :] - partner(dq) * sin_ref[rows, :]).astype(bf16)
        return carry

    lax.fori_loop(0, blocks, last, 0)


def attend_back(qkv, grad, full, logs, cosine, sine, span):
    total = qkv.shape[0]
    heads = span // HEAD_DIM
    block = min(1024, total)
    return pl.pallas_call(
        functools.partial(attend_back_kernel, total=total, span=span, block=block),
        out_shape=jax.ShapeDtypeStruct((total, 3 * span), bf16),
        scratch_shapes=[
            pltpu.VMEM((span, total), f32),
            pltpu.VMEM((block, span), f32),
            pltpu.VMEM((block, span), f32),
            pltpu.VMEM((heads, total), f32),
        ],
        compiler_params=pltpu.CompilerParams(vmem_limit_bytes=60 << 20),
        cost_estimate=pl.CostEstimate(
            flops=20 * total * total * span, bytes_accessed=26 * total * span, transcendentals=total * total * heads // 2
        ),
        name="attend_back",
    )(qkv, grad, full, logs, cosine, sine)


def gathered_forward(queries, keys, values, allowed):
    def one(pieces):
        q, k, v = pieces
        scores = jnp.where(allowed, dot(q, k, NT) * HEAD_DIM**-0.5, -1e30)
        peak = jnp.max(scores, axis=-1, keepdims=True)
        raised = jnp.exp(scores - peak)
        totals = jnp.sum(raised, axis=-1, keepdims=True)
        return dot((raised / totals).astype(bf16), v), peak + jnp.log(totals)

    return lax.map(one, (queries, keys, values))


def gathered_back(queries, keys, values, grads, logs, allowed):
    scale = HEAD_DIM**-0.5

    def one(pieces):
        q, k, v, grad, log = pieces
        scores = jnp.where(allowed, dot(q, k, NT) * scale, -1e30)
        probs = jnp.exp(scores - log)
        d_probs = dot(grad, v, NT)
        centre = jnp.sum(probs * d_probs, axis=-1, keepdims=True)
        d_scores = (probs * (d_probs - centre)).astype(bf16)
        dv = dot(probs.astype(bf16), grad, TN)
        return dot(d_scores, k) * scale, dot(d_scores, q, TN) * scale, dv

    return lax.map(one, (queries, keys, values, grads, logs))


def level_rows(ctx_count, noise_level, rows):
    clips = ctx_count.shape[0]
    seq_devices = lax.axis_size("seq")
    plan = jnp.concatenate([ctx_count[:, None], noise_level], axis=1)
    plan = double_rows(plan, axis_bits("clip"))
    levels = jnp.where(jnp.arange(FRAMES, dtype=jnp.int32) < plan[..., :1], 0, plan[..., 1:])
    if rows < PATCHES:
        levels = jnp.repeat(levels, PATCHES // rows, axis=-1)
    frames = max(1, rows // PATCHES)
    levels = levels.reshape(-1, clips, seq_devices, frames).transpose(0, 2, 1, 3)
    return levels.reshape(-1, seq_devices, clips * frames)


def condition(levels, here, depth, width):
    half_width = width // 2
    feature = here * depth + jnp.arange(depth, dtype=jnp.int32)
    low_half = feature < half_width
    freqs = jnp.exp(-math.log(10000.0) * jnp.where(low_half, feature, feature - half_width).astype(f32) / half_width)
    angles = levels.reshape(-1, 1).astype(f32) * freqs
    return jax.nn.silu(jnp.where(low_half, jnp.sin(angles), jnp.cos(angles))).astype(bf16)


def own_place(shard, here):
    count = lax.axis_size("clip") * lax.axis_size("seq")
    whole = jnp.zeros((count * shard.shape[0],), f32)
    return lax.dynamic_update_slice_in_dim(whole, shard.astype(f32), here * shard.shape[0], 0)


def body_by_heads(
    tokens,
    ctx_count,
    noise_level,
    mod_weight,
    mod_bias,
    qkv_weight,
    qkv_bias,
    out_weight,
    out_bias,
    up_weight,
    up_bias,
    down_weight,
    down_bias,
    cotangent,
):
    clips, rows, width = tokens.shape
    seq_devices = lax.axis_size("seq")
    devices = lax.axis_size("clip") * seq_devices
    order = near_order()
    here = lax.axis_index("clip") * seq_devices + lax.axis_index("seq")
    total = rows * seq_devices
    frames = max(1, rows // PATCHES)
    span = width // seq_devices
    lines = clips * frames
    piece = out_weight.shape[0]

    full_qkv = lax.all_gather(qkv_weight, BOTH, axis=0, tiled=True)
    unit = down_weight.shape[0]
    seq_bits = len(axis_bits("seq"))
    owners = (4,) + (2,) * seq_bits + (unit,)
    by_nearness = (0,) + tuple(range(1, seq_bits + 1))[::-1] + (seq_bits + 1,)

    def reorder(vectors):
        lead = vectors.shape[:-1]
        turn = tuple(range(len(lead))) + tuple(len(lead) + d for d in by_nearness)
        return vectors.reshape(lead + owners).transpose(turn).reshape(vectors.shape)

    down_shard = down_weight.reshape(4, piece, width)
    up_shard = reorder(up_weight).reshape(piece, 4, width).transpose(1, 0, 2)
    up_shard = jnp.concatenate([up_shard, out_weight[None]], axis=0)

    levels = level_rows(ctx_count, noise_level, rows)
    flat_bits = (2,) * len(order)
    bits_clip, bits_seq = len(axis_bits("clip")), len(axis_bits("seq"))
    turn = tuple(range(bits_clip))[::-1] + tuple(range(bits_clip, bits_clip + bits_seq))[::-1] + (len(order),)
    near_levels = levels.reshape(flat_bits + (lines,)).transpose(turn)
    cond_near = condition(near_levels, here, mod_weight.shape[0], width)
    cond = condition(levels, here, mod_weight.shape[0], width)
    cond_late = relative_rows(cond_near, order)
    mod_place = own_place(mod_bias, here)

    def modulate(columns, biases, gates=()):
        weight = mod_weight[:, columns]
        bias = jnp.concatenate([own_place(b, here) for b in biases]).reshape(lines, -1)
        rest = jnp.concatenate([jnp.broadcast_to(mod_place[columns], (lines, weight.shape[1])), bias], axis=1)
        part = jnp.pad(dot(cond_near, weight), ((0, 0), (0, bias.shape[1])))
        line_rows = halve_rows((part.reshape(devices, lines, -1) + rest).reshape(devices * lines, -1), order, gates)
        return line_rows[:, : weight.shape[1]], line_rows[:, weight.shape[1] :].reshape(1, -1)

    def blocks(line_rows):
        return line_rows.reshape(clips, frames, -1, width).transpose(0, 2, 1, 3)

    mod_first, bias_qkv = modulate(slice(0, 2 * width), (qkv_bias,))
    mods_one = blocks(mod_first)

    positions = lax.axis_index("seq") * rows + jnp.arange(rows, dtype=jnp.int32)
    cos_local, sin_local = rotary_lanes(positions, max(span, 256))
    cos_row, sin_row = rotary_lanes(jnp.arange(rows, dtype=jnp.int32), span)
    cos_far, sin_far = rotary_lanes(jnp.arange(seq_devices, dtype=jnp.int32) * rows, span)
    cos_all = (cos_far[:, None] * cos_row[None] - sin_far[:, None] * sin_row[None]).reshape(total, span)
    sin_all = (sin_far[:, None] * cos_row[None] + cos_far[:, None] * sin_row[None]).reshape(total, span)

    def exchange(value):
        return lax.all_to_all(value, "seq", 0, 0, tiled=True)

    def doubled(share, axis, bit, dim=1):
        other = swap_bit(share, axis, bit)
        mine = own_bit(axis, bit) == 0
        pair = jnp.stack([jnp.where(mine, share, other), jnp.where(mine, other, share)], axis=dim)
        return pair.reshape((-1,) + share.shape[1:])

    high_bits, low_bit = axis_bits("seq")[:-1], axis_bits("seq")[-1]
    down_share, up_share = down_shard[None], up_shard[None]
    for axis, bit in high_bits:
        down_share, up_share = doubled(down_share, axis, bit, 0), doubled(up_share, axis, bit)
    full_qkv = after(full_qkv, down_share, up_share)
    up_pair = (up_share, swap_bit(up_share, "clip", 2))
    down_share = doubled(down_share, *low_bit)

    normed, qkv, mixes, fulls, logs, sents = [], [], [], [], [], []
    for c in range(clips):
        weight = full_qkv if c == 0 else after(full_qkv, down_share, up_pair[1])
        sent, normed_c = project(tokens, c, mods_one[c], weight, bias_qkv, cos_local, sin_local, seq_devices)
        normed.append(normed_c)
        if qkv:
            sent = after(sent, qkv[-1])
        qkv.append(exchange(sent))
    backs = []
    for c in range(clips):
        mix, full, log = attend(qkv[c].reshape(total, 3 * span), span)
        mixes.append(mix)
        fulls.append(full)
        logs.append(log)
        backs.append(exchange(after(mix.reshape(seq_devices, rows, span), qkv[-1] if c == 0 else backs[-1])))

    mod_rest, bias_rest = modulate(
        slice(2 * width, 6 * width), (out_bias, up_bias, down_bias), (None, None, normed[-1], mixes[0], mixes[-1])
    )
    mods_two = blocks(mod_rest)
    bias_out = bias_rest[:, :width]
    bias_up = reorder(bias_rest[:, width : 5 * width])
    bias_down = bias_rest[:, 5 * width :]
    def from_clips(pair):
        near, across = [p.reshape((seq_devices // 2, 2) + p.shape[1:]) for p in pair]
        far = swap_bit(after(across, qkv[-1]), "clip", 1)
        return (near, across, swap_bit(near, "clip", 1), far)

    down_shares = from_clips((down_share, swap_bit(down_share, "clip", 2)))
    up_shares = from_clips([doubled(p, *low_bit) for p in up_pair])

    results = []
    d_mixed = []
    for c in range(clips):
        back = after(backs[c], mixes[-1])
        outputs = results[-1][0] if results else None
        results.append(middle(back, tokens, cotangent, c, mods_two[c], up_shares, down_shares, (bias_out, bias_up, bias_down), outputs))
        d_mixed.append(exchange(after(results[c][8], backs[-1] if c == 0 else d_mixed[-1])))

    def late(place):
        return [r[place] for r in results]

    mixed_all, normed_two, active, d_hidden, d_mlp, d_attn = [late(place) for place in (2, 3, 4, 5, 6, 7)]
    def line_sums(sums):
        return sums.transpose(1, 0, 2).reshape(frames, -1)

    def with_bias(lines_now, vectors):
        return jnp.concatenate([jnp.concatenate(lines_now, axis=0), jnp.concatenate(vectors).reshape(lines, -1)], axis=1)

    bias_up_sum = reorder(sum(r[10][0] for r in results))
    bias_pair = sum(r[11] for r in results)
    early = with_bias([line_sums(r[9]) for r in results], [bias_pair[0], bias_up_sum, bias_pair[1]])
    early_rows = lax.all_gather(early, BOTH, axis=0, tiled=True)

    d_qkv, exchanged = [], []
    for c in range(clips):
        if c == clips - 1:
            active = gate(active, *d_qkv, d_mixed[-1])
            down_parts = columns_grad(active, d_mlp)
            down_core = [swap_bit(p, "clip", 1) for p in down_parts[:3]]
            normed_two = gate(normed_two, down_parts[0])
            up_parts = rows_grad([(normed_two, d_hidden), (mixed_all, d_attn)])
            up_core = [swap_bit(p, "clip", 1) for p in up_parts[:2]]
            down_sent = rounded_sum([down_parts[3], after(down_core[0], up_parts[0])])
            down_along = swap_bit(down_sent, "seq", 1)
            up_sent = rounded_sum([up_parts[2], after(up_core[0], down_sent)])
            up_across = swap_bit(up_sent, "clip", 2)
        grad = after(d_mixed[c], results[-1][8] if c == 0 else up_sent)
        grad = grad.reshape(total, span)
        d_qkv.append(attend_back(qkv[c].reshape(total, 3 * span), grad, fulls[c], logs[c], cos_all, sin_all, span))
        sent = d_qkv[c].reshape(seq_devices, rows, 3 * span)
        exchanged.append(exchange(after(sent, d_mixed[-1]) if c == 0 else after(sent, down_along, up_across)))

    near_seq = axis_bits("seq")[::-1]
    down_along, up_across = after(down_along, exchanged[0]), after(up_across, exchanged[0])
    down_across = swap_bit(rounded_sum([down_parts[5][0], down_core[2][0], down_along[1]]), "clip", 2)

    last = []
    for c in range(clips):
        grads = last[-1][0] if last else None
        if c == clips - 1:
            half = up_parts[3].shape[0] // 2
            theirs = (1 - own_bit(*near_seq[0])) * half
            up_near = rounded_sum(
                [lax.dynamic_slice_in_dim(a, theirs, half, 0) for a in (up_parts[3], up_core[1], up_across)]
            )
            up_near = swap_bit(up_near, *near_seq[0])
            exchanged[-1] = after(exchanged[-1], up_near, down_across)
        last.append(project_back(exchanged[c], full_qkv, tokens, c, mods_one[c][1], results[c][1], grads))
    d_projected = [r[1] for r in last]
    qkv_parts = rows_grad([(normed, d_projected)])
    qkv_core = [swap_bit(p, "clip", 1) for p in qkv_parts[:2]]
    qkv_sent = rounded_sum([qkv_parts[2], qkv_core[0]])
    qkv_across = swap_bit(qkv_sent, "clip", 2)
    qkv_trace = []
    grad_qkv = halve([qkv_parts[3], qkv_core[1], qkv_across], near_seq, 0, qkv_trace)
    near_send = qkv_trace[0][0]
    mine = own_bit(*near_seq[0]) * half
    up_addends = [lax.dynamic_slice_in_dim(a, mine, half, 0) for a in (up_parts[3], up_core[1], up_across)]
    grad_up = halve(up_addends + [after(up_near, near_send)], near_seq[1:], 0)
    down_own = sum(a.astype(f32) for a in (down_parts[4][0], down_core[1][0], down_along[0]))
    grad_down = jnp.transpose(halve([down_own, after(down_across, near_send)], near_seq[1:], 1))
    grad_out = grad_up[:, 4 * width :]
    grad_up = reorder(grad_up[:, : 4 * width])
    late_rows = with_bias([line_sums(r[2]) for r in last], [sum(r[3][0] for r in last)])
    late_rows = collect_rows(after(late_rows, near_send), order)
    early_rows = after(early_rows, qkv_sent)

    def own_columns(sums, shard):
        return lax.dynamic_slice_in_dim(sums, here * shard.shape[0], shard.shape[0], 0)

    def spans(all_rows, columns):
        vectors = jnp.sum(all_rows[:, columns:].reshape(devices, -1), axis=0)
        return all_rows[:, :columns], vectors

    late_mod, late_vectors = spans(late_rows, 2 * width)
    early_mod, early_vectors = spans(early_rows, 4 * width)
    grad_mod = jnp.concatenate(
        [
            lax.dot_general(rows_cond.astype(f32), r, TN, precision=highest, preferred_element_type=f32)
            for rows_cond, r in ((cond_late, late_mod), (cond, early_mod))
        ],
        axis=1,
    )
    mod_sum = jnp.concatenate([jnp.sum(late_mod, axis=0), jnp.sum(early_mod, axis=0)])
    return (
        results[-1][0],
        last[-1][0],
        grad_mod,
        own_columns(mod_sum, mod_bias),
        grad_qkv,
        own_columns(late_vectors, qkv_bias),
        grad_out,
        own_columns(early_vectors[:width], out_bias),
        grad_up,
        own_columns(early_vectors[width : 5 * width], up_bias),
        grad_down,
        own_columns(early_vectors[5 * width :], down_bias),
    )


def body_gathered(
    tokens,
    ctx_count,
    noise_level,
    mod_weight,
    mod_bias,
    qkv_weight,
    qkv_bias,
    out_weight,
    out_bias,
    up_weight,
    up_bias,
    down_weight,
    down_bias,
    cotangent,
):
    clips, rows, width = tokens.shape
    seq_devices = lax.axis_size("seq")
    devices = lax.axis_size("clip") * seq_devices
    bits = mesh_bits()
    here = lax.axis_index("clip") * seq_devices + lax.axis_index("seq")
    total = rows * seq_devices
    frames = max(1, rows // PATCHES)
    patch_rows = rows // frames

    full_qkv = lax.all_gather(qkv_weight, BOTH, axis=0, tiled=True)
    full_out = lax.all_gather(out_weight, BOTH, axis=0, tiled=True)
    full_up = lax.all_gather(up_weight, BOTH, axis=0, tiled=True)
    full_down = lax.all_gather(down_weight, BOTH, axis=0, tiled=True)
    biases = (qkv_bias, out_bias, up_bias, down_bias)
    bias_rows = double_rows(jnp.concatenate(biases).astype(f32), bits)
    full_biases = []
    first = 0
    for piece in biases:
        full_biases.append(bias_rows[:, first : first + piece.shape[0]].reshape(1, -1))
        first += piece.shape[0]
    bias_qkv, bias_out, bias_up, bias_down = full_biases

    levels = level_rows(ctx_count, noise_level, rows)
    cond = condition(levels, here, mod_weight.shape[0], width)
    mod_width = mod_weight.shape[1]
    partial = dot(cond, mod_weight) + own_place(mod_bias, here)
    modulation = halve_sum(partial.reshape(devices, clips * frames, mod_width), bits)
    modulation = modulation.reshape(clips, frames, 1, mod_width)

    positions = lax.axis_index("seq") * rows + jnp.arange(rows, dtype=jnp.int32)
    cosine, sine = rotary_lanes(positions, HEAD_DIM)
    key_frame = jnp.arange(total, dtype=jnp.int32) // PATCHES
    allowed = key_frame[None, :] <= (positions // PATCHES)[:, None]

    def flat(value):
        return value.reshape(rows, value.shape[-1])

    def split(value):
        return value.reshape(frames, patch_rows, value.shape[-1])

    def to_heads(value):
        return value.reshape(rows, HEADS, HEAD_DIM).transpose(1, 0, 2)

    saved = []
    for c in range(clips):
        mods = jnp.split(modulation[c], 6, axis=-1)
        tokens_now = split(tokens[c].astype(f32))
        unit, inverse = norm_parts(tokens_now)
        normed = flat((unit * (1.0 + mods[1]) + mods[0]).astype(bf16))
        projected = dot(normed, full_qkv) + bias_qkv
        views = []
        for place in range(3):
            view = to_heads(projected[:, place * width : (place + 1) * width])
            if place < 2:
                    view = view * cosine + jnp.roll(view, HEAD_DIM // 2, -1) * sine
            views.append(view.astype(bf16))
        queries, keys, values = views
        keys = lax.all_gather(keys, "seq", axis=1, tiled=True)
        values = lax.all_gather(values, "seq", axis=1, tiled=True)
        mix, logs = gathered_forward(queries, keys, values, allowed)
        mixed = mix.transpose(1, 0, 2).reshape(rows, width).astype(bf16)
        kept = (queries, keys, values, logs)
        saved.append((mods, tokens_now, unit, inverse, normed, kept, mixed))

    outputs = []
    middle = []
    for c in range(clips):
        mods, tokens_now, unit, inverse, normed, kept, mixed = saved[c]
        _, _, gate_one, shift_two, scale_two, gate_two = mods
        attn_out = split(dot(mixed, full_out) + bias_out)
        resid = tokens_now + gate_one * attn_out
        unit_two, inverse_two = norm_parts(resid)
        normed_two = flat((unit_two * (1.0 + scale_two) + shift_two).astype(bf16))
        hidden = dot(normed_two, full_up) + bias_up
        active_full, gelu_back = jax.vjp(jax.nn.gelu, hidden)
        active = active_full.astype(bf16)
        mlp_out = split(dot(active, full_down) + bias_down)
        outputs.append(flat((resid + gate_two * mlp_out).astype(bf16)))
        grad_out = split(cotangent[c].astype(f32))
        d_mlp = flat((gate_two * grad_out).astype(bf16))
        d_hidden = gelu_back(dot(d_mlp, full_down, NT))[0].astype(bf16)
        d_normed_two = split(dot(d_hidden, full_up, NT))
        d_resid = grad_out + norm_back(unit_two, inverse_two, d_normed_two, scale_two)
        d_attn = flat((gate_one * d_resid).astype(bf16))
        d_mixed = dot(d_attn, full_out, NT).astype(bf16)
        d_early = jnp.concatenate(
            [
                jnp.sum(d_resid * attn_out, axis=1),
                jnp.sum(d_normed_two, axis=1),
                jnp.sum(d_normed_two * unit_two, axis=1),
                jnp.sum(grad_out * mlp_out, axis=1),
            ],
            axis=-1,
        )
        middle.append((mixed, d_attn, normed_two, d_hidden, active, d_mlp, d_resid, d_mixed, d_early))

    def both(place):
        return jnp.concatenate([m[place] for m in middle], axis=0)

    d_attn_all, d_hidden_all, d_mlp_all = both(1), both(3), both(5)
    grad_down = weight_grad(both(4), d_mlp_all)
    grad_up = weight_grad(both(2), d_hidden_all)
    grad_out_weight = weight_grad(both(0), d_attn_all)
    early_rows = lax.all_gather(both(8), BOTH, axis=0, tiled=True)

    inputs_grad = []
    late = []
    projected_grads = []
    for c in range(clips):
        mods, tokens_now, unit, inverse, normed, kept, mixed = saved[c]
        d_resid, d_mixed = middle[c][6], middle[c][7]
        queries, keys, values, logs = kept
        dq, dk, dv = gathered_back(queries, keys, values, to_heads(d_mixed), logs, allowed)
        dk = lax.psum_scatter(dk.astype(bf16), "seq", scatter_dimension=1, tiled=True).astype(f32)
        dv = lax.psum_scatter(dv.astype(bf16), "seq", scatter_dimension=1, tiled=True).astype(f32)
        views = [g * cosine - jnp.roll(g, HEAD_DIM // 2, -1) * sine for g in (dq, dk)] + [dv]
        d_projected = jnp.concatenate([g.transpose(1, 0, 2).reshape(rows, width) for g in views], axis=1).astype(bf16)
        projected_grads.append(d_projected)
        d_normed = split(dot(d_projected, full_qkv, NT))
        inputs_grad.append(flat(d_resid + norm_back(unit, inverse, d_normed, mods[1])))
        late.append(jnp.concatenate([jnp.sum(d_normed, axis=1), jnp.sum(d_normed * unit, axis=1)], axis=-1))

    d_projected_all = jnp.concatenate(projected_grads, axis=0)
    grad_qkv = weight_grad(jnp.concatenate([s[4] for s in saved], axis=0), d_projected_all)
    bias_grads = [
        jnp.sum(g.astype(f32), axis=0).reshape(devices, -1) for g in (d_projected_all, d_attn_all, d_hidden_all, d_mlp_all)
    ]
    bias_sum = halve_sum(jnp.concatenate(bias_grads, axis=1), bits)
    grad_biases = []
    first = 0
    for piece in bias_grads:
        grad_biases.append(bias_sum[first : first + piece.shape[1]])
        first += piece.shape[1]

    late_rows = double_rows(jnp.concatenate(late, axis=0), bits).reshape(-1, 2 * width)
    grad_mod = jnp.concatenate(
        [
            lax.dot_general(cond.astype(f32), r, TN, precision=highest, preferred_element_type=f32)
            for r in (late_rows, early_rows)
        ],
        axis=1,
    )
    mod_sum = jnp.concatenate([jnp.sum(late_rows, axis=0), jnp.sum(early_rows, axis=0)])
    grad_mod_bias = lax.dynamic_slice_in_dim(mod_sum, here * mod_bias.shape[0], mod_bias.shape[0], 0)
    return (
        jnp.stack(outputs),
        jnp.stack(inputs_grad),
        grad_mod,
        grad_mod_bias,
        grad_qkv,
        grad_biases[0],
        grad_out_weight,
        grad_biases[1],
        grad_up,
        grad_biases[2],
        grad_down,
        grad_biases[3],
    )


def solution(mesh):
    by_heads = HEADS % mesh.shape["seq"] == 0
    body = body_by_heads if by_heads else body_gathered
    token_place = P("clip", "seq", None)
    matrix, vector = P(BOTH, None), P(BOTH)
    weights = (matrix, vector) * 5
    return jax.shard_map(
        body,
        mesh=mesh,
        in_specs=(token_place, P("clip"), P("clip", None)) + weights + (token_place,),
        out_specs=(token_place, token_place) + weights,
        check_vma=False,
    )
```

```python
import functools
import math

import jax
import jax.numpy as jnp
from jax import lax
from jax.experimental import pallas as pl
from jax.experimental.pallas import tpu as pltpu
from jax.sharding import PartitionSpec as P

HEADS = 16
HEAD_DIM = 64
FRAMES = 16
PATCHES = 256
BOTH = ("clip", "seq")
NT = (((1,), (1,)), ((), ()))
NN = (((1,), (0,)), ((), ()))
TN = (((0,), (0,)), ((), ()))
bf16 = jnp.bfloat16
f32 = jnp.float32
highest = lax.Precision.HIGHEST


def dot(left, right, dims=NN):
    return lax.dot_general(left, right, dims, preferred_element_type=f32)


def swap_bit(value, axis, bit):
    count = lax.axis_size(axis)
    return lax.ppermute(value, axis, [(i, i ^ bit) for i in range(count)])


def own_bit(axis, bit):
    return lax.shift_right_logical(lax.axis_index(axis), bit.bit_length() - 1) & 1


def axis_bits(axis):
    bits = []
    bit = 1
    while bit < lax.axis_size(axis):
        bits.append((axis, bit))
        bit *= 2
    return bits[::-1]


def exchange_order(bits):
    return sorted(range(len(bits)), key=lambda place: bits[place])


def mesh_bits():
    return axis_bits("clip") + axis_bits("seq")


def halve_sum(parts, bits, wire=f32, hold=None):
    addends = [parts.reshape((2,) * len(bits) + parts.shape[1:])]
    for place in exchange_order(bits):
        axis, bit = bits[place]
        mine = own_bit(axis, bit)
        send = sum(lax.dynamic_index_in_dim(a, 1 - mine, place).astype(f32) for a in addends)
        addends = [lax.dynamic_index_in_dim(a, mine, place) for a in addends]
        received = swap_bit(send.astype(wire), axis, bit)
        if hold is not None and len(addends) == 1:
            received = after(received, hold)
        addends.append(received)
    total = sum(a.astype(f32) for a in addends)
    return total.reshape(total.shape[len(bits) :])


def near_order():
    return axis_bits("clip")[::-1] + axis_bits("seq")[::-1]


def halve_rows(parts, bits, gates=()):
    for place, (axis, bit) in enumerate(bits):
        half = parts.shape[0] // 2
        mine = own_bit(axis, bit)
        keep = lax.dynamic_slice_in_dim(parts, mine * half, half, 0)
        send = lax.dynamic_slice_in_dim(parts, (1 - mine) * half, half, 0)
        other = swap_bit(send, axis, bit)
        if place < len(gates) and gates[place] is not None:
            other = after(other, gates[place])
        parts = keep + other
    return parts


def collect_rows(rows, bits):
    for axis, bit in reversed(bits):
        rows = jnp.concatenate([rows, swap_bit(rows, axis, bit)], axis=0)
    return rows


def relative_rows(rows, bits):
    shape = rows.shape
    rows = rows.reshape((2,) * len(bits) + (-1,) + shape[1:])
    for place, (axis, bit) in enumerate(bits):
        rows = jnp.where(own_bit(axis, bit) == 0, rows, jnp.flip(rows, place))
    return rows.reshape(shape)


def after(value, *others):
    return lax.optimization_barrier((value,) + others)[0]


def double_rows(row, bits):
    rows = row[None]
    for axis, bit in reversed(bits):
        other = swap_bit(rows, axis, bit)
        low = own_bit(axis, bit) == 0
        rows = jnp.concatenate([jnp.where(low, rows, other), jnp.where(low, other, rows)], axis=0)
    return rows


def weight_grad(left, right):
    tokens, rows = left.shape
    quarter = rows // lax.axis_size("clip")
    mine = lax.axis_index("clip")

    def part(flip):
        piece = lax.dynamic_slice_in_dim(left, (mine ^ flip) * quarter, quarter, 1)
        return dot(piece, right, TN)

    far = swap_bit(part(3).astype(bf16), "clip", 1)
    near = swap_bit(part(1).astype(bf16), "clip", 1)
    across = swap_bit((part(2) + far.astype(f32)).astype(bf16), "clip", 2)
    total = part(0) + near.astype(f32) + across.astype(f32)
    return halve_sum(total.reshape((lax.axis_size("seq"), -1, right.shape[1])), axis_bits("seq"), bf16)


def norm_parts(values):
    centre = values - jnp.mean(values, axis=-1, keepdims=True)
    spread = jnp.mean(centre * centre, axis=-1, keepdims=True)
    inverse = lax.rsqrt(spread + 1e-06)
    return centre * inverse, inverse


def norm_back(unit, inverse, grad, scales):
    scaled = grad * (1.0 + scales)
    mean = jnp.mean(scaled, axis=-1, keepdims=True)
    along = jnp.mean(scaled * unit, axis=-1, keepdims=True)
    return inverse * (scaled - mean - unit * along)


def rotary_lanes(positions, width):
    half = HEAD_DIM // 2
    lane = jnp.arange(width, dtype=jnp.int32) % HEAD_DIM
    freqs = jnp.exp(-math.log(10000.0) * 2.0 * (lane % half).astype(f32) / HEAD_DIM)
    angles = positions.astype(f32)[:, None] * freqs[None, :]
    sign = jnp.where(lane < half, -1.0, 1.0).astype(f32)
    return jnp.cos(angles), jnp.sin(angles) * sign[None, :]


def partner(values):
    width = values.shape[1]
    half = HEAD_DIM // 2
    lane = lax.broadcasted_iota(jnp.int32, (1, width), 1) % HEAD_DIM
    return jnp.where(lane < half, pltpu.roll(values, width - half, 1), pltpu.roll(values, half, 1))


def project_kernel(
    token_ref, mod_ref, wq_ref, wk_ref, wv_ref, bq_ref, bk_ref, bv_ref, cos_ref, sin_ref, out_ref, normed_ref, *, span
):
    frames = mod_ref.shape[1]
    patch = token_ref.shape[0] // frames

    @pl.when(pl.program_id(0) == 0)
    def _():
        for f in range(frames):
            rows = slice(f * patch, (f + 1) * patch)
            unit, _ = norm_parts(token_ref[rows, :].astype(f32))
            normed_ref[rows, :] = (unit * (1.0 + mod_ref[1, f : f + 1, :]) + mod_ref[0, f : f + 1, :]).astype(bf16)

    x = normed_ref[...]
    cosine, sine = cos_ref[...], sin_ref[...]
    groups = wq_ref.shape[1] // span
    for place, (w_ref, b_ref) in enumerate(((wq_ref, bq_ref), (wk_ref, bk_ref), (wv_ref, bv_ref))):
        value = dot(x, w_ref[...]) + b_ref[...]
        if place < 2:
            value = value * cosine + partner(value) * sine
        value = value.astype(bf16)
        for g in range(groups):
            out_ref[g, :, place * span : (place + 1) * span] = value[:, g * span : (g + 1) * span]


def whole_block(shape):
    return pl.BlockSpec(shape, lambda j: (0,) * len(shape))


def column_specs(height, block, steps):
    return [pl.BlockSpec((height, block), functools.partial(lambda p, j: (0, p * steps + j), p)) for p in range(3)]


def clip_block(shape, c):
    return pl.BlockSpec((None,) + shape[1:], lambda j: (c,) + (0,) * (len(shape) - 1))


def project(tokens, c, mods, weight, bias, cosine, sine, groups):
    _, rows, width = tokens.shape
    span = width // groups
    block = max(span, 256)
    per_step = block // span
    steps = groups // per_step
    return pl.pallas_call(
        functools.partial(project_kernel, span=span),
        grid=(steps,),
        in_specs=[clip_block(tokens.shape, c), whole_block(mods.shape)]
        + column_specs(width, block, steps)
        + column_specs(1, block, steps)
        + [whole_block((rows, block))] * 2,
        out_specs=(pl.BlockSpec((per_step, rows, 3 * span), lambda j: (j, 0, 0)), whole_block((rows, width))),
        out_shape=(
            jax.ShapeDtypeStruct((groups, rows, 3 * span), bf16),
            jax.ShapeDtypeStruct((rows, width), bf16),
        ),
        compiler_params=pltpu.CompilerParams(vmem_limit_bytes=32 << 20),
        cost_estimate=pl.CostEstimate(
            flops=6 * rows * width * width, bytes_accessed=6 * width * width + 10 * rows * width, transcendentals=0
        ),
        name="project",
    )(tokens, mods, weight, weight, weight, bias, bias, bias, cosine, sine)


def project_back_kernel(
    back_ref, wq_ref, wk_ref, wv_ref, token_ref, scale_ref, resid_ref, *rest, span
):
    grad_ref, proj_ref, sums_ref, bias_ref, acc_ref = rest[-5:]
    frames = scale_ref.shape[0]
    rows_all, width = token_ref.shape
    patch = rows_all // frames
    step = pl.program_id(0)
    block = wq_ref.shape[1]

    @pl.when(step == 0)
    def _():
        acc_ref[...] = jnp.zeros_like(acc_ref)

    for place, w_ref in enumerate((wq_ref, wk_ref, wv_ref)):
        band = slice(place * span, (place + 1) * span)
        piece = jnp.concatenate([back_ref[g, :, band] for g in range(block // span)], axis=1)
        columns = pl.ds(pl.multiple_of(place * width + step * block, block), block)
        proj_ref[:, columns] = piece
        bias_ref[:, columns] = jnp.sum(piece.astype(f32), axis=0, keepdims=True)
        acc_ref[...] += dot(piece, w_ref[...], NT)

    @pl.when(step == pl.num_programs(0) - 1)
    def _():
        for f in range(frames):
            rows = slice(f * patch, (f + 1) * patch)
            unit, inverse = norm_parts(token_ref[rows, :].astype(f32))
            grad = acc_ref[rows, :]
            grad_ref[rows, :] = resid_ref[rows, :] + norm_back(unit, inverse, grad, scale_ref[f : f + 1, :])
            sums_ref[0, f : f + 1, :] = jnp.sum(grad, axis=0, keepdims=True)
            sums_ref[1, f : f + 1, :] = jnp.sum(grad * unit, axis=0, keepdims=True)


def project_back(back, weight, tokens, c, scales, d_resid, grads):
    groups, rows, _ = back.shape
    width = tokens.shape[2]
    span = width // groups
    block = max(span, 256)
    per_step = block // span
    steps = groups // per_step
    earlier = [] if grads is None else [grads]
    return pl.pallas_call(
        functools.partial(project_back_kernel, span=span),
        grid=(steps,),
        in_specs=[pl.BlockSpec((per_step, rows, 3 * span), lambda j: (j, 0, 0))]
        + column_specs(width, block, steps)
        + [clip_block(tokens.shape, c), whole_block(scales.shape), whole_block((rows, width))]
        + [pl.BlockSpec(memory_space=pl.ANY)] * len(earlier),
        out_specs=(
            clip_block(tokens.shape, c),
            whole_block((rows, 3 * width)),
            whole_block((2,) + scales.shape),
            whole_block((1, 3 * width)),
        ),
        out_shape=(
            jax.ShapeDtypeStruct(tokens.shape, f32),
            jax.ShapeDtypeStruct((rows, 3 * width), bf16),
            jax.ShapeDtypeStruct((2,) + scales.shape, f32),
            jax.ShapeDtypeStruct((1, 3 * width), f32),
        ),
        input_output_aliases={7: 0} if earlier else {},
        scratch_shapes=[pltpu.VMEM((rows, width), f32)],
        compiler_params=pltpu.CompilerParams(vmem_limit_bytes=40 << 20),
        cost_estimate=pl.CostEstimate(
            flops=6 * rows * width * width, bytes_accessed=6 * width * width + 22 * rows * width, transcendentals=0
        ),
        name="project_back",
    )(back, weight, weight, weight, tokens, scales, d_resid, *earlier)


GELU_RATE = math.sqrt(2.0 / math.pi)
GELU_CUBE = 0.044715


def middle_kernel(clip_ref, back_ref, token_ref, cot_ref, mod_ref, bo_ref, bup_ref, bdown_ref, *refs):
    wo_refs, up_refs, down_refs = refs[0:4], refs[4:8], refs[8:12]
    (
        out_ref,
        dres_ref,
        mixed_ref,
        normed_ref,
        act_ref,
        dhid_ref,
        dmlp_ref,
        dattn_ref,
        dmix_ref,
        sums_ref,
        bup_sum_ref,
        bsum_ref,
        attn_ref,
        res_ref,
        mlp_ref,
        dn_ref,
        wo_ref,
        up_ref,
        down_ref,
    ) = refs[-19:]
    groups, rows_all, span = back_ref.shape
    width = token_ref.shape[1]
    quarter = width // 4
    frames = mod_ref.shape[1]
    patch = rows_all // frames
    step = pl.program_id(0)
    mine = clip_ref[0]

    def owner_rows(place):
        return pl.ds(pl.multiple_of((mine ^ FLIPS[place]) * quarter, quarter), quarter)

    @pl.when(step == 0)
    def _():
        for place in range(4):
            wo_ref[owner_rows(place), :] = wo_refs[place][...].reshape(quarter, width)
        for g in range(groups):
            mixed_ref[:, g * span : (g + 1) * span] = back_ref[g]
        attn_ref[...] = dot(mixed_ref[...], wo_ref[...]) + bo_ref[...]
        for f in range(frames):
            rows = slice(f * patch, (f + 1) * patch)
            resid = token_ref[rows, :].astype(f32) + mod_ref[0, f : f + 1, :] * attn_ref[rows, :]
            res_ref[rows, :] = resid
            unit, _ = norm_parts(resid)
            normed_ref[rows, :] = (unit * (1.0 + mod_ref[2, f : f + 1, :]) + mod_ref[1, f : f + 1, :]).astype(bf16)
            dmlp_ref[rows, :] = (mod_ref[3, f : f + 1, :] * cot_ref[rows, :].astype(f32)).astype(bf16)
        mlp_ref[...] = jnp.zeros_like(mlp_ref)
        dn_ref[...] = jnp.zeros_like(dn_ref)

    for place in range(4):
        up_ref[owner_rows(place), :] = up_refs[place][...].reshape(quarter, -1)

        @pl.when(step // 2 == place)
        def _(place=place):
            down_ref[...] = down_refs[place][...].reshape(-1, width)

    up = up_ref[...]
    down = down_ref[...]
    hidden = dot(normed_ref[...], up) + bup_ref[...]
    square = hidden * hidden
    bend = jnp.tanh(GELU_RATE * (hidden + GELU_CUBE * (square * hidden)))
    share = 0.5 * (1.0 + bend)
    active = (hidden * share).astype(bf16)
    act_ref[...] = active
    mlp_ref[...] += dot(active, down)
    slope = share + 0.5 * hidden * (1.0 - bend * bend) * (GELU_RATE + (3.0 * GELU_RATE * GELU_CUBE) * square)
    d_hidden = (dot(dmlp_ref[...], down, NT) * slope).astype(bf16)
    dhid_ref[...] = d_hidden
    bup_sum_ref[...] = jnp.sum(d_hidden.astype(f32), axis=0, keepdims=True)
    dn_ref[...] += dot(d_hidden, up, NT)

    @pl.when(step == pl.num_programs(0) - 1)
    def _():
        bsum = None
        for f in range(frames):
            rows = slice(f * patch, (f + 1) * patch)
            resid = res_ref[rows, :]
            mlp = mlp_ref[rows, :] + bdown_ref[...]
            out_ref[rows, :] = (resid + mod_ref[3, f : f + 1, :] * mlp).astype(bf16)
            cot = cot_ref[rows, :].astype(f32)
            sums_ref[3, f : f + 1, :] = jnp.sum(cot * mlp, axis=0, keepdims=True)
            unit, inverse = norm_parts(resid)
            grad = dn_ref[rows, :]
            sums_ref[1, f : f + 1, :] = jnp.sum(grad, axis=0, keepdims=True)
            sums_ref[2, f : f + 1, :] = jnp.sum(grad * unit, axis=0, keepdims=True)
            d_resid = cot + norm_back(unit, inverse, grad, mod_ref[2, f : f + 1, :])
            dres_ref[rows, :] = d_resid
            sums_ref[0, f : f + 1, :] = jnp.sum(d_resid * attn_ref[rows, :], axis=0, keepdims=True)
            d_attn = (mod_ref[0, f : f + 1, :] * d_resid).astype(bf16)
            dattn_ref[rows, :] = d_attn
            term = jnp.concatenate(
                [
                    jnp.sum(d_attn.astype(f32), axis=0, keepdims=True),
                    jnp.sum(dmlp_ref[rows, :].astype(f32), axis=0, keepdims=True),
                ],
                axis=0,
            )
            bsum = term if bsum is None else bsum + term
        bsum_ref[...] = bsum
        d_mixed = dot(dattn_ref[...], wo_ref[...], NT).astype(bf16)
        for g in range(groups):
            dmix_ref[g] = d_mixed[:, g * span : (g + 1) * span]


FLIPS = (0, 2, 1, 3)


def middle(back, tokens, cot, c, mods, up_shares, down_shares, biases, outputs):
    groups, rows, span = back.shape
    _, _, width = tokens.shape
    high, low, _, piece, _ = up_shares[0].shape
    hidden = 4 * width
    steps = 8
    block = hidden // steps
    bias_out, bias_up, bias_down = biases
    mine = lax.axis_index("clip").astype(jnp.int32)[None]
    earlier = [] if outputs is None else [outputs]

    def fixed(shape, **options):
        return pl.BlockSpec(shape, lambda j, q: (0,) * len(shape), **options)

    def clip_part(shape):
        return pl.BlockSpec((None,) + shape[1:], lambda j, q: (c,) + (0,) * (len(shape) - 1))

    def unit_block(j, q):
        owner = q[0] ^ jnp.where(j // 2 == 1, 2, jnp.where(j // 2 == 2, 1, j // 2))
        return owner, j % 2

    def up_index(j, q):
        owner, half = unit_block(j, q)
        return (0, 0, owner, 0, half)

    def hidden_index(j, q):
        owner, half = unit_block(j, q)
        return (0, owner * 2 + half)

    def down_index(place, j, q):
        return (0, jnp.clip(j - 2 * place, 0, 1), 0, 0, 0)

    token_block = fixed((rows, width))
    hidden_block = pl.BlockSpec((rows, block), hidden_index)
    out_spec = [
        pl.BlockSpec((high, low, 1, piece, width), lambda j, q: (0, 0, 4, 0, 0), pipeline_mode=pl.Buffered(1)) for _ in range(4)
    ]
    up_spec = [pl.BlockSpec((high, low, 1, piece, block), up_index) for _ in range(4)]
    down_spec = [
        pl.BlockSpec((high, 1, 4, piece, width), functools.partial(down_index, place)) for place in range(4)
    ]
    return pl.pallas_call(
        middle_kernel,
        grid_spec=pltpu.PrefetchScalarGridSpec(
            num_scalar_prefetch=1,
            grid=(steps,),
            in_specs=[
                fixed(back.shape),
                clip_part(tokens.shape),
                clip_part(tokens.shape),
                fixed(mods.shape),
                fixed((1, width)),
                pl.BlockSpec((1, block), hidden_index),
                fixed((1, width)),
            ]
            + out_spec
            + up_spec
            + down_spec
            + [pl.BlockSpec(memory_space=pl.ANY)] * len(earlier),
            out_specs=(
                clip_part(tokens.shape),
                token_block,
                token_block,
                token_block,
                hidden_block,
                hidden_block,
                token_block,
                token_block,
                fixed(back.shape),
                fixed(mods.shape),
                pl.BlockSpec((1, block), hidden_index),
                fixed((2, width)),
            ),
            scratch_shapes=[pltpu.VMEM((rows, width), f32)] * 4
            + [pltpu.VMEM((width, width), bf16), pltpu.VMEM((width, block), bf16), pltpu.VMEM((block, width), bf16)],
        ),
        out_shape=(
            jax.ShapeDtypeStruct(tokens.shape, bf16),
            jax.ShapeDtypeStruct((rows, width), f32),
            jax.ShapeDtypeStruct((rows, width), bf16),
            jax.ShapeDtypeStruct((rows, width), bf16),
            jax.ShapeDtypeStruct((rows, hidden), bf16),
            jax.ShapeDtypeStruct((rows, hidden), bf16),
            jax.ShapeDtypeStruct((rows, width), bf16),
            jax.ShapeDtypeStruct((rows, width), bf16),
            jax.ShapeDtypeStruct(back.shape, bf16),
            jax.ShapeDtypeStruct(mods.shape, f32),
            jax.ShapeDtypeStruct((1, hidden), f32),
            jax.ShapeDtypeStruct((2, width), f32),
        ),
        input_output_aliases={20: 0} if earlier else {},
        compiler_params=pltpu.CompilerParams(vmem_limit_bytes=60 << 20),
        cost_estimate=pl.CostEstimate(
            flops=4 * rows * width * width, bytes_accessed=2 * width * width + 5 * rows * width, transcendentals=rows * width
        ),
        name="middle",
    )(mine, back, tokens, cot, mods, bias_out, bias_up, bias_down, *up_shares, *up_shares, *down_shares, *earlier)


def near_place(place, count):
    bits = count.bit_length() - 1
    return sum(((place >> b) & 1) << (bits - 1 - b) for b in range(bits))


def weight_grad_kernel(index_ref, *refs, clips, counts, widths, owners, swapped):
    outs = refs[-1 - len(COLUMN_PLACES if swapped else ROW_FLIPS) : -1]
    flat_ref = refs[-1]
    step = pl.program_id(0)
    first, taken = 0, 0
    for count, steps in zip(counts, widths):
        left, right = refs[taken : taken + clips * count], refs[taken + clips * count : taken + clips * (count + 1)]
        taken += clips * (count + 1)
        rows, height = left[0].shape
        piece = height // owners

        @pl.when(step == first)
        def _(left=left, count=count, rows=rows, height=height, piece=piece):
            for c in range(clips):
                for i in range(count):
                    flat = jnp.transpose(left[c * count + i][...])
                    for owner in range(owners):
                        place = i * height + near_place(owner, owners) * piece
                        flat_ref[place : place + piece, c * rows : (c + 1) * rows] = flat[owner * piece : (owner + 1) * piece]

        @pl.when((step >= first) & (step < first + steps))
        def _(right=right, rows=rows):
            total = dot(flat_ref[:, 0:rows], right[0][...])
            for c in range(1, clips):
                total += dot(flat_ref[:, c * rows : (c + 1) * rows], right[c][...])
            total = total.astype(bf16)
            if swapped:
                for ref, (start, blocks) in zip(outs, COLUMN_PLACES):

                    @pl.when((step >= start) & (step < start + blocks))
                    def _(ref=ref):
                        ref[0] = total

            else:
                height = total.shape[0] // len(outs)
                for place, ref in enumerate(outs):
                    ref[...] = total[place * height : (place + 1) * height]

        first += steps


def weight_grad_call(in_specs, operands, indices, steps, shapes, specs, width, depth, **options):
    return pl.pallas_call(
        functools.partial(weight_grad_kernel, **options),
        grid_spec=pltpu.PrefetchScalarGridSpec(
            num_scalar_prefetch=1,
            grid=(steps,),
            in_specs=in_specs,
            out_specs=specs,
            scratch_shapes=[pltpu.VMEM((width, depth), bf16)],
        ),
        out_shape=tuple(jax.ShapeDtypeStruct(shape, bf16) for shape in shapes),
        compiler_params=pltpu.CompilerParams(vmem_limit_bytes=60 << 20),
        cost_estimate=pl.CostEstimate(
            flops=1024 * steps * width * depth, bytes_accessed=steps * 1024 * (width + depth) + 4 * width * depth, transcendentals=0
        ),
        name="weight_grad",
    )(indices, *operands)


BLOCK = 512
ROW_FLIPS = (3, 1, 2, 0)
COLUMN_PLACES = ((0, 2), (2, 1), (3, 1), (4, 2), (6, 1), (7, 1))


def rows_grad(pairs):
    clips = len(pairs[0][0])
    rows, width = pairs[0][0][0].shape
    height = width // 4
    mine = mine_on("clip")
    widths = [right[0].shape[1] // BLOCK for _, right in pairs]
    in_specs, operands = [], []
    first = 0
    for (left, right), steps in zip(pairs, widths):
        for array in left:
            for i in range(4):
                in_specs.append(pl.BlockSpec((rows, height), functools.partial(lambda i, j, q: (0, q[i]), i)))
                operands.append(array)
        where = functools.partial(lambda first, steps, j, q: (0, jnp.clip(j - first, 0, steps - 1)), first, steps)
        in_specs += [pl.BlockSpec((rows, BLOCK), where)] * clips
        operands += right
        first += steps
    shape = (height, first * BLOCK)
    spec = pl.BlockSpec((height, BLOCK), lambda j, q: (0, j))
    return weight_grad_call(
        in_specs,
        operands,
        jnp.stack([mine ^ flip for flip in ROW_FLIPS]),
        first,
        [shape] * 4,
        [spec] * 4,
        width,
        clips * rows,
        clips=clips,
        counts=[4] * len(pairs),
        widths=widths,
        owners=lax.axis_size("seq"),
        swapped=False,
    )


def columns_grad(left, right):
    clips = len(left)
    rows, width = right[0].shape
    mine, low = mine_on("clip"), mine_on("seq") & 1

    def block(clip_flip, low_flip):
        return (mine ^ clip_flip) * 2 + (low ^ low_flip)

    flips = ((0, 1), (2, 1), (0, 0), (2, 0))
    indices = jnp.stack([block(c ^ 1, s) for c, s in flips] + [block(c, s) for c, s in flips])
    in_specs = [pl.BlockSpec((rows, width), lambda j, q: (0, 0))] * clips
    in_specs += [pl.BlockSpec((rows, BLOCK), lambda j, q: (0, q[j]))] * clips
    def place_index(start, blocks, j, q):
        return (jnp.clip(j - start, 0, blocks - 1), 0, 0)

    return weight_grad_call(
        in_specs,
        right + left,
        indices,
        8,
        [(blocks, width, BLOCK) for _, blocks in COLUMN_PLACES],
        [pl.BlockSpec((1, width, BLOCK), functools.partial(place_index, *place)) for place in COLUMN_PLACES],
        width,
        clips * rows,
        clips=clips,
        counts=[1],
        widths=[8],
        owners=1,
        swapped=True,
    )


def mine_on(axis):
    return lax.axis_index(axis).astype(jnp.int32)


def rounded_sum(addends):
    return sum(a.astype(f32) for a in addends).astype(bf16)


def halve(addends, bits, dim, trace=None):
    for axis, bit in bits:
        half = addends[0].shape[dim] // 2
        mine = own_bit(axis, bit)
        send = rounded_sum([lax.dynamic_slice_in_dim(a, (1 - mine) * half, half, dim) for a in addends])
        addends = [lax.dynamic_slice_in_dim(a, mine * half, half, dim) for a in addends]
        received = swap_bit(send, axis, bit)
        if trace is not None:
            trace.append((send, received))
        addends.append(received)
    return sum(a.astype(f32) for a in addends)


def gate(arrays, *others):
    return list(lax.optimization_barrier((tuple(arrays), others))[0])


def height_of(pairs, parts):
    return pairs[0][0][0].shape[1] // parts


def attend_kernel(qkv_ref, mix_ref, full_ref, log_ref, vt_ref, *, total, span, block):
    heads = span // HEAD_DIM
    head = lax.broadcasted_iota(jnp.int32, (1, span), 1) // HEAD_DIM
    key_frame = lax.broadcasted_iota(jnp.int32, (block, block), 0) // PATCHES
    query_frame = lax.broadcasted_iota(jnp.int32, (block, block), 1) // PATCHES
    kept = key_frame <= query_frame

    def flip(j, carry):
        rows = pl.ds(pl.multiple_of(j * block, block), block)
        vt_ref[:, rows] = jnp.transpose(qkv_ref[rows, 2 * span : 3 * span])
        return carry

    lax.fori_loop(0, total // block, flip, 0)

    def query_block(i, carry):
        rows = pl.ds(pl.multiple_of(i * block, block), block)
        query = qkv_ref[rows, 0:span] * jnp.asarray(HEAD_DIM**-0.5, bf16)
        queries = [jnp.where(head == h, query, jnp.zeros_like(query)) for h in range(heads)]

        def step(j, state, masked):
            peaks, sums, mixes = state
            columns = pl.ds(pl.multiple_of(j * block, block), block)
            key = qkv_ref[columns, span : 2 * span]
            new = ([], [], [])
            for h in range(heads):
                scores = dot(key, queries[h], NT)
                if masked:
                    scores = jnp.where(kept, scores, -1e30)
                peak = jnp.maximum(peaks[h], jnp.max(scores, axis=0, keepdims=True))
                raised = jnp.exp(scores - peak)
                fade = jnp.exp(peaks[h] - peak)
                new[0].append(peak)
                new[1].append(fade * sums[h] + jnp.sum(raised, axis=0, keepdims=True))
                term = dot(vt_ref[h * HEAD_DIM : (h + 1) * HEAD_DIM, columns], raised.astype(bf16))
                new[2].append(mixes[h] * fade + term)
            return tuple(map(tuple, new))

        state = (
            tuple(jnp.full((1, block), -1e30, f32) for _ in range(heads)),
            tuple(jnp.zeros((1, block), f32) for _ in range(heads)),
            tuple(jnp.zeros((HEAD_DIM, block), f32) for _ in range(heads)),
        )
        state = lax.fori_loop(0, i, lambda j, s: step(j, s, False), state)
        peaks, sums, mixes = step(i, state, True)
        mixed = jnp.transpose(jnp.concatenate([mixes[h] / sums[h] for h in range(heads)], axis=0))
        full_ref[rows, :] = mixed
        mix_ref[rows, :] = mixed.astype(bf16)
        for h in range(heads):
            log_ref[h : h + 1, rows] = peaks[h] + jnp.log(sums[h])
        return carry

    lax.fori_loop(0, total // block, query_block, 0)


def attend(qkv, span):
    total = qkv.shape[0]
    heads = span // HEAD_DIM
    block = min(1024, total)
    return pl.pallas_call(
        functools.partial(attend_kernel, total=total, span=span, block=block),
        out_shape=(
            jax.ShapeDtypeStruct((total, span), bf16),
            jax.ShapeDtypeStruct((total, span), f32),
            jax.ShapeDtypeStruct((heads, total), f32),
        ),
        scratch_shapes=[pltpu.VMEM((span, total), bf16)],
        compiler_params=pltpu.CompilerParams(vmem_limit_bytes=60 << 20),
        cost_estimate=pl.CostEstimate(
            flops=8 * total * total * span, bytes_accessed=12 * total * span, transcendentals=total * total * heads // 2
        ),
        name="attend",
    )(qkv)


def attend_back_kernel(
    qkv_ref, grad_ref, full_ref, log_ref, cos_ref, sin_ref, out_ref, dq_ref, dk_ref, dv_ref, along_ref, *, total, span, block
):
    heads = span // HEAD_DIM
    scale = HEAD_DIM**-0.5
    head = lax.broadcasted_iota(jnp.int32, (1, span), 1) // HEAD_DIM
    blocks = total // block
    dq_ref[...] = jnp.zeros_like(dq_ref)

    def only(value, h):
        return jnp.where(head == h, value, jnp.zeros_like(value))

    def lead(i, carry):
        rows = pl.ds(pl.multiple_of(i * block, block), block)
        product = jnp.transpose(grad_ref[rows, :].astype(f32) * full_ref[rows, :])
        for h in range(heads):
            along_ref[h : h + 1, rows] = jnp.sum(product[h * HEAD_DIM : (h + 1) * HEAD_DIM], axis=0, keepdims=True)
        return carry

    lax.fori_loop(0, blocks, lead, 0)

    def key_block(j, carry):
        first = pl.multiple_of(j * block, block)
        columns = pl.ds(first, block)
        key = qkv_ref[columns, span : 2 * span]
        value = qkv_ref[columns, 2 * span : 3 * span]
        key_flat = jnp.transpose(key)
        dk_ref[...] = jnp.zeros_like(dk_ref)
        dv_ref[...] = jnp.zeros_like(dv_ref)

        def tile(rows, keys, h, query_h, grad_h):
            band = slice(h * HEAD_DIM, (h + 1) * HEAD_DIM)
            probs = jnp.exp(dot(key[:keys], query_h, NT) - log_ref[h : h + 1, rows])
            d_probs = dot(value[:keys], grad_h, NT)
            d_scores = (probs * (d_probs - along_ref[h : h + 1, rows])).astype(bf16)
            dq_ref[band, rows] += dot(key_flat[band, :keys], d_scores)
            return dot(probs.astype(bf16), grad_h), dot(d_scores, query_h)

        def heads_of(rows):
            query = qkv_ref[rows, 0:span] * jnp.asarray(scale, bf16)
            grad = grad_ref[rows, :]
            return [(h, only(query, h), only(grad, h)) for h in range(heads)]

        for f in range(block // PATCHES):
            rows = pl.ds(pl.multiple_of(first + f * PATCHES, PATCHES), PATCHES)
            keys = (f + 1) * PATCHES
            for h, query_h, grad_h in heads_of(rows):
                dv, dk = tile(rows, keys, h, query_h, grad_h)
                dv_ref[:keys] += dv
                dk_ref[:keys] += dk

        def later(i, c):
            rows = pl.ds(pl.multiple_of(i * block, block), block)
            terms = [tile(rows, block, h, query_h, grad_h) for h, query_h, grad_h in heads_of(rows)]
            dv_ref[...] += sum(t[0] for t in terms)
            dk_ref[...] += sum(t[1] for t in terms)
            return c

        lax.fori_loop(j + 1, blocks, later, 0)
        dk = dk_ref[...]
        out_ref[columns, span : 2 * span] = (dk * cos_ref[columns, :] - partner(dk) * sin_ref[columns, :]).astype(bf16)
        out_ref[columns, 2 * span : 3 * span] = dv_ref[...].astype(bf16)
        return carry

    lax.fori_loop(0, blocks, key_block, 0)

    def last(i, carry):
        rows = pl.ds(pl.multiple_of(i * block, block), block)
        dq = jnp.transpose(dq_ref[:, rows]) * scale
        out_ref[rows, 0:span] = (dq * cos_ref[rows, :] - partner(dq) * sin_ref[rows, :]).astype(bf16)
        return carry

    lax.fori_loop(0, blocks, last, 0)


def attend_back(qkv, grad, full, logs, cosine, sine, span):
    total = qkv.shape[0]
    heads = span // HEAD_DIM
    block = min(1024, total)
    return pl.pallas_call(
        functools.partial(attend_back_kernel, total=total, span=span, block=block),
        out_shape=jax.ShapeDtypeStruct((total, 3 * span), bf16),
        scratch_shapes=[
            pltpu.VMEM((span, total), f32),
            pltpu.VMEM((block, span), f32),
            pltpu.VMEM((block, span), f32),
            pltpu.VMEM((heads, total), f32),
        ],
        compiler_params=pltpu.CompilerParams(vmem_limit_bytes=60 << 20),
        cost_estimate=pl.CostEstimate(
            flops=20 * total * total * span, bytes_accessed=26 * total * span, transcendentals=total * total * heads // 2
        ),
        name="attend_back",
    )(qkv, grad, full, logs, cosine, sine)


def gathered_forward(queries, keys, values, allowed):
    def one(pieces):
        q, k, v = pieces
        scores = jnp.where(allowed, dot(q, k, NT) * HEAD_DIM**-0.5, -1e30)
        peak = jnp.max(scores, axis=-1, keepdims=True)
        raised = jnp.exp(scores - peak)
        totals = jnp.sum(raised, axis=-1, keepdims=True)
        return dot((raised / totals).astype(bf16), v), peak + jnp.log(totals)

    return lax.map(one, (queries, keys, values))


def gathered_back(queries, keys, values, grads, logs, allowed):
    scale = HEAD_DIM**-0.5

    def one(pieces):
        q, k, v, grad, log = pieces
        scores = jnp.where(allowed, dot(q, k, NT) * scale, -1e30)
        probs = jnp.exp(scores - log)
        d_probs = dot(grad, v, NT)
        centre = jnp.sum(probs * d_probs, axis=-1, keepdims=True)
        d_scores = (probs * (d_probs - centre)).astype(bf16)
        dv = dot(probs.astype(bf16), grad, TN)
        return dot(d_scores, k) * scale, dot(d_scores, q, TN) * scale, dv

    return lax.map(one, (queries, keys, values, grads, logs))


def level_rows(ctx_count, noise_level, rows):
    clips = ctx_count.shape[0]
    seq_devices = lax.axis_size("seq")
    plan = jnp.concatenate([ctx_count[:, None], noise_level], axis=1)
    plan = double_rows(plan, axis_bits("clip"))
    levels = jnp.where(jnp.arange(FRAMES, dtype=jnp.int32) < plan[..., :1], 0, plan[..., 1:])
    if rows < PATCHES:
        levels = jnp.repeat(levels, PATCHES // rows, axis=-1)
    frames = max(1, rows // PATCHES)
    levels = levels.reshape(-1, clips, seq_devices, frames).transpose(0, 2, 1, 3)
    return levels.reshape(-1, seq_devices, clips * frames)


def condition(levels, here, depth, width):
    half_width = width // 2
    feature = here * depth + jnp.arange(depth, dtype=jnp.int32)
    low_half = feature < half_width
    freqs = jnp.exp(-math.log(10000.0) * jnp.where(low_half, feature, feature - half_width).astype(f32) / half_width)
    angles = levels.reshape(-1, 1).astype(f32) * freqs
    return jax.nn.silu(jnp.where(low_half, jnp.sin(angles), jnp.cos(angles))).astype(bf16)


def own_place(shard, here):
    count = lax.axis_size("clip") * lax.axis_size("seq")
    whole = jnp.zeros((count * shard.shape[0],), f32)
    return lax.dynamic_update_slice_in_dim(whole, shard.astype(f32), here * shard.shape[0], 0)


def body_by_heads(
    tokens,
    ctx_count,
    noise_level,
    mod_weight,
    mod_bias,
    qkv_weight,
    qkv_bias,
    out_weight,
    out_bias,
    up_weight,
    up_bias,
    down_weight,
    down_bias,
    cotangent,
):
    clips, rows, width = tokens.shape
    seq_devices = lax.axis_size("seq")
    devices = lax.axis_size("clip") * seq_devices
    order = near_order()
    here = lax.axis_index("clip") * seq_devices + lax.axis_index("seq")
    total = rows * seq_devices
    frames = max(1, rows // PATCHES)
    span = width // seq_devices
    lines = clips * frames
    piece = out_weight.shape[0]

    full_qkv = lax.all_gather(qkv_weight, BOTH, axis=0, tiled=True)
    unit = down_weight.shape[0]
    seq_bits = len(axis_bits("seq"))
    owners = (4,) + (2,) * seq_bits + (unit,)
    by_nearness = (0,) + tuple(range(1, seq_bits + 1))[::-1] + (seq_bits + 1,)

    def reorder(vectors):
        lead = vectors.shape[:-1]
        turn = tuple(range(len(lead))) + tuple(len(lead) + d for d in by_nearness)
        return vectors.reshape(lead + owners).transpose(turn).reshape(vectors.shape)

    down_shard = down_weight.reshape(4, piece, width)
    up_shard = reorder(up_weight).reshape(piece, 4, width).transpose(1, 0, 2)
    up_shard = jnp.concatenate([up_shard, out_weight[None]], axis=0)

    levels = level_rows(ctx_count, noise_level, rows)
    flat_bits = (2,) * len(order)
    bits_clip, bits_seq = len(axis_bits("clip")), len(axis_bits("seq"))
    turn = tuple(range(bits_clip))[::-1] + tuple(range(bits_clip, bits_clip + bits_seq))[::-1] + (len(order),)
    near_levels = levels.reshape(flat_bits + (lines,)).transpose(turn)
    cond_near = condition(near_levels, here, mod_weight.shape[0], width)
    cond = condition(levels, here, mod_weight.shape[0], width)
    cond_late = relative_rows(cond_near, order)
    mod_place = own_place(mod_bias, here)

    def modulate(columns, biases, gates=()):
        weight = mod_weight[:, columns]
        bias = jnp.concatenate([own_place(b, here) for b in biases]).reshape(lines, -1)
        rest = jnp.concatenate([jnp.broadcast_to(mod_place[columns], (lines, weight.shape[1])), bias], axis=1)
        part = jnp.pad(dot(cond_near, weight), ((0, 0), (0, bias.shape[1])))
        line_rows = halve_rows((part.reshape(devices, lines, -1) + rest).reshape(devices * lines, -1), order, gates)
        return line_rows[:, : weight.shape[1]], line_rows[:, weight.shape[1] :].reshape(1, -1)

    def blocks(line_rows):
        return line_rows.reshape(clips, frames, -1, width).transpose(0, 2, 1, 3)

    mod_first, bias_qkv = modulate(slice(0, 2 * width), (qkv_bias,))
    mods_one = blocks(mod_first)

    positions = lax.axis_index("seq") * rows + jnp.arange(rows, dtype=jnp.int32)
    cos_local, sin_local = rotary_lanes(positions, max(span, 256))
    cos_row, sin_row = rotary_lanes(jnp.arange(rows, dtype=jnp.int32), span)
    cos_far, sin_far = rotary_lanes(jnp.arange(seq_devices, dtype=jnp.int32) * rows, span)
    cos_all = (cos_far[:, None] * cos_row[None] - sin_far[:, None] * sin_row[None]).reshape(total, span)
    sin_all = (sin_far[:, None] * cos_row[None] + cos_far[:, None] * sin_row[None]).reshape(total, span)

    def exchange(value):
        return lax.all_to_all(value, "seq", 0, 0, tiled=True)

    def doubled(share, axis, bit, dim=1):
        other = swap_bit(share, axis, bit)
        mine = own_bit(axis, bit) == 0
        pair = jnp.stack([jnp.where(mine, share, other), jnp.where(mine, other, share)], axis=dim)
        return pair.reshape((-1,) + share.shape[1:])

    high_bits, low_bit = axis_bits("seq")[:-1], axis_bits("seq")[-1]
    down_share, up_share = down_shard[None], up_shard[None]
    for axis, bit in high_bits:
        down_share, up_share = doubled(down_share, axis, bit, 0), doubled(up_share, axis, bit)
    full_qkv = after(full_qkv, down_share, up_share)
    up_pair = (up_share, swap_bit(up_share, "clip", 2))
    down_share = doubled(down_share, *low_bit)

    normed, qkv, mixes, fulls, logs, sents = [], [], [], [], [], []
    for c in range(clips):
        weight = full_qkv if c == 0 else after(full_qkv, down_share, up_pair[1])
        sent, normed_c = project(tokens, c, mods_one[c], weight, bias_qkv, cos_local, sin_local, seq_devices)
        normed.append(normed_c)
        if qkv:
            sent = after(sent, qkv[-1])
        qkv.append(exchange(sent))
    backs = []
    for c in range(clips):
        mix, full, log = attend(qkv[c].reshape(total, 3 * span), span)
        mixes.append(mix)
        fulls.append(full)
        logs.append(log)
        backs.append(exchange(after(mix.reshape(seq_devices, rows, span), qkv[-1] if c == 0 else backs[-1])))

    mod_rest, bias_rest = modulate(
        slice(2 * width, 6 * width), (out_bias, up_bias, down_bias), (None, None, normed[-1], mixes[0], mixes[-1])
    )
    mods_two = blocks(mod_rest)
    bias_out = bias_rest[:, :width]
    bias_up = reorder(bias_rest[:, width : 5 * width])
    bias_down = bias_rest[:, 5 * width :]
    def from_clips(pair):
        near, across = [p.reshape((seq_devices // 2, 2) + p.shape[1:]) for p in pair]
        far = swap_bit(after(across, qkv[-1]), "clip", 1)
        return (near, across, swap_bit(near, "clip", 1), far)

    down_shares = from_clips((down_share, swap_bit(down_share, "clip", 2)))
    up_shares = from_clips([doubled(p, *low_bit) for p in up_pair])

    results = []
    d_mixed = []
    for c in range(clips):
        back = after(backs[c], mixes[-1])
        outputs = results[-1][0] if results else None
        results.append(middle(back, tokens, cotangent, c, mods_two[c], up_shares, down_shares, (bias_out, bias_up, bias_down), outputs))
        d_mixed.append(exchange(after(results[c][8], backs[-1] if c == 0 else d_mixed[-1])))

    def late(place):
        return [r[place] for r in results]

    mixed_all, normed_two, active, d_hidden, d_mlp, d_attn = [late(place) for place in (2, 3, 4, 5, 6, 7)]
    def line_sums(sums):
        return sums.transpose(1, 0, 2).reshape(frames, -1)

    def with_bias(lines_now, vectors):
        return jnp.concatenate([jnp.concatenate(lines_now, axis=0), jnp.concatenate(vectors).reshape(lines, -1)], axis=1)

    bias_up_sum = reorder(sum(r[10][0] for r in results))
    bias_pair = sum(r[11] for r in results)
    early = with_bias([line_sums(r[9]) for r in results], [bias_pair[0], bias_up_sum, bias_pair[1]])
    early_rows = lax.all_gather(early, BOTH, axis=0, tiled=True)

    d_qkv, exchanged = [], []
    for c in range(clips):
        if c == clips - 1:
            normed_two = gate(normed_two, *d_qkv, d_mixed[-1])
            up_parts = rows_grad([(normed_two, d_hidden), (mixed_all, d_attn)])
            up_core = [swap_bit(p, "clip", 1) for p in up_parts[:2]]
            up_sent = rounded_sum([up_parts[2], up_core[0]])
            up_across = swap_bit(up_sent, "clip", 2)
        grad = after(d_mixed[c], results[-1][8] if c == 0 else up_sent)
        grad = grad.reshape(total, span)
        d_qkv.append(attend_back(qkv[c].reshape(total, 3 * span), grad, fulls[c], logs[c], cos_all, sin_all, span))
        sent = d_qkv[c].reshape(seq_devices, rows, 3 * span)
        exchanged.append(exchange(after(sent, d_mixed[-1]) if c == 0 else after(sent, up_across)))

    near_seq = axis_bits("seq")[::-1]
    half = up_parts[3].shape[0] // 2
    mine = own_bit(*near_seq[0])
    up_across = after(up_across, exchanged[0])
    up_addends = [up_parts[3], up_core[1], up_across]
    up_near_sent = rounded_sum([lax.dynamic_slice_in_dim(a, (1 - mine) * half, half, 0) for a in up_addends])
    up_near = after(swap_bit(up_near_sent, *near_seq[0]), exchanged[-1])
    active = gate(active, d_qkv[-1], up_near_sent)
    down_parts = columns_grad(active, d_mlp)
    exchanged[0] = after(exchanged[0], down_parts[0])
    down_core = [after(swap_bit(p, "clip", 1), exchanged[-1]) for p in down_parts[:3]]

    last = []
    for c in range(clips):
        grads = last[-1][0] if last else None
        last.append(project_back(exchanged[c], full_qkv, tokens, c, mods_one[c][1], results[c][1], grads))
    d_projected = [r[1] for r in last]
    qkv_parts = rows_grad([(normed, d_projected)])
    qkv_core = [swap_bit(p, "clip", 1) for p in qkv_parts[:2]]
    down_sent = rounded_sum([down_parts[3], after(down_core[0], qkv_parts[0])])
    down_along = swap_bit(down_sent, "seq", 1)
    qkv_sent = rounded_sum([qkv_parts[2], qkv_core[0]])
    qkv_across = swap_bit(qkv_sent, "clip", 2)
    up_own = [lax.dynamic_slice_in_dim(a, mine * half, half, 0) for a in up_addends]
    grad_up = halve(up_own + [after(up_near, qkv_sent)], near_seq[1:], 0)
    qkv_trace = []
    grad_qkv = halve([qkv_parts[3], qkv_core[1], qkv_across], near_seq, 0, qkv_trace)
    near_send = qkv_trace[0][0]
    down_along = after(down_along, near_send)
    down_far = rounded_sum([down_parts[5][0], down_core[2][0], down_along[1]])
    down_across = swap_bit(down_far, "clip", 2)
    down_own = sum(a.astype(f32) for a in (down_parts[4][0], down_core[1][0], down_along[0]))
    grad_down = jnp.transpose(halve([down_own, down_across], near_seq[1:], 1))
    grad_out = grad_up[:, 4 * width :]
    grad_up = reorder(grad_up[:, : 4 * width])
    late_rows = with_bias([line_sums(r[2]) for r in last], [sum(r[3][0] for r in last)])
    late_rows = collect_rows(after(late_rows, near_send), order)
    early_rows = after(early_rows, qkv_sent)

    def own_columns(sums, shard):
        return lax.dynamic_slice_in_dim(sums, here * shard.shape[0], shard.shape[0], 0)

    def spans(all_rows, columns):
        vectors = jnp.sum(all_rows[:, columns:].reshape(devices, -1), axis=0)
        return all_rows[:, :columns], vectors

    late_mod, late_vectors = spans(late_rows, 2 * width)
    early_mod, early_vectors = spans(early_rows, 4 * width)
    grad_mod = jnp.concatenate(
        [
            lax.dot_general(rows_cond.astype(f32), r, TN, precision=highest, preferred_element_type=f32)
            for rows_cond, r in ((cond_late, late_mod), (cond, early_mod))
        ],
        axis=1,
    )
    mod_sum = jnp.concatenate([jnp.sum(late_mod, axis=0), jnp.sum(early_mod, axis=0)])
    return (
        results[-1][0],
        last[-1][0],
        grad_mod,
        own_columns(mod_sum, mod_bias),
        grad_qkv,
        own_columns(late_vectors, qkv_bias),
        grad_out,
        own_columns(early_vectors[:width], out_bias),
        grad_up,
        own_columns(early_vectors[width : 5 * width], up_bias),
        grad_down,
        own_columns(early_vectors[5 * width :], down_bias),
    )


def body_gathered(
    tokens,
    ctx_count,
    noise_level,
    mod_weight,
    mod_bias,
    qkv_weight,
    qkv_bias,
    out_weight,
    out_bias,
    up_weight,
    up_bias,
    down_weight,
    down_bias,
    cotangent,
):
    clips, rows, width = tokens.shape
    seq_devices = lax.axis_size("seq")
    devices = lax.axis_size("clip") * seq_devices
    bits = mesh_bits()
    here = lax.axis_index("clip") * seq_devices + lax.axis_index("seq")
    total = rows * seq_devices
    frames = max(1, rows // PATCHES)
    patch_rows = rows // frames

    full_qkv = lax.all_gather(qkv_weight, BOTH, axis=0, tiled=True)
    full_out = lax.all_gather(out_weight, BOTH, axis=0, tiled=True)
    full_up = lax.all_gather(up_weight, BOTH, axis=0, tiled=True)
    full_down = lax.all_gather(down_weight, BOTH, axis=0, tiled=True)
    biases = (qkv_bias, out_bias, up_bias, down_bias)
    bias_rows = double_rows(jnp.concatenate(biases).astype(f32), bits)
    full_biases = []
    first = 0
    for piece in biases:
        full_biases.append(bias_rows[:, first : first + piece.shape[0]].reshape(1, -1))
        first += piece.shape[0]
    bias_qkv, bias_out, bias_up, bias_down = full_biases

    levels = level_rows(ctx_count, noise_level, rows)
    cond = condition(levels, here, mod_weight.shape[0], width)
    mod_width = mod_weight.shape[1]
    partial = dot(cond, mod_weight) + own_place(mod_bias, here)
    modulation = halve_sum(partial.reshape(devices, clips * frames, mod_width), bits)
    modulation = modulation.reshape(clips, frames, 1, mod_width)

    positions = lax.axis_index("seq") * rows + jnp.arange(rows, dtype=jnp.int32)
    cosine, sine = rotary_lanes(positions, HEAD_DIM)
    key_frame = jnp.arange(total, dtype=jnp.int32) // PATCHES
    allowed = key_frame[None, :] <= (positions // PATCHES)[:, None]

    def flat(value):
        return value.reshape(rows, value.shape[-1])

    def split(value):
        return value.reshape(frames, patch_rows, value.shape[-1])

    def to_heads(value):
        return value.reshape(rows, HEADS, HEAD_DIM).transpose(1, 0, 2)

    saved = []
    for c in range(clips):
        mods = jnp.split(modulation[c], 6, axis=-1)
        tokens_now = split(tokens[c].astype(f32))
        unit, inverse = norm_parts(tokens_now)
        normed = flat((unit * (1.0 + mods[1]) + mods[0]).astype(bf16))
        projected = dot(normed, full_qkv) + bias_qkv
        views = []
        for place in range(3):
            view = to_heads(projected[:, place * width : (place + 1) * width])
            if place < 2:
                    view = view * cosine + jnp.roll(view, HEAD_DIM // 2, -1) * sine
            views.append(view.astype(bf16))
        queries, keys, values = views
        keys = lax.all_gather(keys, "seq", axis=1, tiled=True)
        values = lax.all_gather(values, "seq", axis=1, tiled=True)
        mix, logs = gathered_forward(queries, keys, values, allowed)
        mixed = mix.transpose(1, 0, 2).reshape(rows, width).astype(bf16)
        kept = (queries, keys, values, logs)
        saved.append((mods, tokens_now, unit, inverse, normed, kept, mixed))

    outputs = []
    middle = []
    for c in range(clips):
        mods, tokens_now, unit, inverse, normed, kept, mixed = saved[c]
        _, _, gate_one, shift_two, scale_two, gate_two = mods
        attn_out = split(dot(mixed, full_out) + bias_out)
        resid = tokens_now + gate_one * attn_out
        unit_two, inverse_two = norm_parts(resid)
        normed_two = flat((unit_two * (1.0 + scale_two) + shift_two).astype(bf16))
        hidden = dot(normed_two, full_up) + bias_up
        active_full, gelu_back = jax.vjp(jax.nn.gelu, hidden)
        active = active_full.astype(bf16)
        mlp_out = split(dot(active, full_down) + bias_down)
        outputs.append(flat((resid + gate_two * mlp_out).astype(bf16)))
        grad_out = split(cotangent[c].astype(f32))
        d_mlp = flat((gate_two * grad_out).astype(bf16))
        d_hidden = gelu_back(dot(d_mlp, full_down, NT))[0].astype(bf16)
        d_normed_two = split(dot(d_hidden, full_up, NT))
        d_resid = grad_out + norm_back(unit_two, inverse_two, d_normed_two, scale_two)
        d_attn = flat((gate_one * d_resid).astype(bf16))
        d_mixed = dot(d_attn, full_out, NT).astype(bf16)
        d_early = jnp.concatenate(
            [
                jnp.sum(d_resid * attn_out, axis=1),
                jnp.sum(d_normed_two, axis=1),
                jnp.sum(d_normed_two * unit_two, axis=1),
                jnp.sum(grad_out * mlp_out, axis=1),
            ],
            axis=-1,
        )
        middle.append((mixed, d_attn, normed_two, d_hidden, active, d_mlp, d_resid, d_mixed, d_early))

    def both(place):
        return jnp.concatenate([m[place] for m in middle], axis=0)

    d_attn_all, d_hidden_all, d_mlp_all = both(1), both(3), both(5)
    grad_down = weight_grad(both(4), d_mlp_all)
    grad_up = weight_grad(both(2), d_hidden_all)
    grad_out_weight = weight_grad(both(0), d_attn_all)
    early_rows = lax.all_gather(both(8), BOTH, axis=0, tiled=True)

    inputs_grad = []
    late = []
    projected_grads = []
    for c in range(clips):
        mods, tokens_now, unit, inverse, normed, kept, mixed = saved[c]
        d_resid, d_mixed = middle[c][6], middle[c][7]
        queries, keys, values, logs = kept
        dq, dk, dv = gathered_back(queries, keys, values, to_heads(d_mixed), logs, allowed)
        dk = lax.psum_scatter(dk.astype(bf16), "seq", scatter_dimension=1, tiled=True).astype(f32)
        dv = lax.psum_scatter(dv.astype(bf16), "seq", scatter_dimension=1, tiled=True).astype(f32)
        views = [g * cosine - jnp.roll(g, HEAD_DIM // 2, -1) * sine for g in (dq, dk)] + [dv]
        d_projected = jnp.concatenate([g.transpose(1, 0, 2).reshape(rows, width) for g in views], axis=1).astype(bf16)
        projected_grads.append(d_projected)
        d_normed = split(dot(d_projected, full_qkv, NT))
        inputs_grad.append(flat(d_resid + norm_back(unit, inverse, d_normed, mods[1])))
        late.append(jnp.concatenate([jnp.sum(d_normed, axis=1), jnp.sum(d_normed * unit, axis=1)], axis=-1))

    d_projected_all = jnp.concatenate(projected_grads, axis=0)
    grad_qkv = weight_grad(jnp.concatenate([s[4] for s in saved], axis=0), d_projected_all)
    bias_grads = [
        jnp.sum(g.astype(f32), axis=0).reshape(devices, -1) for g in (d_projected_all, d_attn_all, d_hidden_all, d_mlp_all)
    ]
    bias_sum = halve_sum(jnp.concatenate(bias_grads, axis=1), bits)
    grad_biases = []
    first = 0
    for piece in bias_grads:
        grad_biases.append(bias_sum[first : first + piece.shape[1]])
        first += piece.shape[1]

    late_rows = double_rows(jnp.concatenate(late, axis=0), bits).reshape(-1, 2 * width)
    grad_mod = jnp.concatenate(
        [
            lax.dot_general(cond.astype(f32), r, TN, precision=highest, preferred_element_type=f32)
            for r in (late_rows, early_rows)
        ],
        axis=1,
    )
    mod_sum = jnp.concatenate([jnp.sum(late_rows, axis=0), jnp.sum(early_rows, axis=0)])
    grad_mod_bias = lax.dynamic_slice_in_dim(mod_sum, here * mod_bias.shape[0], mod_bias.shape[0], 0)
    return (
        jnp.stack(outputs),
        jnp.stack(inputs_grad),
        grad_mod,
        grad_mod_bias,
        grad_qkv,
        grad_biases[0],
        grad_out_weight,
        grad_biases[1],
        grad_up,
        grad_biases[2],
        grad_down,
        grad_biases[3],
    )


def solution(mesh):
    by_heads = HEADS % mesh.shape["seq"] == 0
    body = body_by_heads if by_heads else body_gathered
    token_place = P("clip", "seq", None)
    matrix, vector = P(BOTH, None), P(BOTH)
    weights = (matrix, vector) * 5
    return jax.shard_map(
        body,
        mesh=mesh,
        in_specs=(token_place, P("clip"), P("clip", None)) + weights + (token_place,),
        out_specs=(token_place, token_place) + weights,
        check_vma=False,
    )
```
